128 devices in a mesh: shot: 4 (over z), row: 8 (over x, y_lo), col: 4 (over y_hi, core).
Axes of the slice: x: 4, y: 4 (y_hi: 2, y_lo: 2; y = y_hi * 2 + y_lo), z: 4, core: 2. Of those that a mesh axis runs over, the one named last changes fastest.
Arguments:
- velocity: float32 [256, 256, 384], P(('row', 'shot'), 'col'), may hold values from 1.5 to 4.5
- momentum: float32 [256, 256, 384], P(('row', 'shot'), 'col'), may hold values from -6 to 6
- mass_diag: float32 [256, 256, 384], P(('row', 'shot'), 'col'), may hold values from 0.5 to 2
- u_prev: float32 [4, 256, 256, 384], P('shot', 'row', 'col'), may hold values from -6 to 6
- u_cur: float32 [4, 256, 256, 384], P('shot', 'row', 'col'), may hold values from -6 to 6
- adj_next: float32 [4, 256, 256, 384], P('shot', 'row', 'col'), may hold values from -6 to 6
- adj_cur: float32 [4, 256, 256, 384], P('shot', 'row', 'col'), may hold values from -6 to 6
- observed: float32 [4, 2, 256, 256], P('shot', None, 'row', 'col'), may hold values from -6 to 6
- rec_depth: int32 [4, 256, 256], P('shot', 'row', 'col'), may hold values from 0 to 383
- src_cell: int32 [4, 3], P('shot'), may hold values from 0 to 255
- wavelet: float32 [4, 2], P('shot'), may hold values from -60 to 60
Outputs:
- v_new: float32 [256, 256, 384], P(('row', 'shot'), 'col')
- p_half: float32 [256, 256, 384], P(('row', 'shot'), 'col')
The draws below stay inside these ranges and needn't reach their ends.
All inputs are finite; a program needn't handle non-finite values.
Results may differ from the reference program's by a relative error of at most 0.0001.
Values sent between devices are 32-bit elements; how exact they have to be, the bound alone decides.
A program may use at most 128 MiB of HBM per device.

```python
import math
import jax
import jax.numpy as jnp
from jax import lax

NZ = 384
SHOTS = 4
NX = 256
NY = 256


def plant(entries, stream_key, low, largest):
    index_at = [jax.random.randint(jax.random.fold_in(stream_key, axis), (), 0, length) for axis, length in enumerate(entries.shape)]
    longest = entries.shape.index(max(entries.shape))
    beside = index_at[:longest] + [(index_at[longest] + 1) % entries.shape[longest]] + index_at[longest + 1:]
    return entries.at[tuple(index_at)].set(low).at[tuple(beside)].set(largest)


def level_of(own_key, dims, cuts, smallest, high):
    gain, own = 1.0, jax.random.fold_in(own_key, 6)
    for axis_at, shards_of in cuts:
        draws = jnp.exp(jax.random.uniform(jax.random.fold_in(own, axis_at), (shards_of,), jnp.float32, smallest / len(cuts), high / len(cuts)))
        gain = gain * jnp.repeat(draws, dims[axis_at] // shards_of).reshape([-1 if axis == axis_at else 1 for axis in range(len(dims))])
    return gain


def scatter_about(rng, shape, spread, bound, split=(), held_as=jnp.bfloat16):
    values = jax.random.normal(rng, shape, jnp.float32) * spread
    if len(split) > 0:
        values = level_of(rng, shape, split, -0.22, 0.18) * values
    return jnp.clip(values, min=-bound, max=bound).astype(held_as)


def setup_inputs(seed: int = 0) -> dict:
    key_of = jax.random.split(jax.random.key(seed), 12)
    velocity = jnp.clip(1.5 + 3.0 * jax.random.uniform(key_of[0], (NX, NY, NZ), jnp.float32) ** level_of(key_of[0], (NX, NY, NZ), ((0, 32), (1, 4)), -0.2, 0.2), 1.5, 4.5)
    momentum = scatter_about(key_of[1], (NX, NY, NZ), 1.0, 6.0, ((0, 32), (1, 4)), jnp.float32)
    mass_diag = jnp.clip(jnp.exp(math.log(2.0) - 1.3862944 * jax.random.uniform(key_of[2], (NX, NY, NZ), jnp.float32) ** level_of(key_of[2], (NX, NY, NZ), ((0, 32), (1, 4)), -0.2, 0.2)), 0.5, 2.0)
    u_prev = scatter_about(key_of[3], (SHOTS, NX, NY, NZ), 1.0, 6.0, ((0, 4), (1, 8), (2, 4)), jnp.float32)
    u_cur = scatter_about(key_of[4], (SHOTS, NX, NY, NZ), 1.0, 6.0, ((0, 4), (1, 8), (2, 4)), jnp.float32)
    adj_next = scatter_about(key_of[5], (SHOTS, NX, NY, NZ), 1.0, 6.0, ((0, 4), (1, 8), (2, 4)), jnp.float32)
    adj_cur = scatter_about(key_of[6], (SHOTS, NX, NY, NZ), 1.0, 6.0, ((0, 4), (1, 8), (2, 4)), jnp.float32)
    observed = scatter_about(key_of[7], (SHOTS, 2, NX, NY), 1.0, 6.0, ((0, 4), (2, 8), (3, 4)), jnp.float32)
    rec_depth = plant(jax.random.randint(key_of[8], (SHOTS, NX, NY), 0, NZ), jax.random.fold_in(key_of[8], 1), 0, NZ - 1).astype(jnp.int32)
    src_cell = plant(jax.random.randint(key_of[9], (SHOTS, 3), 0, min(min(NX, NY), NZ)), jax.random.fold_in(key_of[9], 1), 0, (min(min(NX, NY), NZ)) - 1).astype(jnp.int32)
    wavelet = scatter_about(key_of[10], (SHOTS, 2), 10.0, 60.0, ((0, 4),), jnp.float32)
    return {"velocity": velocity, "momentum": momentum, "mass_diag": mass_diag, "u_prev": u_prev, "u_cur": u_cur, "adj_next": adj_next, "adj_cur": adj_cur, "observed": observed, "rec_depth": rec_depth, "src_cell": src_cell, "wavelet": wavelet}


STENCIL = (-205.0 / 72.0, 8.0 / 5.0, -1.0 / 5.0, 8.0 / 315.0, -1.0 / 560.0)
squared_courant = 0.012
leap_step = 0.2


def laplace(field):
    padded = jnp.pad(field, 4)
    row_count, col_count, depth_cells = field.shape
    center = padded[4:4 + row_count, 4:4 + col_count, 4:4 + depth_cells]
    result = (3.0 * STENCIL[0]) * center
    for offset in range(1, 5):
        along = padded[4 + offset:4 + offset + row_count, 4:4 + col_count, 4:4 + depth_cells] + padded[4 - offset:4 - offset + row_count, 4:4 + col_count, 4:4 + depth_cells]
        along = along + padded[4:4 + row_count, 4 + offset:4 + offset + col_count, 4:4 + depth_cells] + padded[4:4 + row_count, 4 - offset:4 - offset + col_count, 4:4 + depth_cells]
        along = along + padded[4:4 + row_count, 4:4 + col_count, 4 + offset:4 + offset + depth_cells] + padded[4:4 + row_count, 4:4 + col_count, 4 - offset:4 - offset + depth_cells]
        result = result + STENCIL[offset] * along
    return result


def reference(velocity, momentum, mass_diag, u_prev, u_cur, adj_next, adj_cur, observed, rec_depth, src_cell, wavelet):
    stiffness = squared_courant * velocity * velocity
    x_index = lax.iota(jnp.int32, NX)
    y_index = lax.iota(jnp.int32, NY)
    z_index = lax.iota(jnp.int32, NZ)
    summed = jnp.zeros((NX, NY, NZ), jnp.float32)
    for shot_index in range(SHOTS):
        oldest = u_prev[shot_index]
        present = u_cur[shot_index]
        cell = src_cell[shot_index]
        source_mask = ((x_index == cell[0])[:, None, None] & (y_index == cell[1])[None, :, None] & (z_index == cell[2])[None, None, :]).astype(jnp.float32)
        advanced = 2.0 * present - oldest + stiffness * laplace(present) + wavelet[shot_index, 0] * source_mask
        farthest = 2.0 * advanced - present + stiffness * laplace(advanced) + wavelet[shot_index, 1] * source_mask
        receiver_mask = (z_index[None, None, :] == rec_depth[shot_index][:, :, None]).astype(jnp.float32)
        misfit_late = jnp.sum(farthest * receiver_mask, axis=2) - observed[shot_index, 1]
        misfit_early = jnp.sum(advanced * receiver_mask, axis=2) - observed[shot_index, 0]
        adj_now = adj_cur[shot_index]
        adj_two = 2.0 * adj_now - adj_next[shot_index] + stiffness * laplace(adj_now) + misfit_late[:, :, None] * receiver_mask
        adj_one = 2.0 * adj_two - adj_now + stiffness * laplace(adj_two) + misfit_early[:, :, None] * receiver_mask
        imaging = adj_two * (farthest - 2.0 * advanced + present) + adj_one * (advanced - 2.0 * present + oldest)
        summed = summed + imaging
    gradient = (2.0 / velocity) * summed
    p_half = momentum - 0.5 * leap_step * gradient
    v_new = velocity + leap_step * p_half / mass_diag
    return v_new, p_half
```

```python
import functools

import jax
import jax.numpy as jnp
from jax import lax
from jax.experimental import pallas as pl
from jax.experimental.pallas import tpu as pltpu
from jax.sharding import PartitionSpec as P

STENCIL = (-205.0 / 72.0, 8.0 / 5.0, -1.0 / 5.0, 8.0 / 315.0, -1.0 / 560.0)
squared_courant = 0.012
leap_step = 0.2

ROWS_PER_STEP = 8
Y_CHUNK = 8


def halos(block):
    out = []
    for axis, dim in (("row", 0), ("col", 1)):
        count = lax.axis_size(axis)
        forward = [(i, i + 1) for i in range(count - 1)]
        backward = [(target, source) for source, target in forward]
        size = block.shape[dim]
        low = lax.ppermute(lax.slice_in_dim(block, size - 4, None, axis=dim), axis, forward)
        high = lax.ppermute(lax.slice_in_dim(block, 0, 4, axis=dim), axis, backward)
        out += [low, high]
    xlo, xhi, ylo, yhi = out
    ylo = jnp.pad(ylo, ((0, 0), (4, 0), (0, 0)))
    yhi = jnp.pad(yhi, ((0, 0), (0, 4), (0, 0)))
    return xlo, xhi, ylo, yhi


def step_kernel(kind, *refs):
    (f_ref, flo_ref, fhi_ref, xlo_ref, xhi_ref, ylo_ref, yhi_ref, prev_ref, vel_ref, rec_ref) = refs[:10]
    rest = refs[10:]
    if kind in ("wave1", "wave2"):
        src_ref, amp_ref = rest[:2]
        rest = rest[2:]
    else:
        mis_ref = rest[0]
        rest = rest[1:]
    if kind == "adj1":
        dw_ref = rest[0]
        rest = rest[1:]
    elif kind == "adj2":
        dw_ref, part_ref = rest[:2]
        rest = rest[2:]
    outs = rest[:-1]
    pad = rest[-1]

    tb, cols, depth = f_ref.shape
    i = pl.program_id(0)
    n = pl.num_programs(0)

    lo = jnp.where(i == 0, xlo_ref[...], flo_ref[...])
    hi = jnp.where(i == n - 1, xhi_ref[...], fhi_ref[...])
    pad[0:4, 8 : 8 + cols, :] = lo
    pad[4 : 4 + tb, 8 : 8 + cols, :] = f_ref[...]
    pad[4 + tb : 8 + tb, 8 : 8 + cols, :] = hi
    pad[4 : 4 + tb, 0:8, :] = ylo_ref[...]
    pad[4 : 4 + tb, 8 + cols : 16 + cols, :] = yhi_ref[...]

    z_index = lax.broadcasted_iota(jnp.int32, (Y_CHUNK, depth), 1)
    y_index = lax.broadcasted_iota(jnp.int32, (Y_CHUNK, depth), 0)
    if kind in ("wave1", "wave2"):
        src_x = src_ref[0] - i * tb
        src_y = src_ref[1]
        src_z = src_ref[2]
        amp = amp_ref[0]

    def row(r, carry):
        for y0 in range(0, cols, Y_CHUNK):
            ys = pl.ds(8 + y0, Y_CHUNK)
            c = pad[4 + r, ys, :]
            result = (3.0 * STENCIL[0]) * c
            for k in range(1, 5):
                along = pad[4 + r + k, ys, :] + pad[4 + r - k, ys, :]
                along = along + (
                    pad[4 + r, pl.ds(8 + y0 + k, Y_CHUNK), :]
                    + pad[4 + r, pl.ds(8 + y0 - k, Y_CHUNK), :]
                )
                zp = jnp.where(z_index < depth - k, pltpu.roll(c, depth - k, 1), 0.0)
                zm = jnp.where(z_index >= k, pltpu.roll(c, k, 1), 0.0)
                along = along + (zp + zm)
                result = result + STENCIL[k] * along
            v = vel_ref[r, pl.ds(y0, Y_CHUNK), :]
            stiff = squared_courant * v * v
            prev = prev_ref[r, pl.ds(y0, Y_CHUNK), :]
            out = 2.0 * c - prev + stiff * result
            at_rec = z_index == rec_ref[r, pl.ds(y0, Y_CHUNK), :]
            if kind in ("wave1", "wave2"):
                hit = (r == src_x) & (y_index + y0 == src_y) & (z_index == src_z)
                out = out + jnp.where(hit, amp, 0.0)
                picked = jnp.sum(jnp.where(at_rec, out, 0.0), axis=1, keepdims=True)
                outs_now = [(out - 2.0 * c) + prev, picked]
                if kind == "wave1":
                    outs_now = [out] + outs_now
            else:
                out = out + jnp.where(at_rec, mis_ref[r, pl.ds(y0, Y_CHUNK), :], 0.0)
                dw = dw_ref[r, pl.ds(y0, Y_CHUNK), :]
                if kind == "adj1":
                    outs_now = [out, out * dw]
                else:
                    outs_now = [part_ref[r, pl.ds(y0, Y_CHUNK), :] + out * dw]
            for o_ref, val in zip(outs, outs_now):
                o_ref[r, pl.ds(y0, Y_CHUNK), :] = val
        return carry

    lax.fori_loop(0, tb, row, 0)


def leap(kind, f, xlo, xhi, ylo, yhi, prev, vel, rec, *extra):
    rows, cols, depth = f.shape
    tb = ROWS_PER_STEP
    grid = (rows // tb,)
    nq = rows // 4
    block = pl.BlockSpec((tb, cols, depth), lambda i: (i, 0, 0))
    lo_spec = pl.BlockSpec((4, cols, depth), lambda i: (jnp.maximum(2 * i - 1, 0), 0, 0))
    hi_spec = pl.BlockSpec((4, cols, depth), lambda i: (jnp.minimum(2 * i + 2, nq - 1), 0, 0))
    whole4 = pl.BlockSpec((4, cols, depth), lambda i: (0, 0, 0))
    yspec = pl.BlockSpec((tb, 8, depth), lambda i: (i, 0, 0))
    col1 = pl.BlockSpec((tb, cols, 1), lambda i: (i, 0, 0))
    smem = pl.BlockSpec(memory_space=pltpu.SMEM)
    in_specs = [block, lo_spec, hi_spec, whole4, whole4, yspec, yspec, block, block, col1]
    args = [f, f, f, xlo, xhi, ylo, yhi, prev, vel, rec]
    field = jax.ShapeDtypeStruct((rows, cols, depth), jnp.float32)
    picked = jax.ShapeDtypeStruct((rows, cols, 1), jnp.float32)
    if kind in ("wave1", "wave2"):
        src, amp = extra
        in_specs += [smem, smem]
        args += [src, amp]
        if kind == "wave1":
            out_shape = [field, field, picked]
            out_specs = [block, block, col1]
        else:
            out_shape = [field, picked]
            out_specs = [block, col1]
    else:
        mis = extra[0]
        in_specs += [col1] + [block] * (len(extra) - 1)
        args += list(extra)
        if kind == "adj1":
            out_shape = [field, field]
            out_specs = [block, block]
        else:
            out_shape = [field]
            out_specs = [block]
    n_in = len(args)
    cost = pl.CostEstimate(
        flops=60 * rows * cols * depth,
        transcendentals=0,
        bytes_accessed=4 * rows * cols * depth * (n_in - 4 + len(out_shape)),
    )
    return pl.pallas_call(
        functools.partial(step_kernel, kind),
        grid=grid,
        in_specs=in_specs,
        out_specs=out_specs,
        out_shape=out_shape,
        scratch_shapes=[pltpu.VMEM((tb + 8, cols + 16, depth), jnp.float32)],
        compiler_params=pltpu.CompilerParams(vmem_limit_bytes=60 * 1024 * 1024),
        cost_estimate=cost,
        name=f"leap_{kind}",
    )(*args)


def on_device(
    velocity,
    momentum,
    mass_diag,
    u_prev,
    u_cur,
    adj_next,
    adj_cur,
    observed,
    rec_depth,
    src_cell,
    wavelet,
):
    full_velocity = lax.all_gather(velocity, "shot", axis=0, tiled=True)
    row_count, col_count, depth_cells = full_velocity.shape
    oldest = u_prev[0]
    present = u_cur[0]
    adj_later = adj_next[0]
    adj_now = adj_cur[0]
    rec = rec_depth[0][:, :, None]
    cell = src_cell[0]
    src = jnp.stack(
        [
            cell[0] - lax.axis_index("row") * row_count,
            cell[1] - lax.axis_index("col") * col_count,
            cell[2],
        ]
    ).astype(jnp.int32)
    amp = wavelet[0]

    wave_h = halos(present)
    adj_h = halos(adj_now)
    advanced, dw1, pick_adv = leap("wave1", present, *wave_h, oldest, full_velocity, rec, src, amp[0:1])
    dw2, pick_far = leap("wave2", advanced, *halos(advanced), present, full_velocity, rec, src, amp[1:2])
    misfit_late = pick_far - observed[0, 1][:, :, None]
    misfit_early = pick_adv - observed[0, 0][:, :, None]
    adj_two, part = leap("adj1", adj_now, *adj_h, adj_later, full_velocity, rec, misfit_late, dw2)
    (imaging,) = leap("adj2", adj_two, *halos(adj_two), adj_now, full_velocity, rec, misfit_early, dw1, part)
    summed = lax.psum_scatter(imaging, "shot", scatter_dimension=0, tiled=True)
    gradient = 2.0 / velocity * summed
    p_half = momentum - 0.5 * leap_step * gradient
    v_new = velocity + leap_step * p_half / mass_diag
    return (v_new, p_half)


def solution(mesh):
    return jax.shard_map(
        on_device,
        mesh=mesh,
        in_specs=(
            P(("row", "shot"), "col", None),
            P(("row", "shot"), "col", None),
            P(("row", "shot"), "col", None),
            P("shot", "row", "col", None),
            P("shot", "row", "col", None),
            P("shot", "row", "col", None),
            P("shot", "row", "col", None),
            P("shot", None, "row", "col"),
            P("shot", "row", "col"),
            P("shot", None),
            P("shot", None),
        ),
        out_specs=(P(("row", "shot"), "col", None), P(("row", "shot"), "col", None)),
        check_vma=False,
    )
```

```python
import functools

import jax
import jax.numpy as jnp
from jax import lax
from jax.experimental import pallas as pl
from jax.experimental.pallas import tpu as pltpu
from jax.sharding import PartitionSpec as P

STENCIL = (-205.0 / 72.0, 8.0 / 5.0, -1.0 / 5.0, 8.0 / 315.0, -1.0 / 560.0)
squared_courant = 0.012
leap_step = 0.2

ROWS_PER_STEP = 8
Y_CHUNK = 8


def halos(block):
    out = []
    for axis, dim in (("row", 0), ("col", 1)):
        count = lax.axis_size(axis)
        forward = [(i, i + 1) for i in range(count - 1)]
        backward = [(target, source) for source, target in forward]
        size = block.shape[dim]
        low = lax.ppermute(lax.slice_in_dim(block, size - 4, None, axis=dim), axis, forward)
        high = lax.ppermute(lax.slice_in_dim(block, 0, 4, axis=dim), axis, backward)
        out += [low, high]
    xlo, xhi, ylo, yhi = out
    ylo = jnp.pad(ylo, ((0, 0), (4, 0), (0, 0)))
    yhi = jnp.pad(yhi, ((0, 0), (0, 4), (0, 0)))
    return xlo, xhi, ylo, yhi


def step_kernel(kind, *refs):
    (f_ref, flo_ref, fhi_ref, xlo_ref, xhi_ref, ylo_ref, yhi_ref, prev_ref, vel_ref, rec_ref) = refs[:10]
    rest = refs[10:]
    if kind in ("wave1", "wave2"):
        src_ref, amp_ref = rest[:2]
        rest = rest[2:]
    else:
        mis_ref = rest[0]
        rest = rest[1:]
    if kind == "adj1":
        dw_ref = rest[0]
        rest = rest[1:]
    elif kind == "adj2":
        dw_ref, part_ref = rest[:2]
        rest = rest[2:]
    outs = rest[:-1]
    pad = rest[-1]

    tb, cols, depth = f_ref.shape
    i = pl.program_id(0)
    n = pl.num_programs(0)

    lo = jnp.where(i == 0, xlo_ref[...], flo_ref[...])
    hi = jnp.where(i == n - 1, xhi_ref[...], fhi_ref[...])
    pad[0:4, 8 : 8 + cols, :] = lo
    pad[4 : 4 + tb, 8 : 8 + cols, :] = f_ref[...]
    pad[4 + tb : 8 + tb, 8 : 8 + cols, :] = hi
    pad[4 : 4 + tb, 0:8, :] = ylo_ref[...]
    pad[4 : 4 + tb, 8 + cols : 16 + cols, :] = yhi_ref[...]

    z_index = lax.broadcasted_iota(jnp.int32, (Y_CHUNK, depth), 1)
    y_index = lax.broadcasted_iota(jnp.int32, (Y_CHUNK, depth), 0)
    if kind in ("wave1", "wave2"):
        src_x = src_ref[0] - i * tb
        src_y = src_ref[1]
        src_z = src_ref[2]
        amp = amp_ref[0]

    def row(r, carry):
        for y0 in range(0, cols, Y_CHUNK):
            ys = pl.ds(8 + y0, Y_CHUNK)
            c = pad[4 + r, ys, :]
            result = (3.0 * STENCIL[0]) * c
            for k in range(1, 5):
                along = pad[4 + r + k, ys, :] + pad[4 + r - k, ys, :]
                along = along + (
                    pad[4 + r, pl.ds(8 + y0 + k, Y_CHUNK), :]
                    + pad[4 + r, pl.ds(8 + y0 - k, Y_CHUNK), :]
                )
                zp = jnp.where(z_index < depth - k, pltpu.roll(c, depth - k, 1), 0.0)
                zm = jnp.where(z_index >= k, pltpu.roll(c, k, 1), 0.0)
                along = along + (zp + zm)
                result = result + STENCIL[k] * along
            v = vel_ref[r, pl.ds(y0, Y_CHUNK), :]
            stiff = squared_courant * v * v
            prev = prev_ref[r, pl.ds(y0, Y_CHUNK), :]
            out = 2.0 * c - prev + stiff * result
            at_rec = z_index == rec_ref[r, pl.ds(y0, Y_CHUNK), :]
            if kind in ("wave1", "wave2"):
                hit = (r == src_x) & (y_index + y0 == src_y) & (z_index == src_z)
                out = out + jnp.where(hit, amp, 0.0)
                picked = jnp.sum(jnp.where(at_rec, out, 0.0), axis=1, keepdims=True)
                outs_now = [(out - 2.0 * c) + prev, picked]
                if kind == "wave1":
                    outs_now = [out] + outs_now
            else:
                out = out + jnp.where(at_rec, mis_ref[r, pl.ds(y0, Y_CHUNK), :], 0.0)
                dw = dw_ref[r, pl.ds(y0, Y_CHUNK), :]
                if kind == "adj1":
                    outs_now = [out, out * dw]
                else:
                    outs_now = [part_ref[r, pl.ds(y0, Y_CHUNK), :] + out * dw]
            for o_ref, val in zip(outs, outs_now):
                o_ref[r, pl.ds(y0, Y_CHUNK), :] = val
        return carry

    lax.fori_loop(0, tb, row, 0)


def leap(kind, f, xlo, xhi, ylo, yhi, prev, vel, rec, *extra):
    rows, cols, depth = f.shape
    tb = ROWS_PER_STEP
    grid = (rows // tb,)
    nq = rows // 4
    block = pl.BlockSpec((tb, cols, depth), lambda i: (i, 0, 0))
    lo_spec = pl.BlockSpec((4, cols, depth), lambda i: (jnp.maximum(2 * i - 1, 0), 0, 0))
    hi_spec = pl.BlockSpec((4, cols, depth), lambda i: (jnp.minimum(2 * i + 2, nq - 1), 0, 0))
    whole4 = pl.BlockSpec((4, cols, depth), lambda i: (0, 0, 0))
    yspec = pl.BlockSpec((tb, 8, depth), lambda i: (i, 0, 0))
    col1 = pl.BlockSpec((tb, cols, 1), lambda i: (i, 0, 0))
    smem = pl.BlockSpec(memory_space=pltpu.SMEM)
    in_specs = [block, lo_spec, hi_spec, whole4, whole4, yspec, yspec, block, block, col1]
    args = [f, f, f, xlo, xhi, ylo, yhi, prev, vel, rec]
    field = jax.ShapeDtypeStruct((rows, cols, depth), jnp.float32)
    picked = jax.ShapeDtypeStruct((rows, cols, 1), jnp.float32)
    if kind in ("wave1", "wave2"):
        src, amp = extra
        in_specs += [smem, smem]
        args += [src, amp]
        if kind == "wave1":
            out_shape = [field, field, picked]
            out_specs = [block, block, col1]
        else:
            out_shape = [field, picked]
            out_specs = [block, col1]
    else:
        mis = extra[0]
        in_specs += [col1] + [block] * (len(extra) - 1)
        args += list(extra)
        if kind == "adj1":
            out_shape = [field, field]
            out_specs = [block, block]
        else:
            out_shape = [field]
            out_specs = [block]
    n_in = len(args)
    cost = pl.CostEstimate(
        flops=60 * rows * cols * depth,
        transcendentals=0,
        bytes_accessed=4 * rows * cols * depth * (n_in - 4 + len(out_shape)),
    )
    return pl.pallas_call(
        functools.partial(step_kernel, kind),
        grid=grid,
        in_specs=in_specs,
        out_specs=out_specs,
        out_shape=out_shape,
        scratch_shapes=[pltpu.VMEM((tb + 8, cols + 16, depth), jnp.float32)],
        compiler_params=pltpu.CompilerParams(vmem_limit_bytes=60 * 1024 * 1024),
        cost_estimate=cost,
        name=f"leap_{kind}",
    )(*args)


def kick_kernel(img_ref, vel_ref, mom_ref, mass_ref, v_out, p_out, recv, send_sem, recv_sem, own_sem):
    me = lax.axis_index("shot")
    n = lax.axis_size("shot")
    rows = vel_ref.shape[0]
    mesh = pl.DeviceIdType.MESH

    barrier = pltpu.get_barrier_semaphore()
    for d in range(1, n):
        pl.semaphore_signal(barrier, inc=1, device_id={"shot": lax.rem(me + d, n)}, device_id_type=mesh)
    pl.semaphore_wait(barrier, n - 1)

    sends = []
    for d in (1, n - 1) + tuple(range(2, n - 1)):
        peer = lax.rem(me + d, n)
        copy = pltpu.make_async_remote_copy(
            src_ref=img_ref.at[pl.ds(pl.multiple_of(peer * rows, rows), rows)],
            dst_ref=recv.at[me],
            send_sem=send_sem.at[d],
            recv_sem=recv_sem.at[me],
            device_id={"shot": peer},
            device_id_type=mesh,
        )
        copy.start()
        sends.append(copy)
    own = pltpu.make_async_copy(img_ref.at[pl.ds(pl.multiple_of(me * rows, rows), rows)], recv.at[me], own_sem)
    own.start()
    for copy in sends:
        copy.wait_send()
    own.wait()
    for d in range(1, n):
        src = lax.rem(me + d, n)
        pltpu.make_async_remote_copy(
            src_ref=img_ref.at[pl.ds(0, rows)],
            dst_ref=recv.at[src],
            send_sem=send_sem.at[d],
            recv_sem=recv_sem.at[src],
            device_id={"shot": src},
            device_id_type=mesh,
        ).wait_recv()

    def row(r, carry):
        summed = recv[0, r]
        for s in range(1, n):
            summed = summed + recv[s, r]
        v = vel_ref[r]
        gradient = 2.0 / v * summed
        p_half = mom_ref[r] - 0.5 * leap_step * gradient
        p_out[r] = p_half
        v_out[r] = v + leap_step * p_half / mass_ref[r]
        return carry

    lax.fori_loop(0, rows, row, 0)


def kick(imaging, velocity, momentum, mass_diag):
    n = lax.axis_size("shot")
    vmem = pl.BlockSpec(memory_space=pltpu.VMEM)
    slab = jax.ShapeDtypeStruct(velocity.shape, jnp.float32)
    return pl.pallas_call(
        kick_kernel,
        in_specs=[pl.BlockSpec(memory_space=pl.ANY), vmem, vmem, vmem],
        out_specs=[vmem, vmem],
        out_shape=[slab, slab],
        scratch_shapes=[
            pltpu.VMEM((n,) + velocity.shape, jnp.float32),
            pltpu.SemaphoreType.DMA((n,)),
            pltpu.SemaphoreType.DMA((n,)),
            pltpu.SemaphoreType.DMA(()),
        ],
        compiler_params=pltpu.CompilerParams(collective_id=0, has_side_effects=True, vmem_limit_bytes=48 * 1024 * 1024),
        name="kick_reduce_scatter",
    )(imaging, velocity, momentum, mass_diag)


def on_device(
    velocity,
    momentum,
    mass_diag,
    u_prev,
    u_cur,
    adj_next,
    adj_cur,
    observed,
    rec_depth,
    src_cell,
    wavelet,
):
    full_velocity = lax.all_gather(velocity, "shot", axis=0, tiled=True)
    row_count, col_count, depth_cells = full_velocity.shape
    oldest = u_prev[0]
    present = u_cur[0]
    adj_later = adj_next[0]
    adj_now = adj_cur[0]
    rec = rec_depth[0][:, :, None]
    cell = src_cell[0]
    src = jnp.stack(
        [
            cell[0] - lax.axis_index("row") * row_count,
            cell[1] - lax.axis_index("col") * col_count,
            cell[2],
        ]
    ).astype(jnp.int32)
    amp = wavelet[0]

    wave_h = halos(present)
    adj_h = halos(adj_now)
    advanced, dw1, pick_adv = leap("wave1", present, *wave_h, oldest, full_velocity, rec, src, amp[0:1])
    dw2, pick_far = leap("wave2", advanced, *halos(advanced), present, full_velocity, rec, src, amp[1:2])
    misfit_late = pick_far - observed[0, 1][:, :, None]
    misfit_early = pick_adv - observed[0, 0][:, :, None]
    adj_two, part = leap("adj1", adj_now, *adj_h, adj_later, full_velocity, rec, misfit_late, dw2)
    (imaging,) = leap("adj2", adj_two, *halos(adj_two), adj_now, full_velocity, rec, misfit_early, dw1, part)
    v_new, p_half = kick(imaging, velocity, momentum, mass_diag)
    return (v_new, p_half)


def solution(mesh):
    return jax.shard_map(
        on_device,
        mesh=mesh,
        in_specs=(
            P(("row", "shot"), "col", None),
            P(("row", "shot"), "col", None),
            P(("row", "shot"), "col", None),
            P("shot", "row", "col", None),
            P("shot", "row", "col", None),
            P("shot", "row", "col", None),
            P("shot", "row", "col", None),
            P("shot", None, "row", "col"),
            P("shot", "row", "col"),
            P("shot", None),
            P("shot", None),
        ),
        out_specs=(P(("row", "shot"), "col", None), P(("row", "shot"), "col", None)),
        check_vma=False,
    )
```

```python
import functools

import jax
import jax.numpy as jnp
from jax import lax
from jax.experimental import pallas as pl
from jax.experimental.pallas import tpu as pltpu
from jax.sharding import PartitionSpec as P

STENCIL = (-205.0 / 72.0, 8.0 / 5.0, -1.0 / 5.0, 8.0 / 315.0, -1.0 / 560.0)
squared_courant = 0.012
leap_step = 0.2

ROWS_PER_STEP = 8
Y_CHUNK = 8


def exchange_kernel(nf, *refs):
    fields = refs[:nf]
    bufs = refs[nf : 5 * nf]
    zero_x, zero_y, send_sem, recv_sem, zero_sem = refs[5 * nf :]
    mesh = pl.DeviceIdType.MESH
    row, nrow = lax.axis_index("row"), lax.axis_size("row")
    col, ncol = lax.axis_index("col"), lax.axis_size("col")
    rows, cols, depth = fields[0].shape
    has = (row < nrow - 1, row > 0, col < ncol - 1, col > 0)
    peer = ({"row": row + 1}, {"row": row - 1}, {"col": col + 1}, {"col": col - 1})
    filler = (1, 0, 3, 2)

    def source(f, d):
        if d == 0:
            return f.at[pl.ds(rows - 4, 4)]
        if d == 1:
            return f.at[pl.ds(0, 4)]
        if d == 2:
            return f.at[:, pl.ds(cols - 8, 8)]
        return f.at[:, pl.ds(0, 8)]

    def remote(j, d, b):
        return pltpu.make_async_remote_copy(
            src_ref=source(fields[j], d),
            dst_ref=bufs[4 * j + b],
            send_sem=send_sem.at[j, d],
            recv_sem=recv_sem.at[j, b],
            device_id=peer[d],
            device_id_type=mesh,
        )

    barrier = pltpu.get_barrier_semaphore()
    for d in range(4):
        @pl.when(has[d])
        def _():
            pl.semaphore_signal(barrier, inc=1, device_id=peer[d], device_id_type=mesh)

    count = (1 - row // (nrow - 1)) + (row + nrow - 1) // nrow + (1 - col // (ncol - 1)) + (col + ncol - 1) // ncol
    pl.semaphore_wait(barrier, count)

    for j in range(nf):
        for d in range(4):
            @pl.when(has[d])
            def _():
                remote(j, d, d).start()

    @pl.when(jnp.logical_not(has[0] & has[1]))
    def _():
        zero_x[...] = jnp.zeros_like(zero_x)

    @pl.when(jnp.logical_not(has[2] & has[3]))
    def _():
        zero_y[...] = jnp.zeros_like(zero_y)

    for j in range(nf):
        for b in range(4):
            @pl.when(jnp.logical_not(has[filler[b]]))
            def _():
                copy = pltpu.make_async_copy(zero_x if b < 2 else zero_y, bufs[4 * j + b], zero_sem.at[j, b])
                copy.start()
                copy.wait()

    for j in range(nf):
        for d in range(4):
            @pl.when(has[d])
            def _():
                remote(j, d, d).wait_send()
        for b in range(4):
            @pl.when(has[filler[b]])
            def _():
                remote(j, b, b).wait_recv()


def exchange(fields, collective_id):
    nf = len(fields)
    rows, cols, depth = fields[0].shape
    any_spec = pl.BlockSpec(memory_space=pl.ANY)
    shapes = []
    for _ in range(nf):
        shapes += [
            jax.ShapeDtypeStruct((4, cols, depth), jnp.float32),
            jax.ShapeDtypeStruct((4, cols, depth), jnp.float32),
            jax.ShapeDtypeStruct((rows, 8, depth), jnp.float32),
            jax.ShapeDtypeStruct((rows, 8, depth), jnp.float32),
        ]
    outs = pl.pallas_call(
        functools.partial(exchange_kernel, nf),
        in_specs=[any_spec] * nf,
        out_specs=[any_spec] * (4 * nf),
        out_shape=shapes,
        scratch_shapes=[
            pltpu.VMEM((4, cols, depth), jnp.float32),
            pltpu.VMEM((rows, 8, depth), jnp.float32),
            pltpu.SemaphoreType.DMA((nf, 4)),
            pltpu.SemaphoreType.DMA((nf, 4)),
            pltpu.SemaphoreType.DMA((nf, 4)),
        ],
        compiler_params=pltpu.CompilerParams(collective_id=collective_id, has_side_effects=True),
        name=f"halo_exchange_{collective_id}",
    )(*fields)
    return [outs[4 * j : 4 * j + 4] for j in range(nf)]


def step_kernel(kind, *refs):
    (f_ref, flo_ref, fhi_ref, xlo_ref, xhi_ref, ylo_ref, yhi_ref, prev_ref, vel_ref, rec_ref) = refs[:10]
    rest = refs[10:]
    if kind in ("wave1", "wave2"):
        src_ref, amp_ref = rest[:2]
        rest = rest[2:]
    else:
        mis_ref = rest[0]
        rest = rest[1:]
    if kind == "adj1":
        dw_ref = rest[0]
        rest = rest[1:]
    elif kind == "adj2":
        dw_ref, part_ref = rest[:2]
        rest = rest[2:]
    outs = rest[:-1]
    pad = rest[-1]

    tb, cols, depth = f_ref.shape
    i = pl.program_id(0)
    n = pl.num_programs(0)

    lo = jnp.where(i == 0, xlo_ref[...], flo_ref[...])
    hi = jnp.where(i == n - 1, xhi_ref[...], fhi_ref[...])
    pad[0:4, 8 : 8 + cols, :] = lo
    pad[4 : 4 + tb, 8 : 8 + cols, :] = f_ref[...]
    pad[4 + tb : 8 + tb, 8 : 8 + cols, :] = hi
    pad[4 : 4 + tb, 0:8, :] = ylo_ref[...]
    pad[4 : 4 + tb, 8 + cols : 16 + cols, :] = yhi_ref[...]

    z_index = lax.broadcasted_iota(jnp.int32, (Y_CHUNK, depth), 1)
    y_index = lax.broadcasted_iota(jnp.int32, (Y_CHUNK, depth), 0)
    if kind in ("wave1", "wave2"):
        src_x = src_ref[0] - i * tb
        src_y = src_ref[1]
        src_z = src_ref[2]
        amp = amp_ref[0]

    def row(r, carry):
        for y0 in range(0, cols, Y_CHUNK):
            ys = pl.ds(8 + y0, Y_CHUNK)
            c = pad[4 + r, ys, :]
            result = (3.0 * STENCIL[0]) * c
            for k in range(1, 5):
                along = pad[4 + r + k, ys, :] + pad[4 + r - k, ys, :]
                along = along + (
                    pad[4 + r, pl.ds(8 + y0 + k, Y_CHUNK), :]
                    + pad[4 + r, pl.ds(8 + y0 - k, Y_CHUNK), :]
                )
                zp = jnp.where(z_index < depth - k, pltpu.roll(c, depth - k, 1), 0.0)
                zm = jnp.where(z_index >= k, pltpu.roll(c, k, 1), 0.0)
                along = along + (zp + zm)
                result = result + STENCIL[k] * along
            v = vel_ref[r, pl.ds(y0, Y_CHUNK), :]
            stiff = squared_courant * v * v
            prev = prev_ref[r, pl.ds(y0, Y_CHUNK), :]
            out = 2.0 * c - prev + stiff * result
            at_rec = z_index == rec_ref[r, pl.ds(y0, Y_CHUNK), :]
            if kind in ("wave1", "wave2"):
                hit = (r == src_x) & (y_index + y0 == src_y) & (z_index == src_z)
                out = out + jnp.where(hit, amp, 0.0)
                picked = jnp.sum(jnp.where(at_rec, out, 0.0), axis=1, keepdims=True)
                outs_now = [(out - 2.0 * c) + prev, picked]
                if kind == "wave1":
                    outs_now = [out] + outs_now
            else:
                out = out + jnp.where(at_rec, mis_ref[r, pl.ds(y0, Y_CHUNK), :], 0.0)
                dw = dw_ref[r, pl.ds(y0, Y_CHUNK), :]
                if kind == "adj1":
                    outs_now = [out, out * dw]
                else:
                    outs_now = [part_ref[r, pl.ds(y0, Y_CHUNK), :] + out * dw]
            for o_ref, val in zip(outs, outs_now):
                o_ref[r, pl.ds(y0, Y_CHUNK), :] = val
        return carry

    lax.fori_loop(0, tb, row, 0)


def leap(kind, f, xlo, xhi, ylo, yhi, prev, vel, rec, *extra):
    rows, cols, depth = f.shape
    tb = ROWS_PER_STEP
    grid = (rows // tb,)
    nq = rows // 4
    block = pl.BlockSpec((tb, cols, depth), lambda i: (i, 0, 0))
    lo_spec = pl.BlockSpec((4, cols, depth), lambda i: (jnp.maximum(2 * i - 1, 0), 0, 0))
    hi_spec = pl.BlockSpec((4, cols, depth), lambda i: (jnp.minimum(2 * i + 2, nq - 1), 0, 0))
    whole4 = pl.BlockSpec((4, cols, depth), lambda i: (0, 0, 0))
    yspec = pl.BlockSpec((tb, 8, depth), lambda i: (i, 0, 0))
    col1 = pl.BlockSpec((tb, cols, 1), lambda i: (i, 0, 0))
    smem = pl.BlockSpec(memory_space=pltpu.SMEM)
    in_specs = [block, lo_spec, hi_spec, whole4, whole4, yspec, yspec, block, block, col1]
    args = [f, f, f, xlo, xhi, ylo, yhi, prev, vel, rec]
    field = jax.ShapeDtypeStruct((rows, cols, depth), jnp.float32)
    picked = jax.ShapeDtypeStruct((rows, cols, 1), jnp.float32)
    if kind in ("wave1", "wave2"):
        src, amp = extra
        in_specs += [smem, smem]
        args += [src, amp]
        if kind == "wave1":
            out_shape = [field, field, picked]
            out_specs = [block, block, col1]
        else:
            out_shape = [field, picked]
            out_specs = [block, col1]
    else:
        mis = extra[0]
        in_specs += [col1] + [block] * (len(extra) - 1)
        args += list(extra)
        if kind == "adj1":
            out_shape = [field, field]
            out_specs = [block, block]
        else:
            out_shape = [field]
            out_specs = [block]
    n_in = len(args)
    cost = pl.CostEstimate(
        flops=60 * rows * cols * depth,
        transcendentals=0,
        bytes_accessed=4 * rows * cols * depth * (n_in - 4 + len(out_shape)),
    )
    return pl.pallas_call(
        functools.partial(step_kernel, kind),
        grid=grid,
        in_specs=in_specs,
        out_specs=out_specs,
        out_shape=out_shape,
        scratch_shapes=[pltpu.VMEM((tb + 8, cols + 16, depth), jnp.float32)],
        compiler_params=pltpu.CompilerParams(vmem_limit_bytes=60 * 1024 * 1024),
        cost_estimate=cost,
        name=f"leap_{kind}",
    )(*args)


def kick_kernel(img_ref, vel_ref, mom_ref, mass_ref, v_out, p_out, recv, send_sem, recv_sem, own_sem):
    me = lax.axis_index("shot")
    n = lax.axis_size("shot")
    rows = vel_ref.shape[0]
    mesh = pl.DeviceIdType.MESH

    barrier = pltpu.get_barrier_semaphore()
    for d in range(1, n):
        pl.semaphore_signal(barrier, inc=1, device_id={"shot": lax.rem(me + d, n)}, device_id_type=mesh)
    pl.semaphore_wait(barrier, n - 1)

    sends = []
    for d in (1, n - 1) + tuple(range(2, n - 1)):
        peer = lax.rem(me + d, n)
        copy = pltpu.make_async_remote_copy(
            src_ref=img_ref.at[pl.ds(pl.multiple_of(peer * rows, rows), rows)],
            dst_ref=recv.at[me],
            send_sem=send_sem.at[d],
            recv_sem=recv_sem.at[me],
            device_id={"shot": peer},
            device_id_type=mesh,
        )
        copy.start()
        sends.append(copy)
    own = pltpu.make_async_copy(img_ref.at[pl.ds(pl.multiple_of(me * rows, rows), rows)], recv.at[me], own_sem)
    own.start()
    for copy in sends:
        copy.wait_send()
    own.wait()
    for d in range(1, n):
        src = lax.rem(me + d, n)
        pltpu.make_async_remote_copy(
            src_ref=img_ref.at[pl.ds(0, rows)],
            dst_ref=recv.at[src],
            send_sem=send_sem.at[d],
            recv_sem=recv_sem.at[src],
            device_id={"shot": src},
            device_id_type=mesh,
        ).wait_recv()

    def row(r, carry):
        summed = recv[0, r]
        for s in range(1, n):
            summed = summed + recv[s, r]
        v = vel_ref[r]
        gradient = 2.0 / v * summed
        p_half = mom_ref[r] - 0.5 * leap_step * gradient
        p_out[r] = p_half
        v_out[r] = v + leap_step * p_half / mass_ref[r]
        return carry

    lax.fori_loop(0, rows, row, 0)


def kick(imaging, velocity, momentum, mass_diag):
    n = lax.axis_size("shot")
    vmem = pl.BlockSpec(memory_space=pltpu.VMEM)
    slab = jax.ShapeDtypeStruct(velocity.shape, jnp.float32)
    return pl.pallas_call(
        kick_kernel,
        in_specs=[pl.BlockSpec(memory_space=pl.ANY), vmem, vmem, vmem],
        out_specs=[vmem, vmem],
        out_shape=[slab, slab],
        scratch_shapes=[
            pltpu.VMEM((n,) + velocity.shape, jnp.float32),
            pltpu.SemaphoreType.DMA((n,)),
            pltpu.SemaphoreType.DMA((n,)),
            pltpu.SemaphoreType.DMA(()),
        ],
        compiler_params=pltpu.CompilerParams(collective_id=0, has_side_effects=True, vmem_limit_bytes=48 * 1024 * 1024),
        name="kick_reduce_scatter",
    )(imaging, velocity, momentum, mass_diag)


def on_device(
    velocity,
    momentum,
    mass_diag,
    u_prev,
    u_cur,
    adj_next,
    adj_cur,
    observed,
    rec_depth,
    src_cell,
    wavelet,
):
    full_velocity = lax.all_gather(velocity, "shot", axis=0, tiled=True)
    row_count, col_count, depth_cells = full_velocity.shape
    oldest = u_prev[0]
    present = u_cur[0]
    adj_later = adj_next[0]
    adj_now = adj_cur[0]
    rec = rec_depth[0][:, :, None]
    cell = src_cell[0]
    src = jnp.stack(
        [
            cell[0] - lax.axis_index("row") * row_count,
            cell[1] - lax.axis_index("col") * col_count,
            cell[2],
        ]
    ).astype(jnp.int32)
    amp = wavelet[0]

    wave_h, adj_h = exchange([present, adj_now], 1)
    advanced, dw1, pick_adv = leap("wave1", present, *wave_h, oldest, full_velocity, rec, src, amp[0:1])
    dw2, pick_far = leap("wave2", advanced, *exchange([advanced], 2)[0], present, full_velocity, rec, src, amp[1:2])
    misfit_late = pick_far - observed[0, 1][:, :, None]
    misfit_early = pick_adv - observed[0, 0][:, :, None]
    adj_two, part = leap("adj1", adj_now, *adj_h, adj_later, full_velocity, rec, misfit_late, dw2)
    (imaging,) = leap("adj2", adj_two, *exchange([adj_two], 3)[0], adj_now, full_velocity, rec, misfit_early, dw1, part)
    v_new, p_half = kick(imaging, velocity, momentum, mass_diag)
    return (v_new, p_half)


def solution(mesh):
    return jax.shard_map(
        on_device,
        mesh=mesh,
        in_specs=(
            P(("row", "shot"), "col", None),
            P(("row", "shot"), "col", None),
            P(("row", "shot"), "col", None),
            P("shot", "row", "col", None),
            P("shot", "row", "col", None),
            P("shot", "row", "col", None),
            P("shot", "row", "col", None),
            P("shot", None, "row", "col"),
            P("shot", "row", "col"),
            P("shot", None),
            P("shot", None),
        ),
        out_specs=(P(("row", "shot"), "col", None), P(("row", "shot"), "col", None)),
        check_vma=False,
    )
```

```python
import functools

import jax
import jax.numpy as jnp
from jax import lax
from jax.experimental import pallas as pl
from jax.experimental.pallas import tpu as pltpu
from jax.sharding import PartitionSpec as P

STENCIL = (-205.0 / 72.0, 8.0 / 5.0, -1.0 / 5.0, 8.0 / 315.0, -1.0 / 560.0)
squared_courant = 0.012
leap_step = 0.2

ROWS_PER_STEP = 8
Y_CHUNK = 8


def exchange_kernel(nf, *refs):
    fields = refs[:nf]
    bufs = refs[nf : 5 * nf]
    zero_x, zero_y, send_sem, recv_sem, zero_sem = refs[5 * nf :]
    mesh = pl.DeviceIdType.MESH
    row, nrow = lax.axis_index("row"), lax.axis_size("row")
    col, ncol = lax.axis_index("col"), lax.axis_size("col")
    rows, cols, depth = fields[0].shape
    has = (row < nrow - 1, row > 0, col < ncol - 1, col > 0)
    peer = ({"row": row + 1}, {"row": row - 1}, {"col": col + 1}, {"col": col - 1})
    filler = (1, 0, 3, 2)

    def source(f, d):
        if d == 0:
            return f.at[pl.ds(rows - 4, 4)]
        if d == 1:
            return f.at[pl.ds(0, 4)]
        if d == 2:
            return f.at[:, pl.ds(cols - 8, 8)]
        return f.at[:, pl.ds(0, 8)]

    def remote(j, d, b):
        return pltpu.make_async_remote_copy(
            src_ref=source(fields[j], d),
            dst_ref=bufs[4 * j + b],
            send_sem=send_sem.at[j, d],
            recv_sem=recv_sem.at[j, b],
            device_id=peer[d],
            device_id_type=mesh,
        )

    barrier = pltpu.get_barrier_semaphore()
    for d in range(4):
        @pl.when(has[d])
        def _():
            pl.semaphore_signal(barrier, inc=1, device_id=peer[d], device_id_type=mesh)

    count = (1 - row // (nrow - 1)) + (row + nrow - 1) // nrow + (1 - col // (ncol - 1)) + (col + ncol - 1) // ncol
    pl.semaphore_wait(barrier, count)

    for j in range(nf):
        for d in range(4):
            @pl.when(has[d])
            def _():
                remote(j, d, d).start()

    @pl.when(jnp.logical_not(has[0] & has[1]))
    def _():
        zero_x[...] = jnp.zeros_like(zero_x)

    @pl.when(jnp.logical_not(has[2] & has[3]))
    def _():
        zero_y[...] = jnp.zeros_like(zero_y)

    for j in range(nf):
        for b in range(4):
            @pl.when(jnp.logical_not(has[filler[b]]))
            def _():
                copy = pltpu.make_async_copy(zero_x if b < 2 else zero_y, bufs[4 * j + b], zero_sem.at[j, b])
                copy.start()
                copy.wait()

    for j in range(nf):
        for d in range(4):
            @pl.when(has[d])
            def _():
                remote(j, d, d).wait_send()
        for b in range(4):
            @pl.when(has[filler[b]])
            def _():
                remote(j, b, b).wait_recv()


def exchange(fields, collective_id):
    nf = len(fields)
    rows, cols, depth = fields[0].shape
    any_spec = pl.BlockSpec(memory_space=pl.ANY)
    shapes = []
    for _ in range(nf):
        shapes += [
            jax.ShapeDtypeStruct((4, cols, depth), jnp.float32),
            jax.ShapeDtypeStruct((4, cols, depth), jnp.float32),
            jax.ShapeDtypeStruct((rows, 8, depth), jnp.float32),
            jax.ShapeDtypeStruct((rows, 8, depth), jnp.float32),
        ]
    outs = pl.pallas_call(
        functools.partial(exchange_kernel, nf),
        in_specs=[any_spec] * nf,
        out_specs=[any_spec] * (4 * nf),
        out_shape=shapes,
        scratch_shapes=[
            pltpu.VMEM((4, cols, depth), jnp.float32),
            pltpu.VMEM((rows, 8, depth), jnp.float32),
            pltpu.SemaphoreType.DMA((nf, 4)),
            pltpu.SemaphoreType.DMA((nf, 4)),
            pltpu.SemaphoreType.DMA((nf, 4)),
        ],
        compiler_params=pltpu.CompilerParams(collective_id=collective_id, has_side_effects=True),
        name=f"halo_exchange_{collective_id}",
    )(*fields)
    return [outs[4 * j : 4 * j + 4] for j in range(nf)]


def step_kernel(kind, *refs):
    (f_ref, flo_ref, fhi_ref, xlo_ref, xhi_ref, ylo_ref, yhi_ref, prev_ref, vel_ref, rec_ref) = refs[:10]
    rest = refs[10:]
    if kind in ("wave1", "wave2"):
        src_ref, amp_ref = rest[:2]
        rest = rest[2:]
    else:
        mis_ref = rest[0]
        rest = rest[1:]
    if kind == "adj1":
        dw_ref = rest[0]
        rest = rest[1:]
    elif kind == "adj2":
        dw_ref, part_ref = rest[:2]
        rest = rest[2:]
    if kind in ("wave1", "wave2"):
        outs = rest[:-3]
        picked_ref, pad, fold = rest[-3:]
    else:
        outs = rest[:-1]
        pad = rest[-1]

    tb, cols, depth = f_ref.shape
    i = pl.program_id(0)
    n = pl.num_programs(0)

    lo = jnp.where(i == 0, xlo_ref[...], flo_ref[...])
    hi = jnp.where(i == n - 1, xhi_ref[...], fhi_ref[...])
    pad[0:4, 8 : 8 + cols, :] = lo
    pad[4 : 4 + tb, 8 : 8 + cols, :] = f_ref[...]
    pad[4 + tb : 8 + tb, 8 : 8 + cols, :] = hi
    pad[4 : 4 + tb, 0:8, :] = ylo_ref[...]
    pad[4 : 4 + tb, 8 + cols : 16 + cols, :] = yhi_ref[...]

    z_index = lax.broadcasted_iota(jnp.int32, (Y_CHUNK, depth), 1)
    y_index = lax.broadcasted_iota(jnp.int32, (Y_CHUNK, depth), 0)
    if kind in ("wave1", "wave2"):
        src_x = src_ref[0] - i * tb
        src_y = src_ref[1]
        src_z = src_ref[2]
        amp = amp_ref[0]

    def row(r, carry):
        for y0 in range(0, cols, Y_CHUNK):
            ys = pl.ds(8 + y0, Y_CHUNK)
            c = pad[4 + r, ys, :]
            result = (3.0 * STENCIL[0]) * c
            for k in range(1, 5):
                along = pad[4 + r + k, ys, :] + pad[4 + r - k, ys, :]
                along = along + (
                    pad[4 + r, pl.ds(8 + y0 + k, Y_CHUNK), :]
                    + pad[4 + r, pl.ds(8 + y0 - k, Y_CHUNK), :]
                )
                zp = jnp.where(z_index < depth - k, pltpu.roll(c, depth - k, 1), 0.0)
                zm = jnp.where(z_index >= k, pltpu.roll(c, k, 1), 0.0)
                along = along + (zp + zm)
                result = result + STENCIL[k] * along
            v = vel_ref[r, pl.ds(y0, Y_CHUNK), :]
            stiff = squared_courant * v * v
            prev = prev_ref[r, pl.ds(y0, Y_CHUNK), :]
            out = 2.0 * c - prev + stiff * result
            at_rec = z_index == rec_ref[r, pl.ds(y0, Y_CHUNK), :]
            if kind in ("wave1", "wave2"):
                hit = (r == src_x) & (y_index + y0 == src_y) & (z_index == src_z)
                out = out + jnp.where(hit, amp, 0.0)
                sel = jnp.where(at_rec, out, 0.0)
                folded = sel[:, 0:128]
                for t in range(128, depth, 128):
                    folded = folded + sel[:, t : t + 128]
                fold[pl.ds(pl.multiple_of(r * cols + y0, Y_CHUNK), Y_CHUNK), :] = folded
                outs_now = [(out - 2.0 * c) + prev]
                if kind == "wave1":
                    outs_now = [out] + outs_now
            else:
                out = out + jnp.where(at_rec, mis_ref[r, pl.ds(y0, Y_CHUNK), :], 0.0)
                dw = dw_ref[r, pl.ds(y0, Y_CHUNK), :]
                if kind == "adj1":
                    outs_now = [out, out * dw]
                else:
                    outs_now = [part_ref[r, pl.ds(y0, Y_CHUNK), :] + out * dw]
            for o_ref, val in zip(outs, outs_now):
                o_ref[r, pl.ds(y0, Y_CHUNK), :] = val
        return carry

    lax.fori_loop(0, tb, row, 0)
    if kind in ("wave1", "wave2"):
        picked_ref[...] = jnp.sum(fold[...], axis=1, keepdims=True).reshape(picked_ref.shape)


def leap(kind, f, xlo, xhi, ylo, yhi, prev, vel, rec, *extra):
    rows, cols, depth = f.shape
    tb = ROWS_PER_STEP
    grid = (rows // tb,)
    nq = rows // 4
    block = pl.BlockSpec((tb, cols, depth), lambda i: (i, 0, 0))
    lo_spec = pl.BlockSpec((4, cols, depth), lambda i: (jnp.maximum(2 * i - 1, 0), 0, 0))
    hi_spec = pl.BlockSpec((4, cols, depth), lambda i: (jnp.minimum(2 * i + 2, nq - 1), 0, 0))
    whole4 = pl.BlockSpec((4, cols, depth), lambda i: (0, 0, 0))
    yspec = pl.BlockSpec((tb, 8, depth), lambda i: (i, 0, 0))
    col1 = pl.BlockSpec((tb, cols, 1), lambda i: (i, 0, 0))
    smem = pl.BlockSpec(memory_space=pltpu.SMEM)
    in_specs = [block, lo_spec, hi_spec, whole4, whole4, yspec, yspec, block, block, col1]
    args = [f, f, f, xlo, xhi, ylo, yhi, prev, vel, rec]
    field = jax.ShapeDtypeStruct((rows, cols, depth), jnp.float32)
    picked = jax.ShapeDtypeStruct((rows, cols, 1), jnp.float32)
    if kind in ("wave1", "wave2"):
        src, amp = extra
        in_specs += [smem, smem]
        args += [src, amp]
        if kind == "wave1":
            out_shape = [field, field, picked]
            out_specs = [block, block, col1]
        else:
            out_shape = [field, picked]
            out_specs = [block, col1]
    else:
        mis = extra[0]
        in_specs += [col1] + [block] * (len(extra) - 1)
        args += list(extra)
        if kind == "adj1":
            out_shape = [field, field]
            out_specs = [block, block]
        else:
            out_shape = [field]
            out_specs = [block]
    n_in = len(args)
    cost = pl.CostEstimate(
        flops=60 * rows * cols * depth,
        transcendentals=0,
        bytes_accessed=4 * rows * cols * depth * (n_in - 4 + len(out_shape)),
    )
    return pl.pallas_call(
        functools.partial(step_kernel, kind),
        grid=grid,
        in_specs=in_specs,
        out_specs=out_specs,
        out_shape=out_shape,
        scratch_shapes=[pltpu.VMEM((tb + 8, cols + 16, depth), jnp.float32)]
        + ([pltpu.VMEM((tb * cols, 128), jnp.float32)] if kind in ("wave1", "wave2") else []),
        compiler_params=pltpu.CompilerParams(vmem_limit_bytes=60 * 1024 * 1024),
        cost_estimate=cost,
        name=f"leap_{kind}",
    )(*args)


def kick_kernel(img_ref, vel_ref, mom_ref, mass_ref, v_out, p_out, recv, send_sem, recv_sem, own_sem):
    me = lax.axis_index("shot")
    n = lax.axis_size("shot")
    rows = vel_ref.shape[0]
    mesh = pl.DeviceIdType.MESH

    barrier = pltpu.get_barrier_semaphore()
    for d in range(1, n):
        pl.semaphore_signal(barrier, inc=1, device_id={"shot": lax.rem(me + d, n)}, device_id_type=mesh)
    pl.semaphore_wait(barrier, n - 1)

    sends = []
    for d in (1, n - 1) + tuple(range(2, n - 1)):
        peer = lax.rem(me + d, n)
        copy = pltpu.make_async_remote_copy(
            src_ref=img_ref.at[pl.ds(pl.multiple_of(peer * rows, rows), rows)],
            dst_ref=recv.at[me],
            send_sem=send_sem.at[d],
            recv_sem=recv_sem.at[me],
            device_id={"shot": peer},
            device_id_type=mesh,
        )
        copy.start()
        sends.append(copy)
    own = pltpu.make_async_copy(img_ref.at[pl.ds(pl.multiple_of(me * rows, rows), rows)], recv.at[me], own_sem)
    own.start()
    for copy in sends:
        copy.wait_send()
    own.wait()
    for d in range(1, n):
        src = lax.rem(me + d, n)
        pltpu.make_async_remote_copy(
            src_ref=img_ref.at[pl.ds(0, rows)],
            dst_ref=recv.at[src],
            send_sem=send_sem.at[d],
            recv_sem=recv_sem.at[src],
            device_id={"shot": src},
            device_id_type=mesh,
        ).wait_recv()

    def row(r, carry):
        summed = recv[0, r]
        for s in range(1, n):
            summed = summed + recv[s, r]
        v = vel_ref[r]
        gradient = 2.0 / v * summed
        p_half = mom_ref[r] - 0.5 * leap_step * gradient
        p_out[r] = p_half
        v_out[r] = v + leap_step * p_half / mass_ref[r]
        return carry

    lax.fori_loop(0, rows, row, 0)


def kick(imaging, velocity, momentum, mass_diag):
    n = lax.axis_size("shot")
    vmem = pl.BlockSpec(memory_space=pltpu.VMEM)
    slab = jax.ShapeDtypeStruct(velocity.shape, jnp.float32)
    return pl.pallas_call(
        kick_kernel,
        in_specs=[pl.BlockSpec(memory_space=pl.ANY), vmem, vmem, vmem],
        out_specs=[vmem, vmem],
        out_shape=[slab, slab],
        scratch_shapes=[
            pltpu.VMEM((n,) + velocity.shape, jnp.float32),
            pltpu.SemaphoreType.DMA((n,)),
            pltpu.SemaphoreType.DMA((n,)),
            pltpu.SemaphoreType.DMA(()),
        ],
        compiler_params=pltpu.CompilerParams(collective_id=0, has_side_effects=True, vmem_limit_bytes=48 * 1024 * 1024),
        name="kick_reduce_scatter",
    )(imaging, velocity, momentum, mass_diag)


def on_device(
    velocity,
    momentum,
    mass_diag,
    u_prev,
    u_cur,
    adj_next,
    adj_cur,
    observed,
    rec_depth,
    src_cell,
    wavelet,
):
    full_velocity = lax.all_gather(velocity, "shot", axis=0, tiled=True)
    row_count, col_count, depth_cells = full_velocity.shape
    oldest = u_prev[0]
    present = u_cur[0]
    adj_later = adj_next[0]
    adj_now = adj_cur[0]
    rec = rec_depth[0][:, :, None]
    cell = src_cell[0]
    src = jnp.stack(
        [
            cell[0] - lax.axis_index("row") * row_count,
            cell[1] - lax.axis_index("col") * col_count,
            cell[2],
        ]
    ).astype(jnp.int32)
    amp = wavelet[0]

    wave_h, adj_h = exchange([present, adj_now], 1)
    advanced, dw1, pick_adv = leap("wave1", present, *wave_h, oldest, full_velocity, rec, src, amp[0:1])
    dw2, pick_far = leap("wave2", advanced, *exchange([advanced], 2)[0], present, full_velocity, rec, src, amp[1:2])
    misfit_late = pick_far - observed[0, 1][:, :, None]
    misfit_early = pick_adv - observed[0, 0][:, :, None]
    adj_two, part = leap("adj1", adj_now, *adj_h, adj_later, full_velocity, rec, misfit_late, dw2)
    (imaging,) = leap("adj2", adj_two, *exchange([adj_two], 3)[0], adj_now, full_velocity, rec, misfit_early, dw1, part)
    v_new, p_half = kick(imaging, velocity, momentum, mass_diag)
    return (v_new, p_half)


def solution(mesh):
    return jax.shard_map(
        on_device,
        mesh=mesh,
        in_specs=(
            P(("row", "shot"), "col", None),
            P(("row", "shot"), "col", None),
            P(("row", "shot"), "col", None),
            P("shot", "row", "col", None),
            P("shot", "row", "col", None),
            P("shot", "row", "col", None),
            P("shot", "row", "col", None),
            P("shot", None, "row", "col"),
            P("shot", "row", "col"),
            P("shot", None),
            P("shot", None),
        ),
        out_specs=(P(("row", "shot"), "col", None), P(("row", "shot"), "col", None)),
        check_vma=False,
    )
```

```python
import functools

import jax
import jax.numpy as jnp
from jax import lax
from jax.experimental import pallas as pl
from jax.experimental.pallas import tpu as pltpu
from jax.sharding import PartitionSpec as P

STENCIL = (-205.0 / 72.0, 8.0 / 5.0, -1.0 / 5.0, 8.0 / 315.0, -1.0 / 560.0)
squared_courant = 0.012
leap_step = 0.2

ROWS_PER_STEP = 8
Y_CHUNK = 8


def exchange_kernel(nf, *refs):
    fields = refs[:nf]
    bufs = refs[nf : 5 * nf]
    zero_x, zero_y, send_sem, recv_sem, zero_sem = refs[5 * nf :]
    mesh = pl.DeviceIdType.MESH
    row, nrow = lax.axis_index("row"), lax.axis_size("row")
    col, ncol = lax.axis_index("col"), lax.axis_size("col")
    rows, cols, depth = fields[0].shape
    has = (row < nrow - 1, row > 0, col < ncol - 1, col > 0)
    peer = ({"row": row + 1}, {"row": row - 1}, {"col": col + 1}, {"col": col - 1})
    filler = (1, 0, 3, 2)

    def source(f, d):
        if d == 0:
            return f.at[pl.ds(rows - 4, 4)]
        if d == 1:
            return f.at[pl.ds(0, 4)]
        if d == 2:
            return f.at[:, pl.ds(cols - 4, 4)]
        return f.at[:, pl.ds(0, 4)]

    def target(j, b):
        if b == 2:
            return bufs[4 * j + b].at[:, pl.ds(4, 4)]
        if b == 3:
            return bufs[4 * j + b].at[:, pl.ds(0, 4)]
        return bufs[4 * j + b]

    def remote(j, d, b):
        return pltpu.make_async_remote_copy(
            src_ref=source(fields[j], d),
            dst_ref=target(j, b),
            send_sem=send_sem.at[j, d],
            recv_sem=recv_sem.at[j, b],
            device_id=peer[d],
            device_id_type=mesh,
        )

    barrier = pltpu.get_barrier_semaphore()
    for d in range(4):
        @pl.when(has[d])
        def _():
            pl.semaphore_signal(barrier, inc=1, device_id=peer[d], device_id_type=mesh)

    count = (1 - row // (nrow - 1)) + (row + nrow - 1) // nrow + (1 - col // (ncol - 1)) + (col + ncol - 1) // ncol
    pl.semaphore_wait(barrier, count)

    for j in range(nf):
        for d in range(4):
            @pl.when(has[d])
            def _():
                remote(j, d, d).start()

    @pl.when(jnp.logical_not(has[0] & has[1]))
    def _():
        zero_x[...] = jnp.zeros_like(zero_x)

    @pl.when(jnp.logical_not(has[2] & has[3]))
    def _():
        zero_y[...] = jnp.zeros_like(zero_y)

    for j in range(nf):
        for b in range(4):
            @pl.when(jnp.logical_not(has[filler[b]]))
            def _():
                copy = pltpu.make_async_copy(zero_x if b < 2 else zero_y, bufs[4 * j + b], zero_sem.at[j, b])
                copy.start()
                copy.wait()

    for j in range(nf):
        for d in range(4):
            @pl.when(has[d])
            def _():
                remote(j, d, d).wait_send()
        for b in range(4):
            @pl.when(has[filler[b]])
            def _():
                remote(j, b, b).wait_recv()


def exchange(fields, collective_id):
    nf = len(fields)
    rows, cols, depth = fields[0].shape
    any_spec = pl.BlockSpec(memory_space=pl.ANY)
    shapes = []
    for _ in range(nf):
        shapes += [
            jax.ShapeDtypeStruct((4, cols, depth), jnp.float32),
            jax.ShapeDtypeStruct((4, cols, depth), jnp.float32),
            jax.ShapeDtypeStruct((rows, 8, depth), jnp.float32),
            jax.ShapeDtypeStruct((rows, 8, depth), jnp.float32),
        ]
    outs = pl.pallas_call(
        functools.partial(exchange_kernel, nf),
        in_specs=[any_spec] * nf,
        out_specs=[any_spec] * (4 * nf),
        out_shape=shapes,
        scratch_shapes=[
            pltpu.VMEM((4, cols, depth), jnp.float32),
            pltpu.VMEM((rows, 8, depth), jnp.float32),
            pltpu.SemaphoreType.DMA((nf, 4)),
            pltpu.SemaphoreType.DMA((nf, 4)),
            pltpu.SemaphoreType.DMA((nf, 4)),
        ],
        compiler_params=pltpu.CompilerParams(collective_id=collective_id, has_side_effects=True),
        name=f"halo_exchange_{collective_id}",
    )(*fields)
    return [outs[4 * j : 4 * j + 4] for j in range(nf)]


def step_kernel(kind, *refs):
    (f_ref, flo_ref, fhi_ref, xlo_ref, xhi_ref, ylo_ref, yhi_ref, prev_ref, vel_ref, rec_ref) = refs[:10]
    rest = refs[10:]
    if kind in ("wave1", "wave2"):
        src_ref, amp_ref = rest[:2]
        rest = rest[2:]
    else:
        mis_ref = rest[0]
        rest = rest[1:]
    if kind == "adj1":
        dw_ref = rest[0]
        rest = rest[1:]
    elif kind == "adj2":
        dw_ref, part_ref = rest[:2]
        rest = rest[2:]
    if kind in ("wave1", "wave2"):
        outs = rest[:-3]
        picked_ref, pad, fold = rest[-3:]
    else:
        outs = rest[:-1]
        pad = rest[-1]

    tb, cols, depth = f_ref.shape
    i = pl.program_id(0)
    n = pl.num_programs(0)

    lo = jnp.where(i == 0, xlo_ref[...], flo_ref[...])
    hi = jnp.where(i == n - 1, xhi_ref[...], fhi_ref[...])
    pad[0:4, 8 : 8 + cols, :] = lo
    pad[4 : 4 + tb, 8 : 8 + cols, :] = f_ref[...]
    pad[4 + tb : 8 + tb, 8 : 8 + cols, :] = hi
    pad[4 : 4 + tb, 0:8, :] = ylo_ref[...]
    pad[4 : 4 + tb, 8 + cols : 16 + cols, :] = yhi_ref[...]

    z_index = lax.broadcasted_iota(jnp.int32, (Y_CHUNK, depth), 1)
    y_index = lax.broadcasted_iota(jnp.int32, (Y_CHUNK, depth), 0)
    if kind in ("wave1", "wave2"):
        src_x = src_ref[0] - i * tb
        src_y = src_ref[1]
        src_z = src_ref[2]
        amp = amp_ref[0]

    def row(r, carry):
        for y0 in range(0, cols, Y_CHUNK):
            ys = pl.ds(8 + y0, Y_CHUNK)
            c = pad[4 + r, ys, :]
            result = (3.0 * STENCIL[0]) * c
            for k in range(1, 5):
                along = pad[4 + r + k, ys, :] + pad[4 + r - k, ys, :]
                along = along + (
                    pad[4 + r, pl.ds(8 + y0 + k, Y_CHUNK), :]
                    + pad[4 + r, pl.ds(8 + y0 - k, Y_CHUNK), :]
                )
                zp = jnp.where(z_index < depth - k, pltpu.roll(c, depth - k, 1), 0.0)
                zm = jnp.where(z_index >= k, pltpu.roll(c, k, 1), 0.0)
                along = along + (zp + zm)
                result = result + STENCIL[k] * along
            v = vel_ref[r, pl.ds(y0, Y_CHUNK), :]
            stiff = squared_courant * v * v
            prev = prev_ref[r, pl.ds(y0, Y_CHUNK), :]
            out = 2.0 * c - prev + stiff * result
            at_rec = z_index == rec_ref[r, pl.ds(y0, Y_CHUNK), :]
            if kind in ("wave1", "wave2"):
                hit = (r == src_x) & (y_index + y0 == src_y) & (z_index == src_z)
                out = out + jnp.where(hit, amp, 0.0)
                sel = jnp.where(at_rec, out, 0.0)
                folded = sel[:, 0:128]
                for t in range(128, depth, 128):
                    folded = folded + sel[:, t : t + 128]
                fold[pl.ds(pl.multiple_of(r * cols + y0, Y_CHUNK), Y_CHUNK), :] = folded
                outs_now = [(out - 2.0 * c) + prev]
                if kind == "wave1":
                    outs_now = [out] + outs_now
            else:
                out = out + jnp.where(at_rec, mis_ref[r, pl.ds(y0, Y_CHUNK), :], 0.0)
                dw = dw_ref[r, pl.ds(y0, Y_CHUNK), :]
                if kind == "adj1":
                    outs_now = [out, out * dw]
                else:
                    outs_now = [part_ref[r, pl.ds(y0, Y_CHUNK), :] + out * dw]
            for o_ref, val in zip(outs, outs_now):
                o_ref[r, pl.ds(y0, Y_CHUNK), :] = val
        return carry

    lax.fori_loop(0, tb, row, 0)
    if kind in ("wave1", "wave2"):
        picked_ref[...] = jnp.sum(fold[...], axis=1, keepdims=True).reshape(picked_ref.shape)


def leap(kind, f, xlo, xhi, ylo, yhi, prev, vel, rec, *extra):
    rows, cols, depth = f.shape
    tb = ROWS_PER_STEP
    grid = (rows // tb,)
    nq = rows // 4
    block = pl.BlockSpec((tb, cols, depth), lambda i: (i, 0, 0))
    lo_spec = pl.BlockSpec((4, cols, depth), lambda i: (jnp.maximum(2 * i - 1, 0), 0, 0))
    hi_spec = pl.BlockSpec((4, cols, depth), lambda i: (jnp.minimum(2 * i + 2, nq - 1), 0, 0))
    whole4 = pl.BlockSpec((4, cols, depth), lambda i: (0, 0, 0))
    yspec = pl.BlockSpec((tb, 8, depth), lambda i: (i, 0, 0))
    col1 = pl.BlockSpec((tb, cols, 1), lambda i: (i, 0, 0))
    smem = pl.BlockSpec(memory_space=pltpu.SMEM)
    in_specs = [block, lo_spec, hi_spec, whole4, whole4, yspec, yspec, block, block, col1]
    args = [f, f, f, xlo, xhi, ylo, yhi, prev, vel, rec]
    field = jax.ShapeDtypeStruct((rows, cols, depth), jnp.float32)
    picked = jax.ShapeDtypeStruct((rows, cols, 1), jnp.float32)
    if kind in ("wave1", "wave2"):
        src, amp = extra
        in_specs += [smem, smem]
        args += [src, amp]
        if kind == "wave1":
            out_shape = [field, field, picked]
            out_specs = [block, block, col1]
        else:
            out_shape = [field, picked]
            out_specs = [block, col1]
    else:
        mis = extra[0]
        in_specs += [col1] + [block] * (len(extra) - 1)
        args += list(extra)
        if kind == "adj1":
            out_shape = [field, field]
            out_specs = [block, block]
        else:
            out_shape = [field]
            out_specs = [block]
    n_in = len(args)
    cost = pl.CostEstimate(
        flops=60 * rows * cols * depth,
        transcendentals=0,
        bytes_accessed=4 * rows * cols * depth * (n_in - 4 + len(out_shape)),
    )
    return pl.pallas_call(
        functools.partial(step_kernel, kind),
        grid=grid,
        in_specs=in_specs,
        out_specs=out_specs,
        out_shape=out_shape,
        scratch_shapes=[pltpu.VMEM((tb + 8, cols + 16, depth), jnp.float32)]
        + ([pltpu.VMEM((tb * cols, 128), jnp.float32)] if kind in ("wave1", "wave2") else []),
        compiler_params=pltpu.CompilerParams(vmem_limit_bytes=60 * 1024 * 1024),
        cost_estimate=cost,
        name=f"leap_{kind}",
    )(*args)


def kick_kernel(img_ref, vel_ref, mom_ref, mass_ref, v_out, p_out, recv, send_sem, recv_sem, own_sem):
    me = lax.axis_index("shot")
    n = lax.axis_size("shot")
    rows = vel_ref.shape[0]
    mesh = pl.DeviceIdType.MESH

    barrier = pltpu.get_barrier_semaphore()
    for d in range(1, n):
        pl.semaphore_signal(barrier, inc=1, device_id={"shot": lax.rem(me + d, n)}, device_id_type=mesh)
    pl.semaphore_wait(barrier, n - 1)

    sends = []
    for d in (1, n - 1) + tuple(range(2, n - 1)):
        peer = lax.rem(me + d, n)
        copy = pltpu.make_async_remote_copy(
            src_ref=img_ref.at[pl.ds(pl.multiple_of(peer * rows, rows), rows)],
            dst_ref=recv.at[me],
            send_sem=send_sem.at[d],
            recv_sem=recv_sem.at[me],
            device_id={"shot": peer},
            device_id_type=mesh,
        )
        copy.start()
        sends.append(copy)
    own = pltpu.make_async_copy(img_ref.at[pl.ds(pl.multiple_of(me * rows, rows), rows)], recv.at[me], own_sem)
    own.start()
    for copy in sends:
        copy.wait_send()
    own.wait()
    for d in range(1, n):
        src = lax.rem(me + d, n)
        pltpu.make_async_remote_copy(
            src_ref=img_ref.at[pl.ds(0, rows)],
            dst_ref=recv.at[src],
            send_sem=send_sem.at[d],
            recv_sem=recv_sem.at[src],
            device_id={"shot": src},
            device_id_type=mesh,
        ).wait_recv()

    def row(r, carry):
        summed = recv[0, r]
        for s in range(1, n):
            summed = summed + recv[s, r]
        v = vel_ref[r]
        gradient = 2.0 / v * summed
        p_half = mom_ref[r] - 0.5 * leap_step * gradient
        p_out[r] = p_half
        v_out[r] = v + leap_step * p_half / mass_ref[r]
        return carry

    lax.fori_loop(0, rows, row, 0)


def kick(imaging, velocity, momentum, mass_diag):
    n = lax.axis_size("shot")
    vmem = pl.BlockSpec(memory_space=pltpu.VMEM)
    slab = jax.ShapeDtypeStruct(velocity.shape, jnp.float32)
    return pl.pallas_call(
        kick_kernel,
        in_specs=[pl.BlockSpec(memory_space=pl.ANY), vmem, vmem, vmem],
        out_specs=[vmem, vmem],
        out_shape=[slab, slab],
        scratch_shapes=[
            pltpu.VMEM((n,) + velocity.shape, jnp.float32),
            pltpu.SemaphoreType.DMA((n,)),
            pltpu.SemaphoreType.DMA((n,)),
            pltpu.SemaphoreType.DMA(()),
        ],
        compiler_params=pltpu.CompilerParams(collective_id=0, has_side_effects=True, vmem_limit_bytes=48 * 1024 * 1024),
        name="kick_reduce_scatter",
    )(imaging, velocity, momentum, mass_diag)


def on_device(
    velocity,
    momentum,
    mass_diag,
    u_prev,
    u_cur,
    adj_next,
    adj_cur,
    observed,
    rec_depth,
    src_cell,
    wavelet,
):
    full_velocity = lax.all_gather(velocity, "shot", axis=0, tiled=True)
    row_count, col_count, depth_cells = full_velocity.shape
    oldest = u_prev[0]
    present = u_cur[0]
    adj_later = adj_next[0]
    adj_now = adj_cur[0]
    rec = rec_depth[0][:, :, None]
    cell = src_cell[0]
    src = jnp.stack(
        [
            cell[0] - lax.axis_index("row") * row_count,
            cell[1] - lax.axis_index("col") * col_count,
            cell[2],
        ]
    ).astype(jnp.int32)
    amp = wavelet[0]

    wave_h, adj_h = exchange([present, adj_now], 1)
    advanced, dw1, pick_adv = leap("wave1", present, *wave_h, oldest, full_velocity, rec, src, amp[0:1])
    dw2, pick_far = leap("wave2", advanced, *exchange([advanced], 2)[0], present, full_velocity, rec, src, amp[1:2])
    misfit_late = pick_far - observed[0, 1][:, :, None]
    misfit_early = pick_adv - observed[0, 0][:, :, None]
    adj_two, part = leap("adj1", adj_now, *adj_h, adj_later, full_velocity, rec, misfit_late, dw2)
    (imaging,) = leap("adj2", adj_two, *exchange([adj_two], 3)[0], adj_now, full_velocity, rec, misfit_early, dw1, part)
    v_new, p_half = kick(imaging, velocity, momentum, mass_diag)
    return (v_new, p_half)


def solution(mesh):
    return jax.shard_map(
        on_device,
        mesh=mesh,
        in_specs=(
            P(("row", "shot"), "col", None),
            P(("row", "shot"), "col", None),
            P(("row", "shot"), "col", None),
            P("shot", "row", "col", None),
            P("shot", "row", "col", None),
            P("shot", "row", "col", None),
            P("shot", "row", "col", None),
            P("shot", None, "row", "col"),
            P("shot", "row", "col"),
            P("shot", None),
            P("shot", None),
        ),
        out_specs=(P(("row", "shot"), "col", None), P(("row", "shot"), "col", None)),
        check_vma=False,
    )
```

```python
import functools

import jax
import jax.numpy as jnp
from jax import lax
from jax.experimental import pallas as pl
from jax.experimental.pallas import tpu as pltpu
from jax.sharding import PartitionSpec as P

STENCIL = (-205.0 / 72.0, 8.0 / 5.0, -1.0 / 5.0, 8.0 / 315.0, -1.0 / 560.0)
squared_courant = 0.012
leap_step = 0.2

ROWS_PER_STEP = 8
Y_CHUNK = 8


class Exchange:
    def __init__(self, fields, bufs, zero_x, zero_y, send_sem, recv_sem, zero_sem):
        self.fields, self.bufs = fields, bufs
        self.zero_x, self.zero_y = zero_x, zero_y
        self.send_sem, self.recv_sem, self.zero_sem = send_sem, recv_sem, zero_sem
        row, nrow = lax.axis_index("row"), lax.axis_size("row")
        col, ncol = lax.axis_index("col"), lax.axis_size("col")
        self.row, self.nrow, self.col, self.ncol = row, nrow, col, ncol
        self.has = (row < nrow - 1, row > 0, col < ncol - 1, col > 0)
        self.peer = ({"row": row + 1}, {"row": row - 1}, {"col": col + 1}, {"col": col - 1})
        self.filler = (1, 0, 3, 2)

    def source(self, f, d):
        rows, cols, _ = f.shape
        if d == 0:
            return f.at[pl.ds(rows - 4, 4)]
        if d == 1:
            return f.at[pl.ds(0, 4)]
        if d == 2:
            return f.at[:, pl.ds(cols - 4, 4)]
        return f.at[:, pl.ds(0, 4)]

    def target(self, j, b):
        if b == 2:
            return self.bufs[4 * j + b].at[:, pl.ds(4, 4)]
        if b == 3:
            return self.bufs[4 * j + b].at[:, pl.ds(0, 4)]
        return self.bufs[4 * j + b]

    def remote(self, j, d):
        return pltpu.make_async_remote_copy(
            src_ref=self.source(self.fields[j], d),
            dst_ref=self.target(j, d),
            send_sem=self.send_sem.at[j, d],
            recv_sem=self.recv_sem.at[j, d],
            device_id=self.peer[d],
            device_id_type=pl.DeviceIdType.MESH,
        )

    def start(self):
        has, row, nrow, col, ncol = self.has, self.row, self.nrow, self.col, self.ncol
        barrier = pltpu.get_barrier_semaphore()
        for d in range(4):
            @pl.when(has[d])
            def _():
                pl.semaphore_signal(barrier, inc=1, device_id=self.peer[d], device_id_type=pl.DeviceIdType.MESH)

        count = (1 - row // (nrow - 1)) + (row + nrow - 1) // nrow + (1 - col // (ncol - 1)) + (col + ncol - 1) // ncol
        pl.semaphore_wait(barrier, count)

        for j in range(len(self.fields)):
            for d in range(4):
                @pl.when(has[d])
                def _():
                    self.remote(j, d).start()

        @pl.when(jnp.logical_not(has[0] & has[1]))
        def _():
            self.zero_x[...] = jnp.zeros_like(self.zero_x)

        @pl.when(jnp.logical_not(has[2] & has[3]))
        def _():
            self.zero_y[...] = jnp.zeros_like(self.zero_y)

        for j in range(len(self.fields)):
            for b in range(4):
                @pl.when(jnp.logical_not(has[self.filler[b]]))
                def _():
                    zero = self.zero_x if b < 2 else self.zero_y
                    copy = pltpu.make_async_copy(zero, self.bufs[4 * j + b], self.zero_sem.at[j, b])
                    copy.start()
                    copy.wait()

    def finish(self):
        has = self.has
        for j in range(len(self.fields)):
            for d in range(4):
                @pl.when(has[d])
                def _():
                    self.remote(j, d).wait_send()
            for b in range(4):
                @pl.when(has[self.filler[b]])
                def _():
                    self.remote(j, b).wait_recv()


def exchange_io(nf, rows, cols, depth):
    shapes = []
    for _ in range(nf):
        shapes += [
            jax.ShapeDtypeStruct((4, cols, depth), jnp.float32),
            jax.ShapeDtypeStruct((4, cols, depth), jnp.float32),
            jax.ShapeDtypeStruct((rows, 8, depth), jnp.float32),
            jax.ShapeDtypeStruct((rows, 8, depth), jnp.float32),
        ]
    scratch = [
        pltpu.VMEM((4, cols, depth), jnp.float32),
        pltpu.VMEM((rows, 8, depth), jnp.float32),
        pltpu.SemaphoreType.DMA((nf, 4)),
        pltpu.SemaphoreType.DMA((nf, 4)),
        pltpu.SemaphoreType.DMA((nf, 4)),
    ]
    return shapes, scratch


def exchange_kernel(nf, *refs):
    ex = Exchange(refs[:nf], refs[nf : 5 * nf], *refs[5 * nf :])
    ex.start()
    ex.finish()


def exchange(fields, collective_id):
    nf = len(fields)
    rows, cols, depth = fields[0].shape
    any_spec = pl.BlockSpec(memory_space=pl.ANY)
    shapes, scratch = exchange_io(nf, rows, cols, depth)
    outs = pl.pallas_call(
        functools.partial(exchange_kernel, nf),
        in_specs=[any_spec] * nf,
        out_specs=[any_spec] * (4 * nf),
        out_shape=shapes,
        scratch_shapes=scratch,
        compiler_params=pltpu.CompilerParams(collective_id=collective_id, has_side_effects=True),
        name=f"halo_exchange_{collective_id}",
    )(*fields)
    return [outs[4 * j : 4 * j + 4] for j in range(nf)]


def step_kernel(kind, names, nf_ex, *refs):
    ref = dict(zip(names, refs))
    if nf_ex:
        ex = Exchange(
            [ref[f"ex_f{j}"] for j in range(nf_ex)],
            [ref[f"ex_b{k}"] for k in range(4 * nf_ex)],
            *[ref[k] for k in ("ex_zx", "ex_zy", "ex_ss", "ex_rs", "ex_zs")],
        )
    f_ref, pad = ref["f"], ref["pad"]
    tb, cols, depth = f_ref.shape
    i = pl.program_id(0)
    n = pl.num_programs(0)

    if nf_ex:
        @pl.when(i == 0)
        def _():
            ex.start()

    lo = jnp.where(i == 0, ref["xlo"][...], ref["flo"][...])
    hi = jnp.where(i == n - 1, ref["xhi"][...], ref["fhi"][...])
    pad[0:4, 8 : 8 + cols, :] = lo
    pad[4 : 4 + tb, 8 : 8 + cols, :] = f_ref[...]
    pad[4 + tb : 8 + tb, 8 : 8 + cols, :] = hi
    pad[4 : 4 + tb, 0:8, :] = ref["ylo"][...]
    pad[4 : 4 + tb, 8 + cols : 16 + cols, :] = ref["yhi"][...]

    z_index = lax.broadcasted_iota(jnp.int32, (Y_CHUNK, depth), 1)
    y_index = lax.broadcasted_iota(jnp.int32, (Y_CHUNK, depth), 0)
    wave = kind in ("wave1", "wave2")
    if wave:
        src_ref = ref["src"]
        src_x = src_ref[0] - i * tb
        src_y = src_ref[1]
        src_z = src_ref[2]
        amp = ref["amp"][0]

    def row(r, carry):
        for y0 in range(0, cols, Y_CHUNK):
            ys = pl.ds(y0, Y_CHUNK)
            pys = pl.ds(8 + y0, Y_CHUNK)
            c = pad[4 + r, pys, :]
            result = (3.0 * STENCIL[0]) * c
            for k in range(1, 5):
                along = pad[4 + r + k, pys, :] + pad[4 + r - k, pys, :]
                along = along + (
                    pad[4 + r, pl.ds(8 + y0 + k, Y_CHUNK), :]
                    + pad[4 + r, pl.ds(8 + y0 - k, Y_CHUNK), :]
                )
                zp = jnp.where(z_index < depth - k, pltpu.roll(c, depth - k, 1), 0.0)
                zm = jnp.where(z_index >= k, pltpu.roll(c, k, 1), 0.0)
                along = along + (zp + zm)
                result = result + STENCIL[k] * along
            v = ref["vel"][r, ys, :]
            stiff = squared_courant * v * v
            prev = ref["prev"][r, ys, :]
            out = 2.0 * c - prev + stiff * result
            if wave:
                at_rec = z_index == ref["rec"][r, ys, :]
                hit = (r == src_x) & (y_index + y0 == src_y) & (z_index == src_z)
                out = out + jnp.where(hit, amp, 0.0)
                sel = jnp.where(at_rec, out, 0.0)
                folded = sel[:, 0:128]
                for t in range(128, depth, 128):
                    folded = folded + sel[:, t : t + 128]
                ref["fold"][pl.ds(pl.multiple_of(r * cols + y0, Y_CHUNK), Y_CHUNK), :] = folded
                ref["o_dw"][r, ys, :] = (out - 2.0 * c) + prev
                if kind == "wave1":
                    ref["o_f"][r, ys, :] = out
            elif kind == "adjbulk":
                ref["o_f"][r, ys, :] = out
            else:
                at_rec = z_index == ref["rec"][r, ys, :]
                out = out + jnp.where(at_rec, ref["mis"][r, ys, :], 0.0)
                ref["o_img"][r, ys, :] = ref["part"][r, ys, :] + out * ref["dw"][r, ys, :]
        return carry

    lax.fori_loop(0, tb, row, 0)
    if wave:
        ref["o_pick"][...] = jnp.sum(ref["fold"][...], axis=1, keepdims=True).reshape(ref["o_pick"].shape)
    if kind == "wave2":
        def inject(r, carry):
            for y0 in range(0, cols, Y_CHUNK):
                ys = pl.ds(y0, Y_CHUNK)
                at_rec = z_index == ref["rec"][r, ys, :]
                misfit = ref["o_pick"][r, ys, :] - ref["obs"][r, ys, :]
                a2 = ref["a2raw"][r, ys, :] + jnp.where(at_rec, misfit, 0.0)
                ref["o_a2"][r, ys, :] = a2
                ref["o_part"][r, ys, :] = a2 * ref["o_dw"][r, ys, :]
            return carry

        lax.fori_loop(0, tb, inject, 0)

    if nf_ex:
        @pl.when(i == n - 1)
        def _():
            ex.finish()


def leap(kind, f, xlo, xhi, ylo, yhi, prev, vel, extra, exchanged=(), collective_id=None):
    rows, cols, depth = f.shape
    tb = ROWS_PER_STEP
    grid = (rows // tb,)
    nq = rows // 4
    block = pl.BlockSpec((tb, cols, depth), lambda i: (i, 0, 0))
    lo_spec = pl.BlockSpec((4, cols, depth), lambda i: (jnp.maximum(2 * i - 1, 0), 0, 0))
    hi_spec = pl.BlockSpec((4, cols, depth), lambda i: (jnp.minimum(2 * i + 2, nq - 1), 0, 0))
    whole4 = pl.BlockSpec((4, cols, depth), lambda i: (0, 0, 0))
    yspec = pl.BlockSpec((tb, 8, depth), lambda i: (i, 0, 0))
    col1 = pl.BlockSpec((tb, cols, 1), lambda i: (i, 0, 0))
    smem = pl.BlockSpec(memory_space=pltpu.SMEM)
    any_spec = pl.BlockSpec(memory_space=pl.ANY)
    field = jax.ShapeDtypeStruct((rows, cols, depth), jnp.float32)
    picked = jax.ShapeDtypeStruct((rows, cols, 1), jnp.float32)
    spec_of = {"src": smem, "amp": smem, "rec": col1, "mis": col1, "obs": col1}

    names = ["f", "flo", "fhi", "xlo", "xhi", "ylo", "yhi", "prev", "vel"]
    in_specs = [block, lo_spec, hi_spec, whole4, whole4, yspec, yspec, block, block]
    args = [f, f, f, xlo, xhi, ylo, yhi, prev, vel]
    for key, value in extra.items():
        names.append(key)
        in_specs.append(spec_of.get(key, block))
        args.append(value)
    nf_ex = len(exchanged)
    for j, g in enumerate(exchanged):
        names.append(f"ex_f{j}")
        in_specs.append(any_spec)
        args.append(g)

    outs = {
        "wave1": [("o_f", field, block), ("o_dw", field, block), ("o_pick", picked, col1)],
        "wave2": [("o_dw", field, block), ("o_pick", picked, col1), ("o_a2", field, block), ("o_part", field, block)],
        "adjbulk": [("o_f", field, block)],
        "adj2": [("o_img", field, block)],
    }[kind]
    names += [o[0] for o in outs]
    out_shape = [o[1] for o in outs]
    out_specs = [o[2] for o in outs]
    scratch = [pltpu.VMEM((tb + 8, cols + 16, depth), jnp.float32)]
    names.append("pad")
    if kind in ("wave1", "wave2"):
        scratch.append(pltpu.VMEM((tb * cols, 128), jnp.float32))
        names.append("fold")
    if nf_ex:
        ex_shapes, ex_scratch = exchange_io(nf_ex, rows, cols, depth)
        k = len(outs)
        names = names[: len(names) - len(scratch)]
        names += [f"ex_b{m}" for m in range(4 * nf_ex)]
        names += ["pad", "fold"][: len(scratch)]
        names += ["ex_zx", "ex_zy", "ex_ss", "ex_rs", "ex_zs"]
        out_shape += ex_shapes
        out_specs += [any_spec] * len(ex_shapes)
        scratch += ex_scratch
        params = pltpu.CompilerParams(
            collective_id=collective_id, has_side_effects=True, vmem_limit_bytes=60 * 1024 * 1024
        )
    else:
        params = pltpu.CompilerParams(vmem_limit_bytes=60 * 1024 * 1024)
    n_big = sum(1 for sp in in_specs if sp is block) + 1 + sum(1 for sp in out_specs if sp is block)
    cost = pl.CostEstimate(
        flops=60 * rows * cols * depth,
        transcendentals=0,
        bytes_accessed=4 * rows * cols * depth * n_big,
    )
    result = pl.pallas_call(
        functools.partial(step_kernel, kind, tuple(names), nf_ex),
        grid=grid,
        in_specs=in_specs,
        out_specs=out_specs,
        out_shape=out_shape,
        scratch_shapes=scratch,
        compiler_params=params,
        cost_estimate=cost,
        name=f"leap_{kind}",
    )(*args)
    if nf_ex:
        own = result[: len(outs)]
        ex = result[len(outs) :]
        return own, [ex[4 * j : 4 * j + 4] for j in range(nf_ex)]
    return result


def kick_kernel(img_ref, vel_ref, mom_ref, mass_ref, v_out, p_out, recv, send_sem, recv_sem, own_sem):
    me = lax.axis_index("shot")
    n = lax.axis_size("shot")
    rows = vel_ref.shape[0]
    mesh = pl.DeviceIdType.MESH

    barrier = pltpu.get_barrier_semaphore()
    for d in range(1, n):
        pl.semaphore_signal(barrier, inc=1, device_id={"shot": lax.rem(me + d, n)}, device_id_type=mesh)
    pl.semaphore_wait(barrier, n - 1)

    sends = []
    for d in (1, n - 1) + tuple(range(2, n - 1)):
        peer = lax.rem(me + d, n)
        copy = pltpu.make_async_remote_copy(
            src_ref=img_ref.at[pl.ds(pl.multiple_of(peer * rows, rows), rows)],
            dst_ref=recv.at[me],
            send_sem=send_sem.at[d],
            recv_sem=recv_sem.at[me],
            device_id={"shot": peer},
            device_id_type=mesh,
        )
        copy.start()
        sends.append(copy)
    own = pltpu.make_async_copy(img_ref.at[pl.ds(pl.multiple_of(me * rows, rows), rows)], recv.at[me], own_sem)
    own.start()
    for copy in sends:
        copy.wait_send()
    own.wait()
    for d in range(1, n):
        src = lax.rem(me + d, n)
        pltpu.make_async_remote_copy(
            src_ref=img_ref.at[pl.ds(0, rows)],
            dst_ref=recv.at[src],
            send_sem=send_sem.at[d],
            recv_sem=recv_sem.at[src],
            device_id={"shot": src},
            device_id_type=mesh,
        ).wait_recv()

    def row(r, carry):
        summed = recv[0, r]
        for s in range(1, n):
            summed = summed + recv[s, r]
        v = vel_ref[r]
        gradient = 2.0 / v * summed
        p_half = mom_ref[r] - 0.5 * leap_step * gradient
        p_out[r] = p_half
        v_out[r] = v + leap_step * p_half / mass_ref[r]
        return carry

    lax.fori_loop(0, rows, row, 0)


def kick(imaging, velocity, momentum, mass_diag):
    n = lax.axis_size("shot")
    vmem = pl.BlockSpec(memory_space=pltpu.VMEM)
    slab = jax.ShapeDtypeStruct(velocity.shape, jnp.float32)
    return pl.pallas_call(
        kick_kernel,
        in_specs=[pl.BlockSpec(memory_space=pl.ANY), vmem, vmem, vmem],
        out_specs=[vmem, vmem],
        out_shape=[slab, slab],
        scratch_shapes=[
            pltpu.VMEM((n,) + velocity.shape, jnp.float32),
            pltpu.SemaphoreType.DMA((n,)),
            pltpu.SemaphoreType.DMA((n,)),
            pltpu.SemaphoreType.DMA(()),
        ],
        compiler_params=pltpu.CompilerParams(collective_id=0, has_side_effects=True, vmem_limit_bytes=48 * 1024 * 1024),
        name="kick_reduce_scatter",
    )(imaging, velocity, momentum, mass_diag)


def on_device(
    velocity,
    momentum,
    mass_diag,
    u_prev,
    u_cur,
    adj_next,
    adj_cur,
    observed,
    rec_depth,
    src_cell,
    wavelet,
):
    full_velocity = lax.all_gather(velocity, "shot", axis=0, tiled=True)
    row_count, col_count, depth_cells = full_velocity.shape
    oldest = u_prev[0]
    present = u_cur[0]
    adj_later = adj_next[0]
    adj_now = adj_cur[0]
    rec = rec_depth[0][:, :, None]
    cell = src_cell[0]
    src = jnp.stack(
        [
            cell[0] - lax.axis_index("row") * row_count,
            cell[1] - lax.axis_index("col") * col_count,
            cell[2],
        ]
    ).astype(jnp.int32)
    amp = wavelet[0]

    wave_h, adj_h = exchange([present, adj_now], 1)
    advanced, dw1, pick_adv = leap(
        "wave1", present, *wave_h, oldest, full_velocity, {"rec": rec, "src": src, "amp": amp[0:1]}
    )
    (adj_bulk,), (adv_h,) = leap(
        "adjbulk", adj_now, *adj_h, adj_later, full_velocity, {}, exchanged=[advanced], collective_id=2
    )
    dw2, pick_far, adj_two, part = leap(
        "wave2",
        advanced,
        *adv_h,
        present,
        full_velocity,
        {"rec": rec, "src": src, "amp": amp[1:2], "a2raw": adj_bulk, "obs": observed[0, 1][:, :, None]},
    )
    misfit_early = pick_adv - observed[0, 0][:, :, None]
    (imaging,) = leap(
        "adj2",
        adj_two,
        *exchange([adj_two], 3)[0],
        adj_now,
        full_velocity,
        {"rec": rec, "mis": misfit_early, "dw": dw1, "part": part},
    )
    v_new, p_half = kick(imaging, velocity, momentum, mass_diag)
    return (v_new, p_half)


def solution(mesh):
    return jax.shard_map(
        on_device,
        mesh=mesh,
        in_specs=(
            P(("row", "shot"), "col", None),
            P(("row", "shot"), "col", None),
            P(("row", "shot"), "col", None),
            P("shot", "row", "col", None),
            P("shot", "row", "col", None),
            P("shot", "row", "col", None),
            P("shot", "row", "col", None),
            P("shot", None, "row", "col"),
            P("shot", "row", "col"),
            P("shot", None),
            P("shot", None),
        ),
        out_specs=(P(("row", "shot"), "col", None), P(("row", "shot"), "col", None)),
        check_vma=False,
    )
```

```python
import functools

import jax
import jax.numpy as jnp
from jax import lax
from jax.experimental import pallas as pl
from jax.experimental.pallas import tpu as pltpu
from jax.sharding import PartitionSpec as P

STENCIL = (-205.0 / 72.0, 8.0 / 5.0, -1.0 / 5.0, 8.0 / 315.0, -1.0 / 560.0)
squared_courant = 0.012
leap_step = 0.2

ROWS_PER_STEP = 8
Y_CHUNK = 8


class Exchange:
    def __init__(self, fields, bufs, zero_x, zero_y, send_sem, recv_sem, zero_sem):
        self.fields, self.bufs = fields, bufs
        self.zero_x, self.zero_y = zero_x, zero_y
        self.send_sem, self.recv_sem, self.zero_sem = send_sem, recv_sem, zero_sem
        row, nrow = lax.axis_index("row"), lax.axis_size("row")
        col, ncol = lax.axis_index("col"), lax.axis_size("col")
        self.row, self.nrow, self.col, self.ncol = row, nrow, col, ncol
        self.has = (row < nrow - 1, row > 0, col < ncol - 1, col > 0)
        self.peer = ({"row": row + 1}, {"row": row - 1}, {"col": col + 1}, {"col": col - 1})
        self.filler = (1, 0, 3, 2)

    def source(self, f, d):
        rows, cols, _ = f.shape
        if d == 0:
            return f.at[pl.ds(rows - 4, 4)]
        if d == 1:
            return f.at[pl.ds(0, 4)]
        if d == 2:
            return f.at[:, pl.ds(cols - 4, 4)]
        return f.at[:, pl.ds(0, 4)]

    def target(self, j, b):
        if b == 2:
            return self.bufs[4 * j + b].at[:, pl.ds(4, 4)]
        if b == 3:
            return self.bufs[4 * j + b].at[:, pl.ds(0, 4)]
        return self.bufs[4 * j + b]

    def remote(self, j, d):
        return pltpu.make_async_remote_copy(
            src_ref=self.source(self.fields[j], d),
            dst_ref=self.target(j, d),
            send_sem=self.send_sem.at[j, d],
            recv_sem=self.recv_sem.at[j, d],
            device_id=self.peer[d],
            device_id_type=pl.DeviceIdType.MESH,
        )

    def start(self):
        has, row, nrow, col, ncol = self.has, self.row, self.nrow, self.col, self.ncol
        barrier = pltpu.get_barrier_semaphore()
        for d in range(4):
            @pl.when(has[d])
            def _():
                pl.semaphore_signal(barrier, inc=1, device_id=self.peer[d], device_id_type=pl.DeviceIdType.MESH)

        count = (1 - row // (nrow - 1)) + (row + nrow - 1) // nrow + (1 - col // (ncol - 1)) + (col + ncol - 1) // ncol
        pl.semaphore_wait(barrier, count)

        for j in range(len(self.fields)):
            for d in range(4):
                @pl.when(has[d])
                def _():
                    self.remote(j, d).start()

        @pl.when(jnp.logical_not(has[0] & has[1]))
        def _():
            self.zero_x[...] = jnp.zeros_like(self.zero_x)

        @pl.when(jnp.logical_not(has[2] & has[3]))
        def _():
            self.zero_y[...] = jnp.zeros_like(self.zero_y)

        for j in range(len(self.fields)):
            for b in range(4):
                @pl.when(jnp.logical_not(has[self.filler[b]]))
                def _():
                    zero = self.zero_x if b < 2 else self.zero_y
                    copy = pltpu.make_async_copy(zero, self.bufs[4 * j + b], self.zero_sem.at[j, b])
                    copy.start()
                    copy.wait()

    def finish(self):
        has = self.has
        for j in range(len(self.fields)):
            for d in range(4):
                @pl.when(has[d])
                def _():
                    self.remote(j, d).wait_send()
            for b in range(4):
                @pl.when(has[self.filler[b]])
                def _():
                    self.remote(j, b).wait_recv()


def exchange_io(nf, rows, cols, depth):
    shapes = []
    for _ in range(nf):
        shapes += [
            jax.ShapeDtypeStruct((4, cols, depth), jnp.float32),
            jax.ShapeDtypeStruct((4, cols, depth), jnp.float32),
            jax.ShapeDtypeStruct((rows, 8, depth), jnp.float32),
            jax.ShapeDtypeStruct((rows, 8, depth), jnp.float32),
        ]
    scratch = [
        pltpu.VMEM((4, cols, depth), jnp.float32),
        pltpu.VMEM((rows, 8, depth), jnp.float32),
        pltpu.SemaphoreType.DMA((nf, 4)),
        pltpu.SemaphoreType.DMA((nf, 4)),
        pltpu.SemaphoreType.DMA((nf, 4)),
    ]
    return shapes, scratch


def exchange_kernel(nf, *refs):
    ex = Exchange(refs[:nf], refs[nf : 5 * nf], *refs[5 * nf :])
    ex.start()
    ex.finish()


def exchange(fields, collective_id):
    nf = len(fields)
    rows, cols, depth = fields[0].shape
    any_spec = pl.BlockSpec(memory_space=pl.ANY)
    shapes, scratch = exchange_io(nf, rows, cols, depth)
    outs = pl.pallas_call(
        functools.partial(exchange_kernel, nf),
        in_specs=[any_spec] * nf,
        out_specs=[any_spec] * (4 * nf),
        out_shape=shapes,
        scratch_shapes=scratch,
        compiler_params=pltpu.CompilerParams(collective_id=collective_id, has_side_effects=True),
        name=f"halo_exchange_{collective_id}",
    )(*fields)
    return [outs[4 * j : 4 * j + 4] for j in range(nf)]


class HaloSender:
    def __init__(self, ref, nblk, tb):
        self.ref, self.nblk, self.tb = ref, nblk, tb
        row, nrow = lax.axis_index("row"), lax.axis_size("row")
        col, ncol = lax.axis_index("col"), lax.axis_size("col")
        self.row, self.nrow, self.col, self.ncol = row, nrow, col, ncol
        self.has = (row < nrow - 1, row > 0, col < ncol - 1, col > 0)
        self.peer = ({"row": row + 1}, {"row": row - 1}, {"col": col + 1}, {"col": col - 1})
        self.filler = (1, 0, 3, 2)
        self.bufs = [ref[f"h_b{b}"] for b in range(4)]

    def copy(self, d, blk):
        ref, tb = self.ref, self.tb
        rows_here = pl.ds(pl.multiple_of(blk * tb, tb), tb)
        if d == 0:
            src, dst, sem = ref["stg_xlo"], self.bufs[0], ref["h_ss"].at[0, 0]
        elif d == 1:
            src, dst, sem = ref["stg_xhi"], self.bufs[1], ref["h_ss"].at[0, 1]
        elif d == 2:
            src, dst = ref["stg_ylo"].at[rows_here], self.bufs[2].at[rows_here, pl.ds(4, 4)]
            sem = ref["h_ss"].at[blk, 2]
        else:
            src, dst = ref["stg_yhi"].at[rows_here], self.bufs[3].at[rows_here, pl.ds(0, 4)]
            sem = ref["h_ss"].at[blk, 3]
        return pltpu.make_async_remote_copy(
            src_ref=src,
            dst_ref=dst,
            send_sem=sem,
            recv_sem=ref["h_rs"].at[d],
            device_id=self.peer[d],
            device_id_type=pl.DeviceIdType.MESH,
        )

    def whole(self, b):
        ref = self.ref
        src = {0: ref["stg_xlo"], 1: ref["stg_xhi"], 2: ref["stg_ylo"], 3: ref["stg_yhi"]}[b]
        dst = {0: self.bufs[0], 1: self.bufs[1], 2: self.bufs[2].at[:, pl.ds(4, 4)], 3: self.bufs[3].at[:, pl.ds(0, 4)]}[b]
        return pltpu.make_async_remote_copy(
            src_ref=src,
            dst_ref=dst,
            send_sem=ref["h_ss"].at[0, b],
            recv_sem=ref["h_rs"].at[b],
            device_id=self.peer[b],
            device_id_type=pl.DeviceIdType.MESH,
        )

    def begin(self):
        ref, has, row, nrow, col, ncol = self.ref, self.has, self.row, self.nrow, self.col, self.ncol
        barrier = pltpu.get_barrier_semaphore()
        for d in range(4):
            @pl.when(has[d])
            def _():
                pl.semaphore_signal(barrier, inc=1, device_id=self.peer[d], device_id_type=pl.DeviceIdType.MESH)

        count = (1 - row // (nrow - 1)) + (row + nrow - 1) // nrow + (1 - col // (ncol - 1)) + (col + ncol - 1) // ncol
        pl.semaphore_wait(barrier, count)

        @pl.when(jnp.logical_not(has[0] & has[1]))
        def _():
            ref["h_zx"][...] = jnp.zeros_like(ref["h_zx"])

        @pl.when(jnp.logical_not(has[2] & has[3]))
        def _():
            ref["h_zy"][...] = jnp.zeros_like(ref["h_zy"])

        for b in range(4):
            @pl.when(jnp.logical_not(has[self.filler[b]]))
            def _():
                zero = ref["h_zx"] if b < 2 else ref["h_zy"]
                copy = pltpu.make_async_copy(zero, self.bufs[b], ref["h_zs"].at[b])
                copy.start()
                copy.wait()

    def send_block(self, blk):
        ref, has, tb = self.ref, self.has, self.tb

        @pl.when(blk == 0)
        def _():
            ref["stg_xhi"][...] = ref["o_a2"][0:4]

        @pl.when(blk == self.nblk - 1)
        def _():
            ref["stg_xlo"][...] = ref["o_a2"][tb - 4 : tb]

        for d in (2, 3):
            @pl.when(has[d])
            def _():
                self.copy(d, blk).start()

        @pl.when(has[1] & (blk == 0))
        def _():
            self.copy(1, blk).start()

        @pl.when(has[0] & (blk == self.nblk - 1))
        def _():
            self.copy(0, blk).start()

    def finish(self):
        has = self.has
        for blk in range(self.nblk):
            for d in (2, 3):
                @pl.when(has[d])
                def _():
                    self.copy(d, blk).wait_send()

        @pl.when(has[1])
        def _():
            self.copy(1, 0).wait_send()

        @pl.when(has[0])
        def _():
            self.copy(0, self.nblk - 1).wait_send()

        for b in range(4):
            @pl.when(has[self.filler[b]])
            def _():
                self.whole(b).wait_recv()


def step_kernel(kind, names, nf_ex, *refs):
    ref = dict(zip(names, refs))
    if nf_ex:
        ex = Exchange(
            [ref[f"ex_f{j}"] for j in range(nf_ex)],
            [ref[f"ex_b{k}"] for k in range(4 * nf_ex)],
            *[ref[k] for k in ("ex_zx", "ex_zy", "ex_ss", "ex_rs", "ex_zs")],
        )
    f_ref, pad = ref["f"], ref["pad"]
    tb, cols, depth = f_ref.shape
    i = pl.program_id(0)
    n = pl.num_programs(0)

    if nf_ex:
        @pl.when(i == 0)
        def _():
            ex.start()

    lo = jnp.where(i == 0, ref["xlo"][...], ref["flo"][...])
    hi = jnp.where(i == n - 1, ref["xhi"][...], ref["fhi"][...])
    pad[0:4, 8 : 8 + cols, :] = lo
    pad[4 : 4 + tb, 8 : 8 + cols, :] = f_ref[...]
    pad[4 + tb : 8 + tb, 8 : 8 + cols, :] = hi
    pad[4 : 4 + tb, 0:8, :] = ref["ylo"][...]
    pad[4 : 4 + tb, 8 + cols : 16 + cols, :] = ref["yhi"][...]

    z_index = lax.broadcasted_iota(jnp.int32, (Y_CHUNK, depth), 1)
    y_index = lax.broadcasted_iota(jnp.int32, (Y_CHUNK, depth), 0)
    wave = kind in ("wave1", "wave2")
    if wave:
        src_ref = ref["src"]
        src_x = src_ref[0] - i * tb
        src_y = src_ref[1]
        src_z = src_ref[2]
        amp = ref["amp"][0]

    def row(r, carry):
        for y0 in range(0, cols, Y_CHUNK):
            ys = pl.ds(y0, Y_CHUNK)
            pys = pl.ds(8 + y0, Y_CHUNK)
            c = pad[4 + r, pys, :]
            result = (3.0 * STENCIL[0]) * c
            for k in range(1, 5):
                along = pad[4 + r + k, pys, :] + pad[4 + r - k, pys, :]
                along = along + (
                    pad[4 + r, pl.ds(8 + y0 + k, Y_CHUNK), :]
                    + pad[4 + r, pl.ds(8 + y0 - k, Y_CHUNK), :]
                )
                zp = jnp.where(z_index < depth - k, pltpu.roll(c, depth - k, 1), 0.0)
                zm = jnp.where(z_index >= k, pltpu.roll(c, k, 1), 0.0)
                along = along + (zp + zm)
                result = result + STENCIL[k] * along
            v = ref["vel"][r, ys, :]
            stiff = squared_courant * v * v
            prev = ref["prev"][r, ys, :]
            out = 2.0 * c - prev + stiff * result
            if wave:
                at_rec = z_index == ref["rec"][r, ys, :]
                hit = (r == src_x) & (y_index + y0 == src_y) & (z_index == src_z)
                out = out + jnp.where(hit, amp, 0.0)
                sel = jnp.where(at_rec, out, 0.0)
                folded = sel[:, 0:128]
                for t in range(128, depth, 128):
                    folded = folded + sel[:, t : t + 128]
                ref["fold"][pl.ds(pl.multiple_of(r * cols + y0, Y_CHUNK), Y_CHUNK), :] = folded
                ref["o_dw"][r, ys, :] = (out - 2.0 * c) + prev
                if kind == "wave1":
                    ref["o_f"][r, ys, :] = out
            elif kind == "adjbulk":
                ref["o_f"][r, ys, :] = out
            else:
                at_rec = z_index == ref["rec"][r, ys, :]
                out = out + jnp.where(at_rec, ref["mis"][r, ys, :], 0.0)
                ref["o_img"][r, ys, :] = ref["part"][r, ys, :] + out * ref["dw"][r, ys, :]
        return carry

    lax.fori_loop(0, tb, row, 0)
    if wave:
        ref["o_pick"][...] = jnp.sum(ref["fold"][...], axis=1, keepdims=True).reshape(ref["o_pick"].shape)
    if kind == "wave2":
        sender = HaloSender(ref, n, tb)

        @pl.when(i == 0)
        def _():
            sender.begin()

        def inject(r, carry):
            for y0 in range(0, cols, Y_CHUNK):
                ys = pl.ds(y0, Y_CHUNK)
                at_rec = z_index == ref["rec"][r, ys, :]
                misfit = ref["o_pick"][r, ys, :] - ref["obs"][r, ys, :]
                a2 = ref["a2raw"][r, ys, :] + jnp.where(at_rec, misfit, 0.0)
                ref["o_a2"][r, ys, :] = a2
                ref["o_part"][r, ys, :] = a2 * ref["o_dw"][r, ys, :]
                if y0 == 0:
                    ref["stg_yhi"][i * tb + r] = a2[0:4]
                if y0 == cols - Y_CHUNK:
                    ref["stg_ylo"][i * tb + r] = a2[Y_CHUNK - 4 : Y_CHUNK]
            return carry

        lax.fori_loop(0, tb, inject, 0)
        sender.send_block(i)

        @pl.when(i == n - 1)
        def _():
            sender.finish()

    if nf_ex:
        @pl.when(i == n - 1)
        def _():
            ex.finish()


def leap(kind, f, xlo, xhi, ylo, yhi, prev, vel, extra, exchanged=(), collective_id=None):
    rows, cols, depth = f.shape
    tb = ROWS_PER_STEP
    grid = (rows // tb,)
    nq = rows // 4
    block = pl.BlockSpec((tb, cols, depth), lambda i: (i, 0, 0))
    lo_spec = pl.BlockSpec((4, cols, depth), lambda i: (jnp.maximum(2 * i - 1, 0), 0, 0))
    hi_spec = pl.BlockSpec((4, cols, depth), lambda i: (jnp.minimum(2 * i + 2, nq - 1), 0, 0))
    whole4 = pl.BlockSpec((4, cols, depth), lambda i: (0, 0, 0))
    yspec = pl.BlockSpec((tb, 8, depth), lambda i: (i, 0, 0))
    col1 = pl.BlockSpec((tb, cols, 1), lambda i: (i, 0, 0))
    smem = pl.BlockSpec(memory_space=pltpu.SMEM)
    any_spec = pl.BlockSpec(memory_space=pl.ANY)
    field = jax.ShapeDtypeStruct((rows, cols, depth), jnp.float32)
    picked = jax.ShapeDtypeStruct((rows, cols, 1), jnp.float32)
    spec_of = {"src": smem, "amp": smem, "rec": col1, "mis": col1, "obs": col1}

    names = ["f", "flo", "fhi", "xlo", "xhi", "ylo", "yhi", "prev", "vel"]
    in_specs = [block, lo_spec, hi_spec, whole4, whole4, yspec, yspec, block, block]
    args = [f, f, f, xlo, xhi, ylo, yhi, prev, vel]
    for key, value in extra.items():
        names.append(key)
        in_specs.append(spec_of.get(key, block))
        args.append(value)
    nf_ex = len(exchanged)
    for j, g in enumerate(exchanged):
        names.append(f"ex_f{j}")
        in_specs.append(any_spec)
        args.append(g)

    outs = {
        "wave1": [("o_f", field, block), ("o_dw", field, block), ("o_pick", picked, col1)],
        "wave2": [("o_dw", field, block), ("o_pick", picked, col1), ("o_a2", field, block), ("o_part", field, block)],
        "adjbulk": [("o_f", field, block)],
        "adj2": [("o_img", field, block)],
    }[kind]
    names += [o[0] for o in outs]
    out_shape = [o[1] for o in outs]
    out_specs = [o[2] for o in outs]
    scratch = [pltpu.VMEM((tb + 8, cols + 16, depth), jnp.float32)]
    names.append("pad")
    if kind in ("wave1", "wave2"):
        scratch.append(pltpu.VMEM((tb * cols, 128), jnp.float32))
        names.append("fold")
    if kind == "wave2":
        h_shapes, _ = exchange_io(1, rows, cols, depth)
        names = names[: len(names) - len(scratch)]
        names += [f"h_b{m}" for m in range(4)]
        names += ["pad", "fold"]
        names += ["stg_xlo", "stg_xhi", "stg_ylo", "stg_yhi", "h_zx", "h_zy", "h_ss", "h_rs", "h_zs"]
        out_shape += h_shapes
        out_specs += [any_spec] * 4
        scratch += [
            pltpu.VMEM((4, cols, depth), jnp.float32),
            pltpu.VMEM((4, cols, depth), jnp.float32),
            pltpu.VMEM((rows, 4, depth), jnp.float32),
            pltpu.VMEM((rows, 4, depth), jnp.float32),
            pltpu.VMEM((4, cols, depth), jnp.float32),
            pltpu.VMEM((rows, 8, depth), jnp.float32),
            pltpu.SemaphoreType.DMA((rows // tb, 4)),
            pltpu.SemaphoreType.DMA((4,)),
            pltpu.SemaphoreType.DMA((4,)),
        ]
        params = pltpu.CompilerParams(
            collective_id=collective_id, has_side_effects=True, vmem_limit_bytes=60 * 1024 * 1024
        )
    elif nf_ex:
        ex_shapes, ex_scratch = exchange_io(nf_ex, rows, cols, depth)
        k = len(outs)
        names = names[: len(names) - len(scratch)]
        names += [f"ex_b{m}" for m in range(4 * nf_ex)]
        names += ["pad", "fold"][: len(scratch)]
        names += ["ex_zx", "ex_zy", "ex_ss", "ex_rs", "ex_zs"]
        out_shape += ex_shapes
        out_specs += [any_spec] * len(ex_shapes)
        scratch += ex_scratch
        params = pltpu.CompilerParams(
            collective_id=collective_id, has_side_effects=True, vmem_limit_bytes=60 * 1024 * 1024
        )
    else:
        params = pltpu.CompilerParams(vmem_limit_bytes=60 * 1024 * 1024)
    n_big = sum(1 for sp in in_specs if sp is block) + 1 + sum(1 for sp in out_specs if sp is block)
    cost = pl.CostEstimate(
        flops=60 * rows * cols * depth,
        transcendentals=0,
        bytes_accessed=4 * rows * cols * depth * n_big,
    )
    result = pl.pallas_call(
        functools.partial(step_kernel, kind, tuple(names), nf_ex),
        grid=grid,
        in_specs=in_specs,
        out_specs=out_specs,
        out_shape=out_shape,
        scratch_shapes=scratch,
        compiler_params=params,
        cost_estimate=cost,
        name=f"leap_{kind}",
    )(*args)
    if kind == "wave2":
        return result[: len(outs)], result[len(outs) :]
    if nf_ex:
        own = result[: len(outs)]
        ex = result[len(outs) :]
        return own, [ex[4 * j : 4 * j + 4] for j in range(nf_ex)]
    return result


def kick_kernel(img_ref, vel_ref, mom_ref, mass_ref, v_out, p_out, recv, send_sem, recv_sem, own_sem):
    me = lax.axis_index("shot")
    n = lax.axis_size("shot")
    rows = vel_ref.shape[0]
    mesh = pl.DeviceIdType.MESH

    barrier = pltpu.get_barrier_semaphore()
    for d in range(1, n):
        pl.semaphore_signal(barrier, inc=1, device_id={"shot": lax.rem(me + d, n)}, device_id_type=mesh)
    pl.semaphore_wait(barrier, n - 1)

    sends = []
    for d in (1, n - 1) + tuple(range(2, n - 1)):
        peer = lax.rem(me + d, n)
        copy = pltpu.make_async_remote_copy(
            src_ref=img_ref.at[pl.ds(pl.multiple_of(peer * rows, rows), rows)],
            dst_ref=recv.at[me],
            send_sem=send_sem.at[d],
            recv_sem=recv_sem.at[me],
            device_id={"shot": peer},
            device_id_type=mesh,
        )
        copy.start()
        sends.append(copy)
    own = pltpu.make_async_copy(img_ref.at[pl.ds(pl.multiple_of(me * rows, rows), rows)], recv.at[me], own_sem)
    own.start()
    for copy in sends:
        copy.wait_send()
    own.wait()
    for d in range(1, n):
        src = lax.rem(me + d, n)
        pltpu.make_async_remote_copy(
            src_ref=img_ref.at[pl.ds(0, rows)],
            dst_ref=recv.at[src],
            send_sem=send_sem.at[d],
            recv_sem=recv_sem.at[src],
            device_id={"shot": src},
            device_id_type=mesh,
        ).wait_recv()

    def row(r, carry):
        summed = recv[0, r]
        for s in range(1, n):
            summed = summed + recv[s, r]
        v = vel_ref[r]
        gradient = 2.0 / v * summed
        p_half = mom_ref[r] - 0.5 * leap_step * gradient
        p_out[r] = p_half
        v_out[r] = v + leap_step * p_half / mass_ref[r]
        return carry

    lax.fori_loop(0, rows, row, 0)


def kick(imaging, velocity, momentum, mass_diag):
    n = lax.axis_size("shot")
    vmem = pl.BlockSpec(memory_space=pltpu.VMEM)
    slab = jax.ShapeDtypeStruct(velocity.shape, jnp.float32)
    return pl.pallas_call(
        kick_kernel,
        in_specs=[pl.BlockSpec(memory_space=pl.ANY), vmem, vmem, vmem],
        out_specs=[vmem, vmem],
        out_shape=[slab, slab],
        scratch_shapes=[
            pltpu.VMEM((n,) + velocity.shape, jnp.float32),
            pltpu.SemaphoreType.DMA((n,)),
            pltpu.SemaphoreType.DMA((n,)),
            pltpu.SemaphoreType.DMA(()),
        ],
        compiler_params=pltpu.CompilerParams(collective_id=0, has_side_effects=True, vmem_limit_bytes=48 * 1024 * 1024),
        name="kick_reduce_scatter",
    )(imaging, velocity, momentum, mass_diag)


def on_device(
    velocity,
    momentum,
    mass_diag,
    u_prev,
    u_cur,
    adj_next,
    adj_cur,
    observed,
    rec_depth,
    src_cell,
    wavelet,
):
    full_velocity = lax.all_gather(velocity, "shot", axis=0, tiled=True)
    row_count, col_count, depth_cells = full_velocity.shape
    oldest = u_prev[0]
    present = u_cur[0]
    adj_later = adj_next[0]
    adj_now = adj_cur[0]
    rec = rec_depth[0][:, :, None]
    cell = src_cell[0]
    src = jnp.stack(
        [
            cell[0] - lax.axis_index("row") * row_count,
            cell[1] - lax.axis_index("col") * col_count,
            cell[2],
        ]
    ).astype(jnp.int32)
    amp = wavelet[0]

    wave_h, adj_h = exchange([present, adj_now], 1)
    advanced, dw1, pick_adv = leap(
        "wave1", present, *wave_h, oldest, full_velocity, {"rec": rec, "src": src, "amp": amp[0:1]}
    )
    (adj_bulk,), (adv_h,) = leap(
        "adjbulk", adj_now, *adj_h, adj_later, full_velocity, {}, exchanged=[advanced], collective_id=2
    )
    (dw2, pick_far, adj_two, part), adj_two_h = leap(
        "wave2",
        advanced,
        *adv_h,
        present,
        full_velocity,
        {"rec": rec, "src": src, "amp": amp[1:2], "a2raw": adj_bulk, "obs": observed[0, 1][:, :, None]},
        collective_id=3,
    )
    misfit_early = pick_adv - observed[0, 0][:, :, None]
    (imaging,) = leap(
        "adj2",
        adj_two,
        *adj_two_h,
        adj_now,
        full_velocity,
        {"rec": rec, "mis": misfit_early, "dw": dw1, "part": part},
    )
    v_new, p_half = kick(imaging, velocity, momentum, mass_diag)
    return (v_new, p_half)


def solution(mesh):
    return jax.shard_map(
        on_device,
        mesh=mesh,
        in_specs=(
            P(("row", "shot"), "col", None),
            P(("row", "shot"), "col", None),
            P(("row", "shot"), "col", None),
            P("shot", "row", "col", None),
            P("shot", "row", "col", None),
            P("shot", "row", "col", None),
            P("shot", "row", "col", None),
            P("shot", None, "row", "col"),
            P("shot", "row", "col"),
            P("shot", None),
            P("shot", None),
        ),
        out_specs=(P(("row", "shot"), "col", None), P(("row", "shot"), "col", None)),
        check_vma=False,
    )
```

```python
import functools

import jax
import jax.numpy as jnp
from jax import lax
from jax.experimental import pallas as pl
from jax.experimental.pallas import tpu as pltpu
from jax.sharding import PartitionSpec as P

STENCIL = (-205.0 / 72.0, 8.0 / 5.0, -1.0 / 5.0, 8.0 / 315.0, -1.0 / 560.0)
squared_courant = 0.012
leap_step = 0.2

class S:
    a2raw = 0
    amp = 1
    dw = 2
    ex_rs = 3
    ex_ss = 4
    ex_zs = 5
    ex_zx = 6
    ex_zy = 7
    f = 8
    fhi = 9
    flo = 10
    fold = 11
    h_rs = 12
    h_ss = 13
    h_zs = 14
    h_zx = 15
    h_zy = 16
    mass = 17
    mis = 18
    mom = 19
    o_a2 = 20
    o_dw = 21
    o_f = 22
    o_p = 23
    o_part = 24
    o_pick = 25
    o_v = 26
    obs = 27
    pad = 28
    part = 29
    prev = 30
    rec = 31
    rs_own = 32
    rs_rs = 33
    rs_ss = 34
    slot_in = 35
    slot_out = 36
    src = 37
    stg_xhi = 38
    stg_xlo = 39
    stg_yhi = 40
    stg_ylo = 41
    vel = 42
    vslab = 43
    xhi = 44
    xlo = 45
    yhi = 46
    ylo = 47
    ex_f = 100
    ex_b = 110
    h_b = 130


ROWS_PER_STEP = 8
Y_CHUNK = 8


class Exchange:

    def __init__(self, fields, bufs, zero_x, zero_y, send_sem, recv_sem, zero_sem):
        self.fields, self.bufs = fields, bufs
        self.zero_x, self.zero_y = zero_x, zero_y
        self.send_sem, self.recv_sem, self.zero_sem = send_sem, recv_sem, zero_sem
        row, nrow = lax.axis_index("row"), lax.axis_size("row")
        col, ncol = lax.axis_index("col"), lax.axis_size("col")
        self.row, self.nrow, self.col, self.ncol = row, nrow, col, ncol
        self.has = (row < nrow - 1, row > 0, col < ncol - 1, col > 0)
        self.peer = ({"row": row + 1}, {"row": row - 1}, {"col": col + 1}, {"col": col - 1})
        self.filler = (1, 0, 3, 2)

    def source(self, f, d):
        rows, cols, _ = f.shape
        if d == 0:
            return f.at[pl.ds(rows - 4, 4)]
        if d == 1:
            return f.at[pl.ds(0, 4)]
        if d == 2:
            return f.at[:, pl.ds(cols - 4, 4)]
        return f.at[:, pl.ds(0, 4)]

    def target(self, j, b):
        if b == 2:
            return self.bufs[4 * j + b].at[:, pl.ds(4, 4)]
        if b == 3:
            return self.bufs[4 * j + b].at[:, pl.ds(0, 4)]
        return self.bufs[4 * j + b]

    def remote(self, j, d):
        return pltpu.make_async_remote_copy(
            src_ref=self.source(self.fields[j], d),
            dst_ref=self.target(j, d),
            send_sem=self.send_sem.at[j, d],
            recv_sem=self.recv_sem.at[j, d],
            device_id=self.peer[d],
            device_id_type=pl.DeviceIdType.MESH,
        )

    def start(self):
        has, row, nrow, col, ncol = self.has, self.row, self.nrow, self.col, self.ncol
        barrier = pltpu.get_barrier_semaphore()
        for d in range(4):
            @pl.when(has[d])
            def _():
                pl.semaphore_signal(barrier, inc=1, device_id=self.peer[d], device_id_type=pl.DeviceIdType.MESH)

        count = (1 - row // (nrow - 1)) + (row + nrow - 1) // nrow + (1 - col // (ncol - 1)) + (col + ncol - 1) // ncol
        pl.semaphore_wait(barrier, count)

        for j in range(len(self.fields)):
            for d in range(4):
                @pl.when(has[d])
                def _():
                    self.remote(j, d).start()

        @pl.when(jnp.logical_not(has[0] & has[1]))
        def _():
            self.zero_x[...] = jnp.zeros_like(self.zero_x)

        @pl.when(jnp.logical_not(has[2] & has[3]))
        def _():
            self.zero_y[...] = jnp.zeros_like(self.zero_y)

        for j in range(len(self.fields)):
            for b in range(4):
                @pl.when(jnp.logical_not(has[self.filler[b]]))
                def _():
                    zero = self.zero_x if b < 2 else self.zero_y
                    copy = pltpu.make_async_copy(zero, self.bufs[4 * j + b], self.zero_sem.at[j, b])
                    copy.start()
                    copy.wait()

    def finish(self):
        has = self.has
        for j in range(len(self.fields)):
            for d in range(4):
                @pl.when(has[d])
                def _():
                    self.remote(j, d).wait_send()
            for b in range(4):
                @pl.when(has[self.filler[b]])
                def _():
                    self.remote(j, b).wait_recv()


def exchange_io(nf, rows, cols, depth):
    shapes = []
    for _ in range(nf):
        shapes += [
            jax.ShapeDtypeStruct((4, cols, depth), jnp.float32),
            jax.ShapeDtypeStruct((4, cols, depth), jnp.float32),
            jax.ShapeDtypeStruct((rows, 8, depth), jnp.float32),
            jax.ShapeDtypeStruct((rows, 8, depth), jnp.float32),
        ]
    scratch = [
        pltpu.VMEM((4, cols, depth), jnp.float32),
        pltpu.VMEM((rows, 8, depth), jnp.float32),
        pltpu.SemaphoreType.DMA((nf, 4)),
        pltpu.SemaphoreType.DMA((nf, 4)),
        pltpu.SemaphoreType.DMA((nf, 4)),
    ]
    return shapes, scratch


def exchange_kernel(nf, *refs):
    ex = Exchange(refs[:nf], refs[nf : 5 * nf], *refs[5 * nf :])
    ex.start()
    ex.finish()


def exchange(fields, collective_id):
    nf = len(fields)
    rows, cols, depth = fields[0].shape
    any_spec = pl.BlockSpec(memory_space=pl.ANY)
    shapes, scratch = exchange_io(nf, rows, cols, depth)
    outs = pl.pallas_call(
        functools.partial(exchange_kernel, nf),
        in_specs=[any_spec] * nf,
        out_specs=[any_spec] * (4 * nf),
        out_shape=shapes,
        scratch_shapes=scratch,
        compiler_params=pltpu.CompilerParams(collective_id=collective_id, has_side_effects=True),
        name=f"halo_exchange_{collective_id}",
    )(*fields)
    return [outs[4 * j : 4 * j + 4] for j in range(nf)]


class HaloSender:

    def __init__(self, ref, nblk, tb):
        self.ref, self.nblk, self.tb = ref, nblk, tb
        row, nrow = lax.axis_index("row"), lax.axis_size("row")
        col, ncol = lax.axis_index("col"), lax.axis_size("col")
        self.row, self.nrow, self.col, self.ncol = row, nrow, col, ncol
        self.has = (row < nrow - 1, row > 0, col < ncol - 1, col > 0)
        self.peer = ({"row": row + 1}, {"row": row - 1}, {"col": col + 1}, {"col": col - 1})
        self.filler = (1, 0, 3, 2)
        self.bufs = [ref[S.h_b + b] for b in range(4)]

    def copy(self, d, blk):
        ref, tb = self.ref, self.tb
        rows_here = pl.ds(pl.multiple_of(blk * tb, tb), tb)
        if d == 0:
            src, dst, sem = ref[S.stg_xlo], self.bufs[0], ref[S.h_ss].at[0, 0]
        elif d == 1:
            src, dst, sem = ref[S.stg_xhi], self.bufs[1], ref[S.h_ss].at[0, 1]
        elif d == 2:
            src, dst = ref[S.stg_ylo].at[rows_here], self.bufs[2].at[rows_here, pl.ds(4, 4)]
            sem = ref[S.h_ss].at[blk, 2]
        else:
            src, dst = ref[S.stg_yhi].at[rows_here], self.bufs[3].at[rows_here, pl.ds(0, 4)]
            sem = ref[S.h_ss].at[blk, 3]
        return pltpu.make_async_remote_copy(
            src_ref=src,
            dst_ref=dst,
            send_sem=sem,
            recv_sem=ref[S.h_rs].at[d],
            device_id=self.peer[d],
            device_id_type=pl.DeviceIdType.MESH,
        )

    def whole(self, b):
        ref = self.ref
        src = {0: ref[S.stg_xlo], 1: ref[S.stg_xhi], 2: ref[S.stg_ylo], 3: ref[S.stg_yhi]}[b]
        dst = {0: self.bufs[0], 1: self.bufs[1], 2: self.bufs[2].at[:, pl.ds(4, 4)], 3: self.bufs[3].at[:, pl.ds(0, 4)]}[b]
        return pltpu.make_async_remote_copy(
            src_ref=src,
            dst_ref=dst,
            send_sem=ref[S.h_ss].at[0, b],
            recv_sem=ref[S.h_rs].at[b],
            device_id=self.peer[b],
            device_id_type=pl.DeviceIdType.MESH,
        )

    def begin(self):
        ref, has, row, nrow, col, ncol = self.ref, self.has, self.row, self.nrow, self.col, self.ncol
        barrier = pltpu.get_barrier_semaphore()
        for d in range(4):
            @pl.when(has[d])
            def _():
                pl.semaphore_signal(barrier, inc=1, device_id=self.peer[d], device_id_type=pl.DeviceIdType.MESH)

        count = (1 - row // (nrow - 1)) + (row + nrow - 1) // nrow + (1 - col // (ncol - 1)) + (col + ncol - 1) // ncol
        pl.semaphore_wait(barrier, count)

        @pl.when(jnp.logical_not(has[0] & has[1]))
        def _():
            ref[S.h_zx][...] = jnp.zeros_like(ref[S.h_zx])

        @pl.when(jnp.logical_not(has[2] & has[3]))
        def _():
            ref[S.h_zy][...] = jnp.zeros_like(ref[S.h_zy])

        for b in range(4):
            @pl.when(jnp.logical_not(has[self.filler[b]]))
            def _():
                zero = ref[S.h_zx] if b < 2 else ref[S.h_zy]
                copy = pltpu.make_async_copy(zero, self.bufs[b], ref[S.h_zs].at[b])
                copy.start()
                copy.wait()

    def send_block(self, blk):
        ref, has, tb = self.ref, self.has, self.tb

        @pl.when(blk == 0)
        def _():
            ref[S.stg_xhi][...] = ref[S.o_a2][0:4]

        @pl.when(blk == self.nblk - 1)
        def _():
            ref[S.stg_xlo][...] = ref[S.o_a2][tb - 4 : tb]

        for d in (2, 3):
            @pl.when(has[d])
            def _():
                self.copy(d, blk).start()

        @pl.when(has[1] & (blk == 0))
        def _():
            self.copy(1, blk).start()

        @pl.when(has[0] & (blk == self.nblk - 1))
        def _():
            self.copy(0, blk).start()

    def finish(self):
        has = self.has
        for blk in range(self.nblk):
            for d in (2, 3):
                @pl.when(has[d])
                def _():
                    self.copy(d, blk).wait_send()

        @pl.when(has[1])
        def _():
            self.copy(1, 0).wait_send()

        @pl.when(has[0])
        def _():
            self.copy(0, self.nblk - 1).wait_send()

        for b in range(4):
            @pl.when(has[self.filler[b]])
            def _():
                self.whole(b).wait_recv()


class ReduceScatter:

    def __init__(self, ref, me, n):
        self.ref, self.me, self.n = ref, me, n

    def copy(self, blk):
        ref = self.ref
        return pltpu.make_async_remote_copy(
            src_ref=ref[S.slot_out].at[blk],
            dst_ref=ref[S.slot_in].at[self.me],
            send_sem=ref[S.rs_ss].at[blk],
            recv_sem=ref[S.rs_rs].at[self.me],
            device_id={"shot": blk},
            device_id_type=pl.DeviceIdType.MESH,
        )

    def begin(self):
        barrier = pltpu.get_barrier_semaphore()
        for d in range(1, self.n):
            pl.semaphore_signal(
                barrier, inc=1, device_id={"shot": lax.rem(self.me + d, self.n)}, device_id_type=pl.DeviceIdType.MESH
            )
        pl.semaphore_wait(barrier, self.n - 1)

    def send(self, blk):
        self.copy(blk).start()

    def finish(self):
        ref, me, n = self.ref, self.me, self.n
        own = pltpu.make_async_copy(ref[S.slot_out].at[me], ref[S.slot_in].at[me], ref[S.rs_own])
        own.start()
        for d in range(1, n):
            self.copy(lax.rem(me + d, n)).wait_send()
        own.wait()
        for d in range(1, n):
            src = lax.rem(me + d, n)
            pltpu.make_async_remote_copy(
                src_ref=ref[S.slot_out].at[src],
                dst_ref=ref[S.slot_in].at[src],
                send_sem=ref[S.rs_ss].at[src],
                recv_sem=ref[S.rs_rs].at[src],
                device_id={"shot": src},
                device_id_type=pl.DeviceIdType.MESH,
            ).wait_recv()

        slot_in = ref[S.slot_in]

        def row(r, carry):
            summed = slot_in[0, r]
            for s_ in range(1, n):
                summed = summed + slot_in[s_, r]
            v = ref[S.vslab][r]
            gradient = 2.0 / v * summed
            p_half = ref[S.mom][r] - 0.5 * leap_step * gradient
            ref[S.o_p][r] = p_half
            ref[S.o_v][r] = v + leap_step * p_half / ref[S.mass][r]
            return carry

        lax.fori_loop(0, slot_in.shape[1], row, 0)


def step_kernel(kind, names, nf_ex, *refs):
    ref = dict(zip(names, refs))
    if nf_ex:
        ex = Exchange(
            [ref[S.ex_f + j] for j in range(nf_ex)],
            [ref[S.ex_b + k] for k in range(4 * nf_ex)],
            *[ref[k] for k in (S.ex_zx, S.ex_zy, S.ex_ss, S.ex_rs, S.ex_zs)],
        )
    f_ref, pad = ref[S.f], ref[S.pad]
    tb, cols, depth = f_ref.shape
    n = pl.num_programs(0)
    step = pl.program_id(0)
    if kind == "adj2":
        me = lax.axis_index("shot")
        i = lax.rem(me + 1 + step, n)
        rs = ReduceScatter(ref, me, n)

        @pl.when(step == 0)
        def _():
            rs.begin()

        @pl.when(step > 0)
        def _():
            rs.send(lax.rem(me + step, n))
    else:
        i = step

    if nf_ex:
        @pl.when(i == 0)
        def _():
            ex.start()

    lo = jnp.where(i == 0, ref[S.xlo][...], ref[S.flo][...])
    hi = jnp.where(i == n - 1, ref[S.xhi][...], ref[S.fhi][...])
    pad[0:4, 8 : 8 + cols, :] = lo
    pad[4 : 4 + tb, 8 : 8 + cols, :] = f_ref[...]
    pad[4 + tb : 8 + tb, 8 : 8 + cols, :] = hi
    pad[4 : 4 + tb, 0:8, :] = ref[S.ylo][...]
    pad[4 : 4 + tb, 8 + cols : 16 + cols, :] = ref[S.yhi][...]

    z_index = lax.broadcasted_iota(jnp.int32, (Y_CHUNK, depth), 1)
    y_index = lax.broadcasted_iota(jnp.int32, (Y_CHUNK, depth), 0)
    wave = kind in ("wave1", "wave2")
    if wave:
        src_ref = ref[S.src]
        src_x = src_ref[0] - i * tb
        src_y = src_ref[1]
        src_z = src_ref[2]
        amp = ref[S.amp][0]

    def row(r, carry):
        for y0 in range(0, cols, Y_CHUNK):
            ys = pl.ds(y0, Y_CHUNK)
            pys = pl.ds(8 + y0, Y_CHUNK)
            c = pad[4 + r, pys, :]
            result = (3.0 * STENCIL[0]) * c
            for k in range(1, 5):
                along = pad[4 + r + k, pys, :] + pad[4 + r - k, pys, :]
                along = along + (
                    pad[4 + r, pl.ds(8 + y0 + k, Y_CHUNK), :]
                    + pad[4 + r, pl.ds(8 + y0 - k, Y_CHUNK), :]
                )
                zp = jnp.where(z_index < depth - k, pltpu.roll(c, depth - k, 1), 0.0)
                zm = jnp.where(z_index >= k, pltpu.roll(c, k, 1), 0.0)
                along = along + (zp + zm)
                result = result + STENCIL[k] * along
            v = ref[S.vel][r, ys, :]
            stiff = squared_courant * v * v
            prev = ref[S.prev][r, ys, :]
            out = 2.0 * c - prev + stiff * result
            if wave:
                at_rec = z_index == ref[S.rec][r, ys, :]
                hit = (r == src_x) & (y_index + y0 == src_y) & (z_index == src_z)
                out = out + jnp.where(hit, amp, 0.0)
                sel = jnp.where(at_rec, out, 0.0)
                folded = sel[:, 0:128]
                for t in range(128, depth, 128):
                    folded = folded + sel[:, t : t + 128]
                ref[S.fold][pl.ds(pl.multiple_of(r * cols + y0, Y_CHUNK), Y_CHUNK), :] = folded
                ref[S.o_dw][r, ys, :] = (out - 2.0 * c) + prev
                if kind == "wave1":
                    ref[S.o_f][r, ys, :] = out
            elif kind == "adjbulk":
                ref[S.o_f][r, ys, :] = out
            else:
                at_rec = z_index == ref[S.rec][r, ys, :]
                out = out + jnp.where(at_rec, ref[S.mis][r, ys, :], 0.0)
                ref[S.slot_out][i, r, ys, :] = ref[S.part][r, ys, :] + out * ref[S.dw][r, ys, :]
        return carry

    lax.fori_loop(0, tb, row, 0)
    if wave:
        ref[S.o_pick][...] = jnp.sum(ref[S.fold][...], axis=1, keepdims=True).reshape(ref[S.o_pick].shape)
    if kind == "wave2":
        sender = HaloSender(ref, n, tb)

        @pl.when(i == 0)
        def _():
            sender.begin()

        def inject(r, carry):
            for y0 in range(0, cols, Y_CHUNK):
                ys = pl.ds(y0, Y_CHUNK)
                at_rec = z_index == ref[S.rec][r, ys, :]
                misfit = ref[S.o_pick][r, ys, :] - ref[S.obs][r, ys, :]
                a2 = ref[S.a2raw][r, ys, :] + jnp.where(at_rec, misfit, 0.0)
                ref[S.o_a2][r, ys, :] = a2
                ref[S.o_part][r, ys, :] = a2 * ref[S.o_dw][r, ys, :]
                if y0 == 0:
                    ref[S.stg_yhi][i * tb + r] = a2[0:4]
                if y0 == cols - Y_CHUNK:
                    ref[S.stg_ylo][i * tb + r] = a2[Y_CHUNK - 4 : Y_CHUNK]
            return carry

        lax.fori_loop(0, tb, inject, 0)
        sender.send_block(i)

        @pl.when(i == n - 1)
        def _():
            sender.finish()

    if nf_ex:
        @pl.when(i == n - 1)
        def _():
            ex.finish()
    if kind == "adj2":
        @pl.when(step == n - 1)
        def _():
            rs.finish()


def leap(kind, f, xlo, xhi, ylo, yhi, prev, vel, extra, exchanged=(), collective_id=None):
    rows, cols, depth = f.shape
    tb = ROWS_PER_STEP
    nblk = rows // tb
    grid = (nblk,)
    nq = rows // 4
    if kind == "adj2":
        def at(fn):
            return lambda i: fn(lax.rem(lax.axis_index("shot") + 1 + i, nblk))

        fixed = at
    else:
        def at(fn):
            return fn

        fixed = at
    block = pl.BlockSpec((tb, cols, depth), at(lambda i: (i, 0, 0)))
    lo_spec = pl.BlockSpec((4, cols, depth), at(lambda i: (jnp.maximum(2 * i - 1, 0), 0, 0)))
    hi_spec = pl.BlockSpec((4, cols, depth), at(lambda i: (jnp.minimum(2 * i + 2, nq - 1), 0, 0)))
    whole4 = pl.BlockSpec((4, cols, depth), fixed(lambda i: (0, 0, 0)))
    yspec = pl.BlockSpec((tb, 8, depth), at(lambda i: (i, 0, 0)))
    col1 = pl.BlockSpec((tb, cols, 1), at(lambda i: (i, 0, 0)))
    slab = pl.BlockSpec((tb, cols, depth), fixed(lambda i: (0, 0, 0)))
    smem = pl.BlockSpec(memory_space=pltpu.SMEM)
    any_spec = pl.BlockSpec(memory_space=pl.ANY)
    field = jax.ShapeDtypeStruct((rows, cols, depth), jnp.float32)
    picked = jax.ShapeDtypeStruct((rows, cols, 1), jnp.float32)
    spec_of = {S.src: smem, S.amp: smem, S.rec: col1, S.mis: col1, S.obs: col1, S.vslab: slab, S.mom: slab, S.mass: slab}

    names = [S.f, S.flo, S.fhi, S.xlo, S.xhi, S.ylo, S.yhi, S.prev, S.vel]
    in_specs = [block, lo_spec, hi_spec, whole4, whole4, yspec, yspec, block, block]
    args = [f, f, f, xlo, xhi, ylo, yhi, prev, vel]
    for key, value in extra.items():
        names.append(key)
        in_specs.append(spec_of.get(key, block))
        args.append(value)
    nf_ex = len(exchanged)
    for j, g in enumerate(exchanged):
        names.append(S.ex_f + j)
        in_specs.append(any_spec)
        args.append(g)

    outs = {
        "wave1": [(S.o_f, field, block), (S.o_dw, field, block), (S.o_pick, picked, col1)],
        "wave2": [(S.o_dw, field, block), (S.o_pick, picked, col1), (S.o_a2, field, block), (S.o_part, field, block)],
        "adjbulk": [(S.o_f, field, block)],
        "adj2": [
            (S.o_v, jax.ShapeDtypeStruct((tb, cols, depth), jnp.float32), slab),
            (S.o_p, jax.ShapeDtypeStruct((tb, cols, depth), jnp.float32), slab),
        ],
    }[kind]
    names += [o[0] for o in outs]
    out_shape = [o[1] for o in outs]
    out_specs = [o[2] for o in outs]
    scratch = [pltpu.VMEM((tb + 8, cols + 16, depth), jnp.float32)]
    names.append(S.pad)
    if kind in ("wave1", "wave2"):
        scratch.append(pltpu.VMEM((tb * cols, 128), jnp.float32))
        names.append(S.fold)
    if kind == "adj2":
        names += [S.slot_out, S.slot_in, S.rs_ss, S.rs_rs, S.rs_own]
        scratch += [
            pltpu.VMEM((nblk, tb, cols, depth), jnp.float32),
            pltpu.VMEM((nblk, tb, cols, depth), jnp.float32),
            pltpu.SemaphoreType.DMA((nblk,)),
            pltpu.SemaphoreType.DMA((nblk,)),
            pltpu.SemaphoreType.DMA(()),
        ]
        params = pltpu.CompilerParams(
            collective_id=collective_id, has_side_effects=True, vmem_limit_bytes=60 * 1024 * 1024
        )
    elif kind == "wave2":
        h_shapes, _ = exchange_io(1, rows, cols, depth)
        names = names[: len(names) - len(scratch)]
        names += [S.h_b + m for m in range(4)]
        names += [S.pad, S.fold]
        names += [S.stg_xlo, S.stg_xhi, S.stg_ylo, S.stg_yhi, S.h_zx, S.h_zy, S.h_ss, S.h_rs, S.h_zs]
        out_shape += h_shapes
        out_specs += [any_spec] * 4
        scratch += [
            pltpu.VMEM((4, cols, depth), jnp.float32),
            pltpu.VMEM((4, cols, depth), jnp.float32),
            pltpu.VMEM((rows, 4, depth), jnp.float32),
            pltpu.VMEM((rows, 4, depth), jnp.float32),
            pltpu.VMEM((4, cols, depth), jnp.float32),
            pltpu.VMEM((rows, 8, depth), jnp.float32),
            pltpu.SemaphoreType.DMA((rows // tb, 4)),
            pltpu.SemaphoreType.DMA((4,)),
            pltpu.SemaphoreType.DMA((4,)),
        ]
        params = pltpu.CompilerParams(
            collective_id=collective_id, has_side_effects=True, vmem_limit_bytes=60 * 1024 * 1024
        )
    elif nf_ex:
        ex_shapes, ex_scratch = exchange_io(nf_ex, rows, cols, depth)
        k = len(outs)
        names = names[: len(names) - len(scratch)]
        names += [S.ex_b + m for m in range(4 * nf_ex)]
        names += [S.pad, S.fold][: len(scratch)]
        names += [S.ex_zx, S.ex_zy, S.ex_ss, S.ex_rs, S.ex_zs]
        out_shape += ex_shapes
        out_specs += [any_spec] * len(ex_shapes)
        scratch += ex_scratch
        params = pltpu.CompilerParams(
            collective_id=collective_id, has_side_effects=True, vmem_limit_bytes=60 * 1024 * 1024
        )
    else:
        params = pltpu.CompilerParams(vmem_limit_bytes=60 * 1024 * 1024)
    n_big = sum(1 for sp in in_specs if sp is block) + 1 + sum(1 for sp in out_specs if sp is block)
    cost = pl.CostEstimate(
        flops=60 * rows * cols * depth,
        transcendentals=0,
        bytes_accessed=4 * rows * cols * depth * n_big,
    )
    result = pl.pallas_call(
        functools.partial(step_kernel, kind, tuple(names), nf_ex),
        grid=grid,
        in_specs=in_specs,
        out_specs=out_specs,
        out_shape=out_shape,
        scratch_shapes=scratch,
        compiler_params=params,
        cost_estimate=cost,
        name=f"leap_{kind}",
    )(*args)
    if kind == "wave2":
        return result[: len(outs)], result[len(outs) :]
    if nf_ex:
        own = result[: len(outs)]
        ex = result[len(outs) :]
        return own, [ex[4 * j : 4 * j + 4] for j in range(nf_ex)]
    return result


def on_device(
    velocity,
    momentum,
    mass_diag,
    u_prev,
    u_cur,
    adj_next,
    adj_cur,
    observed,
    rec_depth,
    src_cell,
    wavelet,
):
    full_velocity = lax.all_gather(velocity, "shot", axis=0, tiled=True)
    row_count, col_count, depth_cells = full_velocity.shape
    oldest = u_prev[0]
    present = u_cur[0]
    adj_later = adj_next[0]
    adj_now = adj_cur[0]
    rec = rec_depth[0][:, :, None]
    cell = src_cell[0]
    src = jnp.stack(
        [
            cell[0] - lax.axis_index("row") * row_count,
            cell[1] - lax.axis_index("col") * col_count,
            cell[2],
        ]
    ).astype(jnp.int32)
    amp = wavelet[0]

    wave_h, adj_h = exchange([present, adj_now], 1)
    advanced, dw1, pick_adv = leap(
        "wave1", present, *wave_h, oldest, full_velocity, {S.rec: rec, S.src: src, S.amp: amp[0:1]}
    )
    (adj_bulk,), (adv_h,) = leap(
        "adjbulk", adj_now, *adj_h, adj_later, full_velocity, {}, exchanged=[advanced], collective_id=2
    )
    (dw2, pick_far, adj_two, part), adj_two_h = leap(
        "wave2",
        advanced,
        *adv_h,
        present,
        full_velocity,
        {S.rec: rec, S.src: src, S.amp: amp[1:2], S.a2raw: adj_bulk, S.obs: observed[0, 1][:, :, None]},
        collective_id=3,
    )
    misfit_early = pick_adv - observed[0, 0][:, :, None]
    v_new, p_half = leap(
        "adj2",
        adj_two,
        *adj_two_h,
        adj_now,
        full_velocity,
        {
            S.rec: rec,
            S.mis: misfit_early,
            S.dw: dw1,
            S.part: part,
            S.vslab: velocity,
            S.mom: momentum,
            S.mass: mass_diag,
        },
        collective_id=0,
    )
    return (v_new, p_half)


def solution(mesh):
    return jax.shard_map(
        on_device,
        mesh=mesh,
        in_specs=(
            P(("row", "shot"), "col", None),
            P(("row", "shot"), "col", None),
            P(("row", "shot"), "col", None),
            P("shot", "row", "col", None),
            P("shot", "row", "col", None),
            P("shot", "row", "col", None),
            P("shot", "row", "col", None),
            P("shot", None, "row", "col"),
            P("shot", "row", "col"),
            P("shot", None),
            P("shot", None),
        ),
        out_specs=(P(("row", "shot"), "col", None), P(("row", "shot"), "col", None)),
        check_vma=False,
    )
```

```python
import functools

import jax
import jax.numpy as jnp
from jax import lax
from jax.experimental import pallas as pl
from jax.experimental.pallas import tpu as pltpu
from jax.sharding import PartitionSpec as P

STENCIL = (-205.0 / 72.0, 8.0 / 5.0, -1.0 / 5.0, 8.0 / 315.0, -1.0 / 560.0)
squared_courant = 0.012
leap_step = 0.2

class S:
    a2raw = 0
    amp = 1
    dw = 2
    ex_rs = 3
    ex_ss = 4
    ex_zs = 5
    ex_zx = 6
    ex_zy = 7
    f = 8
    fhi = 9
    flo = 10
    fold = 11
    h_rs = 12
    h_ss = 13
    h_zs = 14
    h_zx = 15
    h_zy = 16
    mass = 17
    mis = 18
    mom = 19
    o_a2 = 20
    o_dw = 21
    o_f = 22
    o_p = 23
    o_part = 24
    o_pick = 25
    o_v = 26
    obs = 27
    pad = 28
    part = 29
    prev = 30
    rec = 31
    rs_own = 32
    rs_rs = 33
    rs_ss = 34
    slot_in = 35
    slot_out = 36
    src = 37
    stg_xhi = 38
    stg_xlo = 39
    stg_yhi = 40
    stg_ylo = 41
    vel = 42
    vslab = 43
    xhi = 44
    xlo = 45
    yhi = 46
    ylo = 47
    ex_f = 100
    ex_b = 110
    h_b = 130


ROWS_PER_STEP = 8
Y_CHUNK = 8


class Exchange:

    def __init__(self, fields, bufs, zero_x, zero_y, send_sem, recv_sem, zero_sem):
        self.fields, self.bufs = fields, bufs
        self.zero_x, self.zero_y = zero_x, zero_y
        self.send_sem, self.recv_sem, self.zero_sem = send_sem, recv_sem, zero_sem
        row, nrow = lax.axis_index("row"), lax.axis_size("row")
        col, ncol = lax.axis_index("col"), lax.axis_size("col")
        self.row, self.nrow, self.col, self.ncol = row, nrow, col, ncol
        self.has = (row < nrow - 1, row > 0, col < ncol - 1, col > 0)
        self.peer = ({"row": row + 1}, {"row": row - 1}, {"col": col + 1}, {"col": col - 1})
        self.filler = (1, 0, 3, 2)

    def source(self, f, d):
        rows, cols, _ = f.shape
        if d == 0:
            return f.at[pl.ds(rows - 4, 4)]
        if d == 1:
            return f.at[pl.ds(0, 4)]
        if d == 2:
            return f.at[:, pl.ds(cols - 4, 4)]
        return f.at[:, pl.ds(0, 4)]

    def target(self, j, b):
        if b == 2:
            return self.bufs[4 * j + b].at[:, pl.ds(4, 4)]
        if b == 3:
            return self.bufs[4 * j + b].at[:, pl.ds(0, 4)]
        return self.bufs[4 * j + b]

    def remote(self, j, d):
        return pltpu.make_async_remote_copy(
            src_ref=self.source(self.fields[j], d),
            dst_ref=self.target(j, d),
            send_sem=self.send_sem.at[j, d],
            recv_sem=self.recv_sem.at[j, d],
            device_id=self.peer[d],
            device_id_type=pl.DeviceIdType.MESH,
        )

    def start(self):
        has, row, nrow, col, ncol = self.has, self.row, self.nrow, self.col, self.ncol
        barrier = pltpu.get_barrier_semaphore()
        for d in range(4):
            @pl.when(has[d])
            def _():
                pl.semaphore_signal(barrier, inc=1, device_id=self.peer[d], device_id_type=pl.DeviceIdType.MESH)

        count = (1 - row // (nrow - 1)) + (row + nrow - 1) // nrow + (1 - col // (ncol - 1)) + (col + ncol - 1) // ncol
        pl.semaphore_wait(barrier, count)

        for j in range(len(self.fields)):
            for d in range(4):
                @pl.when(has[d])
                def _():
                    self.remote(j, d).start()

        @pl.when(jnp.logical_not(has[0] & has[1]))
        def _():
            self.zero_x[...] = jnp.zeros_like(self.zero_x)

        @pl.when(jnp.logical_not(has[2] & has[3]))
        def _():
            self.zero_y[...] = jnp.zeros_like(self.zero_y)

        for j in range(len(self.fields)):
            for b in range(4):
                @pl.when(jnp.logical_not(has[self.filler[b]]))
                def _():
                    zero = self.zero_x if b < 2 else self.zero_y
                    copy = pltpu.make_async_copy(zero, self.bufs[4 * j + b], self.zero_sem.at[j, b])
                    copy.start()
                    copy.wait()

    def finish(self):
        has = self.has
        for j in range(len(self.fields)):
            for d in range(4):
                @pl.when(has[d])
                def _():
                    self.remote(j, d).wait_send()
            for b in range(4):
                @pl.when(has[self.filler[b]])
                def _():
                    self.remote(j, b).wait_recv()


def exchange_io(nf, rows, cols, depth):
    shapes = []
    for _ in range(nf):
        shapes += [
            jax.ShapeDtypeStruct((4, cols, depth), jnp.float32),
            jax.ShapeDtypeStruct((4, cols, depth), jnp.float32),
            jax.ShapeDtypeStruct((rows, 8, depth), jnp.float32),
            jax.ShapeDtypeStruct((rows, 8, depth), jnp.float32),
        ]
    scratch = [
        pltpu.VMEM((4, cols, depth), jnp.float32),
        pltpu.VMEM((rows, 8, depth), jnp.float32),
        pltpu.SemaphoreType.DMA((nf, 4)),
        pltpu.SemaphoreType.DMA((nf, 4)),
        pltpu.SemaphoreType.DMA((nf, 4)),
    ]
    return shapes, scratch


def exchange_kernel(nf, *refs):
    ex = Exchange(refs[:nf], refs[nf : 5 * nf], *refs[5 * nf :])
    ex.start()
    ex.finish()


def exchange(fields, collective_id):
    nf = len(fields)
    rows, cols, depth = fields[0].shape
    any_spec = pl.BlockSpec(memory_space=pl.ANY)
    shapes, scratch = exchange_io(nf, rows, cols, depth)
    outs = pl.pallas_call(
        functools.partial(exchange_kernel, nf),
        in_specs=[any_spec] * nf,
        out_specs=[any_spec] * (4 * nf),
        out_shape=shapes,
        scratch_shapes=scratch,
        compiler_params=pltpu.CompilerParams(collective_id=collective_id, has_side_effects=True),
        name=f"halo_exchange_{collective_id}",
    )(*fields)
    return [outs[4 * j : 4 * j + 4] for j in range(nf)]


class HaloSender:

    def __init__(self, ref, nblk, tb):
        self.ref, self.nblk, self.tb = ref, nblk, tb
        row, nrow = lax.axis_index("row"), lax.axis_size("row")
        col, ncol = lax.axis_index("col"), lax.axis_size("col")
        self.row, self.nrow, self.col, self.ncol = row, nrow, col, ncol
        self.has = (row < nrow - 1, row > 0, col < ncol - 1, col > 0)
        self.peer = ({"row": row + 1}, {"row": row - 1}, {"col": col + 1}, {"col": col - 1})
        self.filler = (1, 0, 3, 2)
        self.bufs = [ref[S.h_b + b] for b in range(4)]

    def copy(self, d, blk):
        ref, tb = self.ref, self.tb
        rows_here = pl.ds(pl.multiple_of(blk * tb, tb), tb)
        if d == 0:
            src, dst, sem = ref[S.stg_xlo], self.bufs[0], ref[S.h_ss].at[0, 0]
        elif d == 1:
            src, dst, sem = ref[S.stg_xhi], self.bufs[1], ref[S.h_ss].at[0, 1]
        elif d == 2:
            src, dst = ref[S.stg_ylo].at[rows_here], self.bufs[2].at[rows_here, pl.ds(4, 4)]
            sem = ref[S.h_ss].at[blk, 2]
        else:
            src, dst = ref[S.stg_yhi].at[rows_here], self.bufs[3].at[rows_here, pl.ds(0, 4)]
            sem = ref[S.h_ss].at[blk, 3]
        return pltpu.make_async_remote_copy(
            src_ref=src,
            dst_ref=dst,
            send_sem=sem,
            recv_sem=ref[S.h_rs].at[d],
            device_id=self.peer[d],
            device_id_type=pl.DeviceIdType.MESH,
        )

    def whole(self, b):
        ref = self.ref
        src = {0: ref[S.stg_xlo], 1: ref[S.stg_xhi], 2: ref[S.stg_ylo], 3: ref[S.stg_yhi]}[b]
        dst = {0: self.bufs[0], 1: self.bufs[1], 2: self.bufs[2].at[:, pl.ds(4, 4)], 3: self.bufs[3].at[:, pl.ds(0, 4)]}[b]
        return pltpu.make_async_remote_copy(
            src_ref=src,
            dst_ref=dst,
            send_sem=ref[S.h_ss].at[0, b],
            recv_sem=ref[S.h_rs].at[b],
            device_id=self.peer[b],
            device_id_type=pl.DeviceIdType.MESH,
        )

    def begin(self):
        ref, has, row, nrow, col, ncol = self.ref, self.has, self.row, self.nrow, self.col, self.ncol
        barrier = pltpu.get_barrier_semaphore()
        for d in range(4):
            @pl.when(has[d])
            def _():
                pl.semaphore_signal(barrier, inc=1, device_id=self.peer[d], device_id_type=pl.DeviceIdType.MESH)

        count = (1 - row // (nrow - 1)) + (row + nrow - 1) // nrow + (1 - col // (ncol - 1)) + (col + ncol - 1) // ncol
        pl.semaphore_wait(barrier, count)

        @pl.when(jnp.logical_not(has[0] & has[1]))
        def _():
            ref[S.h_zx][...] = jnp.zeros_like(ref[S.h_zx])

        @pl.when(jnp.logical_not(has[2] & has[3]))
        def _():
            ref[S.h_zy][...] = jnp.zeros_like(ref[S.h_zy])

        for b in range(4):
            @pl.when(jnp.logical_not(has[self.filler[b]]))
            def _():
                zero = ref[S.h_zx] if b < 2 else ref[S.h_zy]
                copy = pltpu.make_async_copy(zero, self.bufs[b], ref[S.h_zs].at[b])
                copy.start()
                copy.wait()

    def send_block(self, blk):
        ref, has, tb = self.ref, self.has, self.tb

        @pl.when(blk == 0)
        def _():
            ref[S.stg_xhi][...] = ref[S.o_a2][0:4]

        @pl.when(blk == self.nblk - 1)
        def _():
            ref[S.stg_xlo][...] = ref[S.o_a2][tb - 4 : tb]

        for d in (2, 3):
            @pl.when(has[d])
            def _():
                self.copy(d, blk).start()

        @pl.when(has[1] & (blk == 0))
        def _():
            self.copy(1, blk).start()

        @pl.when(has[0] & (blk == self.nblk - 1))
        def _():
            self.copy(0, blk).start()

    def finish(self):
        has = self.has
        for blk in range(self.nblk):
            for d in (2, 3):
                @pl.when(has[d])
                def _():
                    self.copy(d, blk).wait_send()

        @pl.when(has[1])
        def _():
            self.copy(1, 0).wait_send()

        @pl.when(has[0])
        def _():
            self.copy(0, self.nblk - 1).wait_send()

        for b in range(4):
            @pl.when(has[self.filler[b]])
            def _():
                self.whole(b).wait_recv()


class ReduceScatter:

    def __init__(self, ref, me, n):
        self.ref, self.me, self.n = ref, me, n

    def copy(self, blk):
        ref = self.ref
        return pltpu.make_async_remote_copy(
            src_ref=ref[S.slot_out].at[blk],
            dst_ref=ref[S.slot_in].at[self.me],
            send_sem=ref[S.rs_ss].at[blk],
            recv_sem=ref[S.rs_rs].at[self.me],
            device_id={"shot": blk},
            device_id_type=pl.DeviceIdType.MESH,
        )

    def begin(self):
        barrier = pltpu.get_barrier_semaphore()
        for d in range(1, self.n):
            pl.semaphore_signal(
                barrier, inc=1, device_id={"shot": lax.rem(self.me + d, self.n)}, device_id_type=pl.DeviceIdType.MESH
            )
        pl.semaphore_wait(barrier, self.n - 1)

    def send(self, blk):
        self.copy(blk).start()

    def finish(self):
        ref, me, n = self.ref, self.me, self.n
        own = pltpu.make_async_copy(ref[S.slot_out].at[me], ref[S.slot_in].at[me], ref[S.rs_own])
        own.start()
        for d in range(1, n):
            self.copy(lax.rem(me + d, n)).wait_send()
        own.wait()
        for d in range(1, n):
            src = lax.rem(me + d, n)
            pltpu.make_async_remote_copy(
                src_ref=ref[S.slot_out].at[src],
                dst_ref=ref[S.slot_in].at[src],
                send_sem=ref[S.rs_ss].at[src],
                recv_sem=ref[S.rs_rs].at[src],
                device_id={"shot": src},
                device_id_type=pl.DeviceIdType.MESH,
            ).wait_recv()

        slot_in = ref[S.slot_in]

        def row(r, carry):
            summed = slot_in[0, r]
            for s_ in range(1, n):
                summed = summed + slot_in[s_, r]
            v = ref[S.vslab][r]
            gradient = 2.0 / v * summed
            p_half = ref[S.mom][r] - 0.5 * leap_step * gradient
            ref[S.o_p][r] = p_half
            ref[S.o_v][r] = v + leap_step * p_half / ref[S.mass][r]
            return carry

        lax.fori_loop(0, slot_in.shape[1], row, 0)


def step_kernel(kind, names, nf_ex, *refs):
    ref = dict(zip(names, refs))
    if nf_ex:
        ex = Exchange(
            [ref[S.ex_f + j] for j in range(nf_ex)],
            [ref[S.ex_b + k] for k in range(4 * nf_ex)],
            *[ref[k] for k in (S.ex_zx, S.ex_zy, S.ex_ss, S.ex_rs, S.ex_zs)],
        )
    f_ref, pad = ref[S.f], ref[S.pad]
    tb, cols, depth = f_ref.shape
    n = pl.num_programs(0)
    step = pl.program_id(0)
    if kind == "adj2":
        me = lax.axis_index("shot")
        i = lax.rem(me + 1 + step, n)
        rs = ReduceScatter(ref, me, n)

        @pl.when(step == 0)
        def _():
            rs.begin()

        @pl.when(step > 0)
        def _():
            rs.send(lax.rem(me + step, n))
    elif kind == "wave2":
        i = lax.rem(step + n - 1, n)
    else:
        i = step

    if nf_ex:
        @pl.when(i == 0)
        def _():
            ex.start()

    lo = jnp.where(i == 0, ref[S.xlo][...], ref[S.flo][...])
    hi = jnp.where(i == n - 1, ref[S.xhi][...], ref[S.fhi][...])
    pad[0:4, 8 : 8 + cols, :] = lo
    pad[4 : 4 + tb, 8 : 8 + cols, :] = f_ref[...]
    pad[4 + tb : 8 + tb, 8 : 8 + cols, :] = hi
    pad[4 : 4 + tb, 0:8, :] = ref[S.ylo][...]
    pad[4 : 4 + tb, 8 + cols : 16 + cols, :] = ref[S.yhi][...]

    z_index = lax.broadcasted_iota(jnp.int32, (Y_CHUNK, depth), 1)
    y_index = lax.broadcasted_iota(jnp.int32, (Y_CHUNK, depth), 0)
    wave = kind in ("wave1", "wave2")
    if wave:
        src_ref = ref[S.src]
        src_x = src_ref[0] - i * tb
        src_y = src_ref[1]
        src_z = src_ref[2]
        amp = ref[S.amp][0]

    def row(r, carry):
        for y0 in range(0, cols, Y_CHUNK):
            ys = pl.ds(y0, Y_CHUNK)
            pys = pl.ds(8 + y0, Y_CHUNK)
            c = pad[4 + r, pys, :]
            result = (3.0 * STENCIL[0]) * c
            for k in range(1, 5):
                along = pad[4 + r + k, pys, :] + pad[4 + r - k, pys, :]
                along = along + (
                    pad[4 + r, pl.ds(8 + y0 + k, Y_CHUNK), :]
                    + pad[4 + r, pl.ds(8 + y0 - k, Y_CHUNK), :]
                )
                zp = jnp.where(z_index < depth - k, pltpu.roll(c, depth - k, 1), 0.0)
                zm = jnp.where(z_index >= k, pltpu.roll(c, k, 1), 0.0)
                along = along + (zp + zm)
                result = result + STENCIL[k] * along
            v = ref[S.vel][r, ys, :]
            stiff = squared_courant * v * v
            prev = ref[S.prev][r, ys, :]
            out = 2.0 * c - prev + stiff * result
            if wave:
                at_rec = z_index == ref[S.rec][r, ys, :]
                hit = (r == src_x) & (y_index + y0 == src_y) & (z_index == src_z)
                out = out + jnp.where(hit, amp, 0.0)
                sel = jnp.where(at_rec, out, 0.0)
                folded = sel[:, 0:128]
                for t in range(128, depth, 128):
                    folded = folded + sel[:, t : t + 128]
                ref[S.fold][pl.ds(pl.multiple_of(r * cols + y0, Y_CHUNK), Y_CHUNK), :] = folded
                ref[S.o_dw][r, ys, :] = (out - 2.0 * c) + prev
                if kind == "wave1":
                    ref[S.o_f][r, ys, :] = out
            elif kind == "adjbulk":
                ref[S.o_f][r, ys, :] = out
            else:
                at_rec = z_index == ref[S.rec][r, ys, :]
                out = out + jnp.where(at_rec, ref[S.mis][r, ys, :], 0.0)
                ref[S.slot_out][i, r, ys, :] = ref[S.part][r, ys, :] + out * ref[S.dw][r, ys, :]
        return carry

    lax.fori_loop(0, tb, row, 0)
    if wave:
        ref[S.o_pick][...] = jnp.sum(ref[S.fold][...], axis=1, keepdims=True).reshape(ref[S.o_pick].shape)
    if kind == "wave2":
        sender = HaloSender(ref, n, tb)

        @pl.when(step == 0)
        def _():
            sender.begin()

        def inject(r, carry):
            for y0 in range(0, cols, Y_CHUNK):
                ys = pl.ds(y0, Y_CHUNK)
                at_rec = z_index == ref[S.rec][r, ys, :]
                misfit = ref[S.o_pick][r, ys, :] - ref[S.obs][r, ys, :]
                a2 = ref[S.a2raw][r, ys, :] + jnp.where(at_rec, misfit, 0.0)
                ref[S.o_a2][r, ys, :] = a2
                ref[S.o_part][r, ys, :] = a2 * ref[S.o_dw][r, ys, :]
                if y0 == 0:
                    ref[S.stg_yhi][i * tb + r] = a2[0:4]
                if y0 == cols - Y_CHUNK:
                    ref[S.stg_ylo][i * tb + r] = a2[Y_CHUNK - 4 : Y_CHUNK]
            return carry

        lax.fori_loop(0, tb, inject, 0)
        sender.send_block(i)

        @pl.when(step == n - 1)
        def _():
            sender.finish()

    if nf_ex:
        @pl.when(i == n - 1)
        def _():
            ex.finish()
    if kind == "adj2":
        @pl.when(step == n - 1)
        def _():
            rs.finish()


def leap(kind, f, xlo, xhi, ylo, yhi, prev, vel, extra, exchanged=(), collective_id=None):
    rows, cols, depth = f.shape
    tb = ROWS_PER_STEP
    nblk = rows // tb
    grid = (nblk,)
    nq = rows // 4
    if kind == "adj2":
        def at(fn):
            return lambda i: fn(lax.rem(lax.axis_index("shot") + 1 + i, nblk))

        fixed = at
    elif kind == "wave2":
        def at(fn):
            return lambda i: fn(lax.rem(i + nblk - 1, nblk))

        def fixed(fn):
            return fn
    else:
        def at(fn):
            return fn

        fixed = at
    block = pl.BlockSpec((tb, cols, depth), at(lambda i: (i, 0, 0)))
    lo_spec = pl.BlockSpec((4, cols, depth), at(lambda i: (jnp.maximum(2 * i - 1, 0), 0, 0)))
    hi_spec = pl.BlockSpec((4, cols, depth), at(lambda i: (jnp.minimum(2 * i + 2, nq - 1), 0, 0)))
    whole4 = pl.BlockSpec((4, cols, depth), fixed(lambda i: (0, 0, 0)))
    yspec = pl.BlockSpec((tb, 8, depth), at(lambda i: (i, 0, 0)))
    col1 = pl.BlockSpec((tb, cols, 1), at(lambda i: (i, 0, 0)))
    slab = pl.BlockSpec((tb, cols, depth), fixed(lambda i: (0, 0, 0)))
    smem = pl.BlockSpec(memory_space=pltpu.SMEM)
    any_spec = pl.BlockSpec(memory_space=pl.ANY)
    field = jax.ShapeDtypeStruct((rows, cols, depth), jnp.float32)
    picked = jax.ShapeDtypeStruct((rows, cols, 1), jnp.float32)
    spec_of = {S.src: smem, S.amp: smem, S.rec: col1, S.mis: col1, S.obs: col1, S.vslab: slab, S.mom: slab, S.mass: slab}

    names = [S.f, S.flo, S.fhi, S.xlo, S.xhi, S.ylo, S.yhi, S.prev, S.vel]
    in_specs = [block, lo_spec, hi_spec, whole4, whole4, yspec, yspec, block, block]
    args = [f, f, f, xlo, xhi, ylo, yhi, prev, vel]
    for key, value in extra.items():
        names.append(key)
        in_specs.append(spec_of.get(key, block))
        args.append(value)
    nf_ex = len(exchanged)
    for j, g in enumerate(exchanged):
        names.append(S.ex_f + j)
        in_specs.append(any_spec)
        args.append(g)

    outs = {
        "wave1": [(S.o_f, field, block), (S.o_dw, field, block), (S.o_pick, picked, col1)],
        "wave2": [(S.o_dw, field, block), (S.o_pick, picked, col1), (S.o_a2, field, block), (S.o_part, field, block)],
        "adjbulk": [(S.o_f, field, block)],
        "adj2": [
            (S.o_v, jax.ShapeDtypeStruct((tb, cols, depth), jnp.float32), slab),
            (S.o_p, jax.ShapeDtypeStruct((tb, cols, depth), jnp.float32), slab),
        ],
    }[kind]
    names += [o[0] for o in outs]
    out_shape = [o[1] for o in outs]
    out_specs = [o[2] for o in outs]
    scratch = [pltpu.VMEM((tb + 8, cols + 16, depth), jnp.float32)]
    names.append(S.pad)
    if kind in ("wave1", "wave2"):
        scratch.append(pltpu.VMEM((tb * cols, 128), jnp.float32))
        names.append(S.fold)
    if kind == "adj2":
        names += [S.slot_out, S.slot_in, S.rs_ss, S.rs_rs, S.rs_own]
        scratch += [
            pltpu.VMEM((nblk, tb, cols, depth), jnp.float32),
            pltpu.VMEM((nblk, tb, cols, depth), jnp.float32),
            pltpu.SemaphoreType.DMA((nblk,)),
            pltpu.SemaphoreType.DMA((nblk,)),
            pltpu.SemaphoreType.DMA(()),
        ]
        params = pltpu.CompilerParams(
            collective_id=collective_id, has_side_effects=True, vmem_limit_bytes=60 * 1024 * 1024
        )
    elif kind == "wave2":
        h_shapes, _ = exchange_io(1, rows, cols, depth)
        names = names[: len(names) - len(scratch)]
        names += [S.h_b + m for m in range(4)]
        names += [S.pad, S.fold]
        names += [S.stg_xlo, S.stg_xhi, S.stg_ylo, S.stg_yhi, S.h_zx, S.h_zy, S.h_ss, S.h_rs, S.h_zs]
        out_shape += h_shapes
        out_specs += [any_spec] * 4
        scratch += [
            pltpu.VMEM((4, cols, depth), jnp.float32),
            pltpu.VMEM((4, cols, depth), jnp.float32),
            pltpu.VMEM((rows, 4, depth), jnp.float32),
            pltpu.VMEM((rows, 4, depth), jnp.float32),
            pltpu.VMEM((4, cols, depth), jnp.float32),
            pltpu.VMEM((rows, 8, depth), jnp.float32),
            pltpu.SemaphoreType.DMA((rows // tb, 4)),
            pltpu.SemaphoreType.DMA((4,)),
            pltpu.SemaphoreType.DMA((4,)),
        ]
        params = pltpu.CompilerParams(
            collective_id=collective_id, has_side_effects=True, vmem_limit_bytes=60 * 1024 * 1024
        )
    elif nf_ex:
        ex_shapes, ex_scratch = exchange_io(nf_ex, rows, cols, depth)
        k = len(outs)
        names = names[: len(names) - len(scratch)]
        names += [S.ex_b + m for m in range(4 * nf_ex)]
        names += [S.pad, S.fold][: len(scratch)]
        names += [S.ex_zx, S.ex_zy, S.ex_ss, S.ex_rs, S.ex_zs]
        out_shape += ex_shapes
        out_specs += [any_spec] * len(ex_shapes)
        scratch += ex_scratch
        params = pltpu.CompilerParams(
            collective_id=collective_id, has_side_effects=True, vmem_limit_bytes=60 * 1024 * 1024
        )
    else:
        params = pltpu.CompilerParams(vmem_limit_bytes=60 * 1024 * 1024)
    n_big = sum(1 for sp in in_specs if sp is block) + 1 + sum(1 for sp in out_specs if sp is block)
    cost = pl.CostEstimate(
        flops=60 * rows * cols * depth,
        transcendentals=0,
        bytes_accessed=4 * rows * cols * depth * n_big,
    )
    result = pl.pallas_call(
        functools.partial(step_kernel, kind, tuple(names), nf_ex),
        grid=grid,
        in_specs=in_specs,
        out_specs=out_specs,
        out_shape=out_shape,
        scratch_shapes=scratch,
        compiler_params=params,
        cost_estimate=cost,
        name=f"leap_{kind}",
    )(*args)
    if kind == "wave2":
        return result[: len(outs)], result[len(outs) :]
    if nf_ex:
        own = result[: len(outs)]
        ex = result[len(outs) :]
        return own, [ex[4 * j : 4 * j + 4] for j in range(nf_ex)]
    return result


def on_device(
    velocity,
    momentum,
    mass_diag,
    u_prev,
    u_cur,
    adj_next,
    adj_cur,
    observed,
    rec_depth,
    src_cell,
    wavelet,
):
    full_velocity = lax.all_gather(velocity, "shot", axis=0, tiled=True)
    row_count, col_count, depth_cells = full_velocity.shape
    oldest = u_prev[0]
    present = u_cur[0]
    adj_later = adj_next[0]
    adj_now = adj_cur[0]
    rec = rec_depth[0][:, :, None]
    cell = src_cell[0]
    src = jnp.stack(
        [
            cell[0] - lax.axis_index("row") * row_count,
            cell[1] - lax.axis_index("col") * col_count,
            cell[2],
        ]
    ).astype(jnp.int32)
    amp = wavelet[0]

    wave_h, adj_h = exchange([present, adj_now], 1)
    advanced, dw1, pick_adv = leap(
        "wave1", present, *wave_h, oldest, full_velocity, {S.rec: rec, S.src: src, S.amp: amp[0:1]}
    )
    (adj_bulk,), (adv_h,) = leap(
        "adjbulk", adj_now, *adj_h, adj_later, full_velocity, {}, exchanged=[advanced], collective_id=2
    )
    (dw2, pick_far, adj_two, part), adj_two_h = leap(
        "wave2",
        advanced,
        *adv_h,
        present,
        full_velocity,
        {S.rec: rec, S.src: src, S.amp: amp[1:2], S.a2raw: adj_bulk, S.obs: observed[0, 1][:, :, None]},
        collective_id=3,
    )
    misfit_early = pick_adv - observed[0, 0][:, :, None]
    v_new, p_half = leap(
        "adj2",
        adj_two,
        *adj_two_h,
        adj_now,
        full_velocity,
        {
            S.rec: rec,
            S.mis: misfit_early,
            S.dw: dw1,
            S.part: part,
            S.vslab: velocity,
            S.mom: momentum,
            S.mass: mass_diag,
        },
        collective_id=0,
    )
    return (v_new, p_half)


def solution(mesh):
    return jax.shard_map(
        on_device,
        mesh=mesh,
        in_specs=(
            P(("row", "shot"), "col", None),
            P(("row", "shot"), "col", None),
            P(("row", "shot"), "col", None),
            P("shot", "row", "col", None),
            P("shot", "row", "col", None),
            P("shot", "row", "col", None),
            P("shot", "row", "col", None),
            P("shot", None, "row", "col"),
            P("shot", "row", "col"),
            P("shot", None),
            P("shot", None),
        ),
        out_specs=(P(("row", "shot"), "col", None), P(("row", "shot"), "col", None)),
        check_vma=False,
    )
```

```python
import functools

import jax
import jax.numpy as jnp
from jax import lax
from jax.experimental import pallas as pl
from jax.experimental.pallas import tpu as pltpu
from jax.sharding import PartitionSpec as P

STENCIL = (-205.0 / 72.0, 8.0 / 5.0, -1.0 / 5.0, 8.0 / 315.0, -1.0 / 560.0)
squared_courant = 0.012
leap_step = 0.2

class S:
    a2raw = 0
    amp = 1
    dw = 2
    ex_rs = 3
    ex_ss = 4
    ex_zs = 5
    ex_zx = 6
    ex_zy = 7
    f = 8
    fhi = 9
    flo = 10
    fold = 11
    h_rs = 12
    h_ss = 13
    h_zs = 14
    h_zx = 15
    h_zy = 16
    mass = 17
    mis = 18
    mom = 19
    o_a2 = 20
    o_dw = 21
    o_f = 22
    o_p = 23
    o_part = 24
    o_pick = 25
    o_v = 26
    obs = 27
    pad = 28
    part = 29
    prev = 30
    rec = 31
    rs_own = 32
    rs_rs = 33
    rs_ss = 34
    slot_in = 35
    slot_out = 36
    src = 37
    stg_xhi = 38
    stg_xlo = 39
    stg_yhi = 40
    stg_ylo = 41
    vel = 42
    vslab = 43
    xhi = 44
    xlo = 45
    yhi = 46
    ylo = 47
    rl_top = 90
    rl_bot = 91
    rl_rs = 92
    ex_f = 100
    ex_b = 110
    h_b = 130


ROWS_PER_STEP = 8
Y_CHUNK = 8


class Exchange:

    def __init__(self, fields, bufs, zero_x, zero_y, send_sem, recv_sem, zero_sem):
        self.fields, self.bufs = fields, bufs
        self.zero_x, self.zero_y = zero_x, zero_y
        self.send_sem, self.recv_sem, self.zero_sem = send_sem, recv_sem, zero_sem
        row, nrow = lax.axis_index("row"), lax.axis_size("row")
        col, ncol = lax.axis_index("col"), lax.axis_size("col")
        self.row, self.nrow, self.col, self.ncol = row, nrow, col, ncol
        self.has = (row < nrow - 1, row > 0, col < ncol - 1, col > 0)
        self.peer = ({"row": row + 1}, {"row": row - 1}, {"col": col + 1}, {"col": col - 1})
        self.filler = (1, 0, 3, 2)

    def source(self, f, d):
        rows, cols, _ = f.shape
        if d == 0:
            return f.at[pl.ds(rows - 4, 4)]
        if d == 1:
            return f.at[pl.ds(0, 4)]
        if d == 2:
            return f.at[:, pl.ds(cols - 4, 4)]
        return f.at[:, pl.ds(0, 4)]

    def target(self, j, b):
        if b == 2:
            return self.bufs[4 * j + b].at[:, pl.ds(4, 4)]
        if b == 3:
            return self.bufs[4 * j + b].at[:, pl.ds(0, 4)]
        return self.bufs[4 * j + b]

    def remote(self, j, d):
        return pltpu.make_async_remote_copy(
            src_ref=self.source(self.fields[j], d),
            dst_ref=self.target(j, d),
            send_sem=self.send_sem.at[j, d],
            recv_sem=self.recv_sem.at[j, d],
            device_id=self.peer[d],
            device_id_type=pl.DeviceIdType.MESH,
        )

    def start(self):
        has, row, nrow, col, ncol = self.has, self.row, self.nrow, self.col, self.ncol
        barrier = pltpu.get_barrier_semaphore()
        for d in range(4):
            @pl.when(has[d])
            def _():
                pl.semaphore_signal(barrier, inc=1, device_id=self.peer[d], device_id_type=pl.DeviceIdType.MESH)

        count = (1 - row // (nrow - 1)) + (row + nrow - 1) // nrow + (1 - col // (ncol - 1)) + (col + ncol - 1) // ncol
        pl.semaphore_wait(barrier, count)

        for j in range(len(self.fields)):
            for d in range(4):
                @pl.when(has[d])
                def _():
                    self.remote(j, d).start()

        @pl.when(jnp.logical_not(has[0] & has[1]))
        def _():
            self.zero_x[...] = jnp.zeros_like(self.zero_x)

        @pl.when(jnp.logical_not(has[2] & has[3]))
        def _():
            self.zero_y[...] = jnp.zeros_like(self.zero_y)

        for j in range(len(self.fields)):
            for b in range(4):
                @pl.when(jnp.logical_not(has[self.filler[b]]))
                def _():
                    zero = self.zero_x if b < 2 else self.zero_y
                    copy = pltpu.make_async_copy(zero, self.bufs[4 * j + b], self.zero_sem.at[j, b])
                    copy.start()
                    copy.wait()

    def finish(self):
        has = self.has
        for j in range(len(self.fields)):
            for d in range(4):
                @pl.when(has[d])
                def _():
                    self.remote(j, d).wait_send()
            for b in range(4):
                @pl.when(has[self.filler[b]])
                def _():
                    self.remote(j, b).wait_recv()


def exchange_io(nf, rows, cols, depth):
    shapes = []
    for _ in range(nf):
        shapes += [
            jax.ShapeDtypeStruct((4, cols, depth), jnp.float32),
            jax.ShapeDtypeStruct((4, cols, depth), jnp.float32),
            jax.ShapeDtypeStruct((rows, 8, depth), jnp.float32),
            jax.ShapeDtypeStruct((rows, 8, depth), jnp.float32),
        ]
    scratch = [
        pltpu.VMEM((4, cols, depth), jnp.float32),
        pltpu.VMEM((rows, 8, depth), jnp.float32),
        pltpu.SemaphoreType.DMA((nf, 4)),
        pltpu.SemaphoreType.DMA((nf, 4)),
        pltpu.SemaphoreType.DMA((nf, 4)),
    ]
    return shapes, scratch


def exchange_kernel(nf, *refs):
    ex = Exchange(refs[:nf], refs[nf : 5 * nf], *refs[5 * nf :])
    ex.start()
    ex.finish()


def exchange(fields, collective_id):
    nf = len(fields)
    rows, cols, depth = fields[0].shape
    any_spec = pl.BlockSpec(memory_space=pl.ANY)
    shapes, scratch = exchange_io(nf, rows, cols, depth)
    outs = pl.pallas_call(
        functools.partial(exchange_kernel, nf),
        in_specs=[any_spec] * nf,
        out_specs=[any_spec] * (4 * nf),
        out_shape=shapes,
        scratch_shapes=scratch,
        compiler_params=pltpu.CompilerParams(collective_id=collective_id, has_side_effects=True),
        name=f"halo_exchange_{collective_id}",
    )(*fields)
    return [outs[4 * j : 4 * j + 4] for j in range(nf)]


class HaloSender:

    def __init__(self, ref, nblk, tb):
        self.ref, self.nblk, self.tb = ref, nblk, tb
        row, nrow = lax.axis_index("row"), lax.axis_size("row")
        col, ncol = lax.axis_index("col"), lax.axis_size("col")
        self.row, self.nrow, self.col, self.ncol = row, nrow, col, ncol
        self.has = (row < nrow - 1, row > 0, col < ncol - 1, col > 0)
        self.peer = ({"row": row + 1}, {"row": row - 1}, {"col": col + 1}, {"col": col - 1})
        self.filler = (1, 0, 3, 2)
        self.bufs = [ref[S.h_b + b] for b in range(4)]

    def copy(self, d, blk):
        ref, tb = self.ref, self.tb
        rows_here = pl.ds(pl.multiple_of(blk * tb, tb), tb)
        if d == 0:
            src, dst, sem = ref[S.stg_xlo], self.bufs[0], ref[S.h_ss].at[0, 0]
        elif d == 1:
            src, dst, sem = ref[S.stg_xhi], self.bufs[1], ref[S.h_ss].at[0, 1]
        elif d == 2:
            src, dst = ref[S.stg_ylo].at[rows_here], self.bufs[2].at[rows_here, pl.ds(4, 4)]
            sem = ref[S.h_ss].at[blk, 2]
        else:
            src, dst = ref[S.stg_yhi].at[rows_here], self.bufs[3].at[rows_here, pl.ds(0, 4)]
            sem = ref[S.h_ss].at[blk, 3]
        return pltpu.make_async_remote_copy(
            src_ref=src,
            dst_ref=dst,
            send_sem=sem,
            recv_sem=ref[S.h_rs].at[d],
            device_id=self.peer[d],
            device_id_type=pl.DeviceIdType.MESH,
        )

    def whole(self, b):
        ref = self.ref
        src = {0: ref[S.stg_xlo], 1: ref[S.stg_xhi], 2: ref[S.stg_ylo], 3: ref[S.stg_yhi]}[b]
        dst = {0: self.bufs[0], 1: self.bufs[1], 2: self.bufs[2].at[:, pl.ds(4, 4)], 3: self.bufs[3].at[:, pl.ds(0, 4)]}[b]
        return pltpu.make_async_remote_copy(
            src_ref=src,
            dst_ref=dst,
            send_sem=ref[S.h_ss].at[0, b],
            recv_sem=ref[S.h_rs].at[b],
            device_id=self.peer[b],
            device_id_type=pl.DeviceIdType.MESH,
        )

    def begin(self):
        ref, has, row, nrow, col, ncol = self.ref, self.has, self.row, self.nrow, self.col, self.ncol
        barrier = pltpu.get_barrier_semaphore()
        for d in range(4):
            @pl.when(has[d])
            def _():
                pl.semaphore_signal(barrier, inc=1, device_id=self.peer[d], device_id_type=pl.DeviceIdType.MESH)

        count = (1 - row // (nrow - 1)) + (row + nrow - 1) // nrow + (1 - col // (ncol - 1)) + (col + ncol - 1) // ncol
        pl.semaphore_wait(barrier, count)

        @pl.when(jnp.logical_not(has[0] & has[1]))
        def _():
            ref[S.h_zx][...] = jnp.zeros_like(ref[S.h_zx])

        @pl.when(jnp.logical_not(has[2] & has[3]))
        def _():
            ref[S.h_zy][...] = jnp.zeros_like(ref[S.h_zy])

        for b in range(4):
            @pl.when(jnp.logical_not(has[self.filler[b]]))
            def _():
                zero = ref[S.h_zx] if b < 2 else ref[S.h_zy]
                copy = pltpu.make_async_copy(zero, self.bufs[b], ref[S.h_zs].at[b])
                copy.start()
                copy.wait()

    def send_block(self, blk):
        ref, has, tb = self.ref, self.has, self.tb

        @pl.when(blk == 0)
        def _():
            ref[S.stg_xhi][...] = ref[S.o_a2][0:4]

        @pl.when(blk == self.nblk - 1)
        def _():
            ref[S.stg_xlo][...] = ref[S.o_a2][tb - 4 : tb]

        for d in (2, 3):
            @pl.when(has[d])
            def _():
                self.copy(d, blk).start()

        @pl.when(has[1] & (blk == 0))
        def _():
            self.copy(1, blk).start()

        @pl.when(has[0] & (blk == self.nblk - 1))
        def _():
            self.copy(0, blk).start()

    def finish(self):
        has = self.has
        for blk in range(self.nblk):
            for d in (2, 3):
                @pl.when(has[d])
                def _():
                    self.copy(d, blk).wait_send()

        @pl.when(has[1])
        def _():
            self.copy(1, 0).wait_send()

        @pl.when(has[0])
        def _():
            self.copy(0, self.nblk - 1).wait_send()

        for b in range(4):
            @pl.when(has[self.filler[b]])
            def _():
                self.whole(b).wait_recv()


class ReduceScatter:

    def __init__(self, ref, me, n):
        self.ref, self.me, self.n = ref, me, n
        self.up, self.down, self.far = lax.rem(me + 1, n), lax.rem(me + n - 1, n), lax.rem(me + 2, n)
        half = ref[S.slot_out].shape[1] // 2
        self.top, self.bot = pl.ds(0, half), pl.ds(half, half)

    def remote(self, src, dst, k, recv_sem, peer):
        return pltpu.make_async_remote_copy(
            src_ref=src,
            dst_ref=dst,
            send_sem=self.ref[S.rs_ss].at[k],
            recv_sem=recv_sem,
            device_id={"shot": peer},
            device_id_type=pl.DeviceIdType.MESH,
        )

    def direct(self, blk, k, peer):
        ref = self.ref
        return self.remote(ref[S.slot_out].at[blk], ref[S.slot_in].at[self.me], k, ref[S.rs_rs].at[self.me], peer)

    def relay_top(self):
        ref = self.ref
        src = ref[S.slot_out].at[self.far, self.top]
        return self.remote(src, ref[S.rl_top], 2, ref[S.rl_rs].at[0], self.up)

    def relay_bot(self):
        ref = self.ref
        src = ref[S.slot_out].at[self.far, self.bot]
        return self.remote(src, ref[S.rl_bot], 3, ref[S.rl_rs].at[1], self.down)

    def fwd_top(self):
        ref = self.ref
        dst = ref[S.slot_in].at[self.down, self.top]
        return self.remote(ref[S.rl_top], dst, 4, ref[S.rl_rs].at[2], self.up)

    def fwd_bot(self):
        ref = self.ref
        dst = ref[S.slot_in].at[self.up, self.bot]
        return self.remote(ref[S.rl_bot], dst, 5, ref[S.rl_rs].at[3], self.down)

    def begin(self):
        barrier = pltpu.get_barrier_semaphore()
        for peer in (self.up, self.down):
            pl.semaphore_signal(barrier, inc=1, device_id={"shot": peer}, device_id_type=pl.DeviceIdType.MESH)
        pl.semaphore_wait(barrier, 2)

    def at_step(self, step):
        @pl.when(step == 1)
        def _():
            self.direct(self.up, 0, self.up).start()

        @pl.when(step == 2)
        def _():
            self.relay_top().start()
            self.relay_bot().start()

        @pl.when(step == 3)
        def _():
            self.direct(self.down, 1, self.down).start()
            self.relay_top().wait_recv()
            self.relay_bot().wait_recv()
            self.fwd_top().start()
            self.fwd_bot().start()

    def finish(self):
        ref, me, n = self.ref, self.me, self.n
        own = pltpu.make_async_copy(ref[S.slot_out].at[me], ref[S.slot_in].at[me], ref[S.rs_own])
        own.start()
        self.direct(self.up, 0, self.up).wait_send()
        self.direct(self.down, 1, self.down).wait_send()
        self.relay_top().wait_send()
        self.relay_bot().wait_send()
        self.fwd_top().wait_send()
        self.fwd_bot().wait_send()
        own.wait()
        for src in (self.down, self.up):
            self.remote(ref[S.slot_out].at[src], ref[S.slot_in].at[src], 0, ref[S.rs_rs].at[src], src).wait_recv()
        far_in = ref[S.slot_in].at[self.far, self.top]
        self.remote(ref[S.rl_top], far_in, 4, ref[S.rl_rs].at[2], self.down).wait_recv()
        far_in = ref[S.slot_in].at[self.far, self.bot]
        self.remote(ref[S.rl_bot], far_in, 5, ref[S.rl_rs].at[3], self.up).wait_recv()

        slot_in = ref[S.slot_in]

        def row(r, carry):
            summed = slot_in[0, r]
            for s_ in range(1, n):
                summed = summed + slot_in[s_, r]
            v = ref[S.vslab][r]
            gradient = 2.0 / v * summed
            p_half = ref[S.mom][r] - 0.5 * leap_step * gradient
            ref[S.o_p][r] = p_half
            ref[S.o_v][r] = v + leap_step * p_half / ref[S.mass][r]
            return carry

        lax.fori_loop(0, slot_in.shape[1], row, 0)


def step_kernel(kind, names, nf_ex, *refs):
    ref = dict(zip(names, refs))
    if nf_ex:
        ex = Exchange(
            [ref[S.ex_f + j] for j in range(nf_ex)],
            [ref[S.ex_b + k] for k in range(4 * nf_ex)],
            *[ref[k] for k in (S.ex_zx, S.ex_zy, S.ex_ss, S.ex_rs, S.ex_zs)],
        )
    f_ref, pad = ref[S.f], ref[S.pad]
    tb, cols, depth = f_ref.shape
    n = pl.num_programs(0)
    step = pl.program_id(0)
    if kind == "adj2":
        me = lax.axis_index("shot")
        i = lax.rem(me + 1 + step, n)
        rs = ReduceScatter(ref, me, n)

        @pl.when(step == 0)
        def _():
            rs.begin()

        rs.at_step(step)
    elif kind == "wave2":
        i = lax.rem(step + n - 1, n)
    else:
        i = step

    if nf_ex:
        @pl.when(i == 0)
        def _():
            ex.start()

    lo = jnp.where(i == 0, ref[S.xlo][...], ref[S.flo][...])
    hi = jnp.where(i == n - 1, ref[S.xhi][...], ref[S.fhi][...])
    pad[0:4, 8 : 8 + cols, :] = lo
    pad[4 : 4 + tb, 8 : 8 + cols, :] = f_ref[...]
    pad[4 + tb : 8 + tb, 8 : 8 + cols, :] = hi
    pad[4 : 4 + tb, 0:8, :] = ref[S.ylo][...]
    pad[4 : 4 + tb, 8 + cols : 16 + cols, :] = ref[S.yhi][...]

    z_index = lax.broadcasted_iota(jnp.int32, (Y_CHUNK, depth), 1)
    y_index = lax.broadcasted_iota(jnp.int32, (Y_CHUNK, depth), 0)
    wave = kind in ("wave1", "wave2")
    if wave:
        src_ref = ref[S.src]
        src_x = src_ref[0] - i * tb
        src_y = src_ref[1]
        src_z = src_ref[2]
        amp = ref[S.amp][0]

    def row(r, carry):
        for y0 in range(0, cols, Y_CHUNK):
            ys = pl.ds(y0, Y_CHUNK)
            pys = pl.ds(8 + y0, Y_CHUNK)
            c = pad[4 + r, pys, :]
            result = (3.0 * STENCIL[0]) * c
            for k in range(1, 5):
                along = pad[4 + r + k, pys, :] + pad[4 + r - k, pys, :]
                along = along + (
                    pad[4 + r, pl.ds(8 + y0 + k, Y_CHUNK), :]
                    + pad[4 + r, pl.ds(8 + y0 - k, Y_CHUNK), :]
                )
                zp = jnp.where(z_index < depth - k, pltpu.roll(c, depth - k, 1), 0.0)
                zm = jnp.where(z_index >= k, pltpu.roll(c, k, 1), 0.0)
                along = along + (zp + zm)
                result = result + STENCIL[k] * along
            v = ref[S.vel][r, ys, :]
            stiff = squared_courant * v * v
            prev = ref[S.prev][r, ys, :]
            out = 2.0 * c - prev + stiff * result
            if wave:
                at_rec = z_index == ref[S.rec][r, ys, :]
                hit = (r == src_x) & (y_index + y0 == src_y) & (z_index == src_z)
                out = out + jnp.where(hit, amp, 0.0)
                sel = jnp.where(at_rec, out, 0.0)
                folded = sel[:, 0:128]
                for t in range(128, depth, 128):
                    folded = folded + sel[:, t : t + 128]
                ref[S.fold][pl.ds(pl.multiple_of(r * cols + y0, Y_CHUNK), Y_CHUNK), :] = folded
                ref[S.o_dw][r, ys, :] = (out - 2.0 * c) + prev
                if kind == "wave1":
                    ref[S.o_f][r, ys, :] = out
            elif kind == "adjbulk":
                ref[S.o_f][r, ys, :] = out
            else:
                at_rec = z_index == ref[S.rec][r, ys, :]
                out = out + jnp.where(at_rec, ref[S.mis][r, ys, :], 0.0)
                ref[S.slot_out][i, r, ys, :] = ref[S.part][r, ys, :] + out * ref[S.dw][r, ys, :]
        return carry

    lax.fori_loop(0, tb, row, 0)
    if wave:
        ref[S.o_pick][...] = jnp.sum(ref[S.fold][...], axis=1, keepdims=True).reshape(ref[S.o_pick].shape)
    if kind == "wave2":
        sender = HaloSender(ref, n, tb)

        @pl.when(step == 0)
        def _():
            sender.begin()

        def inject(r, carry):
            for y0 in range(0, cols, Y_CHUNK):
                ys = pl.ds(y0, Y_CHUNK)
                at_rec = z_index == ref[S.rec][r, ys, :]
                misfit = ref[S.o_pick][r, ys, :] - ref[S.obs][r, ys, :]
                a2 = ref[S.a2raw][r, ys, :] + jnp.where(at_rec, misfit, 0.0)
                ref[S.o_a2][r, ys, :] = a2
                ref[S.o_part][r, ys, :] = a2 * ref[S.o_dw][r, ys, :]
                if y0 == 0:
                    ref[S.stg_yhi][i * tb + r] = a2[0:4]
                if y0 == cols - Y_CHUNK:
                    ref[S.stg_ylo][i * tb + r] = a2[Y_CHUNK - 4 : Y_CHUNK]
            return carry

        lax.fori_loop(0, tb, inject, 0)
        sender.send_block(i)

        @pl.when(step == n - 1)
        def _():
            sender.finish()

    if nf_ex:
        @pl.when(i == n - 1)
        def _():
            ex.finish()
    if kind == "adj2":
        @pl.when(step == n - 1)
        def _():
            rs.finish()


def leap(kind, f, xlo, xhi, ylo, yhi, prev, vel, extra, exchanged=(), collective_id=None):
    rows, cols, depth = f.shape
    tb = ROWS_PER_STEP
    nblk = rows // tb
    grid = (nblk,)
    nq = rows // 4
    if kind == "adj2":
        def at(fn):
            return lambda i: fn(lax.rem(lax.axis_index("shot") + 1 + i, nblk))

        fixed = at
    elif kind == "wave2":
        def at(fn):
            return lambda i: fn(lax.rem(i + nblk - 1, nblk))

        def fixed(fn):
            return fn
    else:
        def at(fn):
            return fn

        fixed = at
    block = pl.BlockSpec((tb, cols, depth), at(lambda i: (i, 0, 0)))
    lo_spec = pl.BlockSpec((4, cols, depth), at(lambda i: (jnp.maximum(2 * i - 1, 0), 0, 0)))
    hi_spec = pl.BlockSpec((4, cols, depth), at(lambda i: (jnp.minimum(2 * i + 2, nq - 1), 0, 0)))
    whole4 = pl.BlockSpec((4, cols, depth), fixed(lambda i: (0, 0, 0)))
    yspec = pl.BlockSpec((tb, 8, depth), at(lambda i: (i, 0, 0)))
    col1 = pl.BlockSpec((tb, cols, 1), at(lambda i: (i, 0, 0)))
    slab = pl.BlockSpec((tb, cols, depth), fixed(lambda i: (0, 0, 0)))
    smem = pl.BlockSpec(memory_space=pltpu.SMEM)
    any_spec = pl.BlockSpec(memory_space=pl.ANY)
    field = jax.ShapeDtypeStruct((rows, cols, depth), jnp.float32)
    picked = jax.ShapeDtypeStruct((rows, cols, 1), jnp.float32)
    spec_of = {S.src: smem, S.amp: smem, S.rec: col1, S.mis: col1, S.obs: col1, S.vslab: slab, S.mom: slab, S.mass: slab}

    names = [S.f, S.flo, S.fhi, S.xlo, S.xhi, S.ylo, S.yhi, S.prev, S.vel]
    in_specs = [block, lo_spec, hi_spec, whole4, whole4, yspec, yspec, block, block]
    args = [f, f, f, xlo, xhi, ylo, yhi, prev, vel]
    for key, value in extra.items():
        names.append(key)
        in_specs.append(spec_of.get(key, block))
        args.append(value)
    nf_ex = len(exchanged)
    for j, g in enumerate(exchanged):
        names.append(S.ex_f + j)
        in_specs.append(any_spec)
        args.append(g)

    outs = {
        "wave1": [(S.o_f, field, block), (S.o_dw, field, block), (S.o_pick, picked, col1)],
        "wave2": [(S.o_dw, field, block), (S.o_pick, picked, col1), (S.o_a2, field, block), (S.o_part, field, block)],
        "adjbulk": [(S.o_f, field, block)],
        "adj2": [
            (S.o_v, jax.ShapeDtypeStruct((tb, cols, depth), jnp.float32), slab),
            (S.o_p, jax.ShapeDtypeStruct((tb, cols, depth), jnp.float32), slab),
        ],
    }[kind]
    names += [o[0] for o in outs]
    out_shape = [o[1] for o in outs]
    out_specs = [o[2] for o in outs]
    scratch = [pltpu.VMEM((tb + 8, cols + 16, depth), jnp.float32)]
    names.append(S.pad)
    if kind in ("wave1", "wave2"):
        scratch.append(pltpu.VMEM((tb * cols, 128), jnp.float32))
        names.append(S.fold)
    if kind == "adj2":
        names += [S.slot_out, S.slot_in, S.rs_ss, S.rs_rs, S.rs_own, S.rl_top, S.rl_bot, S.rl_rs]
        scratch += [
            pltpu.VMEM((nblk, tb, cols, depth), jnp.float32),
            pltpu.VMEM((nblk, tb, cols, depth), jnp.float32),
            pltpu.SemaphoreType.DMA((6,)),
            pltpu.SemaphoreType.DMA((nblk,)),
            pltpu.SemaphoreType.DMA(()),
            pltpu.VMEM((tb // 2, cols, depth), jnp.float32),
            pltpu.VMEM((tb // 2, cols, depth), jnp.float32),
            pltpu.SemaphoreType.DMA((4,)),
        ]
        params = pltpu.CompilerParams(
            collective_id=collective_id, has_side_effects=True, vmem_limit_bytes=60 * 1024 * 1024
        )
    elif kind == "wave2":
        h_shapes, _ = exchange_io(1, rows, cols, depth)
        names = names[: len(names) - len(scratch)]
        names += [S.h_b + m for m in range(4)]
        names += [S.pad, S.fold]
        names += [S.stg_xlo, S.stg_xhi, S.stg_ylo, S.stg_yhi, S.h_zx, S.h_zy, S.h_ss, S.h_rs, S.h_zs]
        out_shape += h_shapes
        out_specs += [any_spec] * 4
        scratch += [
            pltpu.VMEM((4, cols, depth), jnp.float32),
            pltpu.VMEM((4, cols, depth), jnp.float32),
            pltpu.VMEM((rows, 4, depth), jnp.float32),
            pltpu.VMEM((rows, 4, depth), jnp.float32),
            pltpu.VMEM((4, cols, depth), jnp.float32),
            pltpu.VMEM((rows, 8, depth), jnp.float32),
            pltpu.SemaphoreType.DMA((rows // tb, 4)),
            pltpu.SemaphoreType.DMA((4,)),
            pltpu.SemaphoreType.DMA((4,)),
        ]
        params = pltpu.CompilerParams(
            collective_id=collective_id, has_side_effects=True, vmem_limit_bytes=60 * 1024 * 1024
        )
    elif nf_ex:
        ex_shapes, ex_scratch = exchange_io(nf_ex, rows, cols, depth)
        k = len(outs)
        names = names[: len(names) - len(scratch)]
        names += [S.ex_b + m for m in range(4 * nf_ex)]
        names += [S.pad, S.fold][: len(scratch)]
        names += [S.ex_zx, S.ex_zy, S.ex_ss, S.ex_rs, S.ex_zs]
        out_shape += ex_shapes
        out_specs += [any_spec] * len(ex_shapes)
        scratch += ex_scratch
        params = pltpu.CompilerParams(
            collective_id=collective_id, has_side_effects=True, vmem_limit_bytes=60 * 1024 * 1024
        )
    else:
        params = pltpu.CompilerParams(vmem_limit_bytes=60 * 1024 * 1024)
    n_big = sum(1 for sp in in_specs if sp is block) + 1 + sum(1 for sp in out_specs if sp is block)
    cost = pl.CostEstimate(
        flops=60 * rows * cols * depth,
        transcendentals=0,
        bytes_accessed=4 * rows * cols * depth * n_big,
    )
    result = pl.pallas_call(
        functools.partial(step_kernel, kind, tuple(names), nf_ex),
        grid=grid,
        in_specs=in_specs,
        out_specs=out_specs,
        out_shape=out_shape,
        scratch_shapes=scratch,
        compiler_params=params,
        cost_estimate=cost,
        name=f"leap_{kind}",
    )(*args)
    if kind == "wave2":
        return result[: len(outs)], result[len(outs) :]
    if nf_ex:
        own = result[: len(outs)]
        ex = result[len(outs) :]
        return own, [ex[4 * j : 4 * j + 4] for j in range(nf_ex)]
    return result


def on_device(
    velocity,
    momentum,
    mass_diag,
    u_prev,
    u_cur,
    adj_next,
    adj_cur,
    observed,
    rec_depth,
    src_cell,
    wavelet,
):
    full_velocity = lax.all_gather(velocity, "shot", axis=0, tiled=True)
    row_count, col_count, depth_cells = full_velocity.shape
    oldest = u_prev[0]
    present = u_cur[0]
    adj_later = adj_next[0]
    adj_now = adj_cur[0]
    rec = rec_depth[0][:, :, None]
    cell = src_cell[0]
    src = jnp.stack(
        [
            cell[0] - lax.axis_index("row") * row_count,
            cell[1] - lax.axis_index("col") * col_count,
            cell[2],
        ]
    ).astype(jnp.int32)
    amp = wavelet[0]

    wave_h, adj_h = exchange([present, adj_now], 1)
    advanced, dw1, pick_adv = leap(
        "wave1", present, *wave_h, oldest, full_velocity, {S.rec: rec, S.src: src, S.amp: amp[0:1]}
    )
    (adj_bulk,), (adv_h,) = leap(
        "adjbulk", adj_now, *adj_h, adj_later, full_velocity, {}, exchanged=[advanced], collective_id=2
    )
    (dw2, pick_far, adj_two, part), adj_two_h = leap(
        "wave2",
        advanced,
        *adv_h,
        present,
        full_velocity,
        {S.rec: rec, S.src: src, S.amp: amp[1:2], S.a2raw: adj_bulk, S.obs: observed[0, 1][:, :, None]},
        collective_id=3,
    )
    misfit_early = pick_adv - observed[0, 0][:, :, None]
    v_new, p_half = leap(
        "adj2",
        adj_two,
        *adj_two_h,
        adj_now,
        full_velocity,
        {
            S.rec: rec,
            S.mis: misfit_early,
            S.dw: dw1,
            S.part: part,
            S.vslab: velocity,
            S.mom: momentum,
            S.mass: mass_diag,
        },
        collective_id=0,
    )
    return (v_new, p_half)


def solution(mesh):
    return jax.shard_map(
        on_device,
        mesh=mesh,
        in_specs=(
            P(("row", "shot"), "col", None),
            P(("row", "shot"), "col", None),
            P(("row", "shot"), "col", None),
            P("shot", "row", "col", None),
            P("shot", "row", "col", None),
            P("shot", "row", "col", None),
            P("shot", "row", "col", None),
            P("shot", None, "row", "col"),
            P("shot", "row", "col"),
            P("shot", None),
            P("shot", None),
        ),
        out_specs=(P(("row", "shot"), "col", None), P(("row", "shot"), "col", None)),
        check_vma=False,
    )
```

```python
import functools

import jax
import jax.numpy as jnp
from jax import lax
from jax.experimental import pallas as pl
from jax.experimental.pallas import tpu as pltpu
from jax.sharding import PartitionSpec as P

STENCIL = (-205.0 / 72.0, 8.0 / 5.0, -1.0 / 5.0, 8.0 / 315.0, -1.0 / 560.0)
squared_courant = 0.012
leap_step = 0.2

class S:
    a2raw = 0
    amp = 1
    dw = 2
    ex_rs = 3
    ex_ss = 4
    ex_zs = 5
    ex_zx = 6
    ex_zy = 7
    f = 8
    fhi = 9
    flo = 10
    fold = 11
    h_rs = 12
    h_ss = 13
    h_zs = 14
    h_zx = 15
    h_zy = 16
    mass = 17
    mis = 18
    mom = 19
    o_a2 = 20
    o_dw = 21
    o_f = 22
    o_p = 23
    o_part = 24
    o_pick = 25
    o_v = 26
    obs = 27
    pad = 28
    part = 29
    prev = 30
    rec = 31
    rs_own = 32
    rs_rs = 33
    rs_ss = 34
    slot_in = 35
    slot_out = 36
    src = 37
    stg_xhi = 38
    stg_xlo = 39
    stg_yhi = 40
    stg_ylo = 41
    vel = 42
    vslab = 43
    xhi = 44
    xlo = 45
    yhi = 46
    ylo = 47
    rl_top = 90
    rl_bot = 91
    rl_rs = 92
    ex_f = 100
    ex_b = 110
    h_b = 130
    pick = 140


ROWS_PER_STEP = 8
Y_CHUNK = 8


class Exchange:

    def __init__(self, fields, bufs, zero_x, zero_y, send_sem, recv_sem, zero_sem):
        self.fields, self.bufs = fields, bufs
        self.zero_x, self.zero_y = zero_x, zero_y
        self.send_sem, self.recv_sem, self.zero_sem = send_sem, recv_sem, zero_sem
        row, nrow = lax.axis_index("row"), lax.axis_size("row")
        col, ncol = lax.axis_index("col"), lax.axis_size("col")
        self.row, self.nrow, self.col, self.ncol = row, nrow, col, ncol
        self.has = (row < nrow - 1, row > 0, col < ncol - 1, col > 0)
        self.peer = ({"row": row + 1}, {"row": row - 1}, {"col": col + 1}, {"col": col - 1})
        self.filler = (1, 0, 3, 2)

    def source(self, f, d):
        rows, cols, _ = f.shape
        if d == 0:
            return f.at[pl.ds(rows - 4, 4)]
        if d == 1:
            return f.at[pl.ds(0, 4)]
        if d == 2:
            return f.at[:, pl.ds(cols - 4, 4)]
        return f.at[:, pl.ds(0, 4)]

    def target(self, j, b):
        if b == 2:
            return self.bufs[4 * j + b].at[:, pl.ds(4, 4)]
        if b == 3:
            return self.bufs[4 * j + b].at[:, pl.ds(0, 4)]
        return self.bufs[4 * j + b]

    def remote(self, j, d):
        return pltpu.make_async_remote_copy(
            src_ref=self.source(self.fields[j], d),
            dst_ref=self.target(j, d),
            send_sem=self.send_sem.at[j, d],
            recv_sem=self.recv_sem.at[j, d],
            device_id=self.peer[d],
            device_id_type=pl.DeviceIdType.MESH,
        )

    def start(self):
        has, row, nrow, col, ncol = self.has, self.row, self.nrow, self.col, self.ncol
        barrier = pltpu.get_barrier_semaphore()
        for d in range(4):
            @pl.when(has[d])
            def _():
                pl.semaphore_signal(barrier, inc=1, device_id=self.peer[d], device_id_type=pl.DeviceIdType.MESH)

        count = (1 - row // (nrow - 1)) + (row + nrow - 1) // nrow + (1 - col // (ncol - 1)) + (col + ncol - 1) // ncol
        pl.semaphore_wait(barrier, count)

        for j in range(len(self.fields)):
            for d in range(4):
                @pl.when(has[d])
                def _():
                    self.remote(j, d).start()

        @pl.when(jnp.logical_not(has[0] & has[1]))
        def _():
            self.zero_x[...] = jnp.zeros_like(self.zero_x)

        @pl.when(jnp.logical_not(has[2] & has[3]))
        def _():
            self.zero_y[...] = jnp.zeros_like(self.zero_y)

        for j in range(len(self.fields)):
            for b in range(4):
                @pl.when(jnp.logical_not(has[self.filler[b]]))
                def _():
                    zero = self.zero_x if b < 2 else self.zero_y
                    copy = pltpu.make_async_copy(zero, self.bufs[4 * j + b], self.zero_sem.at[j, b])
                    copy.start()
                    copy.wait()

    def finish(self):
        has = self.has
        for j in range(len(self.fields)):
            for d in range(4):
                @pl.when(has[d])
                def _():
                    self.remote(j, d).wait_send()
            for b in range(4):
                @pl.when(has[self.filler[b]])
                def _():
                    self.remote(j, b).wait_recv()


def exchange_io(nf, rows, cols, depth):
    shapes = []
    for _ in range(nf):
        shapes += [
            jax.ShapeDtypeStruct((4, cols, depth), jnp.float32),
            jax.ShapeDtypeStruct((4, cols, depth), jnp.float32),
            jax.ShapeDtypeStruct((rows, 8, depth), jnp.float32),
            jax.ShapeDtypeStruct((rows, 8, depth), jnp.float32),
        ]
    scratch = [
        pltpu.VMEM((4, cols, depth), jnp.float32),
        pltpu.VMEM((rows, 8, depth), jnp.float32),
        pltpu.SemaphoreType.DMA((nf, 4)),
        pltpu.SemaphoreType.DMA((nf, 4)),
        pltpu.SemaphoreType.DMA((nf, 4)),
    ]
    return shapes, scratch


def exchange_kernel(nf, *refs):
    ex = Exchange(refs[:nf], refs[nf : 5 * nf], *refs[5 * nf :])
    ex.start()
    ex.finish()


def exchange(fields, collective_id):
    nf = len(fields)
    rows, cols, depth = fields[0].shape
    any_spec = pl.BlockSpec(memory_space=pl.ANY)
    shapes, scratch = exchange_io(nf, rows, cols, depth)
    outs = pl.pallas_call(
        functools.partial(exchange_kernel, nf),
        in_specs=[any_spec] * nf,
        out_specs=[any_spec] * (4 * nf),
        out_shape=shapes,
        scratch_shapes=scratch,
        compiler_params=pltpu.CompilerParams(collective_id=collective_id, has_side_effects=True),
        name=f"halo_exchange_{collective_id}",
    )(*fields)
    return [outs[4 * j : 4 * j + 4] for j in range(nf)]


class HaloSender:

    def __init__(self, ref, nblk, tb):
        self.ref, self.nblk, self.tb = ref, nblk, tb
        row, nrow = lax.axis_index("row"), lax.axis_size("row")
        col, ncol = lax.axis_index("col"), lax.axis_size("col")
        self.row, self.nrow, self.col, self.ncol = row, nrow, col, ncol
        self.has = (row < nrow - 1, row > 0, col < ncol - 1, col > 0)
        self.peer = ({"row": row + 1}, {"row": row - 1}, {"col": col + 1}, {"col": col - 1})
        self.filler = (1, 0, 3, 2)
        self.bufs = [ref[S.h_b + b] for b in range(4)]

    def copy(self, d, blk):
        ref, tb = self.ref, self.tb
        rows_here = pl.ds(pl.multiple_of(blk * tb, tb), tb)
        if d == 0:
            src, dst, sem = ref[S.stg_xlo], self.bufs[0], ref[S.h_ss].at[0, 0]
        elif d == 1:
            src, dst, sem = ref[S.stg_xhi], self.bufs[1], ref[S.h_ss].at[0, 1]
        elif d == 2:
            src, dst = ref[S.stg_ylo].at[rows_here], self.bufs[2].at[rows_here, pl.ds(4, 4)]
            sem = ref[S.h_ss].at[blk, 2]
        else:
            src, dst = ref[S.stg_yhi].at[rows_here], self.bufs[3].at[rows_here, pl.ds(0, 4)]
            sem = ref[S.h_ss].at[blk, 3]
        return pltpu.make_async_remote_copy(
            src_ref=src,
            dst_ref=dst,
            send_sem=sem,
            recv_sem=ref[S.h_rs].at[d],
            device_id=self.peer[d],
            device_id_type=pl.DeviceIdType.MESH,
        )

    def whole(self, b):
        ref = self.ref
        src = {0: ref[S.stg_xlo], 1: ref[S.stg_xhi], 2: ref[S.stg_ylo], 3: ref[S.stg_yhi]}[b]
        dst = {0: self.bufs[0], 1: self.bufs[1], 2: self.bufs[2].at[:, pl.ds(4, 4)], 3: self.bufs[3].at[:, pl.ds(0, 4)]}[b]
        return pltpu.make_async_remote_copy(
            src_ref=src,
            dst_ref=dst,
            send_sem=ref[S.h_ss].at[0, b],
            recv_sem=ref[S.h_rs].at[b],
            device_id=self.peer[b],
            device_id_type=pl.DeviceIdType.MESH,
        )

    def begin(self):
        ref, has, row, nrow, col, ncol = self.ref, self.has, self.row, self.nrow, self.col, self.ncol
        barrier = pltpu.get_barrier_semaphore()
        for d in range(4):
            @pl.when(has[d])
            def _():
                pl.semaphore_signal(barrier, inc=1, device_id=self.peer[d], device_id_type=pl.DeviceIdType.MESH)

        count = (1 - row // (nrow - 1)) + (row + nrow - 1) // nrow + (1 - col // (ncol - 1)) + (col + ncol - 1) // ncol
        pl.semaphore_wait(barrier, count)

        @pl.when(jnp.logical_not(has[0] & has[1]))
        def _():
            ref[S.h_zx][...] = jnp.zeros_like(ref[S.h_zx])

        @pl.when(jnp.logical_not(has[2] & has[3]))
        def _():
            ref[S.h_zy][...] = jnp.zeros_like(ref[S.h_zy])

        for b in range(4):
            @pl.when(jnp.logical_not(has[self.filler[b]]))
            def _():
                zero = ref[S.h_zx] if b < 2 else ref[S.h_zy]
                copy = pltpu.make_async_copy(zero, self.bufs[b], ref[S.h_zs].at[b])
                copy.start()
                copy.wait()

    def send_block(self, blk):
        ref, has, tb = self.ref, self.has, self.tb

        @pl.when(blk == 0)
        def _():
            ref[S.stg_xhi][...] = ref[S.o_a2][0:4]

        @pl.when(blk == self.nblk - 1)
        def _():
            ref[S.stg_xlo][...] = ref[S.o_a2][tb - 4 : tb]

        for d in (2, 3):
            @pl.when(has[d])
            def _():
                self.copy(d, blk).start()

        @pl.when(has[1] & (blk == 0))
        def _():
            self.copy(1, blk).start()

        @pl.when(has[0] & (blk == self.nblk - 1))
        def _():
            self.copy(0, blk).start()

    def finish(self):
        has = self.has
        for blk in range(self.nblk):
            for d in (2, 3):
                @pl.when(has[d])
                def _():
                    self.copy(d, blk).wait_send()

        @pl.when(has[1])
        def _():
            self.copy(1, 0).wait_send()

        @pl.when(has[0])
        def _():
            self.copy(0, self.nblk - 1).wait_send()

        for b in range(4):
            @pl.when(has[self.filler[b]])
            def _():
                self.whole(b).wait_recv()


class ReduceScatter:

    def __init__(self, ref, me, n):
        self.ref, self.me, self.n = ref, me, n
        self.up, self.down, self.far = lax.rem(me + 1, n), lax.rem(me + n - 1, n), lax.rem(me + 2, n)
        half = ref[S.slot_out].shape[1] // 2
        self.top, self.bot = pl.ds(0, half), pl.ds(half, half)

    def remote(self, src, dst, k, recv_sem, peer):
        return pltpu.make_async_remote_copy(
            src_ref=src,
            dst_ref=dst,
            send_sem=self.ref[S.rs_ss].at[k],
            recv_sem=recv_sem,
            device_id={"shot": peer},
            device_id_type=pl.DeviceIdType.MESH,
        )

    def direct(self, blk, k, peer):
        ref = self.ref
        return self.remote(ref[S.slot_out].at[blk], ref[S.slot_in].at[self.me], k, ref[S.rs_rs].at[self.me], peer)

    def relay_top(self):
        ref = self.ref
        src = ref[S.slot_out].at[self.far, self.top]
        return self.remote(src, ref[S.rl_top], 2, ref[S.rl_rs].at[0], self.up)

    def relay_bot(self):
        ref = self.ref
        src = ref[S.slot_out].at[self.far, self.bot]
        return self.remote(src, ref[S.rl_bot], 3, ref[S.rl_rs].at[1], self.down)

    def fwd_top(self):
        ref = self.ref
        dst = ref[S.slot_in].at[self.down, self.top]
        return self.remote(ref[S.rl_top], dst, 4, ref[S.rl_rs].at[2], self.up)

    def fwd_bot(self):
        ref = self.ref
        dst = ref[S.slot_in].at[self.up, self.bot]
        return self.remote(ref[S.rl_bot], dst, 5, ref[S.rl_rs].at[3], self.down)

    def begin(self):
        barrier = pltpu.get_barrier_semaphore()
        for peer in (self.up, self.down):
            pl.semaphore_signal(barrier, inc=1, device_id={"shot": peer}, device_id_type=pl.DeviceIdType.MESH)
        pl.semaphore_wait(barrier, 2)

    def at_step(self, step):
        @pl.when(step == 1)
        def _():
            self.direct(self.up, 0, self.up).start()

        @pl.when(step == 2)
        def _():
            self.relay_top().start()
            self.relay_bot().start()

        @pl.when(step == 3)
        def _():
            self.direct(self.down, 1, self.down).start()
            self.relay_top().wait_recv()
            self.relay_bot().wait_recv()
            self.fwd_top().start()
            self.fwd_bot().start()

    def finish(self):
        ref, me, n = self.ref, self.me, self.n
        own = pltpu.make_async_copy(ref[S.slot_out].at[me], ref[S.slot_in].at[me], ref[S.rs_own])
        own.start()
        self.direct(self.up, 0, self.up).wait_send()
        self.direct(self.down, 1, self.down).wait_send()
        self.relay_top().wait_send()
        self.relay_bot().wait_send()
        self.fwd_top().wait_send()
        self.fwd_bot().wait_send()
        own.wait()
        for src in (self.down, self.up):
            self.remote(ref[S.slot_out].at[src], ref[S.slot_in].at[src], 0, ref[S.rs_rs].at[src], src).wait_recv()
        far_in = ref[S.slot_in].at[self.far, self.top]
        self.remote(ref[S.rl_top], far_in, 4, ref[S.rl_rs].at[2], self.down).wait_recv()
        far_in = ref[S.slot_in].at[self.far, self.bot]
        self.remote(ref[S.rl_bot], far_in, 5, ref[S.rl_rs].at[3], self.up).wait_recv()

        slot_in = ref[S.slot_in]

        def row(r, carry):
            summed = slot_in[0, r]
            for s_ in range(1, n):
                summed = summed + slot_in[s_, r]
            v = ref[S.vslab][r]
            gradient = 2.0 / v * summed
            p_half = ref[S.mom][r] - 0.5 * leap_step * gradient
            ref[S.o_p][r] = p_half
            ref[S.o_v][r] = v + leap_step * p_half / ref[S.mass][r]
            return carry

        lax.fori_loop(0, slot_in.shape[1], row, 0)


def step_kernel(kind, names, nf_ex, *refs):
    ref = dict(zip(names, refs))
    if nf_ex:
        ex = Exchange(
            [ref[S.ex_f + j] for j in range(nf_ex)],
            [ref[S.ex_b + k] for k in range(4 * nf_ex)],
            *[ref[k] for k in (S.ex_zx, S.ex_zy, S.ex_ss, S.ex_rs, S.ex_zs)],
        )
    f_ref, pad = ref[S.f], ref[S.pad]
    tb, cols, depth = f_ref.shape
    n = pl.num_programs(0)
    step = pl.program_id(0)
    if kind == "adj2":
        me = lax.axis_index("shot")
        i = lax.rem(me + 1 + step, n)
        rs = ReduceScatter(ref, me, n)

        @pl.when(step == 0)
        def _():
            rs.begin()

        rs.at_step(step)
    elif kind == "wave2":
        i = lax.rem(step + n - 1, n)
    else:
        i = step

    if nf_ex:
        @pl.when(i == 0)
        def _():
            ex.start()

    lo = jnp.where(i == 0, ref[S.xlo][...], ref[S.flo][...])
    hi = jnp.where(i == n - 1, ref[S.xhi][...], ref[S.fhi][...])
    pad[0:4, 8 : 8 + cols, :] = lo
    pad[4 : 4 + tb, 8 : 8 + cols, :] = f_ref[...]
    pad[4 + tb : 8 + tb, 8 : 8 + cols, :] = hi
    pad[4 : 4 + tb, 0:8, :] = ref[S.ylo][...]
    pad[4 : 4 + tb, 8 + cols : 16 + cols, :] = ref[S.yhi][...]

    z_index = lax.broadcasted_iota(jnp.int32, (Y_CHUNK, depth), 1)
    y_index = lax.broadcasted_iota(jnp.int32, (Y_CHUNK, depth), 0)
    wave = kind in ("wave1", "wave2")
    if wave:
        src_ref = ref[S.src]
        src_x = src_ref[0] - i * tb
        src_y = src_ref[1]
        src_z = src_ref[2]
        amp = ref[S.amp][0]

    def row(r, carry):
        for y0 in range(0, cols, Y_CHUNK):
            ys = pl.ds(y0, Y_CHUNK)
            pys = pl.ds(8 + y0, Y_CHUNK)
            c = pad[4 + r, pys, :]
            result = (3.0 * STENCIL[0]) * c
            for k in range(1, 5):
                along = pad[4 + r + k, pys, :] + pad[4 + r - k, pys, :]
                along = along + (
                    pad[4 + r, pl.ds(8 + y0 + k, Y_CHUNK), :]
                    + pad[4 + r, pl.ds(8 + y0 - k, Y_CHUNK), :]
                )
                zp = jnp.where(z_index < depth - k, pltpu.roll(c, depth - k, 1), 0.0)
                zm = jnp.where(z_index >= k, pltpu.roll(c, k, 1), 0.0)
                along = along + (zp + zm)
                result = result + STENCIL[k] * along
            v = ref[S.vel][r, ys, :]
            stiff = squared_courant * v * v
            prev = ref[S.prev][r, ys, :]
            out = 2.0 * c - prev + stiff * result
            if wave:
                at_rec = z_index == ref[S.rec][r, ys, :]
                hit = (r == src_x) & (y_index + y0 == src_y) & (z_index == src_z)
                out = out + jnp.where(hit, amp, 0.0)
                sel = jnp.where(at_rec, out, 0.0)
                folded = sel[:, 0:128]
                for t in range(128, depth, 128):
                    folded = folded + sel[:, t : t + 128]
                ref[S.fold][pl.ds(pl.multiple_of(r * cols + y0, Y_CHUNK), Y_CHUNK), :] = folded
                ref[S.o_dw][r, ys, :] = (out - 2.0 * c) + prev
                if kind == "wave1":
                    ref[S.o_f][r, ys, :] = out
            elif kind == "adjbulk":
                ref[S.o_f][r, ys, :] = out
            else:
                at_rec = z_index == ref[S.rec][r, ys, :]
                misfit = ref[S.pick][r, ys, :] - ref[S.obs][r, ys, :]
                out = out + jnp.where(at_rec, misfit, 0.0)
                ref[S.slot_out][i, r, ys, :] = ref[S.part][r, ys, :] + out * ref[S.dw][r, ys, :]
        return carry

    lax.fori_loop(0, tb, row, 0)
    if wave:
        ref[S.o_pick][...] = jnp.sum(ref[S.fold][...], axis=1, keepdims=True).reshape(ref[S.o_pick].shape)
    if kind == "wave2":
        sender = HaloSender(ref, n, tb)

        @pl.when(step == 0)
        def _():
            sender.begin()

        def inject(r, carry):
            for y0 in range(0, cols, Y_CHUNK):
                ys = pl.ds(y0, Y_CHUNK)
                at_rec = z_index == ref[S.rec][r, ys, :]
                misfit = ref[S.o_pick][r, ys, :] - ref[S.obs][r, ys, :]
                a2 = ref[S.a2raw][r, ys, :] + jnp.where(at_rec, misfit, 0.0)
                ref[S.o_a2][r, ys, :] = a2
                ref[S.o_part][r, ys, :] = a2 * ref[S.o_dw][r, ys, :]
                if y0 == 0:
                    ref[S.stg_yhi][i * tb + r] = a2[0:4]
                if y0 == cols - Y_CHUNK:
                    ref[S.stg_ylo][i * tb + r] = a2[Y_CHUNK - 4 : Y_CHUNK]
            return carry

        lax.fori_loop(0, tb, inject, 0)
        sender.send_block(i)

        @pl.when(step == n - 1)
        def _():
            sender.finish()

    if nf_ex:
        @pl.when(i == n - 1)
        def _():
            ex.finish()
    if kind == "adj2":
        @pl.when(step == n - 1)
        def _():
            rs.finish()


def leap(kind, f, xlo, xhi, ylo, yhi, prev, vel, extra, exchanged=(), collective_id=None):
    rows, cols, depth = f.shape
    tb = ROWS_PER_STEP
    nblk = rows // tb
    grid = (nblk,)
    nq = rows // 4
    if kind == "adj2":
        def at(fn):
            return lambda i: fn(lax.rem(lax.axis_index("shot") + 1 + i, nblk))

        fixed = at
    elif kind == "wave2":
        def at(fn):
            return lambda i: fn(lax.rem(i + nblk - 1, nblk))

        def fixed(fn):
            return fn
    else:
        def at(fn):
            return fn

        fixed = at
    block = pl.BlockSpec((tb, cols, depth), at(lambda i: (i, 0, 0)))
    lo_spec = pl.BlockSpec((4, cols, depth), at(lambda i: (jnp.maximum(2 * i - 1, 0), 0, 0)))
    hi_spec = pl.BlockSpec((4, cols, depth), at(lambda i: (jnp.minimum(2 * i + 2, nq - 1), 0, 0)))
    whole4 = pl.BlockSpec((4, cols, depth), fixed(lambda i: (0, 0, 0)))
    yspec = pl.BlockSpec((tb, 8, depth), at(lambda i: (i, 0, 0)))
    col1 = pl.BlockSpec((tb, cols, 1), at(lambda i: (i, 0, 0)))
    slab = pl.BlockSpec((tb, cols, depth), fixed(lambda i: (0, 0, 0)))
    smem = pl.BlockSpec(memory_space=pltpu.SMEM)
    any_spec = pl.BlockSpec(memory_space=pl.ANY)
    field = jax.ShapeDtypeStruct((rows, cols, depth), jnp.float32)
    picked = jax.ShapeDtypeStruct((rows, cols, 1), jnp.float32)
    spec_of = {S.src: smem, S.amp: smem, S.rec: col1, S.mis: col1, S.obs: col1, S.pick: col1, S.vslab: slab, S.mom: slab, S.mass: slab}

    names = [S.f, S.flo, S.fhi, S.xlo, S.xhi, S.ylo, S.yhi, S.prev, S.vel]
    in_specs = [block, lo_spec, hi_spec, whole4, whole4, yspec, yspec, block, block]
    args = [f, f, f, xlo, xhi, ylo, yhi, prev, vel]
    for key, value in extra.items():
        names.append(key)
        in_specs.append(spec_of.get(key, block))
        args.append(value)
    nf_ex = len(exchanged)
    for j, g in enumerate(exchanged):
        names.append(S.ex_f + j)
        in_specs.append(any_spec)
        args.append(g)

    outs = {
        "wave1": [(S.o_f, field, block), (S.o_dw, field, block), (S.o_pick, picked, col1)],
        "wave2": [(S.o_dw, field, block), (S.o_pick, picked, col1), (S.o_a2, field, block), (S.o_part, field, block)],
        "adjbulk": [(S.o_f, field, block)],
        "adj2": [
            (S.o_v, jax.ShapeDtypeStruct((tb, cols, depth), jnp.float32), slab),
            (S.o_p, jax.ShapeDtypeStruct((tb, cols, depth), jnp.float32), slab),
        ],
    }[kind]
    names += [o[0] for o in outs]
    out_shape = [o[1] for o in outs]
    out_specs = [o[2] for o in outs]
    scratch = [pltpu.VMEM((tb + 8, cols + 16, depth), jnp.float32)]
    names.append(S.pad)
    if kind in ("wave1", "wave2"):
        scratch.append(pltpu.VMEM((tb * cols, 128), jnp.float32))
        names.append(S.fold)
    if kind == "adj2":
        names += [S.slot_out, S.slot_in, S.rs_ss, S.rs_rs, S.rs_own, S.rl_top, S.rl_bot, S.rl_rs]
        scratch += [
            pltpu.VMEM((nblk, tb, cols, depth), jnp.float32),
            pltpu.VMEM((nblk, tb, cols, depth), jnp.float32),
            pltpu.SemaphoreType.DMA((6,)),
            pltpu.SemaphoreType.DMA((nblk,)),
            pltpu.SemaphoreType.DMA(()),
            pltpu.VMEM((tb // 2, cols, depth), jnp.float32),
            pltpu.VMEM((tb // 2, cols, depth), jnp.float32),
            pltpu.SemaphoreType.DMA((4,)),
        ]
        params = pltpu.CompilerParams(
            collective_id=collective_id, has_side_effects=True, vmem_limit_bytes=60 * 1024 * 1024
        )
    elif kind == "wave2":
        h_shapes, _ = exchange_io(1, rows, cols, depth)
        names = names[: len(names) - len(scratch)]
        names += [S.h_b + m for m in range(4)]
        names += [S.pad, S.fold]
        names += [S.stg_xlo, S.stg_xhi, S.stg_ylo, S.stg_yhi, S.h_zx, S.h_zy, S.h_ss, S.h_rs, S.h_zs]
        out_shape += h_shapes
        out_specs += [any_spec] * 4
        scratch += [
            pltpu.VMEM((4, cols, depth), jnp.float32),
            pltpu.VMEM((4, cols, depth), jnp.float32),
            pltpu.VMEM((rows, 4, depth), jnp.float32),
            pltpu.VMEM((rows, 4, depth), jnp.float32),
            pltpu.VMEM((4, cols, depth), jnp.float32),
            pltpu.VMEM((rows, 8, depth), jnp.float32),
            pltpu.SemaphoreType.DMA((rows // tb, 4)),
            pltpu.SemaphoreType.DMA((4,)),
            pltpu.SemaphoreType.DMA((4,)),
        ]
        params = pltpu.CompilerParams(
            collective_id=collective_id, has_side_effects=True, vmem_limit_bytes=60 * 1024 * 1024
        )
    elif nf_ex:
        ex_shapes, ex_scratch = exchange_io(nf_ex, rows, cols, depth)
        k = len(outs)
        names = names[: len(names) - len(scratch)]
        names += [S.ex_b + m for m in range(4 * nf_ex)]
        names += [S.pad, S.fold][: len(scratch)]
        names += [S.ex_zx, S.ex_zy, S.ex_ss, S.ex_rs, S.ex_zs]
        out_shape += ex_shapes
        out_specs += [any_spec] * len(ex_shapes)
        scratch += ex_scratch
        params = pltpu.CompilerParams(
            collective_id=collective_id, has_side_effects=True, vmem_limit_bytes=60 * 1024 * 1024
        )
    else:
        params = pltpu.CompilerParams(vmem_limit_bytes=60 * 1024 * 1024)
    n_big = sum(1 for sp in in_specs if sp is block) + 1 + sum(1 for sp in out_specs if sp is block)
    cost = pl.CostEstimate(
        flops=60 * rows * cols * depth,
        transcendentals=0,
        bytes_accessed=4 * rows * cols * depth * n_big,
    )
    result = pl.pallas_call(
        functools.partial(step_kernel, kind, tuple(names), nf_ex),
        grid=grid,
        in_specs=in_specs,
        out_specs=out_specs,
        out_shape=out_shape,
        scratch_shapes=scratch,
        compiler_params=params,
        cost_estimate=cost,
        name=f"leap_{kind}",
    )(*args)
    if kind == "wave2":
        return result[: len(outs)], result[len(outs) :]
    if nf_ex:
        own = result[: len(outs)]
        ex = result[len(outs) :]
        return own, [ex[4 * j : 4 * j + 4] for j in range(nf_ex)]
    return result


def on_device(
    velocity,
    momentum,
    mass_diag,
    u_prev,
    u_cur,
    adj_next,
    adj_cur,
    observed,
    rec_depth,
    src_cell,
    wavelet,
):
    full_velocity = lax.all_gather(velocity, "shot", axis=0, tiled=True)
    row_count, col_count, depth_cells = full_velocity.shape
    oldest = u_prev[0]
    present = u_cur[0]
    adj_later = adj_next[0]
    adj_now = adj_cur[0]
    rec = rec_depth[0][:, :, None]
    cell = src_cell[0]
    src = jnp.stack(
        [
            cell[0] - lax.axis_index("row") * row_count,
            cell[1] - lax.axis_index("col") * col_count,
            cell[2],
        ]
    ).astype(jnp.int32)
    amp = wavelet[0]

    wave_h, adj_h = exchange([present, adj_now], 1)
    advanced, dw1, pick_adv = leap(
        "wave1", present, *wave_h, oldest, full_velocity, {S.rec: rec, S.src: src, S.amp: amp[0:1]}
    )
    (adj_bulk,), (adv_h,) = leap(
        "adjbulk", adj_now, *adj_h, adj_later, full_velocity, {}, exchanged=[advanced], collective_id=2
    )
    (dw2, pick_far, adj_two, part), adj_two_h = leap(
        "wave2",
        advanced,
        *adv_h,
        present,
        full_velocity,
        {S.rec: rec, S.src: src, S.amp: amp[1:2], S.a2raw: adj_bulk, S.obs: observed[0, 1][:, :, None]},
        collective_id=3,
    )
    v_new, p_half = leap(
        "adj2",
        adj_two,
        *adj_two_h,
        adj_now,
        full_velocity,
        {
            S.rec: rec,
            S.pick: pick_adv,
            S.obs: observed[0, 0][:, :, None],
            S.dw: dw1,
            S.part: part,
            S.vslab: velocity,
            S.mom: momentum,
            S.mass: mass_diag,
        },
        collective_id=0,
    )
    return (v_new, p_half)


def solution(mesh):
    return jax.shard_map(
        on_device,
        mesh=mesh,
        in_specs=(
            P(("row", "shot"), "col", None),
            P(("row", "shot"), "col", None),
            P(("row", "shot"), "col", None),
            P("shot", "row", "col", None),
            P("shot", "row", "col", None),
            P("shot", "row", "col", None),
            P("shot", "row", "col", None),
            P("shot", None, "row", "col"),
            P("shot", "row", "col"),
            P("shot", None),
            P("shot", None),
        ),
        out_specs=(P(("row", "shot"), "col", None), P(("row", "shot"), "col", None)),
        check_vma=False,
    )
```

```python
import functools

import jax
import jax.numpy as jnp
from jax import lax
from jax.experimental import pallas as pl
from jax.experimental.pallas import tpu as pltpu
from jax.sharding import PartitionSpec as P

STENCIL = (-205.0 / 72.0, 8.0 / 5.0, -1.0 / 5.0, 8.0 / 315.0, -1.0 / 560.0)
squared_courant = 0.012
leap_step = 0.2

class S:
    a2raw = 0
    amp = 1
    dw = 2
    ex_rs = 3
    ex_ss = 4
    ex_zs = 5
    ex_zx = 6
    ex_zy = 7
    f = 8
    fhi = 9
    flo = 10
    fold = 11
    h_rs = 12
    h_ss = 13
    h_zs = 14
    h_zx = 15
    h_zy = 16
    mass = 17
    mis = 18
    mom = 19
    o_a2 = 20
    o_dw = 21
    o_f = 22
    o_p = 23
    o_part = 24
    o_pick = 25
    o_v = 26
    obs = 27
    pad = 28
    part = 29
    prev = 30
    rec = 31
    rs_own = 32
    rs_rs = 33
    rs_ss = 34
    slot_in = 35
    slot_out = 36
    src = 37
    stg_xhi = 38
    stg_xlo = 39
    stg_yhi = 40
    stg_ylo = 41
    vel = 42
    vslab = 43
    xhi = 44
    xlo = 45
    yhi = 46
    ylo = 47
    rl_top = 90
    rl_bot = 91
    rl_rs = 92
    ex_f = 100
    ex_b = 110
    h_b = 130
    pick = 140


ROWS_PER_STEP = 8
Y_CHUNK = 8


class Exchange:

    def __init__(self, fields, bufs, zero_x, zero_y, send_sem, recv_sem, zero_sem):
        self.fields, self.bufs = fields, bufs
        self.zero_x, self.zero_y = zero_x, zero_y
        self.send_sem, self.recv_sem, self.zero_sem = send_sem, recv_sem, zero_sem
        row, nrow = lax.axis_index("row"), lax.axis_size("row")
        col, ncol = lax.axis_index("col"), lax.axis_size("col")
        self.row, self.nrow, self.col, self.ncol = row, nrow, col, ncol
        self.has = (row < nrow - 1, row > 0, col < ncol - 1, col > 0)
        self.peer = ({"row": row + 1}, {"row": row - 1}, {"col": col + 1}, {"col": col - 1})
        self.filler = (1, 0, 3, 2)

    def source(self, f, d):
        rows, cols, _ = f.shape
        if d == 0:
            return f.at[pl.ds(rows - 4, 4)]
        if d == 1:
            return f.at[pl.ds(0, 4)]
        if d == 2:
            return f.at[:, pl.ds(cols - 4, 4)]
        return f.at[:, pl.ds(0, 4)]

    def target(self, j, b):
        if b == 2:
            return self.bufs[4 * j + b].at[:, pl.ds(4, 4)]
        if b == 3:
            return self.bufs[4 * j + b].at[:, pl.ds(0, 4)]
        return self.bufs[4 * j + b]

    def remote(self, j, d):
        return pltpu.make_async_remote_copy(
            src_ref=self.source(self.fields[j], d),
            dst_ref=self.target(j, d),
            send_sem=self.send_sem.at[j, d],
            recv_sem=self.recv_sem.at[j, d],
            device_id=self.peer[d],
            device_id_type=pl.DeviceIdType.MESH,
        )

    def start(self):
        has, row, nrow, col, ncol = self.has, self.row, self.nrow, self.col, self.ncol
        barrier = pltpu.get_barrier_semaphore()
        for d in range(4):
            @pl.when(has[d])
            def _():
                pl.semaphore_signal(barrier, inc=1, device_id=self.peer[d], device_id_type=pl.DeviceIdType.MESH)

        count = (1 - row // (nrow - 1)) + (row + nrow - 1) // nrow + (1 - col // (ncol - 1)) + (col + ncol - 1) // ncol
        pl.semaphore_wait(barrier, count)

        for j in range(len(self.fields)):
            for d in range(4):
                @pl.when(has[d])
                def _():
                    self.remote(j, d).start()

        @pl.when(jnp.logical_not(has[0] & has[1]))
        def _():
            self.zero_x[...] = jnp.zeros_like(self.zero_x)

        @pl.when(jnp.logical_not(has[2] & has[3]))
        def _():
            self.zero_y[...] = jnp.zeros_like(self.zero_y)

        for j in range(len(self.fields)):
            for b in range(4):
                @pl.when(jnp.logical_not(has[self.filler[b]]))
                def _():
                    zero = self.zero_x if b < 2 else self.zero_y
                    copy = pltpu.make_async_copy(zero, self.bufs[4 * j + b], self.zero_sem.at[j, b])
                    copy.start()
                    copy.wait()

    def finish(self):
        has = self.has
        for j in range(len(self.fields)):
            for d in range(4):
                @pl.when(has[d])
                def _():
                    self.remote(j, d).wait_send()
            for b in range(4):
                @pl.when(has[self.filler[b]])
                def _():
                    self.remote(j, b).wait_recv()


def exchange_io(nf, rows, cols, depth):
    shapes = []
    for _ in range(nf):
        shapes += [
            jax.ShapeDtypeStruct((4, cols, depth), jnp.float32),
            jax.ShapeDtypeStruct((4, cols, depth), jnp.float32),
            jax.ShapeDtypeStruct((rows, 8, depth), jnp.float32),
            jax.ShapeDtypeStruct((rows, 8, depth), jnp.float32),
        ]
    scratch = [
        pltpu.VMEM((4, cols, depth), jnp.float32),
        pltpu.VMEM((rows, 8, depth), jnp.float32),
        pltpu.SemaphoreType.DMA((nf, 4)),
        pltpu.SemaphoreType.DMA((nf, 4)),
        pltpu.SemaphoreType.DMA((nf, 4)),
    ]
    return shapes, scratch


def exchange_kernel(nf, *refs):
    ex = Exchange(refs[:nf], refs[nf : 5 * nf], *refs[5 * nf :])
    ex.start()
    ex.finish()


def exchange(fields, collective_id):
    nf = len(fields)
    rows, cols, depth = fields[0].shape
    any_spec = pl.BlockSpec(memory_space=pl.ANY)
    shapes, scratch = exchange_io(nf, rows, cols, depth)
    outs = pl.pallas_call(
        functools.partial(exchange_kernel, nf),
        in_specs=[any_spec] * nf,
        out_specs=[any_spec] * (4 * nf),
        out_shape=shapes,
        scratch_shapes=scratch,
        compiler_params=pltpu.CompilerParams(collective_id=collective_id, has_side_effects=True),
        name=f"halo_exchange_{collective_id}",
    )(*fields)
    return [outs[4 * j : 4 * j + 4] for j in range(nf)]


class HaloSender:

    def __init__(self, ref, nblk, tb):
        self.ref, self.nblk, self.tb = ref, nblk, tb
        row, nrow = lax.axis_index("row"), lax.axis_size("row")
        col, ncol = lax.axis_index("col"), lax.axis_size("col")
        self.row, self.nrow, self.col, self.ncol = row, nrow, col, ncol
        self.has = (row < nrow - 1, row > 0, col < ncol - 1, col > 0)
        self.peer = ({"row": row + 1}, {"row": row - 1}, {"col": col + 1}, {"col": col - 1})
        self.filler = (1, 0, 3, 2)
        self.bufs = [ref[S.h_b + b] for b in range(4)]

    def copy(self, d, blk):
        ref, tb = self.ref, self.tb
        rows_here = pl.ds(pl.multiple_of(blk * tb, tb), tb)
        if d == 0:
            src, dst, sem = ref[S.stg_xlo], self.bufs[0], ref[S.h_ss].at[0, 0]
        elif d == 1:
            src, dst, sem = ref[S.stg_xhi], self.bufs[1], ref[S.h_ss].at[0, 1]
        elif d == 2:
            src, dst = ref[S.stg_ylo].at[rows_here], self.bufs[2].at[rows_here, pl.ds(4, 4)]
            sem = ref[S.h_ss].at[blk, 2]
        else:
            src, dst = ref[S.stg_yhi].at[rows_here], self.bufs[3].at[rows_here, pl.ds(0, 4)]
            sem = ref[S.h_ss].at[blk, 3]
        return pltpu.make_async_remote_copy(
            src_ref=src,
            dst_ref=dst,
            send_sem=sem,
            recv_sem=ref[S.h_rs].at[d],
            device_id=self.peer[d],
            device_id_type=pl.DeviceIdType.MESH,
        )

    def whole(self, b):
        ref = self.ref
        src = {0: ref[S.stg_xlo], 1: ref[S.stg_xhi], 2: ref[S.stg_ylo], 3: ref[S.stg_yhi]}[b]
        dst = {0: self.bufs[0], 1: self.bufs[1], 2: self.bufs[2].at[:, pl.ds(4, 4)], 3: self.bufs[3].at[:, pl.ds(0, 4)]}[b]
        return pltpu.make_async_remote_copy(
            src_ref=src,
            dst_ref=dst,
            send_sem=ref[S.h_ss].at[0, b],
            recv_sem=ref[S.h_rs].at[b],
            device_id=self.peer[b],
            device_id_type=pl.DeviceIdType.MESH,
        )

    def begin(self):
        ref, has, row, nrow, col, ncol = self.ref, self.has, self.row, self.nrow, self.col, self.ncol
        barrier = pltpu.get_barrier_semaphore()
        for d in range(4):
            @pl.when(has[d])
            def _():
                pl.semaphore_signal(barrier, inc=1, device_id=self.peer[d], device_id_type=pl.DeviceIdType.MESH)

        count = (1 - row // (nrow - 1)) + (row + nrow - 1) // nrow + (1 - col // (ncol - 1)) + (col + ncol - 1) // ncol
        pl.semaphore_wait(barrier, count)

        @pl.when(jnp.logical_not(has[0] & has[1]))
        def _():
            ref[S.h_zx][...] = jnp.zeros_like(ref[S.h_zx])

        @pl.when(jnp.logical_not(has[2] & has[3]))
        def _():
            ref[S.h_zy][...] = jnp.zeros_like(ref[S.h_zy])

        for b in range(4):
            @pl.when(jnp.logical_not(has[self.filler[b]]))
            def _():
                zero = ref[S.h_zx] if b < 2 else ref[S.h_zy]
                copy = pltpu.make_async_copy(zero, self.bufs[b], ref[S.h_zs].at[b])
                copy.start()
                copy.wait()

    def send_block(self, blk):
        ref, has, tb = self.ref, self.has, self.tb

        @pl.when(blk == 0)
        def _():
            ref[S.stg_xhi][...] = ref[S.o_a2][0:4]

        @pl.when(blk == self.nblk - 1)
        def _():
            ref[S.stg_xlo][...] = ref[S.o_a2][tb - 4 : tb]

        for d in (2, 3):
            @pl.when(has[d])
            def _():
                self.copy(d, blk).start()

        @pl.when(has[1] & (blk == 0))
        def _():
            self.copy(1, blk).start()

        @pl.when(has[0] & (blk == self.nblk - 1))
        def _():
            self.copy(0, blk).start()

    def finish(self):
        has = self.has
        for blk in range(self.nblk):
            for d in (2, 3):
                @pl.when(has[d])
                def _():
                    self.copy(d, blk).wait_send()

        @pl.when(has[1])
        def _():
            self.copy(1, 0).wait_send()

        @pl.when(has[0])
        def _():
            self.copy(0, self.nblk - 1).wait_send()

        for b in range(4):
            @pl.when(has[self.filler[b]])
            def _():
                self.whole(b).wait_recv()


class ReduceScatter:

    def __init__(self, ref, me, n):
        self.ref, self.me, self.n = ref, me, n
        self.up, self.down, self.far = lax.rem(me + 1, n), lax.rem(me + n - 1, n), lax.rem(me + 2, n)
        half = ref[S.slot_out].shape[1] // 2
        self.top, self.bot = pl.ds(0, half), pl.ds(half, half)

    def remote(self, src, dst, k, recv_sem, peer):
        return pltpu.make_async_remote_copy(
            src_ref=src,
            dst_ref=dst,
            send_sem=self.ref[S.rs_ss].at[k],
            recv_sem=recv_sem,
            device_id={"shot": peer},
            device_id_type=pl.DeviceIdType.MESH,
        )

    def direct(self, blk, k, peer):
        ref = self.ref
        return self.remote(ref[S.slot_out].at[blk], ref[S.slot_in].at[self.me], k, ref[S.rs_rs].at[self.me], peer)

    def relay_top(self):
        ref = self.ref
        src = ref[S.slot_out].at[self.far, self.top]
        return self.remote(src, ref[S.rl_top], 2, ref[S.rl_rs].at[0], self.up)

    def relay_bot(self):
        ref = self.ref
        src = ref[S.slot_out].at[self.far, self.bot]
        return self.remote(src, ref[S.rl_bot], 3, ref[S.rl_rs].at[1], self.down)

    def fwd_top(self):
        ref = self.ref
        dst = ref[S.slot_in].at[self.down, self.top]
        return self.remote(ref[S.rl_top], dst, 4, ref[S.rl_rs].at[2], self.up)

    def fwd_bot(self):
        ref = self.ref
        dst = ref[S.slot_in].at[self.up, self.bot]
        return self.remote(ref[S.rl_bot], dst, 5, ref[S.rl_rs].at[3], self.down)

    def begin(self):
        barrier = pltpu.get_barrier_semaphore()
        for peer in (self.up, self.down):
            pl.semaphore_signal(barrier, inc=1, device_id={"shot": peer}, device_id_type=pl.DeviceIdType.MESH)
        pl.semaphore_wait(barrier, 2)

    def at_step(self, step):
        @pl.when(step == 1)
        def _():
            self.direct(self.up, 0, self.up).start()

        @pl.when(step == 2)
        def _():
            self.relay_top().start()
            self.relay_bot().start()

        @pl.when(step == 3)
        def _():
            self.direct(self.down, 1, self.down).start()
            self.relay_top().wait_recv()
            self.relay_bot().wait_recv()
            self.fwd_top().start()
            self.fwd_bot().start()

    def finish(self):
        ref, me, n = self.ref, self.me, self.n
        own = pltpu.make_async_copy(ref[S.slot_out].at[me], ref[S.slot_in].at[me], ref[S.rs_own])
        own.start()
        self.direct(self.up, 0, self.up).wait_send()
        self.direct(self.down, 1, self.down).wait_send()
        self.relay_top().wait_send()
        self.relay_bot().wait_send()
        self.fwd_top().wait_send()
        self.fwd_bot().wait_send()
        own.wait()
        for src in (self.down, self.up):
            self.remote(ref[S.slot_out].at[src], ref[S.slot_in].at[src], 0, ref[S.rs_rs].at[src], src).wait_recv()
        far_in = ref[S.slot_in].at[self.far, self.top]
        self.remote(ref[S.rl_top], far_in, 4, ref[S.rl_rs].at[2], self.down).wait_recv()
        far_in = ref[S.slot_in].at[self.far, self.bot]
        self.remote(ref[S.rl_bot], far_in, 5, ref[S.rl_rs].at[3], self.up).wait_recv()

        slot_in = ref[S.slot_in]

        def row(r, carry):
            summed = slot_in[0, r]
            for s_ in range(1, n):
                summed = summed + slot_in[s_, r]
            ref[S.o_v][r] = summed
            return carry

        lax.fori_loop(0, slot_in.shape[1], row, 0)


def step_kernel(kind, names, nf_ex, *refs):
    ref = dict(zip(names, refs))
    if nf_ex:
        ex = Exchange(
            [ref[S.ex_f + j] for j in range(nf_ex)],
            [ref[S.ex_b + k] for k in range(4 * nf_ex)],
            *[ref[k] for k in (S.ex_zx, S.ex_zy, S.ex_ss, S.ex_rs, S.ex_zs)],
        )
    f_ref, pad = ref[S.f], ref[S.pad]
    tb, cols, depth = f_ref.shape
    n = pl.num_programs(0)
    step = pl.program_id(0)
    if kind == "adj2":
        me = lax.axis_index("shot")
        i = lax.rem(me + 1 + step, n)
        rs = ReduceScatter(ref, me, n)

        @pl.when(step == 0)
        def _():
            rs.begin()

        rs.at_step(step)
    elif kind == "wave2":
        i = lax.rem(step + n - 1, n)
    else:
        i = step

    if nf_ex:
        @pl.when(i == 0)
        def _():
            ex.start()

    lo = jnp.where(i == 0, ref[S.xlo][...], ref[S.flo][...])
    hi = jnp.where(i == n - 1, ref[S.xhi][...], ref[S.fhi][...])
    pad[0:4, 8 : 8 + cols, :] = lo
    pad[4 : 4 + tb, 8 : 8 + cols, :] = f_ref[...]
    pad[4 + tb : 8 + tb, 8 : 8 + cols, :] = hi
    pad[4 : 4 + tb, 0:8, :] = ref[S.ylo][...]
    pad[4 : 4 + tb, 8 + cols : 16 + cols, :] = ref[S.yhi][...]

    z_index = lax.broadcasted_iota(jnp.int32, (Y_CHUNK, depth), 1)
    y_index = lax.broadcasted_iota(jnp.int32, (Y_CHUNK, depth), 0)
    wave = kind in ("wave1", "wave2")
    if wave:
        src_ref = ref[S.src]
        src_x = src_ref[0] - i * tb
        src_y = src_ref[1]
        src_z = src_ref[2]
        amp = ref[S.amp][0]

    def row(r, carry):
        for y0 in range(0, cols, Y_CHUNK):
            ys = pl.ds(y0, Y_CHUNK)
            pys = pl.ds(8 + y0, Y_CHUNK)
            c = pad[4 + r, pys, :]
            result = (3.0 * STENCIL[0]) * c
            for k in range(1, 5):
                along = pad[4 + r + k, pys, :] + pad[4 + r - k, pys, :]
                along = along + (
                    pad[4 + r, pl.ds(8 + y0 + k, Y_CHUNK), :]
                    + pad[4 + r, pl.ds(8 + y0 - k, Y_CHUNK), :]
                )
                zp = jnp.where(z_index < depth - k, pltpu.roll(c, depth - k, 1), 0.0)
                zm = jnp.where(z_index >= k, pltpu.roll(c, k, 1), 0.0)
                along = along + (zp + zm)
                result = result + STENCIL[k] * along
            v = ref[S.vel][r, ys, :]
            stiff = squared_courant * v * v
            prev = ref[S.prev][r, ys, :]
            out = 2.0 * c - prev + stiff * result
            if wave:
                at_rec = z_index == ref[S.rec][r, ys, :]
                hit = (r == src_x) & (y_index + y0 == src_y) & (z_index == src_z)
                out = out + jnp.where(hit, amp, 0.0)
                sel = jnp.where(at_rec, out, 0.0)
                folded = sel[:, 0:128]
                for t in range(128, depth, 128):
                    folded = folded + sel[:, t : t + 128]
                ref[S.fold][pl.ds(pl.multiple_of(r * cols + y0, Y_CHUNK), Y_CHUNK), :] = folded
                ref[S.o_dw][r, ys, :] = (out - 2.0 * c) + prev
                if kind == "wave1":
                    ref[S.o_f][r, ys, :] = out
            elif kind == "adjbulk":
                ref[S.o_f][r, ys, :] = out
            else:
                at_rec = z_index == ref[S.rec][r, ys, :]
                misfit = ref[S.pick][r, ys, :] - ref[S.obs][r, ys, :]
                out = out + jnp.where(at_rec, misfit, 0.0)
                ref[S.slot_out][i, r, ys, :] = ref[S.part][r, ys, :] + out * ref[S.dw][r, ys, :]
        return carry

    lax.fori_loop(0, tb, row, 0)
    if wave:
        ref[S.o_pick][...] = jnp.sum(ref[S.fold][...], axis=1, keepdims=True).reshape(ref[S.o_pick].shape)
    if kind == "wave2":
        sender = HaloSender(ref, n, tb)

        @pl.when(step == 0)
        def _():
            sender.begin()

        def inject(r, carry):
            for y0 in range(0, cols, Y_CHUNK):
                ys = pl.ds(y0, Y_CHUNK)
                at_rec = z_index == ref[S.rec][r, ys, :]
                misfit = ref[S.o_pick][r, ys, :] - ref[S.obs][r, ys, :]
                a2 = ref[S.a2raw][r, ys, :] + jnp.where(at_rec, misfit, 0.0)
                ref[S.o_a2][r, ys, :] = a2
                ref[S.o_part][r, ys, :] = a2 * ref[S.o_dw][r, ys, :]
                if y0 == 0:
                    ref[S.stg_yhi][i * tb + r] = a2[0:4]
                if y0 == cols - Y_CHUNK:
                    ref[S.stg_ylo][i * tb + r] = a2[Y_CHUNK - 4 : Y_CHUNK]
            return carry

        lax.fori_loop(0, tb, inject, 0)
        sender.send_block(i)

        @pl.when(step == n - 1)
        def _():
            sender.finish()

    if nf_ex:
        @pl.when(i == n - 1)
        def _():
            ex.finish()
    if kind == "adj2":
        @pl.when(step == n - 1)
        def _():
            rs.finish()


def leap(kind, f, xlo, xhi, ylo, yhi, prev, vel, extra, exchanged=(), collective_id=None):
    rows, cols, depth = f.shape
    tb = ROWS_PER_STEP
    nblk = rows // tb
    grid = (nblk,)
    nq = rows // 4
    if kind == "adj2":
        def at(fn):
            return lambda i: fn(lax.rem(lax.axis_index("shot") + 1 + i, nblk))

        fixed = at
    elif kind == "wave2":
        def at(fn):
            return lambda i: fn(lax.rem(i + nblk - 1, nblk))

        def fixed(fn):
            return fn
    else:
        def at(fn):
            return fn

        fixed = at
    block = pl.BlockSpec((tb, cols, depth), at(lambda i: (i, 0, 0)))
    lo_spec = pl.BlockSpec((4, cols, depth), at(lambda i: (jnp.maximum(2 * i - 1, 0), 0, 0)))
    hi_spec = pl.BlockSpec((4, cols, depth), at(lambda i: (jnp.minimum(2 * i + 2, nq - 1), 0, 0)))
    whole4 = pl.BlockSpec((4, cols, depth), fixed(lambda i: (0, 0, 0)))
    yspec = pl.BlockSpec((tb, 8, depth), at(lambda i: (i, 0, 0)))
    col1 = pl.BlockSpec((tb, cols, 1), at(lambda i: (i, 0, 0)))
    slab = pl.BlockSpec((tb, cols, depth), fixed(lambda i: (0, 0, 0)))
    smem = pl.BlockSpec(memory_space=pltpu.SMEM)
    any_spec = pl.BlockSpec(memory_space=pl.ANY)
    field = jax.ShapeDtypeStruct((rows, cols, depth), jnp.float32)
    picked = jax.ShapeDtypeStruct((rows, cols, 1), jnp.float32)
    spec_of = {S.src: smem, S.amp: smem, S.rec: col1, S.mis: col1, S.obs: col1, S.pick: col1, S.vslab: slab, S.mom: slab, S.mass: slab}

    names = [S.f, S.flo, S.fhi, S.xlo, S.xhi, S.ylo, S.yhi, S.prev, S.vel]
    in_specs = [block, lo_spec, hi_spec, whole4, whole4, yspec, yspec, block, block]
    args = [f, f, f, xlo, xhi, ylo, yhi, prev, vel]
    for key, value in extra.items():
        names.append(key)
        in_specs.append(spec_of.get(key, block))
        args.append(value)
    nf_ex = len(exchanged)
    for j, g in enumerate(exchanged):
        names.append(S.ex_f + j)
        in_specs.append(any_spec)
        args.append(g)

    outs = {
        "wave1": [(S.o_f, field, block), (S.o_dw, field, block), (S.o_pick, picked, col1)],
        "wave2": [(S.o_dw, field, block), (S.o_pick, picked, col1), (S.o_a2, field, block), (S.o_part, field, block)],
        "adjbulk": [(S.o_f, field, block)],
        "adj2": [(S.o_v, jax.ShapeDtypeStruct((tb, cols, depth), jnp.float32), slab)],
    }[kind]
    names += [o[0] for o in outs]
    out_shape = [o[1] for o in outs]
    out_specs = [o[2] for o in outs]
    scratch = [pltpu.VMEM((tb + 8, cols + 16, depth), jnp.float32)]
    names.append(S.pad)
    if kind in ("wave1", "wave2"):
        scratch.append(pltpu.VMEM((tb * cols, 128), jnp.float32))
        names.append(S.fold)
    if kind == "adj2":
        names += [S.slot_out, S.slot_in, S.rs_ss, S.rs_rs, S.rs_own, S.rl_top, S.rl_bot, S.rl_rs]
        scratch += [
            pltpu.VMEM((nblk, tb, cols, depth), jnp.float32),
            pltpu.VMEM((nblk, tb, cols, depth), jnp.float32),
            pltpu.SemaphoreType.DMA((6,)),
            pltpu.SemaphoreType.DMA((nblk,)),
            pltpu.SemaphoreType.DMA(()),
            pltpu.VMEM((tb // 2, cols, depth), jnp.float32),
            pltpu.VMEM((tb // 2, cols, depth), jnp.float32),
            pltpu.SemaphoreType.DMA((4,)),
        ]
        params = pltpu.CompilerParams(
            collective_id=collective_id, has_side_effects=True, vmem_limit_bytes=60 * 1024 * 1024
        )
    elif kind == "wave2":
        h_shapes, _ = exchange_io(1, rows, cols, depth)
        names = names[: len(names) - len(scratch)]
        names += [S.h_b + m for m in range(4)]
        names += [S.pad, S.fold]
        names += [S.stg_xlo, S.stg_xhi, S.stg_ylo, S.stg_yhi, S.h_zx, S.h_zy, S.h_ss, S.h_rs, S.h_zs]
        out_shape += h_shapes
        out_specs += [any_spec] * 4
        scratch += [
            pltpu.VMEM((4, cols, depth), jnp.float32),
            pltpu.VMEM((4, cols, depth), jnp.float32),
            pltpu.VMEM((rows, 4, depth), jnp.float32),
            pltpu.VMEM((rows, 4, depth), jnp.float32),
            pltpu.VMEM((4, cols, depth), jnp.float32),
            pltpu.VMEM((rows, 8, depth), jnp.float32),
            pltpu.SemaphoreType.DMA((rows // tb, 4)),
            pltpu.SemaphoreType.DMA((4,)),
            pltpu.SemaphoreType.DMA((4,)),
        ]
        params = pltpu.CompilerParams(
            collective_id=collective_id, has_side_effects=True, vmem_limit_bytes=60 * 1024 * 1024
        )
    elif nf_ex:
        ex_shapes, ex_scratch = exchange_io(nf_ex, rows, cols, depth)
        k = len(outs)
        names = names[: len(names) - len(scratch)]
        names += [S.ex_b + m for m in range(4 * nf_ex)]
        names += [S.pad, S.fold][: len(scratch)]
        names += [S.ex_zx, S.ex_zy, S.ex_ss, S.ex_rs, S.ex_zs]
        out_shape += ex_shapes
        out_specs += [any_spec] * len(ex_shapes)
        scratch += ex_scratch
        params = pltpu.CompilerParams(
            collective_id=collective_id, has_side_effects=True, vmem_limit_bytes=60 * 1024 * 1024
        )
    else:
        params = pltpu.CompilerParams(vmem_limit_bytes=60 * 1024 * 1024)
    n_big = sum(1 for sp in in_specs if sp is block) + 1 + sum(1 for sp in out_specs if sp is block)
    cost = pl.CostEstimate(
        flops=60 * rows * cols * depth,
        transcendentals=0,
        bytes_accessed=4 * rows * cols * depth * n_big,
    )
    result = pl.pallas_call(
        functools.partial(step_kernel, kind, tuple(names), nf_ex),
        grid=grid,
        in_specs=in_specs,
        out_specs=out_specs,
        out_shape=out_shape,
        scratch_shapes=scratch,
        compiler_params=params,
        cost_estimate=cost,
        name=f"leap_{kind}",
    )(*args)
    if kind == "wave2":
        return result[: len(outs)], result[len(outs) :]
    if nf_ex:
        own = result[: len(outs)]
        ex = result[len(outs) :]
        return own, [ex[4 * j : 4 * j + 4] for j in range(nf_ex)]
    return result


def on_device(
    velocity,
    momentum,
    mass_diag,
    u_prev,
    u_cur,
    adj_next,
    adj_cur,
    observed,
    rec_depth,
    src_cell,
    wavelet,
):
    full_velocity = lax.all_gather(velocity, "shot", axis=0, tiled=True)
    row_count, col_count, depth_cells = full_velocity.shape
    oldest = u_prev[0]
    present = u_cur[0]
    adj_later = adj_next[0]
    adj_now = adj_cur[0]
    rec = rec_depth[0][:, :, None]
    cell = src_cell[0]
    src = jnp.stack(
        [
            cell[0] - lax.axis_index("row") * row_count,
            cell[1] - lax.axis_index("col") * col_count,
            cell[2],
        ]
    ).astype(jnp.int32)
    amp = wavelet[0]

    wave_h, adj_h = exchange([present, adj_now], 1)
    advanced, dw1, pick_adv = leap(
        "wave1", present, *wave_h, oldest, full_velocity, {S.rec: rec, S.src: src, S.amp: amp[0:1]}
    )
    (adj_bulk,), (adv_h,) = leap(
        "adjbulk", adj_now, *adj_h, adj_later, full_velocity, {}, exchanged=[advanced], collective_id=2
    )
    (dw2, pick_far, adj_two, part), adj_two_h = leap(
        "wave2",
        advanced,
        *adv_h,
        present,
        full_velocity,
        {S.rec: rec, S.src: src, S.amp: amp[1:2], S.a2raw: adj_bulk, S.obs: observed[0, 1][:, :, None]},
        collective_id=3,
    )
    (summed,) = leap(
        "adj2",
        adj_two,
        *adj_two_h,
        adj_now,
        full_velocity,
        {
            S.rec: rec,
            S.pick: pick_adv,
            S.obs: observed[0, 0][:, :, None],
            S.dw: dw1,
            S.part: part,
        },
        collective_id=0,
    )
    gradient = 2.0 / velocity * summed
    p_half = momentum - 0.5 * leap_step * gradient
    v_new = velocity + leap_step * p_half / mass_diag
    return (v_new, p_half)


def solution(mesh):
    return jax.shard_map(
        on_device,
        mesh=mesh,
        in_specs=(
            P(("row", "shot"), "col", None),
            P(("row", "shot"), "col", None),
            P(("row", "shot"), "col", None),
            P("shot", "row", "col", None),
            P("shot", "row", "col", None),
            P("shot", "row", "col", None),
            P("shot", "row", "col", None),
            P("shot", None, "row", "col"),
            P("shot", "row", "col"),
            P("shot", None),
            P("shot", None),
        ),
        out_specs=(P(("row", "shot"), "col", None), P(("row", "shot"), "col", None)),
        check_vma=False,
    )
```

```python
import functools

import jax
import jax.numpy as jnp
from jax import lax
from jax.experimental import pallas as pl
from jax.experimental.pallas import tpu as pltpu
from jax.sharding import PartitionSpec as P

STENCIL = (-205.0 / 72.0, 8.0 / 5.0, -1.0 / 5.0, 8.0 / 315.0, -1.0 / 560.0)
squared_courant = 0.012
leap_step = 0.2

class S:
    a2raw = 0
    amp = 1
    dw = 2
    ex_rs = 3
    ex_ss = 4
    ex_zs = 5
    ex_zx = 6
    ex_zy = 7
    f = 8
    fhi = 9
    flo = 10
    fold = 11
    h_rs = 12
    h_ss = 13
    h_zs = 14
    h_zx = 15
    h_zy = 16
    mass = 17
    mis = 18
    mom = 19
    o_a2 = 20
    o_dw = 21
    o_f = 22
    o_p = 23
    o_part = 24
    o_pick = 25
    o_v = 26
    obs = 27
    pad = 28
    part = 29
    prev = 30
    rec = 31
    rs_own = 32
    rs_rs = 33
    rs_ss = 34
    slot_in = 35
    slot_out = 36
    src = 37
    stg_xhi = 38
    stg_xlo = 39
    stg_yhi = 40
    stg_ylo = 41
    vel = 42
    vslab = 43
    xhi = 44
    xlo = 45
    yhi = 46
    ylo = 47
    rl_top = 90
    rl_bot = 91
    rl_rs = 92
    ex_f = 100
    ex_b = 110
    h_b = 130
    pick = 140


ROWS_PER_STEP = 8
Y_CHUNK = 8


class Exchange:

    def __init__(self, fields, bufs, zero_x, zero_y, send_sem, recv_sem, zero_sem):
        self.fields, self.bufs = fields, bufs
        self.zero_x, self.zero_y = zero_x, zero_y
        self.send_sem, self.recv_sem, self.zero_sem = send_sem, recv_sem, zero_sem
        row, nrow = lax.axis_index("row"), lax.axis_size("row")
        col, ncol = lax.axis_index("col"), lax.axis_size("col")
        self.row, self.nrow, self.col, self.ncol = row, nrow, col, ncol
        self.has = (row < nrow - 1, row > 0, col < ncol - 1, col > 0)
        self.peer = ({"row": row + 1}, {"row": row - 1}, {"col": col + 1}, {"col": col - 1})
        self.filler = (1, 0, 3, 2)

    def source(self, f, d):
        rows, cols, _ = f.shape
        if d == 0:
            return f.at[pl.ds(rows - 4, 4)]
        if d == 1:
            return f.at[pl.ds(0, 4)]
        if d == 2:
            return f.at[:, pl.ds(cols - 4, 4)]
        return f.at[:, pl.ds(0, 4)]

    def target(self, j, b):
        if b == 2:
            return self.bufs[4 * j + b].at[:, pl.ds(4, 4)]
        if b == 3:
            return self.bufs[4 * j + b].at[:, pl.ds(0, 4)]
        return self.bufs[4 * j + b]

    def remote(self, j, d):
        return pltpu.make_async_remote_copy(
            src_ref=self.source(self.fields[j], d),
            dst_ref=self.target(j, d),
            send_sem=self.send_sem.at[j, d],
            recv_sem=self.recv_sem.at[j, d],
            device_id=self.peer[d],
            device_id_type=pl.DeviceIdType.MESH,
        )

    def start(self):
        has, row, nrow, col, ncol = self.has, self.row, self.nrow, self.col, self.ncol
        barrier = pltpu.get_barrier_semaphore()
        for d in range(4):
            @pl.when(has[d])
            def _():
                pl.semaphore_signal(barrier, inc=1, device_id=self.peer[d], device_id_type=pl.DeviceIdType.MESH)

        count = (1 - row // (nrow - 1)) + (row + nrow - 1) // nrow + (1 - col // (ncol - 1)) + (col + ncol - 1) // ncol
        pl.semaphore_wait(barrier, count)

        for j in range(len(self.fields)):
            for d in range(4):
                @pl.when(has[d])
                def _():
                    self.remote(j, d).start()

        @pl.when(jnp.logical_not(has[0] & has[1]))
        def _():
            self.zero_x[...] = jnp.zeros_like(self.zero_x)

        @pl.when(jnp.logical_not(has[2] & has[3]))
        def _():
            self.zero_y[...] = jnp.zeros_like(self.zero_y)

        for j in range(len(self.fields)):
            for b in range(4):
                @pl.when(jnp.logical_not(has[self.filler[b]]))
                def _():
                    zero = self.zero_x if b < 2 else self.zero_y
                    copy = pltpu.make_async_copy(zero, self.bufs[4 * j + b], self.zero_sem.at[j, b])
                    copy.start()
                    copy.wait()

    def finish(self):
        has = self.has
        for j in range(len(self.fields)):
            for d in range(4):
                @pl.when(has[d])
                def _():
                    self.remote(j, d).wait_send()
            for b in range(4):
                @pl.when(has[self.filler[b]])
                def _():
                    self.remote(j, b).wait_recv()


def exchange_io(nf, rows, cols, depth):
    shapes = []
    for _ in range(nf):
        shapes += [
            jax.ShapeDtypeStruct((4, cols, depth), jnp.float32),
            jax.ShapeDtypeStruct((4, cols, depth), jnp.float32),
            jax.ShapeDtypeStruct((rows, 8, depth), jnp.float32),
            jax.ShapeDtypeStruct((rows, 8, depth), jnp.float32),
        ]
    scratch = [
        pltpu.VMEM((4, cols, depth), jnp.float32),
        pltpu.VMEM((rows, 8, depth), jnp.float32),
        pltpu.SemaphoreType.DMA((nf, 4)),
        pltpu.SemaphoreType.DMA((nf, 4)),
        pltpu.SemaphoreType.DMA((nf, 4)),
    ]
    return shapes, scratch


def exchange_kernel(nf, *refs):
    ex = Exchange(refs[:nf], refs[nf : 5 * nf], *refs[5 * nf :])
    ex.start()
    ex.finish()


def exchange(fields, collective_id):
    nf = len(fields)
    rows, cols, depth = fields[0].shape
    any_spec = pl.BlockSpec(memory_space=pl.ANY)
    shapes, scratch = exchange_io(nf, rows, cols, depth)
    outs = pl.pallas_call(
        functools.partial(exchange_kernel, nf),
        in_specs=[any_spec] * nf,
        out_specs=[any_spec] * (4 * nf),
        out_shape=shapes,
        scratch_shapes=scratch,
        compiler_params=pltpu.CompilerParams(collective_id=collective_id, has_side_effects=True),
        name=f"halo_exchange_{collective_id}",
    )(*fields)
    return [outs[4 * j : 4 * j + 4] for j in range(nf)]


class HaloSender:

    def __init__(self, ref, nblk, tb):
        self.ref, self.nblk, self.tb = ref, nblk, tb
        row, nrow = lax.axis_index("row"), lax.axis_size("row")
        col, ncol = lax.axis_index("col"), lax.axis_size("col")
        self.row, self.nrow, self.col, self.ncol = row, nrow, col, ncol
        self.has = (row < nrow - 1, row > 0, col < ncol - 1, col > 0)
        self.peer = ({"row": row + 1}, {"row": row - 1}, {"col": col + 1}, {"col": col - 1})
        self.filler = (1, 0, 3, 2)
        self.bufs = [ref[S.h_b + b] for b in range(4)]

    def copy(self, d, blk):
        ref, tb = self.ref, self.tb
        rows_here = pl.ds(pl.multiple_of(blk * tb, tb), tb)
        if d == 0:
            src, dst, sem = ref[S.stg_xlo], self.bufs[0], ref[S.h_ss].at[0, 0]
        elif d == 1:
            src, dst, sem = ref[S.stg_xhi], self.bufs[1], ref[S.h_ss].at[0, 1]
        elif d == 2:
            src, dst = ref[S.stg_ylo].at[rows_here], self.bufs[2].at[rows_here, pl.ds(4, 4)]
            sem = ref[S.h_ss].at[blk, 2]
        else:
            src, dst = ref[S.stg_yhi].at[rows_here], self.bufs[3].at[rows_here, pl.ds(0, 4)]
            sem = ref[S.h_ss].at[blk, 3]
        return pltpu.make_async_remote_copy(
            src_ref=src,
            dst_ref=dst,
            send_sem=sem,
            recv_sem=ref[S.h_rs].at[d],
            device_id=self.peer[d],
            device_id_type=pl.DeviceIdType.MESH,
        )

    def whole(self, b):
        ref = self.ref
        src = {0: ref[S.stg_xlo], 1: ref[S.stg_xhi], 2: ref[S.stg_ylo], 3: ref[S.stg_yhi]}[b]
        dst = {0: self.bufs[0], 1: self.bufs[1], 2: self.bufs[2].at[:, pl.ds(4, 4)], 3: self.bufs[3].at[:, pl.ds(0, 4)]}[b]
        return pltpu.make_async_remote_copy(
            src_ref=src,
            dst_ref=dst,
            send_sem=ref[S.h_ss].at[0, b],
            recv_sem=ref[S.h_rs].at[b],
            device_id=self.peer[b],
            device_id_type=pl.DeviceIdType.MESH,
        )

    def begin(self):
        ref, has, row, nrow, col, ncol = self.ref, self.has, self.row, self.nrow, self.col, self.ncol
        barrier = pltpu.get_barrier_semaphore()
        for d in range(4):
            @pl.when(has[d])
            def _():
                pl.semaphore_signal(barrier, inc=1, device_id=self.peer[d], device_id_type=pl.DeviceIdType.MESH)

        count = (1 - row // (nrow - 1)) + (row + nrow - 1) // nrow + (1 - col // (ncol - 1)) + (col + ncol - 1) // ncol
        pl.semaphore_wait(barrier, count)

        @pl.when(jnp.logical_not(has[0] & has[1]))
        def _():
            ref[S.h_zx][...] = jnp.zeros_like(ref[S.h_zx])

        @pl.when(jnp.logical_not(has[2] & has[3]))
        def _():
            ref[S.h_zy][...] = jnp.zeros_like(ref[S.h_zy])

        for b in range(4):
            @pl.when(jnp.logical_not(has[self.filler[b]]))
            def _():
                zero = ref[S.h_zx] if b < 2 else ref[S.h_zy]
                copy = pltpu.make_async_copy(zero, self.bufs[b], ref[S.h_zs].at[b])
                copy.start()
                copy.wait()

    def send_block(self, blk):
        ref, has, tb = self.ref, self.has, self.tb

        @pl.when(blk == 0)
        def _():
            ref[S.stg_xhi][...] = ref[S.o_a2][0:4]

        @pl.when(blk == self.nblk - 1)
        def _():
            ref[S.stg_xlo][...] = ref[S.o_a2][tb - 4 : tb]

        for d in (2, 3):
            @pl.when(has[d])
            def _():
                self.copy(d, blk).start()

        @pl.when(has[1] & (blk == 0))
        def _():
            self.copy(1, blk).start()

        @pl.when(has[0] & (blk == self.nblk - 1))
        def _():
            self.copy(0, blk).start()

    def finish(self):
        has = self.has
        for blk in range(self.nblk):
            for d in (2, 3):
                @pl.when(has[d])
                def _():
                    self.copy(d, blk).wait_send()

        @pl.when(has[1])
        def _():
            self.copy(1, 0).wait_send()

        @pl.when(has[0])
        def _():
            self.copy(0, self.nblk - 1).wait_send()

        for b in range(4):
            @pl.when(has[self.filler[b]])
            def _():
                self.whole(b).wait_recv()


class ReduceScatter:

    def __init__(self, ref, me, n):
        self.ref, self.me, self.n = ref, me, n
        self.up, self.down, self.far = lax.rem(me + 1, n), lax.rem(me + n - 1, n), lax.rem(me + 2, n)
        half = ref[S.slot_out].shape[1] // 2
        self.top, self.bot = pl.ds(0, half), pl.ds(half, half)

    def remote(self, src, dst, k, recv_sem, peer):
        return pltpu.make_async_remote_copy(
            src_ref=src,
            dst_ref=dst,
            send_sem=self.ref[S.rs_ss].at[k],
            recv_sem=recv_sem,
            device_id={"shot": peer},
            device_id_type=pl.DeviceIdType.MESH,
        )

    def direct(self, blk, k, peer):
        ref = self.ref
        return self.remote(ref[S.slot_out].at[blk], ref[S.slot_in].at[self.me], k, ref[S.rs_rs].at[self.me], peer)

    def relay_top(self):
        ref = self.ref
        src = ref[S.slot_out].at[self.far, self.top]
        return self.remote(src, ref[S.rl_top], 2, ref[S.rl_rs].at[0], self.up)

    def relay_bot(self):
        ref = self.ref
        src = ref[S.slot_out].at[self.far, self.bot]
        return self.remote(src, ref[S.rl_bot], 3, ref[S.rl_rs].at[1], self.down)

    def fwd_top(self):
        ref = self.ref
        dst = ref[S.slot_in].at[self.down, self.top]
        return self.remote(ref[S.rl_top], dst, 4, ref[S.rl_rs].at[2], self.up)

    def fwd_bot(self):
        ref = self.ref
        dst = ref[S.slot_in].at[self.up, self.bot]
        return self.remote(ref[S.rl_bot], dst, 5, ref[S.rl_rs].at[3], self.down)

    def begin(self):
        barrier = pltpu.get_barrier_semaphore()
        for peer in (self.up, self.down):
            pl.semaphore_signal(barrier, inc=1, device_id={"shot": peer}, device_id_type=pl.DeviceIdType.MESH)
        pl.semaphore_wait(barrier, 2)

    def at_step(self, step):
        @pl.when(step == 1)
        def _():
            self.direct(self.up, 0, self.up).start()

        @pl.when(step == 2)
        def _():
            self.relay_top().start()
            self.relay_bot().start()

        @pl.when(step == 3)
        def _():
            self.direct(self.down, 1, self.down).start()
            self.relay_top().wait_recv()
            self.relay_bot().wait_recv()
            self.fwd_top().start()
            self.fwd_bot().start()

    def finish(self):
        ref, me, n = self.ref, self.me, self.n
        own = pltpu.make_async_copy(ref[S.slot_out].at[me], ref[S.slot_in].at[me], ref[S.rs_own])
        own.start()
        self.direct(self.up, 0, self.up).wait_send()
        self.direct(self.down, 1, self.down).wait_send()
        self.relay_top().wait_send()
        self.relay_bot().wait_send()
        self.fwd_top().wait_send()
        self.fwd_bot().wait_send()
        own.wait()
        for src in (self.down, self.up):
            self.remote(ref[S.slot_out].at[src], ref[S.slot_in].at[src], 0, ref[S.rs_rs].at[src], src).wait_recv()
        far_in = ref[S.slot_in].at[self.far, self.top]
        self.remote(ref[S.rl_top], far_in, 4, ref[S.rl_rs].at[2], self.down).wait_recv()
        far_in = ref[S.slot_in].at[self.far, self.bot]
        self.remote(ref[S.rl_bot], far_in, 5, ref[S.rl_rs].at[3], self.up).wait_recv()

        slot_in = ref[S.slot_in]

        def row(r, carry):
            summed = slot_in[0, r]
            for s_ in range(1, n):
                summed = summed + slot_in[s_, r]
            ref[S.o_v][r] = summed
            return carry

        lax.fori_loop(0, slot_in.shape[1], row, 0)


def step_kernel(kind, names, nf_ex, *refs):
    ref = dict(zip(names, refs))
    if nf_ex:
        ex = Exchange(
            [ref[S.ex_f + j] for j in range(nf_ex)],
            [ref[S.ex_b + k] for k in range(4 * nf_ex)],
            *[ref[k] for k in (S.ex_zx, S.ex_zy, S.ex_ss, S.ex_rs, S.ex_zs)],
        )
    f_ref, pad = ref[S.f], ref[S.pad]
    tb, cols, depth = f_ref.shape
    n = pl.num_programs(0)
    step = pl.program_id(0)
    if kind == "adj2":
        me = lax.axis_index("shot")
        i = lax.rem(me + 1 + step, n)
        rs = ReduceScatter(ref, me, n)

        @pl.when(step == 0)
        def _():
            rs.begin()

        rs.at_step(step)
    elif kind == "wave2":
        i = lax.rem(step + n - 1, n)
    else:
        i = step

    if nf_ex:
        @pl.when(i == 0)
        def _():
            ex.start()

    lo = jnp.where(i == 0, ref[S.xlo][...], ref[S.flo][...])
    hi = jnp.where(i == n - 1, ref[S.xhi][...], ref[S.fhi][...])
    pad[0:4, 8 : 8 + cols, :] = lo
    pad[4 : 4 + tb, 8 : 8 + cols, :] = f_ref[...]
    pad[4 + tb : 8 + tb, 8 : 8 + cols, :] = hi
    pad[4 : 4 + tb, 0:8, :] = ref[S.ylo][...]
    pad[4 : 4 + tb, 8 + cols : 16 + cols, :] = ref[S.yhi][...]

    z_index = lax.broadcasted_iota(jnp.int32, (Y_CHUNK, depth), 1)
    y_index = lax.broadcasted_iota(jnp.int32, (Y_CHUNK, depth), 0)
    wave = kind in ("wave1", "wave2")
    if wave:
        src_ref = ref[S.src]
        src_x = src_ref[0] - lax.axis_index("row") * (tb * n) - i * tb
        src_y = src_ref[1] - lax.axis_index("col") * cols
        src_z = src_ref[2]
        amp = ref[S.amp][0 if kind == "wave1" else 1]

    def row(r, carry):
        for y0 in range(0, cols, Y_CHUNK):
            ys = pl.ds(y0, Y_CHUNK)
            pys = pl.ds(8 + y0, Y_CHUNK)
            c = pad[4 + r, pys, :]
            result = (3.0 * STENCIL[0]) * c
            for k in range(1, 5):
                along = pad[4 + r + k, pys, :] + pad[4 + r - k, pys, :]
                along = along + (
                    pad[4 + r, pl.ds(8 + y0 + k, Y_CHUNK), :]
                    + pad[4 + r, pl.ds(8 + y0 - k, Y_CHUNK), :]
                )
                zp = jnp.where(z_index < depth - k, pltpu.roll(c, depth - k, 1), 0.0)
                zm = jnp.where(z_index >= k, pltpu.roll(c, k, 1), 0.0)
                along = along + (zp + zm)
                result = result + STENCIL[k] * along
            v = ref[S.vel][r, ys, :]
            stiff = squared_courant * v * v
            prev = ref[S.prev][r, ys, :]
            out = 2.0 * c - prev + stiff * result
            if wave:
                at_rec = z_index == ref[S.rec][r, ys, :]
                hit = (r == src_x) & (y_index + y0 == src_y) & (z_index == src_z)
                out = out + jnp.where(hit, amp, 0.0)
                sel = jnp.where(at_rec, out, 0.0)
                folded = sel[:, 0:128]
                for t in range(128, depth, 128):
                    folded = folded + sel[:, t : t + 128]
                ref[S.fold][pl.ds(pl.multiple_of(r * cols + y0, Y_CHUNK), Y_CHUNK), :] = folded
                ref[S.o_dw][r, ys, :] = (out - 2.0 * c) + prev
                if kind == "wave1":
                    ref[S.o_f][r, ys, :] = out
            elif kind == "adjbulk":
                ref[S.o_f][r, ys, :] = out
            else:
                at_rec = z_index == ref[S.rec][r, ys, :]
                misfit = ref[S.pick][r, ys, :] - ref[S.obs][r, ys, :]
                out = out + jnp.where(at_rec, misfit, 0.0)
                ref[S.slot_out][i, r, ys, :] = ref[S.part][r, ys, :] + out * ref[S.dw][r, ys, :]
        return carry

    lax.fori_loop(0, tb, row, 0)
    if wave:
        ref[S.o_pick][...] = jnp.sum(ref[S.fold][...], axis=1, keepdims=True).reshape(ref[S.o_pick].shape)
    if kind == "wave2":
        sender = HaloSender(ref, n, tb)

        @pl.when(step == 0)
        def _():
            sender.begin()

        def inject(r, carry):
            for y0 in range(0, cols, Y_CHUNK):
                ys = pl.ds(y0, Y_CHUNK)
                at_rec = z_index == ref[S.rec][r, ys, :]
                misfit = ref[S.o_pick][r, ys, :] - ref[S.obs][r, ys, :]
                a2 = ref[S.a2raw][r, ys, :] + jnp.where(at_rec, misfit, 0.0)
                ref[S.o_a2][r, ys, :] = a2
                ref[S.o_part][r, ys, :] = a2 * ref[S.o_dw][r, ys, :]
                if y0 == 0:
                    ref[S.stg_yhi][i * tb + r] = a2[0:4]
                if y0 == cols - Y_CHUNK:
                    ref[S.stg_ylo][i * tb + r] = a2[Y_CHUNK - 4 : Y_CHUNK]
            return carry

        lax.fori_loop(0, tb, inject, 0)
        sender.send_block(i)

        @pl.when(step == n - 1)
        def _():
            sender.finish()

    if nf_ex:
        @pl.when(i == n - 1)
        def _():
            ex.finish()
    if kind == "adj2":
        @pl.when(step == n - 1)
        def _():
            rs.finish()


def leap(kind, f, xlo, xhi, ylo, yhi, prev, vel, extra, exchanged=(), collective_id=None):
    rows, cols, depth = f.shape
    tb = ROWS_PER_STEP
    nblk = rows // tb
    grid = (nblk,)
    nq = rows // 4
    if kind == "adj2":
        def at(fn):
            return lambda i: fn(lax.rem(lax.axis_index("shot") + 1 + i, nblk))

        fixed = at
    elif kind == "wave2":
        def at(fn):
            return lambda i: fn(lax.rem(i + nblk - 1, nblk))

        def fixed(fn):
            return fn
    else:
        def at(fn):
            return fn

        fixed = at
    block = pl.BlockSpec((tb, cols, depth), at(lambda i: (i, 0, 0)))
    lo_spec = pl.BlockSpec((4, cols, depth), at(lambda i: (jnp.maximum(2 * i - 1, 0), 0, 0)))
    hi_spec = pl.BlockSpec((4, cols, depth), at(lambda i: (jnp.minimum(2 * i + 2, nq - 1), 0, 0)))
    whole4 = pl.BlockSpec((4, cols, depth), fixed(lambda i: (0, 0, 0)))
    yspec = pl.BlockSpec((tb, 8, depth), at(lambda i: (i, 0, 0)))
    col1 = pl.BlockSpec((tb, cols, 1), at(lambda i: (i, 0, 0)))
    slab = pl.BlockSpec((tb, cols, depth), fixed(lambda i: (0, 0, 0)))
    smem = pl.BlockSpec(memory_space=pltpu.SMEM)
    any_spec = pl.BlockSpec(memory_space=pl.ANY)
    field = jax.ShapeDtypeStruct((rows, cols, depth), jnp.float32)
    picked = jax.ShapeDtypeStruct((rows, cols, 1), jnp.float32)
    spec_of = {S.src: smem, S.amp: smem, S.rec: col1, S.mis: col1, S.obs: col1, S.pick: col1, S.vslab: slab, S.mom: slab, S.mass: slab}

    names = [S.f, S.flo, S.fhi, S.xlo, S.xhi, S.ylo, S.yhi, S.prev, S.vel]
    in_specs = [block, lo_spec, hi_spec, whole4, whole4, yspec, yspec, block, block]
    args = [f, f, f, xlo, xhi, ylo, yhi, prev, vel]
    for key, value in extra.items():
        names.append(key)
        in_specs.append(spec_of.get(key, block))
        args.append(value)
    nf_ex = len(exchanged)
    for j, g in enumerate(exchanged):
        names.append(S.ex_f + j)
        in_specs.append(any_spec)
        args.append(g)

    outs = {
        "wave1": [(S.o_f, field, block), (S.o_dw, field, block), (S.o_pick, picked, col1)],
        "wave2": [(S.o_dw, field, block), (S.o_pick, picked, col1), (S.o_a2, field, block), (S.o_part, field, block)],
        "adjbulk": [(S.o_f, field, block)],
        "adj2": [(S.o_v, jax.ShapeDtypeStruct((tb, cols, depth), jnp.float32), slab)],
    }[kind]
    names += [o[0] for o in outs]
    out_shape = [o[1] for o in outs]
    out_specs = [o[2] for o in outs]
    scratch = [pltpu.VMEM((tb + 8, cols + 16, depth), jnp.float32)]
    names.append(S.pad)
    if kind in ("wave1", "wave2"):
        scratch.append(pltpu.VMEM((tb * cols, 128), jnp.float32))
        names.append(S.fold)
    if kind == "adj2":
        names += [S.slot_out, S.slot_in, S.rs_ss, S.rs_rs, S.rs_own, S.rl_top, S.rl_bot, S.rl_rs]
        scratch += [
            pltpu.VMEM((nblk, tb, cols, depth), jnp.float32),
            pltpu.VMEM((nblk, tb, cols, depth), jnp.float32),
            pltpu.SemaphoreType.DMA((6,)),
            pltpu.SemaphoreType.DMA((nblk,)),
            pltpu.SemaphoreType.DMA(()),
            pltpu.VMEM((tb // 2, cols, depth), jnp.float32),
            pltpu.VMEM((tb // 2, cols, depth), jnp.float32),
            pltpu.SemaphoreType.DMA((4,)),
        ]
        params = pltpu.CompilerParams(
            collective_id=collective_id, has_side_effects=True, vmem_limit_bytes=60 * 1024 * 1024
        )
    elif kind == "wave2":
        h_shapes, _ = exchange_io(1, rows, cols, depth)
        names = names[: len(names) - len(scratch)]
        names += [S.h_b + m for m in range(4)]
        names += [S.pad, S.fold]
        names += [S.stg_xlo, S.stg_xhi, S.stg_ylo, S.stg_yhi, S.h_zx, S.h_zy, S.h_ss, S.h_rs, S.h_zs]
        out_shape += h_shapes
        out_specs += [any_spec] * 4
        scratch += [
            pltpu.VMEM((4, cols, depth), jnp.float32),
            pltpu.VMEM((4, cols, depth), jnp.float32),
            pltpu.VMEM((rows, 4, depth), jnp.float32),
            pltpu.VMEM((rows, 4, depth), jnp.float32),
            pltpu.VMEM((4, cols, depth), jnp.float32),
            pltpu.VMEM((rows, 8, depth), jnp.float32),
            pltpu.SemaphoreType.DMA((rows // tb, 4)),
            pltpu.SemaphoreType.DMA((4,)),
            pltpu.SemaphoreType.DMA((4,)),
        ]
        params = pltpu.CompilerParams(
            collective_id=collective_id, has_side_effects=True, vmem_limit_bytes=60 * 1024 * 1024
        )
    elif nf_ex:
        ex_shapes, ex_scratch = exchange_io(nf_ex, rows, cols, depth)
        k = len(outs)
        names = names[: len(names) - len(scratch)]
        names += [S.ex_b + m for m in range(4 * nf_ex)]
        names += [S.pad, S.fold][: len(scratch)]
        names += [S.ex_zx, S.ex_zy, S.ex_ss, S.ex_rs, S.ex_zs]
        out_shape += ex_shapes
        out_specs += [any_spec] * len(ex_shapes)
        scratch += ex_scratch
        params = pltpu.CompilerParams(
            collective_id=collective_id, has_side_effects=True, vmem_limit_bytes=60 * 1024 * 1024
        )
    else:
        params = pltpu.CompilerParams(vmem_limit_bytes=60 * 1024 * 1024)
    n_big = sum(1 for sp in in_specs if sp is block) + 1 + sum(1 for sp in out_specs if sp is block)
    cost = pl.CostEstimate(
        flops=60 * rows * cols * depth,
        transcendentals=0,
        bytes_accessed=4 * rows * cols * depth * n_big,
    )
    result = pl.pallas_call(
        functools.partial(step_kernel, kind, tuple(names), nf_ex),
        grid=grid,
        in_specs=in_specs,
        out_specs=out_specs,
        out_shape=out_shape,
        scratch_shapes=scratch,
        compiler_params=params,
        cost_estimate=cost,
        name=f"leap_{kind}",
    )(*args)
    if kind == "wave2":
        return result[: len(outs)], result[len(outs) :]
    if nf_ex:
        own = result[: len(outs)]
        ex = result[len(outs) :]
        return own, [ex[4 * j : 4 * j + 4] for j in range(nf_ex)]
    return result


def on_device(
    velocity,
    momentum,
    mass_diag,
    u_prev,
    u_cur,
    adj_next,
    adj_cur,
    observed,
    rec_depth,
    src_cell,
    wavelet,
):
    full_velocity = lax.all_gather(velocity, "shot", axis=0, tiled=True)
    row_count, col_count, depth_cells = full_velocity.shape
    oldest = u_prev[0]
    present = u_cur[0]
    adj_later = adj_next[0]
    adj_now = adj_cur[0]
    rec = rec_depth[0][:, :, None]
    cell = src_cell[0]
    src = src_cell[0]
    amp = wavelet[0]

    wave_h, adj_h = exchange([present, adj_now], 1)
    advanced, dw1, pick_adv = leap(
        "wave1", present, *wave_h, oldest, full_velocity, {S.rec: rec, S.src: src, S.amp: amp}
    )
    (adj_bulk,), (adv_h,) = leap(
        "adjbulk", adj_now, *adj_h, adj_later, full_velocity, {}, exchanged=[advanced], collective_id=2
    )
    (dw2, pick_far, adj_two, part), adj_two_h = leap(
        "wave2",
        advanced,
        *adv_h,
        present,
        full_velocity,
        {S.rec: rec, S.src: src, S.amp: amp, S.a2raw: adj_bulk, S.obs: observed[0, 1][:, :, None]},
        collective_id=3,
    )
    (summed,) = leap(
        "adj2",
        adj_two,
        *adj_two_h,
        adj_now,
        full_velocity,
        {
            S.rec: rec,
            S.pick: pick_adv,
            S.obs: observed[0, 0][:, :, None],
            S.dw: dw1,
            S.part: part,
        },
        collective_id=0,
    )
    gradient = 2.0 / velocity * summed
    p_half = momentum - 0.5 * leap_step * gradient
    v_new = velocity + leap_step * p_half / mass_diag
    return (v_new, p_half)


def solution(mesh):
    return jax.shard_map(
        on_device,
        mesh=mesh,
        in_specs=(
            P(("row", "shot"), "col", None),
            P(("row", "shot"), "col", None),
            P(("row", "shot"), "col", None),
            P("shot", "row", "col", None),
            P("shot", "row", "col", None),
            P("shot", "row", "col", None),
            P("shot", "row", "col", None),
            P("shot", None, "row", "col"),
            P("shot", "row", "col"),
            P("shot", None),
            P("shot", None),
        ),
        out_specs=(P(("row", "shot"), "col", None), P(("row", "shot"), "col", None)),
        check_vma=False,
    )
```

```python
import functools

import jax
import jax.numpy as jnp
from jax import lax
from jax.experimental import pallas as pl
from jax.experimental.pallas import tpu as pltpu
from jax.sharding import PartitionSpec as P

STENCIL = (-205.0 / 72.0, 8.0 / 5.0, -1.0 / 5.0, 8.0 / 315.0, -1.0 / 560.0)
squared_courant = 0.012
leap_step = 0.2

class S:
    a2raw = 0
    amp = 1
    dw = 2
    ex_rs = 3
    ex_ss = 4
    ex_zs = 5
    ex_zx = 6
    ex_zy = 7
    f = 8
    fhi = 9
    flo = 10
    fold = 11
    h_rs = 12
    h_ss = 13
    h_zs = 14
    h_zx = 15
    h_zy = 16
    mass = 17
    mis = 18
    mom = 19
    o_a2 = 20
    o_dw = 21
    o_f = 22
    o_p = 23
    o_part = 24
    o_pick = 25
    o_v = 26
    obs = 27
    pad = 28
    part = 29
    prev = 30
    rec = 31
    rs_own = 32
    rs_rs = 33
    rs_ss = 34
    slot_in = 35
    slot_out = 36
    src = 37
    stg_xhi = 38
    stg_xlo = 39
    stg_yhi = 40
    stg_ylo = 41
    vel = 42
    vslab = 43
    xhi = 44
    xlo = 45
    yhi = 46
    ylo = 47
    rl_top = 90
    rl_bot = 91
    rl_rs = 92
    ex_f = 100
    ex_b = 110
    h_b = 130
    pick = 140


ROWS_PER_STEP = 8
Y_CHUNK = 8


class Exchange:

    def __init__(self, fields, bufs, zero_x, zero_y, send_sem, recv_sem, zero_sem):
        self.fields, self.bufs = fields, bufs
        self.zero_x, self.zero_y = zero_x, zero_y
        self.send_sem, self.recv_sem, self.zero_sem = send_sem, recv_sem, zero_sem
        row, nrow = lax.axis_index("row"), lax.axis_size("row")
        col, ncol = lax.axis_index("col"), lax.axis_size("col")
        self.row, self.nrow, self.col, self.ncol = row, nrow, col, ncol
        self.has = (row < nrow - 1, row > 0, col < ncol - 1, col > 0)
        self.peer = ({"row": row + 1}, {"row": row - 1}, {"col": col + 1}, {"col": col - 1})
        self.filler = (1, 0, 3, 2)

    def source(self, f, d):
        rows, cols, _ = f.shape
        if d == 0:
            return f.at[pl.ds(rows - 4, 4)]
        if d == 1:
            return f.at[pl.ds(0, 4)]
        if d == 2:
            return f.at[:, pl.ds(cols - 4, 4)]
        return f.at[:, pl.ds(0, 4)]

    def target(self, j, b):
        if b == 2:
            return self.bufs[4 * j + b].at[:, pl.ds(4, 4)]
        if b == 3:
            return self.bufs[4 * j + b].at[:, pl.ds(0, 4)]
        return self.bufs[4 * j + b]

    def remote(self, j, d):
        return pltpu.make_async_remote_copy(
            src_ref=self.source(self.fields[j], d),
            dst_ref=self.target(j, d),
            send_sem=self.send_sem.at[j, d],
            recv_sem=self.recv_sem.at[j, d],
            device_id=self.peer[d],
            device_id_type=pl.DeviceIdType.MESH,
        )

    def start(self, extra=0):
        has, row, nrow, col, ncol = self.has, self.row, self.nrow, self.col, self.ncol
        barrier = pltpu.get_barrier_semaphore()
        for d in range(4):
            @pl.when(has[d])
            def _():
                pl.semaphore_signal(barrier, inc=1, device_id=self.peer[d], device_id_type=pl.DeviceIdType.MESH)

        count = (1 - row // (nrow - 1)) + (row + nrow - 1) // nrow + (1 - col // (ncol - 1)) + (col + ncol - 1) // ncol
        pl.semaphore_wait(barrier, count + extra)

        for j in range(len(self.fields)):
            for d in range(4):
                @pl.when(has[d])
                def _():
                    self.remote(j, d).start()

        @pl.when(jnp.logical_not(has[0] & has[1]))
        def _():
            self.zero_x[...] = jnp.zeros_like(self.zero_x)

        @pl.when(jnp.logical_not(has[2] & has[3]))
        def _():
            self.zero_y[...] = jnp.zeros_like(self.zero_y)

        for j in range(len(self.fields)):
            for b in range(4):
                @pl.when(jnp.logical_not(has[self.filler[b]]))
                def _():
                    zero = self.zero_x if b < 2 else self.zero_y
                    copy = pltpu.make_async_copy(zero, self.bufs[4 * j + b], self.zero_sem.at[j, b])
                    copy.start()
                    copy.wait()

    def finish(self):
        has = self.has
        for j in range(len(self.fields)):
            for d in range(4):
                @pl.when(has[d])
                def _():
                    self.remote(j, d).wait_send()
            for b in range(4):
                @pl.when(has[self.filler[b]])
                def _():
                    self.remote(j, b).wait_recv()


def exchange_io(nf, rows, cols, depth):
    shapes = []
    for _ in range(nf):
        shapes += [
            jax.ShapeDtypeStruct((4, cols, depth), jnp.float32),
            jax.ShapeDtypeStruct((4, cols, depth), jnp.float32),
            jax.ShapeDtypeStruct((rows, 8, depth), jnp.float32),
            jax.ShapeDtypeStruct((rows, 8, depth), jnp.float32),
        ]
    scratch = [
        pltpu.VMEM((4, cols, depth), jnp.float32),
        pltpu.VMEM((rows, 8, depth), jnp.float32),
        pltpu.SemaphoreType.DMA((nf, 4)),
        pltpu.SemaphoreType.DMA((nf, 4)),
        pltpu.SemaphoreType.DMA((nf, 4)),
    ]
    return shapes, scratch


def exchange_kernel(nf, gather, *refs):
    if not gather:
        ex = Exchange(refs[:nf], refs[nf : 5 * nf], *refs[5 * nf :])
        ex.start()
        ex.finish()
        return
    vel = refs[nf]
    bufs = refs[nf + 1 : 5 * nf + 1]
    full = refs[5 * nf + 1]
    ag_ss, ag_rs, ag_own = refs[-3:]
    ex = Exchange(refs[:nf], bufs, *refs[5 * nf + 2 : -3])
    me, n = lax.axis_index("shot"), lax.axis_size("shot")
    rows = vel.shape[0]
    barrier = pltpu.get_barrier_semaphore()
    for d in range(1, n):
        pl.semaphore_signal(barrier, inc=1, device_id={"shot": lax.rem(me + d, n)}, device_id_type=pl.DeviceIdType.MESH)

    def send(d):
        peer = lax.rem(me + d, n)
        return pltpu.make_async_remote_copy(
            src_ref=vel,
            dst_ref=full.at[pl.ds(pl.multiple_of(me * rows, rows), rows)],
            send_sem=ag_ss.at[d],
            recv_sem=ag_rs.at[me],
            device_id={"shot": peer},
            device_id_type=pl.DeviceIdType.MESH,
        )

    ex.start(extra=n - 1)
    for d in range(1, n):
        send(d).start()
    own = pltpu.make_async_copy(vel, full.at[pl.ds(pl.multiple_of(me * rows, rows), rows)], ag_own)
    own.start()
    ex.finish()
    for d in range(1, n):
        send(d).wait_send()
    own.wait()
    for d in range(1, n):
        src = lax.rem(me + d, n)
        pltpu.make_async_remote_copy(
            src_ref=vel,
            dst_ref=full.at[pl.ds(pl.multiple_of(src * rows, rows), rows)],
            send_sem=ag_ss.at[d],
            recv_sem=ag_rs.at[src],
            device_id={"shot": src},
            device_id_type=pl.DeviceIdType.MESH,
        ).wait_recv()


def exchange(fields, collective_id, velocity=None):
    nf = len(fields)
    rows, cols, depth = fields[0].shape
    any_spec = pl.BlockSpec(memory_space=pl.ANY)
    shapes, scratch = exchange_io(nf, rows, cols, depth)
    args = list(fields)
    gather = velocity is not None
    if gather:
        n = lax.axis_size("shot")
        args.append(velocity)
        shapes = shapes + [jax.ShapeDtypeStruct((n * velocity.shape[0],) + velocity.shape[1:], jnp.float32)]
        scratch = scratch + [pltpu.SemaphoreType.DMA((n,)), pltpu.SemaphoreType.DMA((n,)), pltpu.SemaphoreType.DMA(())]
    outs = pl.pallas_call(
        functools.partial(exchange_kernel, nf, gather),
        in_specs=[any_spec] * len(args),
        out_specs=[any_spec] * len(shapes),
        out_shape=shapes,
        scratch_shapes=scratch,
        compiler_params=pltpu.CompilerParams(collective_id=collective_id, has_side_effects=True),
        name=f"halo_exchange_{collective_id}",
    )(*args)
    halos = [outs[4 * j : 4 * j + 4] for j in range(nf)]
    if gather:
        return halos, outs[-1]
    return halos


class HaloSender:

    def __init__(self, ref, nblk, tb):
        self.ref, self.nblk, self.tb = ref, nblk, tb
        row, nrow = lax.axis_index("row"), lax.axis_size("row")
        col, ncol = lax.axis_index("col"), lax.axis_size("col")
        self.row, self.nrow, self.col, self.ncol = row, nrow, col, ncol
        self.has = (row < nrow - 1, row > 0, col < ncol - 1, col > 0)
        self.peer = ({"row": row + 1}, {"row": row - 1}, {"col": col + 1}, {"col": col - 1})
        self.filler = (1, 0, 3, 2)
        self.bufs = [ref[S.h_b + b] for b in range(4)]

    def copy(self, d, blk):
        ref, tb = self.ref, self.tb
        rows_here = pl.ds(pl.multiple_of(blk * tb, tb), tb)
        if d == 0:
            src, dst, sem = ref[S.stg_xlo], self.bufs[0], ref[S.h_ss].at[0, 0]
        elif d == 1:
            src, dst, sem = ref[S.stg_xhi], self.bufs[1], ref[S.h_ss].at[0, 1]
        elif d == 2:
            src, dst = ref[S.stg_ylo].at[rows_here], self.bufs[2].at[rows_here, pl.ds(4, 4)]
            sem = ref[S.h_ss].at[blk, 2]
        else:
            src, dst = ref[S.stg_yhi].at[rows_here], self.bufs[3].at[rows_here, pl.ds(0, 4)]
            sem = ref[S.h_ss].at[blk, 3]
        return pltpu.make_async_remote_copy(
            src_ref=src,
            dst_ref=dst,
            send_sem=sem,
            recv_sem=ref[S.h_rs].at[d],
            device_id=self.peer[d],
            device_id_type=pl.DeviceIdType.MESH,
        )

    def whole(self, b):
        ref = self.ref
        src = {0: ref[S.stg_xlo], 1: ref[S.stg_xhi], 2: ref[S.stg_ylo], 3: ref[S.stg_yhi]}[b]
        dst = {0: self.bufs[0], 1: self.bufs[1], 2: self.bufs[2].at[:, pl.ds(4, 4)], 3: self.bufs[3].at[:, pl.ds(0, 4)]}[b]
        return pltpu.make_async_remote_copy(
            src_ref=src,
            dst_ref=dst,
            send_sem=ref[S.h_ss].at[0, b],
            recv_sem=ref[S.h_rs].at[b],
            device_id=self.peer[b],
            device_id_type=pl.DeviceIdType.MESH,
        )

    def begin(self):
        ref, has, row, nrow, col, ncol = self.ref, self.has, self.row, self.nrow, self.col, self.ncol
        barrier = pltpu.get_barrier_semaphore()
        for d in range(4):
            @pl.when(has[d])
            def _():
                pl.semaphore_signal(barrier, inc=1, device_id=self.peer[d], device_id_type=pl.DeviceIdType.MESH)

        count = (1 - row // (nrow - 1)) + (row + nrow - 1) // nrow + (1 - col // (ncol - 1)) + (col + ncol - 1) // ncol
        pl.semaphore_wait(barrier, count)

        @pl.when(jnp.logical_not(has[0] & has[1]))
        def _():
            ref[S.h_zx][...] = jnp.zeros_like(ref[S.h_zx])

        @pl.when(jnp.logical_not(has[2] & has[3]))
        def _():
            ref[S.h_zy][...] = jnp.zeros_like(ref[S.h_zy])

        for b in range(4):
            @pl.when(jnp.logical_not(has[self.filler[b]]))
            def _():
                zero = ref[S.h_zx] if b < 2 else ref[S.h_zy]
                copy = pltpu.make_async_copy(zero, self.bufs[b], ref[S.h_zs].at[b])
                copy.start()
                copy.wait()

    def send_block(self, blk):
        ref, has, tb = self.ref, self.has, self.tb

        @pl.when(blk == 0)
        def _():
            ref[S.stg_xhi][...] = ref[S.o_a2][0:4]

        @pl.when(blk == self.nblk - 1)
        def _():
            ref[S.stg_xlo][...] = ref[S.o_a2][tb - 4 : tb]

        for d in (2, 3):
            @pl.when(has[d])
            def _():
                self.copy(d, blk).start()

        @pl.when(has[1] & (blk == 0))
        def _():
            self.copy(1, blk).start()

        @pl.when(has[0] & (blk == self.nblk - 1))
        def _():
            self.copy(0, blk).start()

    def finish(self):
        has = self.has
        for blk in range(self.nblk):
            for d in (2, 3):
                @pl.when(has[d])
                def _():
                    self.copy(d, blk).wait_send()

        @pl.when(has[1])
        def _():
            self.copy(1, 0).wait_send()

        @pl.when(has[0])
        def _():
            self.copy(0, self.nblk - 1).wait_send()

        for b in range(4):
            @pl.when(has[self.filler[b]])
            def _():
                self.whole(b).wait_recv()


class ReduceScatter:

    def __init__(self, ref, me, n):
        self.ref, self.me, self.n = ref, me, n
        self.up, self.down, self.far = lax.rem(me + 1, n), lax.rem(me + n - 1, n), lax.rem(me + 2, n)
        half = ref[S.slot_out].shape[1] // 2
        self.top, self.bot = pl.ds(0, half), pl.ds(half, half)

    def remote(self, src, dst, k, recv_sem, peer):
        return pltpu.make_async_remote_copy(
            src_ref=src,
            dst_ref=dst,
            send_sem=self.ref[S.rs_ss].at[k],
            recv_sem=recv_sem,
            device_id={"shot": peer},
            device_id_type=pl.DeviceIdType.MESH,
        )

    def direct(self, blk, k, peer):
        ref = self.ref
        return self.remote(ref[S.slot_out].at[blk], ref[S.slot_in].at[self.me], k, ref[S.rs_rs].at[self.me], peer)

    def relay_top(self):
        ref = self.ref
        src = ref[S.slot_out].at[self.far, self.top]
        return self.remote(src, ref[S.rl_top], 2, ref[S.rl_rs].at[0], self.up)

    def relay_bot(self):
        ref = self.ref
        src = ref[S.slot_out].at[self.far, self.bot]
        return self.remote(src, ref[S.rl_bot], 3, ref[S.rl_rs].at[1], self.down)

    def fwd_top(self):
        ref = self.ref
        dst = ref[S.slot_in].at[self.down, self.top]
        return self.remote(ref[S.rl_top], dst, 4, ref[S.rl_rs].at[2], self.up)

    def fwd_bot(self):
        ref = self.ref
        dst = ref[S.slot_in].at[self.up, self.bot]
        return self.remote(ref[S.rl_bot], dst, 5, ref[S.rl_rs].at[3], self.down)

    def begin(self):
        barrier = pltpu.get_barrier_semaphore()
        for peer in (self.up, self.down):
            pl.semaphore_signal(barrier, inc=1, device_id={"shot": peer}, device_id_type=pl.DeviceIdType.MESH)
        pl.semaphore_wait(barrier, 2)

    def at_step(self, step):
        @pl.when(step == 1)
        def _():
            self.direct(self.up, 0, self.up).start()

        @pl.when(step == 2)
        def _():
            self.relay_top().start()
            self.relay_bot().start()

        @pl.when(step == 3)
        def _():
            self.direct(self.down, 1, self.down).start()
            self.relay_top().wait_recv()
            self.relay_bot().wait_recv()
            self.fwd_top().start()
            self.fwd_bot().start()

    def finish(self):
        ref, me, n = self.ref, self.me, self.n
        own = pltpu.make_async_copy(ref[S.slot_out].at[me], ref[S.slot_in].at[me], ref[S.rs_own])
        own.start()
        self.direct(self.up, 0, self.up).wait_send()
        self.direct(self.down, 1, self.down).wait_send()
        self.relay_top().wait_send()
        self.relay_bot().wait_send()
        self.fwd_top().wait_send()
        self.fwd_bot().wait_send()
        own.wait()
        for src in (self.down, self.up):
            self.remote(ref[S.slot_out].at[src], ref[S.slot_in].at[src], 0, ref[S.rs_rs].at[src], src).wait_recv()
        far_in = ref[S.slot_in].at[self.far, self.top]
        self.remote(ref[S.rl_top], far_in, 4, ref[S.rl_rs].at[2], self.down).wait_recv()
        far_in = ref[S.slot_in].at[self.far, self.bot]
        self.remote(ref[S.rl_bot], far_in, 5, ref[S.rl_rs].at[3], self.up).wait_recv()

        slot_in = ref[S.slot_in]

        def row(r, carry):
            summed = slot_in[0, r]
            for s_ in range(1, n):
                summed = summed + slot_in[s_, r]
            ref[S.o_v][r] = summed
            return carry

        lax.fori_loop(0, slot_in.shape[1], row, 0)


def step_kernel(kind, names, nf_ex, *refs):
    ref = dict(zip(names, refs))
    if nf_ex:
        ex = Exchange(
            [ref[S.ex_f + j] for j in range(nf_ex)],
            [ref[S.ex_b + k] for k in range(4 * nf_ex)],
            *[ref[k] for k in (S.ex_zx, S.ex_zy, S.ex_ss, S.ex_rs, S.ex_zs)],
        )
    f_ref, pad = ref[S.f], ref[S.pad]
    tb, cols, depth = f_ref.shape
    n = pl.num_programs(0)
    step = pl.program_id(0)
    if kind == "adj2":
        me = lax.axis_index("shot")
        i = lax.rem(me + 1 + step, n)
        rs = ReduceScatter(ref, me, n)

        @pl.when(step == 0)
        def _():
            rs.begin()

        rs.at_step(step)
    elif kind == "wave2":
        i = lax.rem(step + n - 1, n)
    else:
        i = step

    if nf_ex:
        @pl.when(i == 0)
        def _():
            ex.start()

    lo = jnp.where(i == 0, ref[S.xlo][...], ref[S.flo][...])
    hi = jnp.where(i == n - 1, ref[S.xhi][...], ref[S.fhi][...])
    pad[0:4, 8 : 8 + cols, :] = lo
    pad[4 : 4 + tb, 8 : 8 + cols, :] = f_ref[...]
    pad[4 + tb : 8 + tb, 8 : 8 + cols, :] = hi
    pad[4 : 4 + tb, 0:8, :] = ref[S.ylo][...]
    pad[4 : 4 + tb, 8 + cols : 16 + cols, :] = ref[S.yhi][...]

    z_index = lax.broadcasted_iota(jnp.int32, (Y_CHUNK, depth), 1)
    y_index = lax.broadcasted_iota(jnp.int32, (Y_CHUNK, depth), 0)
    wave = kind in ("wave1", "wave2")
    if wave:
        src_ref = ref[S.src]
        src_x = src_ref[0] - lax.axis_index("row") * (tb * n) - i * tb
        src_y = src_ref[1] - lax.axis_index("col") * cols
        src_z = src_ref[2]
        amp = ref[S.amp][0 if kind == "wave1" else 1]

    def row(r, carry):
        for y0 in range(0, cols, Y_CHUNK):
            ys = pl.ds(y0, Y_CHUNK)
            pys = pl.ds(8 + y0, Y_CHUNK)
            c = pad[4 + r, pys, :]
            result = (3.0 * STENCIL[0]) * c
            for k in range(1, 5):
                along = pad[4 + r + k, pys, :] + pad[4 + r - k, pys, :]
                along = along + (
                    pad[4 + r, pl.ds(8 + y0 + k, Y_CHUNK), :]
                    + pad[4 + r, pl.ds(8 + y0 - k, Y_CHUNK), :]
                )
                zp = jnp.where(z_index < depth - k, pltpu.roll(c, depth - k, 1), 0.0)
                zm = jnp.where(z_index >= k, pltpu.roll(c, k, 1), 0.0)
                along = along + (zp + zm)
                result = result + STENCIL[k] * along
            v = ref[S.vel][r, ys, :]
            stiff = squared_courant * v * v
            prev = ref[S.prev][r, ys, :]
            out = 2.0 * c - prev + stiff * result
            if wave:
                at_rec = z_index == ref[S.rec][r, ys, :]
                hit = (r == src_x) & (y_index + y0 == src_y) & (z_index == src_z)
                out = out + jnp.where(hit, amp, 0.0)
                sel = jnp.where(at_rec, out, 0.0)
                folded = sel[:, 0:128]
                for t in range(128, depth, 128):
                    folded = folded + sel[:, t : t + 128]
                ref[S.fold][pl.ds(pl.multiple_of(r * cols + y0, Y_CHUNK), Y_CHUNK), :] = folded
                ref[S.o_dw][r, ys, :] = (out - 2.0 * c) + prev
                if kind == "wave1":
                    ref[S.o_f][r, ys, :] = out
            elif kind == "adjbulk":
                ref[S.o_f][r, ys, :] = out
            else:
                at_rec = z_index == ref[S.rec][r, ys, :]
                misfit = ref[S.pick][r, ys, :] - ref[S.obs][r, ys, :]
                out = out + jnp.where(at_rec, misfit, 0.0)
                ref[S.slot_out][i, r, ys, :] = ref[S.part][r, ys, :] + out * ref[S.dw][r, ys, :]
        return carry

    lax.fori_loop(0, tb, row, 0)
    if wave:
        ref[S.o_pick][...] = jnp.sum(ref[S.fold][...], axis=1, keepdims=True).reshape(ref[S.o_pick].shape)
    if kind == "wave2":
        sender = HaloSender(ref, n, tb)

        @pl.when(step == 0)
        def _():
            sender.begin()

        def inject(r, carry):
            for y0 in range(0, cols, Y_CHUNK):
                ys = pl.ds(y0, Y_CHUNK)
                at_rec = z_index == ref[S.rec][r, ys, :]
                misfit = ref[S.o_pick][r, ys, :] - ref[S.obs][r, ys, :]
                a2 = ref[S.a2raw][r, ys, :] + jnp.where(at_rec, misfit, 0.0)
                ref[S.o_a2][r, ys, :] = a2
                ref[S.o_part][r, ys, :] = a2 * ref[S.o_dw][r, ys, :]
                if y0 == 0:
                    ref[S.stg_yhi][i * tb + r] = a2[0:4]
                if y0 == cols - Y_CHUNK:
                    ref[S.stg_ylo][i * tb + r] = a2[Y_CHUNK - 4 : Y_CHUNK]
            return carry

        lax.fori_loop(0, tb, inject, 0)
        sender.send_block(i)

        @pl.when(step == n - 1)
        def _():
            sender.finish()

    if nf_ex:
        @pl.when(i == n - 1)
        def _():
            ex.finish()
    if kind == "adj2":
        @pl.when(step == n - 1)
        def _():
            rs.finish()


def leap(kind, f, xlo, xhi, ylo, yhi, prev, vel, extra, exchanged=(), collective_id=None):
    rows, cols, depth = f.shape
    tb = ROWS_PER_STEP
    nblk = rows // tb
    grid = (nblk,)
    nq = rows // 4
    if kind == "adj2":
        def at(fn):
            return lambda i: fn(lax.rem(lax.axis_index("shot") + 1 + i, nblk))

        fixed = at
    elif kind == "wave2":
        def at(fn):
            return lambda i: fn(lax.rem(i + nblk - 1, nblk))

        def fixed(fn):
            return fn
    else:
        def at(fn):
            return fn

        fixed = at
    block = pl.BlockSpec((tb, cols, depth), at(lambda i: (i, 0, 0)))
    lo_spec = pl.BlockSpec((4, cols, depth), at(lambda i: (jnp.maximum(2 * i - 1, 0), 0, 0)))
    hi_spec = pl.BlockSpec((4, cols, depth), at(lambda i: (jnp.minimum(2 * i + 2, nq - 1), 0, 0)))
    whole4 = pl.BlockSpec((4, cols, depth), fixed(lambda i: (0, 0, 0)))
    yspec = pl.BlockSpec((tb, 8, depth), at(lambda i: (i, 0, 0)))
    col1 = pl.BlockSpec((tb, cols, 1), at(lambda i: (i, 0, 0)))
    slab = pl.BlockSpec((tb, cols, depth), fixed(lambda i: (0, 0, 0)))
    smem = pl.BlockSpec(memory_space=pltpu.SMEM)
    any_spec = pl.BlockSpec(memory_space=pl.ANY)
    field = jax.ShapeDtypeStruct((rows, cols, depth), jnp.float32)
    picked = jax.ShapeDtypeStruct((rows, cols, 1), jnp.float32)
    spec_of = {S.src: smem, S.amp: smem, S.rec: col1, S.mis: col1, S.obs: col1, S.pick: col1, S.vslab: slab, S.mom: slab, S.mass: slab}

    names = [S.f, S.flo, S.fhi, S.xlo, S.xhi, S.ylo, S.yhi, S.prev, S.vel]
    in_specs = [block, lo_spec, hi_spec, whole4, whole4, yspec, yspec, block, block]
    args = [f, f, f, xlo, xhi, ylo, yhi, prev, vel]
    for key, value in extra.items():
        names.append(key)
        in_specs.append(spec_of.get(key, block))
        args.append(value)
    nf_ex = len(exchanged)
    for j, g in enumerate(exchanged):
        names.append(S.ex_f + j)
        in_specs.append(any_spec)
        args.append(g)

    outs = {
        "wave1": [(S.o_f, field, block), (S.o_dw, field, block), (S.o_pick, picked, col1)],
        "wave2": [(S.o_dw, field, block), (S.o_pick, picked, col1), (S.o_a2, field, block), (S.o_part, field, block)],
        "adjbulk": [(S.o_f, field, block)],
        "adj2": [(S.o_v, jax.ShapeDtypeStruct((tb, cols, depth), jnp.float32), slab)],
    }[kind]
    names += [o[0] for o in outs]
    out_shape = [o[1] for o in outs]
    out_specs = [o[2] for o in outs]
    scratch = [pltpu.VMEM((tb + 8, cols + 16, depth), jnp.float32)]
    names.append(S.pad)
    if kind in ("wave1", "wave2"):
        scratch.append(pltpu.VMEM((tb * cols, 128), jnp.float32))
        names.append(S.fold)
    if kind == "adj2":
        names += [S.slot_out, S.slot_in, S.rs_ss, S.rs_rs, S.rs_own, S.rl_top, S.rl_bot, S.rl_rs]
        scratch += [
            pltpu.VMEM((nblk, tb, cols, depth), jnp.float32),
            pltpu.VMEM((nblk, tb, cols, depth), jnp.float32),
            pltpu.SemaphoreType.DMA((6,)),
            pltpu.SemaphoreType.DMA((nblk,)),
            pltpu.SemaphoreType.DMA(()),
            pltpu.VMEM((tb // 2, cols, depth), jnp.float32),
            pltpu.VMEM((tb // 2, cols, depth), jnp.float32),
            pltpu.SemaphoreType.DMA((4,)),
        ]
        params = pltpu.CompilerParams(
            collective_id=collective_id, has_side_effects=True, vmem_limit_bytes=60 * 1024 * 1024
        )
    elif kind == "wave2":
        h_shapes, _ = exchange_io(1, rows, cols, depth)
        names = names[: len(names) - len(scratch)]
        names += [S.h_b + m for m in range(4)]
        names += [S.pad, S.fold]
        names += [S.stg_xlo, S.stg_xhi, S.stg_ylo, S.stg_yhi, S.h_zx, S.h_zy, S.h_ss, S.h_rs, S.h_zs]
        out_shape += h_shapes
        out_specs += [any_spec] * 4
        scratch += [
            pltpu.VMEM((4, cols, depth), jnp.float32),
            pltpu.VMEM((4, cols, depth), jnp.float32),
            pltpu.VMEM((rows, 4, depth), jnp.float32),
            pltpu.VMEM((rows, 4, depth), jnp.float32),
            pltpu.VMEM((4, cols, depth), jnp.float32),
            pltpu.VMEM((rows, 8, depth), jnp.float32),
            pltpu.SemaphoreType.DMA((rows // tb, 4)),
            pltpu.SemaphoreType.DMA((4,)),
            pltpu.SemaphoreType.DMA((4,)),
        ]
        params = pltpu.CompilerParams(
            collective_id=collective_id, has_side_effects=True, vmem_limit_bytes=60 * 1024 * 1024
        )
    elif nf_ex:
        ex_shapes, ex_scratch = exchange_io(nf_ex, rows, cols, depth)
        k = len(outs)
        names = names[: len(names) - len(scratch)]
        names += [S.ex_b + m for m in range(4 * nf_ex)]
        names += [S.pad, S.fold][: len(scratch)]
        names += [S.ex_zx, S.ex_zy, S.ex_ss, S.ex_rs, S.ex_zs]
        out_shape += ex_shapes
        out_specs += [any_spec] * len(ex_shapes)
        scratch += ex_scratch
        params = pltpu.CompilerParams(
            collective_id=collective_id, has_side_effects=True, vmem_limit_bytes=60 * 1024 * 1024
        )
    else:
        params = pltpu.CompilerParams(vmem_limit_bytes=60 * 1024 * 1024)
    n_big = sum(1 for sp in in_specs if sp is block) + 1 + sum(1 for sp in out_specs if sp is block)
    cost = pl.CostEstimate(
        flops=60 * rows * cols * depth,
        transcendentals=0,
        bytes_accessed=4 * rows * cols * depth * n_big,
    )
    result = pl.pallas_call(
        functools.partial(step_kernel, kind, tuple(names), nf_ex),
        grid=grid,
        in_specs=in_specs,
        out_specs=out_specs,
        out_shape=out_shape,
        scratch_shapes=scratch,
        compiler_params=params,
        cost_estimate=cost,
        name=f"leap_{kind}",
    )(*args)
    if kind == "wave2":
        return result[: len(outs)], result[len(outs) :]
    if nf_ex:
        own = result[: len(outs)]
        ex = result[len(outs) :]
        return own, [ex[4 * j : 4 * j + 4] for j in range(nf_ex)]
    return result


def on_device(
    velocity,
    momentum,
    mass_diag,
    u_prev,
    u_cur,
    adj_next,
    adj_cur,
    observed,
    rec_depth,
    src_cell,
    wavelet,
):
    oldest = u_prev[0]
    present = u_cur[0]
    adj_later = adj_next[0]
    adj_now = adj_cur[0]
    rec = rec_depth[0][:, :, None]
    cell = src_cell[0]
    src = src_cell[0]
    amp = wavelet[0]

    (wave_h, adj_h), full_velocity = exchange([present, adj_now], 1, velocity)
    advanced, dw1, pick_adv = leap(
        "wave1", present, *wave_h, oldest, full_velocity, {S.rec: rec, S.src: src, S.amp: amp}
    )
    (adj_bulk,), (adv_h,) = leap(
        "adjbulk", adj_now, *adj_h, adj_later, full_velocity, {}, exchanged=[advanced], collective_id=2
    )
    (dw2, pick_far, adj_two, part), adj_two_h = leap(
        "wave2",
        advanced,
        *adv_h,
        present,
        full_velocity,
        {S.rec: rec, S.src: src, S.amp: amp, S.a2raw: adj_bulk, S.obs: observed[0, 1][:, :, None]},
        collective_id=3,
    )
    (summed,) = leap(
        "adj2",
        adj_two,
        *adj_two_h,
        adj_now,
        full_velocity,
        {
            S.rec: rec,
            S.pick: pick_adv,
            S.obs: observed[0, 0][:, :, None],
            S.dw: dw1,
            S.part: part,
        },
        collective_id=0,
    )
    gradient = 2.0 / velocity * summed
    p_half = momentum - 0.5 * leap_step * gradient
    v_new = velocity + leap_step * p_half / mass_diag
    return (v_new, p_half)


def solution(mesh):
    return jax.shard_map(
        on_device,
        mesh=mesh,
        in_specs=(
            P(("row", "shot"), "col", None),
            P(("row", "shot"), "col", None),
            P(("row", "shot"), "col", None),
            P("shot", "row", "col", None),
            P("shot", "row", "col", None),
            P("shot", "row", "col", None),
            P("shot", "row", "col", None),
            P("shot", None, "row", "col"),
            P("shot", "row", "col"),
            P("shot", None),
            P("shot", None),
        ),
        out_specs=(P(("row", "shot"), "col", None), P(("row", "shot"), "col", None)),
        check_vma=False,
    )
```

```python
import functools

import jax
import jax.numpy as jnp
from jax import lax
from jax.experimental import pallas as pl
from jax.experimental.pallas import tpu as pltpu
from jax.sharding import PartitionSpec as P

STENCIL = (-205.0 / 72.0, 8.0 / 5.0, -1.0 / 5.0, 8.0 / 315.0, -1.0 / 560.0)
squared_courant = 0.012
leap_step = 0.2

class S:
    a2raw = 0
    amp = 1
    dw = 2
    ex_rs = 3
    ex_ss = 4
    ex_zs = 5
    ex_zx = 6
    ex_zy = 7
    f = 8
    fhi = 9
    flo = 10
    fold = 11
    h_rs = 12
    h_ss = 13
    h_zs = 14
    h_zx = 15
    h_zy = 16
    mass = 17
    mis = 18
    mom = 19
    o_a2 = 20
    o_dw = 21
    o_f = 22
    o_p = 23
    o_part = 24
    o_pick = 25
    o_v = 26
    obs = 27
    pad = 28
    part = 29
    prev = 30
    rec = 31
    rs_own = 32
    rs_rs = 33
    rs_ss = 34
    slot_in = 35
    slot_out = 36
    src = 37
    stg_xhi = 38
    stg_xlo = 39
    stg_yhi = 40
    stg_ylo = 41
    vel = 42
    vslab = 43
    xhi = 44
    xlo = 45
    yhi = 46
    ylo = 47
    rl_top = 90
    rl_bot = 91
    rl_rs = 92
    ex_f = 100
    ex_b = 110
    h_b = 130
    pick = 140
    aux = 141


ROWS_PER_STEP = 8
Y_CHUNK = 8


class Exchange:

    def __init__(self, fields, bufs, zero_x, zero_y, send_sem, recv_sem, zero_sem):
        self.fields, self.bufs = fields, bufs
        self.zero_x, self.zero_y = zero_x, zero_y
        self.send_sem, self.recv_sem, self.zero_sem = send_sem, recv_sem, zero_sem
        row, nrow = lax.axis_index("row"), lax.axis_size("row")
        col, ncol = lax.axis_index("col"), lax.axis_size("col")
        self.row, self.nrow, self.col, self.ncol = row, nrow, col, ncol
        self.has = (row < nrow - 1, row > 0, col < ncol - 1, col > 0)
        self.peer = ({"row": row + 1}, {"row": row - 1}, {"col": col + 1}, {"col": col - 1})
        self.filler = (1, 0, 3, 2)

    def source(self, f, d):
        rows, cols, _ = f.shape
        if d == 0:
            return f.at[pl.ds(rows - 4, 4)]
        if d == 1:
            return f.at[pl.ds(0, 4)]
        if d == 2:
            return f.at[:, pl.ds(cols - 4, 4)]
        return f.at[:, pl.ds(0, 4)]

    def target(self, j, b):
        if b == 2:
            return self.bufs[4 * j + b].at[:, pl.ds(4, 4)]
        if b == 3:
            return self.bufs[4 * j + b].at[:, pl.ds(0, 4)]
        return self.bufs[4 * j + b]

    def remote(self, j, d):
        return pltpu.make_async_remote_copy(
            src_ref=self.source(self.fields[j], d),
            dst_ref=self.target(j, d),
            send_sem=self.send_sem.at[j, d],
            recv_sem=self.recv_sem.at[j, d],
            device_id=self.peer[d],
            device_id_type=pl.DeviceIdType.MESH,
        )

    def start(self, extra=0):
        has, row, nrow, col, ncol = self.has, self.row, self.nrow, self.col, self.ncol
        barrier = pltpu.get_barrier_semaphore()
        for d in range(4):
            @pl.when(has[d])
            def _():
                pl.semaphore_signal(barrier, inc=1, device_id=self.peer[d], device_id_type=pl.DeviceIdType.MESH)

        count = (1 - row // (nrow - 1)) + (row + nrow - 1) // nrow + (1 - col // (ncol - 1)) + (col + ncol - 1) // ncol
        pl.semaphore_wait(barrier, count + extra)

        for j in range(len(self.fields)):
            for d in range(4):
                @pl.when(has[d])
                def _():
                    self.remote(j, d).start()

        @pl.when(jnp.logical_not(has[0] & has[1]))
        def _():
            self.zero_x[...] = jnp.zeros_like(self.zero_x)

        @pl.when(jnp.logical_not(has[2] & has[3]))
        def _():
            self.zero_y[...] = jnp.zeros_like(self.zero_y)

        for j in range(len(self.fields)):
            for b in range(4):
                @pl.when(jnp.logical_not(has[self.filler[b]]))
                def _():
                    zero = self.zero_x if b < 2 else self.zero_y
                    copy = pltpu.make_async_copy(zero, self.bufs[4 * j + b], self.zero_sem.at[j, b])
                    copy.start()
                    copy.wait()

    def finish(self):
        has = self.has
        for j in range(len(self.fields)):
            for d in range(4):
                @pl.when(has[d])
                def _():
                    self.remote(j, d).wait_send()
            for b in range(4):
                @pl.when(has[self.filler[b]])
                def _():
                    self.remote(j, b).wait_recv()


def exchange_io(nf, rows, cols, depth):
    shapes = []
    for _ in range(nf):
        shapes += [
            jax.ShapeDtypeStruct((4, cols, depth), jnp.float32),
            jax.ShapeDtypeStruct((4, cols, depth), jnp.float32),
            jax.ShapeDtypeStruct((rows, 8, depth), jnp.float32),
            jax.ShapeDtypeStruct((rows, 8, depth), jnp.float32),
        ]
    scratch = [
        pltpu.VMEM((4, cols, depth), jnp.float32),
        pltpu.VMEM((rows, 8, depth), jnp.float32),
        pltpu.SemaphoreType.DMA((nf, 4)),
        pltpu.SemaphoreType.DMA((nf, 4)),
        pltpu.SemaphoreType.DMA((nf, 4)),
    ]
    return shapes, scratch


def exchange_kernel(nf, gather, *refs):
    if not gather:
        ex = Exchange(refs[:nf], refs[nf : 5 * nf], *refs[5 * nf :])
        ex.start()
        ex.finish()
        return
    vel = refs[nf]
    bufs = refs[nf + 1 : 5 * nf + 1]
    full = refs[5 * nf + 1]
    ag_ss, ag_rs, ag_own = refs[-3:]
    ex = Exchange(refs[:nf], bufs, *refs[5 * nf + 2 : -3])
    me, n = lax.axis_index("shot"), lax.axis_size("shot")
    rows = vel.shape[0]
    barrier = pltpu.get_barrier_semaphore()
    for d in range(1, n):
        pl.semaphore_signal(barrier, inc=1, device_id={"shot": lax.rem(me + d, n)}, device_id_type=pl.DeviceIdType.MESH)

    def send(d):
        peer = lax.rem(me + d, n)
        return pltpu.make_async_remote_copy(
            src_ref=vel,
            dst_ref=full.at[pl.ds(pl.multiple_of(me * rows, rows), rows)],
            send_sem=ag_ss.at[d],
            recv_sem=ag_rs.at[me],
            device_id={"shot": peer},
            device_id_type=pl.DeviceIdType.MESH,
        )

    ex.start(extra=n - 1)
    for d in range(1, n):
        send(d).start()
    own = pltpu.make_async_copy(vel, full.at[pl.ds(pl.multiple_of(me * rows, rows), rows)], ag_own)
    own.start()
    ex.finish()
    for d in range(1, n):
        send(d).wait_send()
    own.wait()
    for d in range(1, n):
        src = lax.rem(me + d, n)
        pltpu.make_async_remote_copy(
            src_ref=vel,
            dst_ref=full.at[pl.ds(pl.multiple_of(src * rows, rows), rows)],
            send_sem=ag_ss.at[d],
            recv_sem=ag_rs.at[src],
            device_id={"shot": src},
            device_id_type=pl.DeviceIdType.MESH,
        ).wait_recv()


def exchange(fields, collective_id, velocity=None):
    nf = len(fields)
    rows, cols, depth = fields[0].shape
    any_spec = pl.BlockSpec(memory_space=pl.ANY)
    shapes, scratch = exchange_io(nf, rows, cols, depth)
    args = list(fields)
    gather = velocity is not None
    if gather:
        n = lax.axis_size("shot")
        args.append(velocity)
        shapes = shapes + [jax.ShapeDtypeStruct((n * velocity.shape[0],) + velocity.shape[1:], jnp.float32)]
        scratch = scratch + [pltpu.SemaphoreType.DMA((n,)), pltpu.SemaphoreType.DMA((n,)), pltpu.SemaphoreType.DMA(())]
    outs = pl.pallas_call(
        functools.partial(exchange_kernel, nf, gather),
        in_specs=[any_spec] * len(args),
        out_specs=[any_spec] * len(shapes),
        out_shape=shapes,
        scratch_shapes=scratch,
        compiler_params=pltpu.CompilerParams(collective_id=collective_id, has_side_effects=True),
        name=f"halo_exchange_{collective_id}",
    )(*args)
    halos = [outs[4 * j : 4 * j + 4] for j in range(nf)]
    if gather:
        return halos, outs[-1]
    return halos


class HaloSender:

    def __init__(self, ref, nblk, tb):
        self.ref, self.nblk, self.tb = ref, nblk, tb
        row, nrow = lax.axis_index("row"), lax.axis_size("row")
        col, ncol = lax.axis_index("col"), lax.axis_size("col")
        self.row, self.nrow, self.col, self.ncol = row, nrow, col, ncol
        self.has = (row < nrow - 1, row > 0, col < ncol - 1, col > 0)
        self.peer = ({"row": row + 1}, {"row": row - 1}, {"col": col + 1}, {"col": col - 1})
        self.filler = (1, 0, 3, 2)
        self.bufs = [ref[S.h_b + b] for b in range(4)]

    def copy(self, d, blk):
        ref, tb = self.ref, self.tb
        rows_here = pl.ds(pl.multiple_of(blk * tb, tb), tb)
        if d == 0:
            src, dst, sem = ref[S.stg_xlo], self.bufs[0], ref[S.h_ss].at[0, 0]
        elif d == 1:
            src, dst, sem = ref[S.stg_xhi], self.bufs[1], ref[S.h_ss].at[0, 1]
        elif d == 2:
            src, dst = ref[S.stg_ylo].at[rows_here], self.bufs[2].at[rows_here, pl.ds(4, 4)]
            sem = ref[S.h_ss].at[blk, 2]
        else:
            src, dst = ref[S.stg_yhi].at[rows_here], self.bufs[3].at[rows_here, pl.ds(0, 4)]
            sem = ref[S.h_ss].at[blk, 3]
        return pltpu.make_async_remote_copy(
            src_ref=src,
            dst_ref=dst,
            send_sem=sem,
            recv_sem=ref[S.h_rs].at[d],
            device_id=self.peer[d],
            device_id_type=pl.DeviceIdType.MESH,
        )

    def whole(self, b):
        ref = self.ref
        src = {0: ref[S.stg_xlo], 1: ref[S.stg_xhi], 2: ref[S.stg_ylo], 3: ref[S.stg_yhi]}[b]
        dst = {0: self.bufs[0], 1: self.bufs[1], 2: self.bufs[2].at[:, pl.ds(4, 4)], 3: self.bufs[3].at[:, pl.ds(0, 4)]}[b]
        return pltpu.make_async_remote_copy(
            src_ref=src,
            dst_ref=dst,
            send_sem=ref[S.h_ss].at[0, b],
            recv_sem=ref[S.h_rs].at[b],
            device_id=self.peer[b],
            device_id_type=pl.DeviceIdType.MESH,
        )

    def begin(self):
        ref, has, row, nrow, col, ncol = self.ref, self.has, self.row, self.nrow, self.col, self.ncol
        barrier = pltpu.get_barrier_semaphore()
        for d in range(4):
            @pl.when(has[d])
            def _():
                pl.semaphore_signal(barrier, inc=1, device_id=self.peer[d], device_id_type=pl.DeviceIdType.MESH)

        count = (1 - row // (nrow - 1)) + (row + nrow - 1) // nrow + (1 - col // (ncol - 1)) + (col + ncol - 1) // ncol
        pl.semaphore_wait(barrier, count)

        @pl.when(jnp.logical_not(has[0] & has[1]))
        def _():
            ref[S.h_zx][...] = jnp.zeros_like(ref[S.h_zx])

        @pl.when(jnp.logical_not(has[2] & has[3]))
        def _():
            ref[S.h_zy][...] = jnp.zeros_like(ref[S.h_zy])

        for b in range(4):
            @pl.when(jnp.logical_not(has[self.filler[b]]))
            def _():
                zero = ref[S.h_zx] if b < 2 else ref[S.h_zy]
                copy = pltpu.make_async_copy(zero, self.bufs[b], ref[S.h_zs].at[b])
                copy.start()
                copy.wait()

    def send_block(self, blk):
        ref, has, tb = self.ref, self.has, self.tb

        @pl.when(blk == 0)
        def _():
            ref[S.stg_xhi][...] = ref[S.o_a2][0:4]

        @pl.when(blk == self.nblk - 1)
        def _():
            ref[S.stg_xlo][...] = ref[S.o_a2][tb - 4 : tb]

        for d in (2, 3):
            @pl.when(has[d])
            def _():
                self.copy(d, blk).start()

        @pl.when(has[1] & (blk == 0))
        def _():
            self.copy(1, blk).start()

        @pl.when(has[0] & (blk == self.nblk - 1))
        def _():
            self.copy(0, blk).start()

    def finish(self):
        has = self.has
        for blk in range(self.nblk):
            for d in (2, 3):
                @pl.when(has[d])
                def _():
                    self.copy(d, blk).wait_send()

        @pl.when(has[1])
        def _():
            self.copy(1, 0).wait_send()

        @pl.when(has[0])
        def _():
            self.copy(0, self.nblk - 1).wait_send()

        for b in range(4):
            @pl.when(has[self.filler[b]])
            def _():
                self.whole(b).wait_recv()


class ReduceScatter:

    def __init__(self, ref, me, n):
        self.ref, self.me, self.n = ref, me, n
        self.up, self.down, self.far = lax.rem(me + 1, n), lax.rem(me + n - 1, n), lax.rem(me + 2, n)
        half = ref[S.slot_out].shape[1] // 2
        self.top, self.bot = pl.ds(0, half), pl.ds(half, half)

    def remote(self, src, dst, k, recv_sem, peer):
        return pltpu.make_async_remote_copy(
            src_ref=src,
            dst_ref=dst,
            send_sem=self.ref[S.rs_ss].at[k],
            recv_sem=recv_sem,
            device_id={"shot": peer},
            device_id_type=pl.DeviceIdType.MESH,
        )

    def direct(self, blk, k, peer):
        ref = self.ref
        return self.remote(ref[S.slot_out].at[blk], ref[S.slot_in].at[self.me], k, ref[S.rs_rs].at[self.me], peer)

    def relay_top(self):
        ref = self.ref
        src = ref[S.slot_out].at[self.far, self.top]
        return self.remote(src, ref[S.rl_top], 2, ref[S.rl_rs].at[0], self.up)

    def relay_bot(self):
        ref = self.ref
        src = ref[S.slot_out].at[self.far, self.bot]
        return self.remote(src, ref[S.rl_bot], 3, ref[S.rl_rs].at[1], self.down)

    def fwd_top(self):
        ref = self.ref
        dst = ref[S.slot_in].at[self.down, self.top]
        return self.remote(ref[S.rl_top], dst, 4, ref[S.rl_rs].at[2], self.up)

    def fwd_bot(self):
        ref = self.ref
        dst = ref[S.slot_in].at[self.up, self.bot]
        return self.remote(ref[S.rl_bot], dst, 5, ref[S.rl_rs].at[3], self.down)

    def begin(self):
        barrier = pltpu.get_barrier_semaphore()
        for peer in (self.up, self.down):
            pl.semaphore_signal(barrier, inc=1, device_id={"shot": peer}, device_id_type=pl.DeviceIdType.MESH)
        pl.semaphore_wait(barrier, 2)

    def at_step(self, step):
        @pl.when(step == 1)
        def _():
            self.direct(self.up, 0, self.up).start()

        @pl.when(step == 2)
        def _():
            self.relay_top().start()
            self.relay_bot().start()

        @pl.when(step == 3)
        def _():
            self.direct(self.down, 1, self.down).start()
            self.relay_top().wait_recv()
            self.relay_bot().wait_recv()
            self.fwd_top().start()
            self.fwd_bot().start()

    def finish(self):
        ref, me, n = self.ref, self.me, self.n
        own = pltpu.make_async_copy(ref[S.slot_out].at[me], ref[S.slot_in].at[me], ref[S.rs_own])
        own.start()
        self.direct(self.up, 0, self.up).wait_send()
        self.direct(self.down, 1, self.down).wait_send()
        self.relay_top().wait_send()
        self.relay_bot().wait_send()
        self.fwd_top().wait_send()
        self.fwd_bot().wait_send()
        own.wait()
        for src in (self.down, self.up):
            self.remote(ref[S.slot_out].at[src], ref[S.slot_in].at[src], 0, ref[S.rs_rs].at[src], src).wait_recv()
        far_in = ref[S.slot_in].at[self.far, self.top]
        self.remote(ref[S.rl_top], far_in, 4, ref[S.rl_rs].at[2], self.down).wait_recv()
        far_in = ref[S.slot_in].at[self.far, self.bot]
        self.remote(ref[S.rl_bot], far_in, 5, ref[S.rl_rs].at[3], self.up).wait_recv()

        slot_in = ref[S.slot_in]

        def row(r, carry):
            summed = slot_in[0, r]
            for s_ in range(1, n):
                summed = summed + slot_in[s_, r]
            ref[S.o_v][r] = summed
            return carry

        lax.fori_loop(0, slot_in.shape[1], row, 0)


def step_kernel(kind, names, nf_ex, *refs):
    ref = dict(zip(names, refs))
    if nf_ex:
        ex = Exchange(
            [ref[S.ex_f + j] for j in range(nf_ex)],
            [ref[S.ex_b + k] for k in range(4 * nf_ex)],
            *[ref[k] for k in (S.ex_zx, S.ex_zy, S.ex_ss, S.ex_rs, S.ex_zs)],
        )
    f_ref, pad = ref[S.f], ref[S.pad]
    tb, cols, depth = f_ref.shape
    n = pl.num_programs(0)
    step = pl.program_id(0)
    if kind == "adj2":
        me = lax.axis_index("shot")
        i = lax.rem(me + 1 + step, n)
        rs = ReduceScatter(ref, me, n)

        @pl.when(step == 0)
        def _():
            rs.begin()

        rs.at_step(step)
    elif kind == "wave2":
        i = lax.rem(step + n - 1, n)
    else:
        i = step

    if nf_ex:
        @pl.when(i == 0)
        def _():
            ex.start()

    lo = jnp.where(i == 0, ref[S.xlo][...], ref[S.flo][...])
    hi = jnp.where(i == n - 1, ref[S.xhi][...], ref[S.fhi][...])
    pad[0:4, 8 : 8 + cols, :] = lo
    pad[4 : 4 + tb, 8 : 8 + cols, :] = f_ref[...]
    pad[4 + tb : 8 + tb, 8 : 8 + cols, :] = hi
    pad[4 : 4 + tb, 0:8, :] = ref[S.ylo][...]
    pad[4 : 4 + tb, 8 + cols : 16 + cols, :] = ref[S.yhi][...]

    z_index = lax.broadcasted_iota(jnp.int32, (Y_CHUNK, depth), 1)
    y_index = lax.broadcasted_iota(jnp.int32, (Y_CHUNK, depth), 0)
    obs_at = 2 if kind == "wave2" else 1
    wave = kind in ("wave1", "wave2")
    if wave:
        src_ref = ref[S.src]
        src_x = src_ref[0] - lax.axis_index("row") * (tb * n) - i * tb
        src_y = src_ref[1] - lax.axis_index("col") * cols
        src_z = src_ref[2]
        amp = ref[S.amp][0 if kind == "wave1" else 1]

    def row(r, carry):
        for y0 in range(0, cols, Y_CHUNK):
            ys = pl.ds(y0, Y_CHUNK)
            pys = pl.ds(8 + y0, Y_CHUNK)
            c = pad[4 + r, pys, :]
            result = (3.0 * STENCIL[0]) * c
            for k in range(1, 5):
                along = pad[4 + r + k, pys, :] + pad[4 + r - k, pys, :]
                along = along + (
                    pad[4 + r, pl.ds(8 + y0 + k, Y_CHUNK), :]
                    + pad[4 + r, pl.ds(8 + y0 - k, Y_CHUNK), :]
                )
                zp = jnp.where(z_index < depth - k, pltpu.roll(c, depth - k, 1), 0.0)
                zm = jnp.where(z_index >= k, pltpu.roll(c, k, 1), 0.0)
                along = along + (zp + zm)
                result = result + STENCIL[k] * along
            v = ref[S.vel][r, ys, :]
            stiff = squared_courant * v * v
            prev = ref[S.prev][r, ys, :]
            out = 2.0 * c - prev + stiff * result
            if wave:
                at_rec = z_index == ref[S.aux][r, ys, 0:1].astype(jnp.int32)
                hit = (r == src_x) & (y_index + y0 == src_y) & (z_index == src_z)
                out = out + jnp.where(hit, amp, 0.0)
                sel = jnp.where(at_rec, out, 0.0)
                folded = sel[:, 0:128]
                for t in range(128, depth, 128):
                    folded = folded + sel[:, t : t + 128]
                ref[S.fold][pl.ds(pl.multiple_of(r * cols + y0, Y_CHUNK), Y_CHUNK), :] = folded
                ref[S.o_dw][r, ys, :] = (out - 2.0 * c) + prev
                if kind == "wave1":
                    ref[S.o_f][r, ys, :] = out
            elif kind == "adjbulk":
                ref[S.o_f][r, ys, :] = out
            else:
                at_rec = z_index == ref[S.aux][r, ys, 0:1].astype(jnp.int32)
                misfit = ref[S.pick][r, ys, :] - ref[S.aux][r, ys, obs_at : obs_at + 1]
                out = out + jnp.where(at_rec, misfit, 0.0)
                ref[S.slot_out][i, r, ys, :] = ref[S.part][r, ys, :] + out * ref[S.dw][r, ys, :]
        return carry

    lax.fori_loop(0, tb, row, 0)
    if wave:
        ref[S.o_pick][...] = jnp.sum(ref[S.fold][...], axis=1, keepdims=True).reshape(ref[S.o_pick].shape)
    if kind == "wave2":
        sender = HaloSender(ref, n, tb)

        @pl.when(step == 0)
        def _():
            sender.begin()

        def inject(r, carry):
            for y0 in range(0, cols, Y_CHUNK):
                ys = pl.ds(y0, Y_CHUNK)
                at_rec = z_index == ref[S.aux][r, ys, 0:1].astype(jnp.int32)
                misfit = ref[S.o_pick][r, ys, :] - ref[S.aux][r, ys, obs_at : obs_at + 1]
                a2 = ref[S.a2raw][r, ys, :] + jnp.where(at_rec, misfit, 0.0)
                ref[S.o_a2][r, ys, :] = a2
                ref[S.o_part][r, ys, :] = a2 * ref[S.o_dw][r, ys, :]
                if y0 == 0:
                    ref[S.stg_yhi][i * tb + r] = a2[0:4]
                if y0 == cols - Y_CHUNK:
                    ref[S.stg_ylo][i * tb + r] = a2[Y_CHUNK - 4 : Y_CHUNK]
            return carry

        lax.fori_loop(0, tb, inject, 0)
        sender.send_block(i)

        @pl.when(step == n - 1)
        def _():
            sender.finish()

    if nf_ex:
        @pl.when(i == n - 1)
        def _():
            ex.finish()
    if kind == "adj2":
        @pl.when(step == n - 1)
        def _():
            rs.finish()


def leap(kind, f, xlo, xhi, ylo, yhi, prev, vel, extra, exchanged=(), collective_id=None):
    rows, cols, depth = f.shape
    tb = ROWS_PER_STEP
    nblk = rows // tb
    grid = (nblk,)
    nq = rows // 4
    if kind == "adj2":
        def at(fn):
            return lambda i: fn(lax.rem(lax.axis_index("shot") + 1 + i, nblk))

        fixed = at
    elif kind == "wave2":
        def at(fn):
            return lambda i: fn(lax.rem(i + nblk - 1, nblk))

        def fixed(fn):
            return fn
    else:
        def at(fn):
            return fn

        fixed = at
    block = pl.BlockSpec((tb, cols, depth), at(lambda i: (i, 0, 0)))
    lo_spec = pl.BlockSpec((4, cols, depth), at(lambda i: (jnp.maximum(2 * i - 1, 0), 0, 0)))
    hi_spec = pl.BlockSpec((4, cols, depth), at(lambda i: (jnp.minimum(2 * i + 2, nq - 1), 0, 0)))
    whole4 = pl.BlockSpec((4, cols, depth), fixed(lambda i: (0, 0, 0)))
    yspec = pl.BlockSpec((tb, 8, depth), at(lambda i: (i, 0, 0)))
    col1 = pl.BlockSpec((tb, cols, 1), at(lambda i: (i, 0, 0)))
    col3 = pl.BlockSpec((tb, cols, 3), at(lambda i: (i, 0, 0)))
    slab = pl.BlockSpec((tb, cols, depth), fixed(lambda i: (0, 0, 0)))
    smem = pl.BlockSpec(memory_space=pltpu.SMEM)
    any_spec = pl.BlockSpec(memory_space=pl.ANY)
    field = jax.ShapeDtypeStruct((rows, cols, depth), jnp.float32)
    picked = jax.ShapeDtypeStruct((rows, cols, 1), jnp.float32)
    spec_of = {S.aux: col3, S.src: smem, S.amp: smem, S.rec: col1, S.mis: col1, S.obs: col1, S.pick: col1, S.vslab: slab, S.mom: slab, S.mass: slab}

    names = [S.f, S.flo, S.fhi, S.xlo, S.xhi, S.ylo, S.yhi, S.prev, S.vel]
    in_specs = [block, lo_spec, hi_spec, whole4, whole4, yspec, yspec, block, block]
    args = [f, f, f, xlo, xhi, ylo, yhi, prev, vel]
    for key, value in extra.items():
        names.append(key)
        in_specs.append(spec_of.get(key, block))
        args.append(value)
    nf_ex = len(exchanged)
    for j, g in enumerate(exchanged):
        names.append(S.ex_f + j)
        in_specs.append(any_spec)
        args.append(g)

    outs = {
        "wave1": [(S.o_f, field, block), (S.o_dw, field, block), (S.o_pick, picked, col1)],
        "wave2": [(S.o_dw, field, block), (S.o_pick, picked, col1), (S.o_a2, field, block), (S.o_part, field, block)],
        "adjbulk": [(S.o_f, field, block)],
        "adj2": [(S.o_v, jax.ShapeDtypeStruct((tb, cols, depth), jnp.float32), slab)],
    }[kind]
    names += [o[0] for o in outs]
    out_shape = [o[1] for o in outs]
    out_specs = [o[2] for o in outs]
    scratch = [pltpu.VMEM((tb + 8, cols + 16, depth), jnp.float32)]
    names.append(S.pad)
    if kind in ("wave1", "wave2"):
        scratch.append(pltpu.VMEM((tb * cols, 128), jnp.float32))
        names.append(S.fold)
    if kind == "adj2":
        names += [S.slot_out, S.slot_in, S.rs_ss, S.rs_rs, S.rs_own, S.rl_top, S.rl_bot, S.rl_rs]
        scratch += [
            pltpu.VMEM((nblk, tb, cols, depth), jnp.float32),
            pltpu.VMEM((nblk, tb, cols, depth), jnp.float32),
            pltpu.SemaphoreType.DMA((6,)),
            pltpu.SemaphoreType.DMA((nblk,)),
            pltpu.SemaphoreType.DMA(()),
            pltpu.VMEM((tb // 2, cols, depth), jnp.float32),
            pltpu.VMEM((tb // 2, cols, depth), jnp.float32),
            pltpu.SemaphoreType.DMA((4,)),
        ]
        params = pltpu.CompilerParams(
            collective_id=collective_id, has_side_effects=True, vmem_limit_bytes=60 * 1024 * 1024
        )
    elif kind == "wave2":
        h_shapes, _ = exchange_io(1, rows, cols, depth)
        names = names[: len(names) - len(scratch)]
        names += [S.h_b + m for m in range(4)]
        names += [S.pad, S.fold]
        names += [S.stg_xlo, S.stg_xhi, S.stg_ylo, S.stg_yhi, S.h_zx, S.h_zy, S.h_ss, S.h_rs, S.h_zs]
        out_shape += h_shapes
        out_specs += [any_spec] * 4
        scratch += [
            pltpu.VMEM((4, cols, depth), jnp.float32),
            pltpu.VMEM((4, cols, depth), jnp.float32),
            pltpu.VMEM((rows, 4, depth), jnp.float32),
            pltpu.VMEM((rows, 4, depth), jnp.float32),
            pltpu.VMEM((4, cols, depth), jnp.float32),
            pltpu.VMEM((rows, 8, depth), jnp.float32),
            pltpu.SemaphoreType.DMA((rows // tb, 4)),
            pltpu.SemaphoreType.DMA((4,)),
            pltpu.SemaphoreType.DMA((4,)),
        ]
        params = pltpu.CompilerParams(
            collective_id=collective_id, has_side_effects=True, vmem_limit_bytes=60 * 1024 * 1024
        )
    elif nf_ex:
        ex_shapes, ex_scratch = exchange_io(nf_ex, rows, cols, depth)
        k = len(outs)
        names = names[: len(names) - len(scratch)]
        names += [S.ex_b + m for m in range(4 * nf_ex)]
        names += [S.pad, S.fold][: len(scratch)]
        names += [S.ex_zx, S.ex_zy, S.ex_ss, S.ex_rs, S.ex_zs]
        out_shape += ex_shapes
        out_specs += [any_spec] * len(ex_shapes)
        scratch += ex_scratch
        params = pltpu.CompilerParams(
            collective_id=collective_id, has_side_effects=True, vmem_limit_bytes=60 * 1024 * 1024
        )
    else:
        params = pltpu.CompilerParams(vmem_limit_bytes=60 * 1024 * 1024)
    n_big = sum(1 for sp in in_specs if sp is block) + 1 + sum(1 for sp in out_specs if sp is block)
    cost = pl.CostEstimate(
        flops=60 * rows * cols * depth,
        transcendentals=0,
        bytes_accessed=4 * rows * cols * depth * n_big,
    )
    result = pl.pallas_call(
        functools.partial(step_kernel, kind, tuple(names), nf_ex),
        grid=grid,
        in_specs=in_specs,
        out_specs=out_specs,
        out_shape=out_shape,
        scratch_shapes=scratch,
        compiler_params=params,
        cost_estimate=cost,
        name=f"leap_{kind}",
    )(*args)
    if kind == "wave2":
        return result[: len(outs)], result[len(outs) :]
    if nf_ex:
        own = result[: len(outs)]
        ex = result[len(outs) :]
        return own, [ex[4 * j : 4 * j + 4] for j in range(nf_ex)]
    return result


def on_device(
    velocity,
    momentum,
    mass_diag,
    u_prev,
    u_cur,
    adj_next,
    adj_cur,
    observed,
    rec_depth,
    src_cell,
    wavelet,
):
    oldest = u_prev[0]
    present = u_cur[0]
    adj_later = adj_next[0]
    adj_now = adj_cur[0]
    aux = jnp.stack([rec_depth[0].astype(jnp.float32), observed[0, 0], observed[0, 1]], axis=-1)
    cell = src_cell[0]
    src = src_cell[0]
    amp = wavelet[0]

    (wave_h, adj_h), full_velocity = exchange([present, adj_now], 1, velocity)
    advanced, dw1, pick_adv = leap(
        "wave1", present, *wave_h, oldest, full_velocity, {S.aux: aux, S.src: src, S.amp: amp}
    )
    (adj_bulk,), (adv_h,) = leap(
        "adjbulk", adj_now, *adj_h, adj_later, full_velocity, {}, exchanged=[advanced], collective_id=2
    )
    (dw2, pick_far, adj_two, part), adj_two_h = leap(
        "wave2",
        advanced,
        *adv_h,
        present,
        full_velocity,
        {S.aux: aux, S.src: src, S.amp: amp, S.a2raw: adj_bulk},
        collective_id=3,
    )
    (summed,) = leap(
        "adj2",
        adj_two,
        *adj_two_h,
        adj_now,
        full_velocity,
        {
            S.aux: aux,
            S.pick: pick_adv,
            S.dw: dw1,
            S.part: part,
        },
        collective_id=0,
    )
    gradient = 2.0 / velocity * summed
    p_half = momentum - 0.5 * leap_step * gradient
    v_new = velocity + leap_step * p_half / mass_diag
    return (v_new, p_half)


def solution(mesh):
    return jax.shard_map(
        on_device,
        mesh=mesh,
        in_specs=(
            P(("row", "shot"), "col", None),
            P(("row", "shot"), "col", None),
            P(("row", "shot"), "col", None),
            P("shot", "row", "col", None),
            P("shot", "row", "col", None),
            P("shot", "row", "col", None),
            P("shot", "row", "col", None),
            P("shot", None, "row", "col"),
            P("shot", "row", "col"),
            P("shot", None),
            P("shot", None),
        ),
        out_specs=(P(("row", "shot"), "col", None), P(("row", "shot"), "col", None)),
        check_vma=False,
    )
```

```python
import functools

import jax
import jax.numpy as jnp
from jax import lax
from jax.experimental import pallas as pl
from jax.experimental.pallas import tpu as pltpu
from jax.sharding import PartitionSpec as P

STENCIL = (-205.0 / 72.0, 8.0 / 5.0, -1.0 / 5.0, 8.0 / 315.0, -1.0 / 560.0)
squared_courant = 0.012
leap_step = 0.2

class S:
    a2raw = 0
    amp = 1
    dw = 2
    ex_rs = 3
    ex_ss = 4
    ex_zs = 5
    ex_zx = 6
    ex_zy = 7
    f = 8
    fhi = 9
    flo = 10
    fold = 11
    h_rs = 12
    h_ss = 13
    h_zs = 14
    h_zx = 15
    h_zy = 16
    mass = 17
    mis = 18
    mom = 19
    o_a2 = 20
    o_dw = 21
    o_f = 22
    o_p = 23
    o_part = 24
    o_pick = 25
    o_v = 26
    obs = 27
    pad = 28
    part = 29
    prev = 30
    rec = 31
    rs_own = 32
    rs_rs = 33
    rs_ss = 34
    slot_in = 35
    slot_out = 36
    src = 37
    stg_xhi = 38
    stg_xlo = 39
    stg_yhi = 40
    stg_ylo = 41
    vel = 42
    vslab = 43
    xhi = 44
    xlo = 45
    yhi = 46
    ylo = 47
    rl_top = 90
    rl_bot = 91
    rl_rs = 92
    ex_f = 100
    ex_b = 110
    h_b = 130
    pick = 140


ROWS_PER_STEP = 8
Y_CHUNK = 8


class Exchange:

    def __init__(self, fields, bufs, zero_x, zero_y, send_sem, recv_sem, zero_sem):
        self.fields, self.bufs = fields, bufs
        self.zero_x, self.zero_y = zero_x, zero_y
        self.send_sem, self.recv_sem, self.zero_sem = send_sem, recv_sem, zero_sem
        row, nrow = lax.axis_index("row"), lax.axis_size("row")
        col, ncol = lax.axis_index("col"), lax.axis_size("col")
        self.row, self.nrow, self.col, self.ncol = row, nrow, col, ncol
        self.has = (row < nrow - 1, row > 0, col < ncol - 1, col > 0)
        self.peer = ({"row": row + 1}, {"row": row - 1}, {"col": col + 1}, {"col": col - 1})
        self.filler = (1, 0, 3, 2)

    def source(self, f, d):
        rows, cols, _ = f.shape
        if d == 0:
            return f.at[pl.ds(rows - 4, 4)]
        if d == 1:
            return f.at[pl.ds(0, 4)]
        if d == 2:
            return f.at[:, pl.ds(cols - 4, 4)]
        return f.at[:, pl.ds(0, 4)]

    def target(self, j, b):
        if b == 2:
            return self.bufs[4 * j + b].at[:, pl.ds(4, 4)]
        if b == 3:
            return self.bufs[4 * j + b].at[:, pl.ds(0, 4)]
        return self.bufs[4 * j + b]

    def remote(self, j, d):
        return pltpu.make_async_remote_copy(
            src_ref=self.source(self.fields[j], d),
            dst_ref=self.target(j, d),
            send_sem=self.send_sem.at[j, d],
            recv_sem=self.recv_sem.at[j, d],
            device_id=self.peer[d],
            device_id_type=pl.DeviceIdType.MESH,
        )

    def start(self, extra=0):
        has, row, nrow, col, ncol = self.has, self.row, self.nrow, self.col, self.ncol
        barrier = pltpu.get_barrier_semaphore()
        for d in range(4):
            @pl.when(has[d])
            def _():
                pl.semaphore_signal(barrier, inc=1, device_id=self.peer[d], device_id_type=pl.DeviceIdType.MESH)

        count = (1 - row // (nrow - 1)) + (row + nrow - 1) // nrow + (1 - col // (ncol - 1)) + (col + ncol - 1) // ncol
        pl.semaphore_wait(barrier, count + extra)

        for j in range(len(self.fields)):
            for d in range(4):
                @pl.when(has[d])
                def _():
                    self.remote(j, d).start()

        @pl.when(jnp.logical_not(has[0] & has[1]))
        def _():
            self.zero_x[...] = jnp.zeros_like(self.zero_x)

        @pl.when(jnp.logical_not(has[2] & has[3]))
        def _():
            self.zero_y[...] = jnp.zeros_like(self.zero_y)

        for j in range(len(self.fields)):
            for b in range(4):
                @pl.when(jnp.logical_not(has[self.filler[b]]))
                def _():
                    zero = self.zero_x if b < 2 else self.zero_y
                    copy = pltpu.make_async_copy(zero, self.bufs[4 * j + b], self.zero_sem.at[j, b])
                    copy.start()
                    copy.wait()

    def finish(self):
        has = self.has
        for j in range(len(self.fields)):
            for d in range(4):
                @pl.when(has[d])
                def _():
                    self.remote(j, d).wait_send()
            for b in range(4):
                @pl.when(has[self.filler[b]])
                def _():
                    self.remote(j, b).wait_recv()


def exchange_io(nf, rows, cols, depth):
    shapes = []
    for _ in range(nf):
        shapes += [
            jax.ShapeDtypeStruct((4, cols, depth), jnp.float32),
            jax.ShapeDtypeStruct((4, cols, depth), jnp.float32),
            jax.ShapeDtypeStruct((rows, 8, depth), jnp.float32),
            jax.ShapeDtypeStruct((rows, 8, depth), jnp.float32),
        ]
    scratch = [
        pltpu.VMEM((4, cols, depth), jnp.float32),
        pltpu.VMEM((rows, 8, depth), jnp.float32),
        pltpu.SemaphoreType.DMA((nf, 4)),
        pltpu.SemaphoreType.DMA((nf, 4)),
        pltpu.SemaphoreType.DMA((nf, 4)),
    ]
    return shapes, scratch


def exchange_kernel(nf, gather, *refs):
    if not gather:
        ex = Exchange(refs[:nf], refs[nf : 5 * nf], *refs[5 * nf :])
        ex.start()
        ex.finish()
        return
    vel = refs[nf]
    bufs = refs[nf + 1 : 5 * nf + 1]
    full = refs[5 * nf + 1]
    ag_ss, ag_rs, ag_own = refs[-3:]
    ex = Exchange(refs[:nf], bufs, *refs[5 * nf + 2 : -3])
    me, n = lax.axis_index("shot"), lax.axis_size("shot")
    rows = vel.shape[0]
    barrier = pltpu.get_barrier_semaphore()
    for d in range(1, n):
        pl.semaphore_signal(barrier, inc=1, device_id={"shot": lax.rem(me + d, n)}, device_id_type=pl.DeviceIdType.MESH)

    def send(d):
        peer = lax.rem(me + d, n)
        return pltpu.make_async_remote_copy(
            src_ref=vel,
            dst_ref=full.at[pl.ds(pl.multiple_of(me * rows, rows), rows)],
            send_sem=ag_ss.at[d],
            recv_sem=ag_rs.at[me],
            device_id={"shot": peer},
            device_id_type=pl.DeviceIdType.MESH,
        )

    ex.start(extra=n - 1)
    for d in range(1, n):
        send(d).start()
    own = pltpu.make_async_copy(vel, full.at[pl.ds(pl.multiple_of(me * rows, rows), rows)], ag_own)
    own.start()
    ex.finish()
    for d in range(1, n):
        send(d).wait_send()
    own.wait()
    for d in range(1, n):
        src = lax.rem(me + d, n)
        pltpu.make_async_remote_copy(
            src_ref=vel,
            dst_ref=full.at[pl.ds(pl.multiple_of(src * rows, rows), rows)],
            send_sem=ag_ss.at[d],
            recv_sem=ag_rs.at[src],
            device_id={"shot": src},
            device_id_type=pl.DeviceIdType.MESH,
        ).wait_recv()


def exchange(fields, collective_id, velocity=None):
    nf = len(fields)
    rows, cols, depth = fields[0].shape
    any_spec = pl.BlockSpec(memory_space=pl.ANY)
    shapes, scratch = exchange_io(nf, rows, cols, depth)
    args = list(fields)
    gather = velocity is not None
    if gather:
        n = lax.axis_size("shot")
        args.append(velocity)
        shapes = shapes + [jax.ShapeDtypeStruct((n * velocity.shape[0],) + velocity.shape[1:], jnp.float32)]
        scratch = scratch + [pltpu.SemaphoreType.DMA((n,)), pltpu.SemaphoreType.DMA((n,)), pltpu.SemaphoreType.DMA(())]
    outs = pl.pallas_call(
        functools.partial(exchange_kernel, nf, gather),
        in_specs=[any_spec] * len(args),
        out_specs=[any_spec] * len(shapes),
        out_shape=shapes,
        scratch_shapes=scratch,
        compiler_params=pltpu.CompilerParams(collective_id=collective_id, has_side_effects=True),
        name=f"halo_exchange_{collective_id}",
    )(*args)
    halos = [outs[4 * j : 4 * j + 4] for j in range(nf)]
    if gather:
        return halos, outs[-1]
    return halos


class HaloSender:

    def __init__(self, ref, nblk, tb):
        self.ref, self.nblk, self.tb = ref, nblk, tb
        row, nrow = lax.axis_index("row"), lax.axis_size("row")
        col, ncol = lax.axis_index("col"), lax.axis_size("col")
        self.row, self.nrow, self.col, self.ncol = row, nrow, col, ncol
        self.has = (row < nrow - 1, row > 0, col < ncol - 1, col > 0)
        self.peer = ({"row": row + 1}, {"row": row - 1}, {"col": col + 1}, {"col": col - 1})
        self.filler = (1, 0, 3, 2)
        self.bufs = [ref[S.h_b + b] for b in range(4)]

    def copy(self, d, blk):
        ref, tb = self.ref, self.tb
        rows_here = pl.ds(pl.multiple_of(blk * tb, tb), tb)
        if d == 0:
            src, dst, sem = ref[S.stg_xlo], self.bufs[0], ref[S.h_ss].at[0, 0]
        elif d == 1:
            src, dst, sem = ref[S.stg_xhi], self.bufs[1], ref[S.h_ss].at[0, 1]
        elif d == 2:
            src, dst = ref[S.stg_ylo].at[rows_here], self.bufs[2].at[rows_here, pl.ds(4, 4)]
            sem = ref[S.h_ss].at[blk, 2]
        else:
            src, dst = ref[S.stg_yhi].at[rows_here], self.bufs[3].at[rows_here, pl.ds(0, 4)]
            sem = ref[S.h_ss].at[blk, 3]
        return pltpu.make_async_remote_copy(
            src_ref=src,
            dst_ref=dst,
            send_sem=sem,
            recv_sem=ref[S.h_rs].at[d],
            device_id=self.peer[d],
            device_id_type=pl.DeviceIdType.MESH,
        )

    def whole(self, b):
        ref = self.ref
        src = {0: ref[S.stg_xlo], 1: ref[S.stg_xhi], 2: ref[S.stg_ylo], 3: ref[S.stg_yhi]}[b]
        dst = {0: self.bufs[0], 1: self.bufs[1], 2: self.bufs[2].at[:, pl.ds(4, 4)], 3: self.bufs[3].at[:, pl.ds(0, 4)]}[b]
        return pltpu.make_async_remote_copy(
            src_ref=src,
            dst_ref=dst,
            send_sem=ref[S.h_ss].at[0, b],
            recv_sem=ref[S.h_rs].at[b],
            device_id=self.peer[b],
            device_id_type=pl.DeviceIdType.MESH,
        )

    def begin(self):
        ref, has, row, nrow, col, ncol = self.ref, self.has, self.row, self.nrow, self.col, self.ncol
        barrier = pltpu.get_barrier_semaphore()
        for d in range(4):
            @pl.when(has[d])
            def _():
                pl.semaphore_signal(barrier, inc=1, device_id=self.peer[d], device_id_type=pl.DeviceIdType.MESH)

        count = (1 - row // (nrow - 1)) + (row + nrow - 1) // nrow + (1 - col // (ncol - 1)) + (col + ncol - 1) // ncol
        pl.semaphore_wait(barrier, count)

        @pl.when(jnp.logical_not(has[0] & has[1]))
        def _():
            ref[S.h_zx][...] = jnp.zeros_like(ref[S.h_zx])

        @pl.when(jnp.logical_not(has[2] & has[3]))
        def _():
            ref[S.h_zy][...] = jnp.zeros_like(ref[S.h_zy])

        for b in range(4):
            @pl.when(jnp.logical_not(has[self.filler[b]]))
            def _():
                zero = ref[S.h_zx] if b < 2 else ref[S.h_zy]
                copy = pltpu.make_async_copy(zero, self.bufs[b], ref[S.h_zs].at[b])
                copy.start()
                copy.wait()

    def send_block(self, blk):
        ref, has, tb = self.ref, self.has, self.tb

        @pl.when(blk == 0)
        def _():
            ref[S.stg_xhi][...] = ref[S.o_a2][0:4]

        @pl.when(blk == self.nblk - 1)
        def _():
            ref[S.stg_xlo][...] = ref[S.o_a2][tb - 4 : tb]

        for d in (2, 3):
            @pl.when(has[d])
            def _():
                self.copy(d, blk).start()

        @pl.when(has[1] & (blk == 0))
        def _():
            self.copy(1, blk).start()

        @pl.when(has[0] & (blk == self.nblk - 1))
        def _():
            self.copy(0, blk).start()

    def finish(self):
        has = self.has
        for blk in range(self.nblk):
            for d in (2, 3):
                @pl.when(has[d])
                def _():
                    self.copy(d, blk).wait_send()

        @pl.when(has[1])
        def _():
            self.copy(1, 0).wait_send()

        @pl.when(has[0])
        def _():
            self.copy(0, self.nblk - 1).wait_send()

        for b in range(4):
            @pl.when(has[self.filler[b]])
            def _():
                self.whole(b).wait_recv()


class ReduceScatter:

    def __init__(self, ref, me, n):
        self.ref, self.me, self.n = ref, me, n
        self.up, self.down, self.far = lax.rem(me + 1, n), lax.rem(me + n - 1, n), lax.rem(me + 2, n)
        half = ref[S.slot_out].shape[1] // 2
        self.top, self.bot = pl.ds(0, half), pl.ds(half, half)

    def remote(self, src, dst, k, recv_sem, peer):
        return pltpu.make_async_remote_copy(
            src_ref=src,
            dst_ref=dst,
            send_sem=self.ref[S.rs_ss].at[k],
            recv_sem=recv_sem,
            device_id={"shot": peer},
            device_id_type=pl.DeviceIdType.MESH,
        )

    def direct(self, blk, k, peer):
        ref = self.ref
        return self.remote(ref[S.slot_out].at[blk], ref[S.slot_in].at[self.me], k, ref[S.rs_rs].at[self.me], peer)

    def relay_top(self):
        ref = self.ref
        src = ref[S.slot_out].at[self.far, self.top]
        return self.remote(src, ref[S.rl_top], 2, ref[S.rl_rs].at[0], self.up)

    def relay_bot(self):
        ref = self.ref
        src = ref[S.slot_out].at[self.far, self.bot]
        return self.remote(src, ref[S.rl_bot], 3, ref[S.rl_rs].at[1], self.down)

    def fwd_top(self):
        ref = self.ref
        dst = ref[S.slot_in].at[self.down, self.top]
        return self.remote(ref[S.rl_top], dst, 4, ref[S.rl_rs].at[2], self.up)

    def fwd_bot(self):
        ref = self.ref
        dst = ref[S.slot_in].at[self.up, self.bot]
        return self.remote(ref[S.rl_bot], dst, 5, ref[S.rl_rs].at[3], self.down)

    def begin(self):
        barrier = pltpu.get_barrier_semaphore()
        for peer in (self.up, self.down):
            pl.semaphore_signal(barrier, inc=1, device_id={"shot": peer}, device_id_type=pl.DeviceIdType.MESH)
        pl.semaphore_wait(barrier, 2)

    def at_step(self, step):
        @pl.when(step == 1)
        def _():
            self.direct(self.up, 0, self.up).start()

        @pl.when(step == 2)
        def _():
            self.relay_top().start()
            self.relay_bot().start()

        @pl.when(step == 3)
        def _():
            self.direct(self.down, 1, self.down).start()
            self.relay_top().wait_recv()
            self.relay_bot().wait_recv()
            self.fwd_top().start()
            self.fwd_bot().start()

    def finish(self):
        ref, me, n = self.ref, self.me, self.n
        own = pltpu.make_async_copy(ref[S.slot_out].at[me], ref[S.slot_in].at[me], ref[S.rs_own])
        own.start()
        self.direct(self.up, 0, self.up).wait_send()
        self.direct(self.down, 1, self.down).wait_send()
        self.relay_top().wait_send()
        self.relay_bot().wait_send()
        self.fwd_top().wait_send()
        self.fwd_bot().wait_send()
        own.wait()
        for src in (self.down, self.up):
            self.remote(ref[S.slot_out].at[src], ref[S.slot_in].at[src], 0, ref[S.rs_rs].at[src], src).wait_recv()
        far_in = ref[S.slot_in].at[self.far, self.top]
        self.remote(ref[S.rl_top], far_in, 4, ref[S.rl_rs].at[2], self.down).wait_recv()
        far_in = ref[S.slot_in].at[self.far, self.bot]
        self.remote(ref[S.rl_bot], far_in, 5, ref[S.rl_rs].at[3], self.up).wait_recv()

        slot_in = ref[S.slot_in]

        def row(r, carry):
            summed = slot_in[0, r]
            for s_ in range(1, n):
                summed = summed + slot_in[s_, r]
            ref[S.o_v][r] = summed
            return carry

        lax.fori_loop(0, slot_in.shape[1], row, 0)


def step_kernel(kind, names, nf_ex, *refs):
    ref = dict(zip(names, refs))
    if nf_ex:
        ex = Exchange(
            [ref[S.ex_f + j] for j in range(nf_ex)],
            [ref[S.ex_b + k] for k in range(4 * nf_ex)],
            *[ref[k] for k in (S.ex_zx, S.ex_zy, S.ex_ss, S.ex_rs, S.ex_zs)],
        )
    f_ref, pad = ref[S.f], ref[S.pad]
    tb, cols, depth = f_ref.shape
    n = pl.num_programs(0)
    step = pl.program_id(0)
    if kind == "adj2":
        me = lax.axis_index("shot")
        i = lax.rem(me + 1 + step, n)
        rs = ReduceScatter(ref, me, n)

        @pl.when(step == 0)
        def _():
            rs.begin()

        rs.at_step(step)
    elif kind == "wave2":
        i = lax.rem(step + n - 1, n)
    else:
        i = step

    if nf_ex:
        @pl.when(i == 0)
        def _():
            ex.start()

    lo = jnp.where(i == 0, ref[S.xlo][...], ref[S.flo][...])
    hi = jnp.where(i == n - 1, ref[S.xhi][...], ref[S.fhi][...])
    pad[0:4, 8 : 8 + cols, :] = lo
    pad[4 : 4 + tb, 8 : 8 + cols, :] = f_ref[...]
    pad[4 + tb : 8 + tb, 8 : 8 + cols, :] = hi
    pad[4 : 4 + tb, 0:8, :] = ref[S.ylo][...]
    pad[4 : 4 + tb, 8 + cols : 16 + cols, :] = ref[S.yhi][...]

    z_index = lax.broadcasted_iota(jnp.int32, (Y_CHUNK, depth), 1)
    y_index = lax.broadcasted_iota(jnp.int32, (Y_CHUNK, depth), 0)
    wave = kind in ("wave1", "wave2")
    if wave:
        src_ref = ref[S.src]
        src_x = src_ref[0] - lax.axis_index("row") * (tb * n) - i * tb
        src_y = src_ref[1] - lax.axis_index("col") * cols
        src_z = src_ref[2]
        amp = ref[S.amp][0 if kind == "wave1" else 1]

    def row(r, carry):
        for y0 in range(0, cols, Y_CHUNK):
            ys = pl.ds(y0, Y_CHUNK)
            pys = pl.ds(8 + y0, Y_CHUNK)
            c = pad[4 + r, pys, :]
            result = (3.0 * STENCIL[0]) * c
            for k in range(1, 5):
                along = pad[4 + r + k, pys, :] + pad[4 + r - k, pys, :]
                along = along + (
                    pad[4 + r, pl.ds(8 + y0 + k, Y_CHUNK), :]
                    + pad[4 + r, pl.ds(8 + y0 - k, Y_CHUNK), :]
                )
                zp = jnp.where(z_index < depth - k, pltpu.roll(c, depth - k, 1), 0.0)
                zm = jnp.where(z_index >= k, pltpu.roll(c, k, 1), 0.0)
                along = along + (zp + zm)
                result = result + STENCIL[k] * along
            v = ref[S.vel][r, ys, :]
            stiff = squared_courant * v * v
            prev = ref[S.prev][r, ys, :]
            out = 2.0 * c - prev + stiff * result
            if wave:
                at_rec = z_index == ref[S.rec][r, ys, :]
                hit = (r == src_x) & (y_index + y0 == src_y) & (z_index == src_z)
                out = out + jnp.where(hit, amp, 0.0)
                sel = jnp.where(at_rec, out, 0.0)
                folded = sel[:, 0:128]
                for t in range(128, depth, 128):
                    folded = folded + sel[:, t : t + 128]
                ref[S.fold][pl.ds(pl.multiple_of(r * cols + y0, Y_CHUNK), Y_CHUNK), :] = folded
                ref[S.o_dw][r, ys, :] = (out - 2.0 * c) + prev
                if kind == "wave1":
                    ref[S.o_f][r, ys, :] = out
            elif kind == "adjbulk":
                ref[S.o_f][r, ys, :] = out
            else:
                at_rec = z_index == ref[S.rec][r, ys, :]
                misfit = ref[S.pick][r, ys, :] - ref[S.obs][r, ys, :]
                out = out + jnp.where(at_rec, misfit, 0.0)
                ref[S.slot_out][i, r, ys, :] = ref[S.part][r, ys, :] + out * ref[S.dw][r, ys, :]
        return carry

    lax.fori_loop(0, tb, row, 0)
    if wave:
        ref[S.o_pick][...] = jnp.sum(ref[S.fold][...], axis=1, keepdims=True).reshape(ref[S.o_pick].shape)
    if kind == "wave2":
        sender = HaloSender(ref, n, tb)

        @pl.when(step == 0)
        def _():
            sender.begin()

        def inject(r, carry):
            for y0 in range(0, cols, Y_CHUNK):
                ys = pl.ds(y0, Y_CHUNK)
                at_rec = z_index == ref[S.rec][r, ys, :]
                misfit = ref[S.o_pick][r, ys, :] - ref[S.obs][r, ys, :]
                a2 = ref[S.a2raw][r, ys, :] + jnp.where(at_rec, misfit, 0.0)
                ref[S.o_a2][r, ys, :] = a2
                ref[S.o_part][r, ys, :] = a2 * ref[S.o_dw][r, ys, :]
                if y0 == 0:
                    ref[S.stg_yhi][i * tb + r] = a2[0:4]
                if y0 == cols - Y_CHUNK:
                    ref[S.stg_ylo][i * tb + r] = a2[Y_CHUNK - 4 : Y_CHUNK]
            return carry

        lax.fori_loop(0, tb, inject, 0)
        sender.send_block(i)

        @pl.when(step == n - 1)
        def _():
            sender.finish()

    if nf_ex:
        @pl.when(i == n - 1)
        def _():
            ex.finish()
    if kind == "adj2":
        @pl.when(step == n - 1)
        def _():
            rs.finish()


def leap(kind, f, xlo, xhi, ylo, yhi, prev, vel, extra, exchanged=(), collective_id=None):
    rows, cols, depth = f.shape
    tb = 4 if kind in ("wave1", "adjbulk") else ROWS_PER_STEP
    nblk = rows // tb
    grid = (nblk,)
    nq = rows // 4
    if kind == "adj2":
        def at(fn):
            return lambda i: fn(lax.rem(lax.axis_index("shot") + 1 + i, nblk))

        fixed = at
    elif kind == "wave2":
        def at(fn):
            return lambda i: fn(lax.rem(i + nblk - 1, nblk))

        def fixed(fn):
            return fn
    else:
        def at(fn):
            return fn

        fixed = at
    block = pl.BlockSpec((tb, cols, depth), at(lambda i: (i, 0, 0)))
    q = tb // 4
    lo_spec = pl.BlockSpec((4, cols, depth), at(lambda i: (jnp.maximum(q * i - 1, 0), 0, 0)))
    hi_spec = pl.BlockSpec((4, cols, depth), at(lambda i: (jnp.minimum(q * i + q, nq - 1), 0, 0)))
    whole4 = pl.BlockSpec((4, cols, depth), fixed(lambda i: (0, 0, 0)))
    yspec = pl.BlockSpec((tb, 8, depth), at(lambda i: (i, 0, 0)))
    col1 = pl.BlockSpec((tb, cols, 1), at(lambda i: (i, 0, 0)))
    slab = pl.BlockSpec((tb, cols, depth), fixed(lambda i: (0, 0, 0)))
    smem = pl.BlockSpec(memory_space=pltpu.SMEM)
    any_spec = pl.BlockSpec(memory_space=pl.ANY)
    field = jax.ShapeDtypeStruct((rows, cols, depth), jnp.float32)
    picked = jax.ShapeDtypeStruct((rows, cols, 1), jnp.float32)
    spec_of = {S.src: smem, S.amp: smem, S.rec: col1, S.mis: col1, S.obs: col1, S.pick: col1, S.vslab: slab, S.mom: slab, S.mass: slab}

    names = [S.f, S.flo, S.fhi, S.xlo, S.xhi, S.ylo, S.yhi, S.prev, S.vel]
    in_specs = [block, lo_spec, hi_spec, whole4, whole4, yspec, yspec, block, block]
    args = [f, f, f, xlo, xhi, ylo, yhi, prev, vel]
    for key, value in extra.items():
        names.append(key)
        in_specs.append(spec_of.get(key, block))
        args.append(value)
    nf_ex = len(exchanged)
    for j, g in enumerate(exchanged):
        names.append(S.ex_f + j)
        in_specs.append(any_spec)
        args.append(g)

    outs = {
        "wave1": [(S.o_f, field, block), (S.o_dw, field, block), (S.o_pick, picked, col1)],
        "wave2": [(S.o_dw, field, block), (S.o_pick, picked, col1), (S.o_a2, field, block), (S.o_part, field, block)],
        "adjbulk": [(S.o_f, field, block)],
        "adj2": [(S.o_v, jax.ShapeDtypeStruct((tb, cols, depth), jnp.float32), slab)],
    }[kind]
    names += [o[0] for o in outs]
    out_shape = [o[1] for o in outs]
    out_specs = [o[2] for o in outs]
    scratch = [pltpu.VMEM((tb + 8, cols + 16, depth), jnp.float32)]
    names.append(S.pad)
    if kind in ("wave1", "wave2"):
        scratch.append(pltpu.VMEM((tb * cols, 128), jnp.float32))
        names.append(S.fold)
    if kind == "adj2":
        names += [S.slot_out, S.slot_in, S.rs_ss, S.rs_rs, S.rs_own, S.rl_top, S.rl_bot, S.rl_rs]
        scratch += [
            pltpu.VMEM((nblk, tb, cols, depth), jnp.float32),
            pltpu.VMEM((nblk, tb, cols, depth), jnp.float32),
            pltpu.SemaphoreType.DMA((6,)),
            pltpu.SemaphoreType.DMA((nblk,)),
            pltpu.SemaphoreType.DMA(()),
            pltpu.VMEM((tb // 2, cols, depth), jnp.float32),
            pltpu.VMEM((tb // 2, cols, depth), jnp.float32),
            pltpu.SemaphoreType.DMA((4,)),
        ]
        params = pltpu.CompilerParams(
            collective_id=collective_id, has_side_effects=True, vmem_limit_bytes=60 * 1024 * 1024
        )
    elif kind == "wave2":
        h_shapes, _ = exchange_io(1, rows, cols, depth)
        names = names[: len(names) - len(scratch)]
        names += [S.h_b + m for m in range(4)]
        names += [S.pad, S.fold]
        names += [S.stg_xlo, S.stg_xhi, S.stg_ylo, S.stg_yhi, S.h_zx, S.h_zy, S.h_ss, S.h_rs, S.h_zs]
        out_shape += h_shapes
        out_specs += [any_spec] * 4
        scratch += [
            pltpu.VMEM((4, cols, depth), jnp.float32),
            pltpu.VMEM((4, cols, depth), jnp.float32),
            pltpu.VMEM((rows, 4, depth), jnp.float32),
            pltpu.VMEM((rows, 4, depth), jnp.float32),
            pltpu.VMEM((4, cols, depth), jnp.float32),
            pltpu.VMEM((rows, 8, depth), jnp.float32),
            pltpu.SemaphoreType.DMA((rows // tb, 4)),
            pltpu.SemaphoreType.DMA((4,)),
            pltpu.SemaphoreType.DMA((4,)),
        ]
        params = pltpu.CompilerParams(
            collective_id=collective_id, has_side_effects=True, vmem_limit_bytes=60 * 1024 * 1024
        )
    elif nf_ex:
        ex_shapes, ex_scratch = exchange_io(nf_ex, rows, cols, depth)
        k = len(outs)
        names = names[: len(names) - len(scratch)]
        names += [S.ex_b + m for m in range(4 * nf_ex)]
        names += [S.pad, S.fold][: len(scratch)]
        names += [S.ex_zx, S.ex_zy, S.ex_ss, S.ex_rs, S.ex_zs]
        out_shape += ex_shapes
        out_specs += [any_spec] * len(ex_shapes)
        scratch += ex_scratch
        params = pltpu.CompilerParams(
            collective_id=collective_id, has_side_effects=True, vmem_limit_bytes=60 * 1024 * 1024
        )
    else:
        params = pltpu.CompilerParams(vmem_limit_bytes=60 * 1024 * 1024)
    n_big = sum(1 for sp in in_specs if sp is block) + 1 + sum(1 for sp in out_specs if sp is block)
    cost = pl.CostEstimate(
        flops=60 * rows * cols * depth,
        transcendentals=0,
        bytes_accessed=4 * rows * cols * depth * n_big,
    )
    result = pl.pallas_call(
        functools.partial(step_kernel, kind, tuple(names), nf_ex),
        grid=grid,
        in_specs=in_specs,
        out_specs=out_specs,
        out_shape=out_shape,
        scratch_shapes=scratch,
        compiler_params=params,
        cost_estimate=cost,
        name=f"leap_{kind}",
    )(*args)
    if kind == "wave2":
        return result[: len(outs)], result[len(outs) :]
    if nf_ex:
        own = result[: len(outs)]
        ex = result[len(outs) :]
        return own, [ex[4 * j : 4 * j + 4] for j in range(nf_ex)]
    return result


def on_device(
    velocity,
    momentum,
    mass_diag,
    u_prev,
    u_cur,
    adj_next,
    adj_cur,
    observed,
    rec_depth,
    src_cell,
    wavelet,
):
    oldest = u_prev[0]
    present = u_cur[0]
    adj_later = adj_next[0]
    adj_now = adj_cur[0]
    rec = rec_depth[0][:, :, None]
    cell = src_cell[0]
    src = src_cell[0]
    amp = wavelet[0]

    (wave_h, adj_h), full_velocity = exchange([present, adj_now], 1, velocity)
    advanced, dw1, pick_adv = leap(
        "wave1", present, *wave_h, oldest, full_velocity, {S.rec: rec, S.src: src, S.amp: amp}
    )
    (adj_bulk,), (adv_h,) = leap(
        "adjbulk", adj_now, *adj_h, adj_later, full_velocity, {}, exchanged=[advanced], collective_id=2
    )
    (dw2, pick_far, adj_two, part), adj_two_h = leap(
        "wave2",
        advanced,
        *adv_h,
        present,
        full_velocity,
        {S.rec: rec, S.src: src, S.amp: amp, S.a2raw: adj_bulk, S.obs: observed[0, 1][:, :, None]},
        collective_id=3,
    )
    (summed,) = leap(
        "adj2",
        adj_two,
        *adj_two_h,
        adj_now,
        full_velocity,
        {
            S.rec: rec,
            S.pick: pick_adv,
            S.obs: observed[0, 0][:, :, None],
            S.dw: dw1,
            S.part: part,
        },
        collective_id=0,
    )
    gradient = 2.0 / velocity * summed
    p_half = momentum - 0.5 * leap_step * gradient
    v_new = velocity + leap_step * p_half / mass_diag
    return (v_new, p_half)


def solution(mesh):
    return jax.shard_map(
        on_device,
        mesh=mesh,
        in_specs=(
            P(("row", "shot"), "col", None),
            P(("row", "shot"), "col", None),
            P(("row", "shot"), "col", None),
            P("shot", "row", "col", None),
            P("shot", "row", "col", None),
            P("shot", "row", "col", None),
            P("shot", "row", "col", None),
            P("shot", None, "row", "col"),
            P("shot", "row", "col"),
            P("shot", None),
            P("shot", None),
        ),
        out_specs=(P(("row", "shot"), "col", None), P(("row", "shot"), "col", None)),
        check_vma=False,
    )
```

```python
import functools

import jax
import jax.numpy as jnp
from jax import lax
from jax.experimental import pallas as pl
from jax.experimental.pallas import tpu as pltpu
from jax.sharding import PartitionSpec as P

STENCIL = (-205.0 / 72.0, 8.0 / 5.0, -1.0 / 5.0, 8.0 / 315.0, -1.0 / 560.0)
squared_courant = 0.012
leap_step = 0.2

class S:
    a2raw = 0
    amp = 1
    dw = 2
    ex_rs = 3
    ex_ss = 4
    ex_zs = 5
    ex_zx = 6
    ex_zy = 7
    f = 8
    fhi = 9
    flo = 10
    fold = 11
    h_rs = 12
    h_ss = 13
    h_zs = 14
    h_zx = 15
    h_zy = 16
    mass = 17
    mis = 18
    mom = 19
    o_a2 = 20
    o_dw = 21
    o_f = 22
    o_p = 23
    o_part = 24
    o_pick = 25
    o_v = 26
    obs = 27
    pad = 28
    part = 29
    prev = 30
    rec = 31
    rs_own = 32
    rs_rs = 33
    rs_ss = 34
    slot_in = 35
    slot_out = 36
    src = 37
    stg_xhi = 38
    stg_xlo = 39
    stg_yhi = 40
    stg_ylo = 41
    vel = 42
    vslab = 43
    xhi = 44
    xlo = 45
    yhi = 46
    ylo = 47
    rl_top = 90
    rl_bot = 91
    rl_rs = 92
    ex_f = 100
    ex_b = 110
    h_b = 130
    pick = 140


ROWS_PER_STEP = 8
Y_CHUNK = 8


class Exchange:

    def __init__(self, fields, bufs, zero_x, zero_y, send_sem, recv_sem, zero_sem):
        self.fields, self.bufs = fields, bufs
        self.zero_x, self.zero_y = zero_x, zero_y
        self.send_sem, self.recv_sem, self.zero_sem = send_sem, recv_sem, zero_sem
        row, nrow = lax.axis_index("row"), lax.axis_size("row")
        col, ncol = lax.axis_index("col"), lax.axis_size("col")
        self.row, self.nrow, self.col, self.ncol = row, nrow, col, ncol
        self.has = (row < nrow - 1, row > 0, col < ncol - 1, col > 0)
        self.peer = ({"row": row + 1}, {"row": row - 1}, {"col": col + 1}, {"col": col - 1})
        self.filler = (1, 0, 3, 2)

    def source(self, f, d):
        rows, cols, _ = f.shape
        if d == 0:
            return f.at[pl.ds(rows - 4, 4)]
        if d == 1:
            return f.at[pl.ds(0, 4)]
        if d == 2:
            return f.at[:, pl.ds(cols - 4, 4)]
        return f.at[:, pl.ds(0, 4)]

    def target(self, j, b):
        if b == 2:
            return self.bufs[4 * j + b].at[:, pl.ds(4, 4)]
        if b == 3:
            return self.bufs[4 * j + b].at[:, pl.ds(0, 4)]
        return self.bufs[4 * j + b]

    def remote(self, j, d):
        return pltpu.make_async_remote_copy(
            src_ref=self.source(self.fields[j], d),
            dst_ref=self.target(j, d),
            send_sem=self.send_sem.at[j, d],
            recv_sem=self.recv_sem.at[j, d],
            device_id=self.peer[d],
            device_id_type=pl.DeviceIdType.MESH,
        )

    def start(self, extra=0):
        has, row, nrow, col, ncol = self.has, self.row, self.nrow, self.col, self.ncol
        barrier = pltpu.get_barrier_semaphore()
        for d in range(4):
            @pl.when(has[d])
            def _():
                pl.semaphore_signal(barrier, inc=1, device_id=self.peer[d], device_id_type=pl.DeviceIdType.MESH)

        count = (1 - row // (nrow - 1)) + (row + nrow - 1) // nrow + (1 - col // (ncol - 1)) + (col + ncol - 1) // ncol
        pl.semaphore_wait(barrier, count + extra)

        for j in range(len(self.fields)):
            for d in range(4):
                @pl.when(has[d])
                def _():
                    self.remote(j, d).start()

        @pl.when(jnp.logical_not(has[0] & has[1]))
        def _():
            self.zero_x[...] = jnp.zeros_like(self.zero_x)

        @pl.when(jnp.logical_not(has[2] & has[3]))
        def _():
            self.zero_y[...] = jnp.zeros_like(self.zero_y)

        for j in range(len(self.fields)):
            for b in range(4):
                @pl.when(jnp.logical_not(has[self.filler[b]]))
                def _():
                    zero = self.zero_x if b < 2 else self.zero_y
                    copy = pltpu.make_async_copy(zero, self.bufs[4 * j + b], self.zero_sem.at[j, b])
                    copy.start()
                    copy.wait()

    def finish(self):
        has = self.has
        for j in range(len(self.fields)):
            for d in range(4):
                @pl.when(has[d])
                def _():
                    self.remote(j, d).wait_send()
            for b in range(4):
                @pl.when(has[self.filler[b]])
                def _():
                    self.remote(j, b).wait_recv()


def exchange_io(nf, rows, cols, depth):
    shapes = []
    for _ in range(nf):
        shapes += [
            jax.ShapeDtypeStruct((4, cols, depth), jnp.float32),
            jax.ShapeDtypeStruct((4, cols, depth), jnp.float32),
            jax.ShapeDtypeStruct((rows, 8, depth), jnp.float32),
            jax.ShapeDtypeStruct((rows, 8, depth), jnp.float32),
        ]
    scratch = [
        pltpu.VMEM((4, cols, depth), jnp.float32),
        pltpu.VMEM((rows, 8, depth), jnp.float32),
        pltpu.SemaphoreType.DMA((nf, 4)),
        pltpu.SemaphoreType.DMA((nf, 4)),
        pltpu.SemaphoreType.DMA((nf, 4)),
    ]
    return shapes, scratch


def exchange_kernel(nf, gather, *refs):
    if not gather:
        ex = Exchange(refs[:nf], refs[nf : 5 * nf], *refs[5 * nf :])
        ex.start()
        ex.finish()
        return
    vel = refs[nf]
    bufs = refs[nf + 1 : 5 * nf + 1]
    full = refs[5 * nf + 1]
    ag_ss, ag_rs, ag_own, rl_top, rl_bot, rl_rs = refs[-6:]
    ex = Exchange(refs[:nf], bufs, *refs[5 * nf + 2 : -6])
    me, n = lax.axis_index("shot"), lax.axis_size("shot")
    up, down, far = lax.rem(me + 1, n), lax.rem(me + n - 1, n), lax.rem(me + 2, n)
    rows = vel.shape[0]
    half = rows // 2
    mesh = pl.DeviceIdType.MESH

    def at_rows(who):
        return full.at[pl.ds(pl.multiple_of(who * rows, rows), rows)]

    def remote(src, dst, k, recv_sem, peer):
        return pltpu.make_async_remote_copy(
            src_ref=src, dst_ref=dst, send_sem=ag_ss.at[k], recv_sem=recv_sem, device_id={"shot": peer}, device_id_type=mesh
        )

    to_up = remote(vel, at_rows(me), 0, ag_rs.at[me], up)
    to_down = remote(vel, at_rows(me), 1, ag_rs.at[me], down)
    relay_top = remote(vel.at[pl.ds(0, half)], rl_top, 2, rl_rs.at[0], up)
    relay_bot = remote(vel.at[pl.ds(half, half)], rl_bot, 3, rl_rs.at[1], down)
    fwd_top = remote(rl_top, at_rows(down).at[pl.ds(0, half)], 4, rl_rs.at[2], up)
    fwd_bot = remote(rl_bot, at_rows(up).at[pl.ds(half, half)], 5, rl_rs.at[3], down)

    barrier = pltpu.get_barrier_semaphore()
    for peer in (up, down):
        pl.semaphore_signal(barrier, inc=1, device_id={"shot": peer}, device_id_type=mesh)
    ex.start(extra=2)
    for copy in (to_up, to_down, relay_top, relay_bot):
        copy.start()
    own = pltpu.make_async_copy(vel, at_rows(me), ag_own)
    own.start()
    relay_top.wait_recv()
    relay_bot.wait_recv()
    fwd_top.start()
    fwd_bot.start()
    ex.finish()
    for copy in (to_up, to_down, relay_top, relay_bot, fwd_top, fwd_bot):
        copy.wait_send()
    own.wait()
    for src in (up, down):
        remote(vel, at_rows(src), 0, ag_rs.at[src], src).wait_recv()
    remote(rl_top, at_rows(far).at[pl.ds(0, half)], 4, rl_rs.at[2], down).wait_recv()
    remote(rl_bot, at_rows(far).at[pl.ds(half, half)], 5, rl_rs.at[3], up).wait_recv()


def exchange(fields, collective_id, velocity=None):
    nf = len(fields)
    rows, cols, depth = fields[0].shape
    any_spec = pl.BlockSpec(memory_space=pl.ANY)
    shapes, scratch = exchange_io(nf, rows, cols, depth)
    args = list(fields)
    gather = velocity is not None
    if gather:
        n = lax.axis_size("shot")
        args.append(velocity)
        shapes = shapes + [jax.ShapeDtypeStruct((n * velocity.shape[0],) + velocity.shape[1:], jnp.float32)]
        half_slab = (velocity.shape[0] // 2,) + velocity.shape[1:]
        scratch = scratch + [
            pltpu.SemaphoreType.DMA((6,)),
            pltpu.SemaphoreType.DMA((n,)),
            pltpu.SemaphoreType.DMA(()),
            pltpu.VMEM(half_slab, jnp.float32),
            pltpu.VMEM(half_slab, jnp.float32),
            pltpu.SemaphoreType.DMA((4,)),
        ]
    outs = pl.pallas_call(
        functools.partial(exchange_kernel, nf, gather),
        in_specs=[any_spec] * len(args),
        out_specs=[any_spec] * len(shapes),
        out_shape=shapes,
        scratch_shapes=scratch,
        compiler_params=pltpu.CompilerParams(collective_id=collective_id, has_side_effects=True),
        name=f"halo_exchange_{collective_id}",
    )(*args)
    halos = [outs[4 * j : 4 * j + 4] for j in range(nf)]
    if gather:
        return halos, outs[-1]
    return halos


class HaloSender:

    def __init__(self, ref, nblk, tb):
        self.ref, self.nblk, self.tb = ref, nblk, tb
        row, nrow = lax.axis_index("row"), lax.axis_size("row")
        col, ncol = lax.axis_index("col"), lax.axis_size("col")
        self.row, self.nrow, self.col, self.ncol = row, nrow, col, ncol
        self.has = (row < nrow - 1, row > 0, col < ncol - 1, col > 0)
        self.peer = ({"row": row + 1}, {"row": row - 1}, {"col": col + 1}, {"col": col - 1})
        self.filler = (1, 0, 3, 2)
        self.bufs = [ref[S.h_b + b] for b in range(4)]

    def copy(self, d, blk):
        ref, tb = self.ref, self.tb
        rows_here = pl.ds(pl.multiple_of(blk * tb, tb), tb)
        if d == 0:
            src, dst, sem = ref[S.stg_xlo], self.bufs[0], ref[S.h_ss].at[0, 0]
        elif d == 1:
            src, dst, sem = ref[S.stg_xhi], self.bufs[1], ref[S.h_ss].at[0, 1]
        elif d == 2:
            src, dst = ref[S.stg_ylo].at[rows_here], self.bufs[2].at[rows_here, pl.ds(4, 4)]
            sem = ref[S.h_ss].at[blk, 2]
        else:
            src, dst = ref[S.stg_yhi].at[rows_here], self.bufs[3].at[rows_here, pl.ds(0, 4)]
            sem = ref[S.h_ss].at[blk, 3]
        return pltpu.make_async_remote_copy(
            src_ref=src,
            dst_ref=dst,
            send_sem=sem,
            recv_sem=ref[S.h_rs].at[d],
            device_id=self.peer[d],
            device_id_type=pl.DeviceIdType.MESH,
        )

    def whole(self, b):
        ref = self.ref
        src = {0: ref[S.stg_xlo], 1: ref[S.stg_xhi], 2: ref[S.stg_ylo], 3: ref[S.stg_yhi]}[b]
        dst = {0: self.bufs[0], 1: self.bufs[1], 2: self.bufs[2].at[:, pl.ds(4, 4)], 3: self.bufs[3].at[:, pl.ds(0, 4)]}[b]
        return pltpu.make_async_remote_copy(
            src_ref=src,
            dst_ref=dst,
            send_sem=ref[S.h_ss].at[0, b],
            recv_sem=ref[S.h_rs].at[b],
            device_id=self.peer[b],
            device_id_type=pl.DeviceIdType.MESH,
        )

    def begin(self):
        ref, has, row, nrow, col, ncol = self.ref, self.has, self.row, self.nrow, self.col, self.ncol
        barrier = pltpu.get_barrier_semaphore()
        for d in range(4):
            @pl.when(has[d])
            def _():
                pl.semaphore_signal(barrier, inc=1, device_id=self.peer[d], device_id_type=pl.DeviceIdType.MESH)

        count = (1 - row // (nrow - 1)) + (row + nrow - 1) // nrow + (1 - col // (ncol - 1)) + (col + ncol - 1) // ncol
        pl.semaphore_wait(barrier, count)

        @pl.when(jnp.logical_not(has[0] & has[1]))
        def _():
            ref[S.h_zx][...] = jnp.zeros_like(ref[S.h_zx])

        @pl.when(jnp.logical_not(has[2] & has[3]))
        def _():
            ref[S.h_zy][...] = jnp.zeros_like(ref[S.h_zy])

        for b in range(4):
            @pl.when(jnp.logical_not(has[self.filler[b]]))
            def _():
                zero = ref[S.h_zx] if b < 2 else ref[S.h_zy]
                copy = pltpu.make_async_copy(zero, self.bufs[b], ref[S.h_zs].at[b])
                copy.start()
                copy.wait()

    def send_block(self, blk):
        ref, has, tb = self.ref, self.has, self.tb

        @pl.when(blk == 0)
        def _():
            ref[S.stg_xhi][...] = ref[S.o_a2][0:4]

        @pl.when(blk == self.nblk - 1)
        def _():
            ref[S.stg_xlo][...] = ref[S.o_a2][tb - 4 : tb]

        for d in (2, 3):
            @pl.when(has[d])
            def _():
                self.copy(d, blk).start()

        @pl.when(has[1] & (blk == 0))
        def _():
            self.copy(1, blk).start()

        @pl.when(has[0] & (blk == self.nblk - 1))
        def _():
            self.copy(0, blk).start()

    def finish(self):
        has = self.has
        for blk in range(self.nblk):
            for d in (2, 3):
                @pl.when(has[d])
                def _():
                    self.copy(d, blk).wait_send()

        @pl.when(has[1])
        def _():
            self.copy(1, 0).wait_send()

        @pl.when(has[0])
        def _():
            self.copy(0, self.nblk - 1).wait_send()

        for b in range(4):
            @pl.when(has[self.filler[b]])
            def _():
                self.whole(b).wait_recv()


class ReduceScatter:

    def __init__(self, ref, me, n):
        self.ref, self.me, self.n = ref, me, n
        self.up, self.down, self.far = lax.rem(me + 1, n), lax.rem(me + n - 1, n), lax.rem(me + 2, n)
        half = ref[S.slot_out].shape[1] // 2
        self.top, self.bot = pl.ds(0, half), pl.ds(half, half)

    def remote(self, src, dst, k, recv_sem, peer):
        return pltpu.make_async_remote_copy(
            src_ref=src,
            dst_ref=dst,
            send_sem=self.ref[S.rs_ss].at[k],
            recv_sem=recv_sem,
            device_id={"shot": peer},
            device_id_type=pl.DeviceIdType.MESH,
        )

    def direct(self, blk, k, peer):
        ref = self.ref
        return self.remote(ref[S.slot_out].at[blk], ref[S.slot_in].at[self.me], k, ref[S.rs_rs].at[self.me], peer)

    def relay_top(self):
        ref = self.ref
        src = ref[S.slot_out].at[self.far, self.top]
        return self.remote(src, ref[S.rl_top], 2, ref[S.rl_rs].at[0], self.up)

    def relay_bot(self):
        ref = self.ref
        src = ref[S.slot_out].at[self.far, self.bot]
        return self.remote(src, ref[S.rl_bot], 3, ref[S.rl_rs].at[1], self.down)

    def fwd_top(self):
        ref = self.ref
        dst = ref[S.slot_in].at[self.down, self.top]
        return self.remote(ref[S.rl_top], dst, 4, ref[S.rl_rs].at[2], self.up)

    def fwd_bot(self):
        ref = self.ref
        dst = ref[S.slot_in].at[self.up, self.bot]
        return self.remote(ref[S.rl_bot], dst, 5, ref[S.rl_rs].at[3], self.down)

    def begin(self):
        barrier = pltpu.get_barrier_semaphore()
        for peer in (self.up, self.down):
            pl.semaphore_signal(barrier, inc=1, device_id={"shot": peer}, device_id_type=pl.DeviceIdType.MESH)
        pl.semaphore_wait(barrier, 2)

    def at_step(self, step):
        @pl.when(step == 1)
        def _():
            self.direct(self.up, 0, self.up).start()

        @pl.when(step == 2)
        def _():
            self.relay_top().start()
            self.relay_bot().start()

        @pl.when(step == 3)
        def _():
            self.direct(self.down, 1, self.down).start()
            self.relay_top().wait_recv()
            self.relay_bot().wait_recv()
            self.fwd_top().start()
            self.fwd_bot().start()

    def finish(self):
        ref, me, n = self.ref, self.me, self.n
        own = pltpu.make_async_copy(ref[S.slot_out].at[me], ref[S.slot_in].at[me], ref[S.rs_own])
        own.start()
        self.direct(self.up, 0, self.up).wait_send()
        self.direct(self.down, 1, self.down).wait_send()
        self.relay_top().wait_send()
        self.relay_bot().wait_send()
        self.fwd_top().wait_send()
        self.fwd_bot().wait_send()
        own.wait()
        for src in (self.down, self.up):
            self.remote(ref[S.slot_out].at[src], ref[S.slot_in].at[src], 0, ref[S.rs_rs].at[src], src).wait_recv()
        far_in = ref[S.slot_in].at[self.far, self.top]
        self.remote(ref[S.rl_top], far_in, 4, ref[S.rl_rs].at[2], self.down).wait_recv()
        far_in = ref[S.slot_in].at[self.far, self.bot]
        self.remote(ref[S.rl_bot], far_in, 5, ref[S.rl_rs].at[3], self.up).wait_recv()

        slot_in = ref[S.slot_in]

        def row(r, carry):
            summed = slot_in[0, r]
            for s_ in range(1, n):
                summed = summed + slot_in[s_, r]
            ref[S.o_v][r] = summed
            return carry

        lax.fori_loop(0, slot_in.shape[1], row, 0)


def step_kernel(kind, names, nf_ex, *refs):
    ref = dict(zip(names, refs))
    if nf_ex:
        ex = Exchange(
            [ref[S.ex_f + j] for j in range(nf_ex)],
            [ref[S.ex_b + k] for k in range(4 * nf_ex)],
            *[ref[k] for k in (S.ex_zx, S.ex_zy, S.ex_ss, S.ex_rs, S.ex_zs)],
        )
    f_ref, pad = ref[S.f], ref[S.pad]
    tb, cols, depth = f_ref.shape
    n = pl.num_programs(0)
    step = pl.program_id(0)
    if kind == "adj2":
        me = lax.axis_index("shot")
        i = lax.rem(me + 1 + step, n)
        rs = ReduceScatter(ref, me, n)

        @pl.when(step == 0)
        def _():
            rs.begin()

        rs.at_step(step)
    elif kind == "wave2":
        i = lax.rem(step + n - 1, n)
    else:
        i = step

    if nf_ex:
        @pl.when(i == 0)
        def _():
            ex.start()

    lo = jnp.where(i == 0, ref[S.xlo][...], ref[S.flo][...])
    hi = jnp.where(i == n - 1, ref[S.xhi][...], ref[S.fhi][...])
    pad[0:4, 8 : 8 + cols, :] = lo
    pad[4 : 4 + tb, 8 : 8 + cols, :] = f_ref[...]
    pad[4 + tb : 8 + tb, 8 : 8 + cols, :] = hi
    pad[4 : 4 + tb, 0:8, :] = ref[S.ylo][...]
    pad[4 : 4 + tb, 8 + cols : 16 + cols, :] = ref[S.yhi][...]

    z_index = lax.broadcasted_iota(jnp.int32, (Y_CHUNK, depth), 1)
    y_index = lax.broadcasted_iota(jnp.int32, (Y_CHUNK, depth), 0)
    wave = kind in ("wave1", "wave2")
    if wave:
        src_ref = ref[S.src]
        src_x = src_ref[0] - lax.axis_index("row") * (tb * n) - i * tb
        src_y = src_ref[1] - lax.axis_index("col") * cols
        src_z = src_ref[2]
        amp = ref[S.amp][0 if kind == "wave1" else 1]

    def row(r, carry):
        for y0 in range(0, cols, Y_CHUNK):
            ys = pl.ds(y0, Y_CHUNK)
            pys = pl.ds(8 + y0, Y_CHUNK)
            c = pad[4 + r, pys, :]
            result = (3.0 * STENCIL[0]) * c
            for k in range(1, 5):
                along = pad[4 + r + k, pys, :] + pad[4 + r - k, pys, :]
                along = along + (
                    pad[4 + r, pl.ds(8 + y0 + k, Y_CHUNK), :]
                    + pad[4 + r, pl.ds(8 + y0 - k, Y_CHUNK), :]
                )
                zp = jnp.where(z_index < depth - k, pltpu.roll(c, depth - k, 1), 0.0)
                zm = jnp.where(z_index >= k, pltpu.roll(c, k, 1), 0.0)
                along = along + (zp + zm)
                result = result + STENCIL[k] * along
            v = ref[S.vel][r, ys, :]
            stiff = squared_courant * v * v
            prev = ref[S.prev][r, ys, :]
            out = 2.0 * c - prev + stiff * result
            if wave:
                at_rec = z_index == ref[S.rec][r, ys, :]
                hit = (r == src_x) & (y_index + y0 == src_y) & (z_index == src_z)
                out = out + jnp.where(hit, amp, 0.0)
                sel = jnp.where(at_rec, out, 0.0)
                folded = sel[:, 0:128]
                for t in range(128, depth, 128):
                    folded = folded + sel[:, t : t + 128]
                ref[S.fold][pl.ds(pl.multiple_of(r * cols + y0, Y_CHUNK), Y_CHUNK), :] = folded
                ref[S.o_dw][r, ys, :] = (out - 2.0 * c) + prev
                if kind == "wave1":
                    ref[S.o_f][r, ys, :] = out
            elif kind == "adjbulk":
                ref[S.o_f][r, ys, :] = out
            else:
                at_rec = z_index == ref[S.rec][r, ys, :]
                misfit = ref[S.pick][r, ys, :] - ref[S.obs][r, ys, :]
                out = out + jnp.where(at_rec, misfit, 0.0)
                ref[S.slot_out][i, r, ys, :] = ref[S.part][r, ys, :] + out * ref[S.dw][r, ys, :]
        return carry

    lax.fori_loop(0, tb, row, 0)
    if wave:
        ref[S.o_pick][...] = jnp.sum(ref[S.fold][...], axis=1, keepdims=True).reshape(ref[S.o_pick].shape)
    if kind == "wave2":
        sender = HaloSender(ref, n, tb)

        @pl.when(step == 0)
        def _():
            sender.begin()

        def inject(r, carry):
            for y0 in range(0, cols, Y_CHUNK):
                ys = pl.ds(y0, Y_CHUNK)
                at_rec = z_index == ref[S.rec][r, ys, :]
                misfit = ref[S.o_pick][r, ys, :] - ref[S.obs][r, ys, :]
                a2 = ref[S.a2raw][r, ys, :] + jnp.where(at_rec, misfit, 0.0)
                ref[S.o_a2][r, ys, :] = a2
                ref[S.o_part][r, ys, :] = a2 * ref[S.o_dw][r, ys, :]
                if y0 == 0:
                    ref[S.stg_yhi][i * tb + r] = a2[0:4]
                if y0 == cols - Y_CHUNK:
                    ref[S.stg_ylo][i * tb + r] = a2[Y_CHUNK - 4 : Y_CHUNK]
            return carry

        lax.fori_loop(0, tb, inject, 0)
        sender.send_block(i)

        @pl.when(step == n - 1)
        def _():
            sender.finish()

    if nf_ex:
        @pl.when(i == n - 1)
        def _():
            ex.finish()
    if kind == "adj2":
        @pl.when(step == n - 1)
        def _():
            rs.finish()


def leap(kind, f, xlo, xhi, ylo, yhi, prev, vel, extra, exchanged=(), collective_id=None):
    rows, cols, depth = f.shape
    tb = ROWS_PER_STEP
    nblk = rows // tb
    grid = (nblk,)
    nq = rows // 4
    if kind == "adj2":
        def at(fn):
            return lambda i: fn(lax.rem(lax.axis_index("shot") + 1 + i, nblk))

        fixed = at
    elif kind == "wave2":
        def at(fn):
            return lambda i: fn(lax.rem(i + nblk - 1, nblk))

        def fixed(fn):
            return fn
    else:
        def at(fn):
            return fn

        fixed = at
    block = pl.BlockSpec((tb, cols, depth), at(lambda i: (i, 0, 0)))
    lo_spec = pl.BlockSpec((4, cols, depth), at(lambda i: (jnp.maximum(2 * i - 1, 0), 0, 0)))
    hi_spec = pl.BlockSpec((4, cols, depth), at(lambda i: (jnp.minimum(2 * i + 2, nq - 1), 0, 0)))
    whole4 = pl.BlockSpec((4, cols, depth), fixed(lambda i: (0, 0, 0)))
    yspec = pl.BlockSpec((tb, 8, depth), at(lambda i: (i, 0, 0)))
    col1 = pl.BlockSpec((tb, cols, 1), at(lambda i: (i, 0, 0)))
    slab = pl.BlockSpec((tb, cols, depth), fixed(lambda i: (0, 0, 0)))
    smem = pl.BlockSpec(memory_space=pltpu.SMEM)
    any_spec = pl.BlockSpec(memory_space=pl.ANY)
    field = jax.ShapeDtypeStruct((rows, cols, depth), jnp.float32)
    picked = jax.ShapeDtypeStruct((rows, cols, 1), jnp.float32)
    spec_of = {S.src: smem, S.amp: smem, S.rec: col1, S.mis: col1, S.obs: col1, S.pick: col1, S.vslab: slab, S.mom: slab, S.mass: slab}

    names = [S.f, S.flo, S.fhi, S.xlo, S.xhi, S.ylo, S.yhi, S.prev, S.vel]
    in_specs = [block, lo_spec, hi_spec, whole4, whole4, yspec, yspec, block, block]
    args = [f, f, f, xlo, xhi, ylo, yhi, prev, vel]
    for key, value in extra.items():
        names.append(key)
        in_specs.append(spec_of.get(key, block))
        args.append(value)
    nf_ex = len(exchanged)
    for j, g in enumerate(exchanged):
        names.append(S.ex_f + j)
        in_specs.append(any_spec)
        args.append(g)

    outs = {
        "wave1": [(S.o_f, field, block), (S.o_dw, field, block), (S.o_pick, picked, col1)],
        "wave2": [(S.o_dw, field, block), (S.o_pick, picked, col1), (S.o_a2, field, block), (S.o_part, field, block)],
        "adjbulk": [(S.o_f, field, block)],
        "adj2": [(S.o_v, jax.ShapeDtypeStruct((tb, cols, depth), jnp.float32), slab)],
    }[kind]
    names += [o[0] for o in outs]
    out_shape = [o[1] for o in outs]
    out_specs = [o[2] for o in outs]
    scratch = [pltpu.VMEM((tb + 8, cols + 16, depth), jnp.float32)]
    names.append(S.pad)
    if kind in ("wave1", "wave2"):
        scratch.append(pltpu.VMEM((tb * cols, 128), jnp.float32))
        names.append(S.fold)
    if kind == "adj2":
        names += [S.slot_out, S.slot_in, S.rs_ss, S.rs_rs, S.rs_own, S.rl_top, S.rl_bot, S.rl_rs]
        scratch += [
            pltpu.VMEM((nblk, tb, cols, depth), jnp.float32),
            pltpu.VMEM((nblk, tb, cols, depth), jnp.float32),
            pltpu.SemaphoreType.DMA((6,)),
            pltpu.SemaphoreType.DMA((nblk,)),
            pltpu.SemaphoreType.DMA(()),
            pltpu.VMEM((tb // 2, cols, depth), jnp.float32),
            pltpu.VMEM((tb // 2, cols, depth), jnp.float32),
            pltpu.SemaphoreType.DMA((4,)),
        ]
        params = pltpu.CompilerParams(
            collective_id=collective_id, has_side_effects=True, vmem_limit_bytes=60 * 1024 * 1024
        )
    elif kind == "wave2":
        h_shapes, _ = exchange_io(1, rows, cols, depth)
        names = names[: len(names) - len(scratch)]
        names += [S.h_b + m for m in range(4)]
        names += [S.pad, S.fold]
        names += [S.stg_xlo, S.stg_xhi, S.stg_ylo, S.stg_yhi, S.h_zx, S.h_zy, S.h_ss, S.h_rs, S.h_zs]
        out_shape += h_shapes
        out_specs += [any_spec] * 4
        scratch += [
            pltpu.VMEM((4, cols, depth), jnp.float32),
            pltpu.VMEM((4, cols, depth), jnp.float32),
            pltpu.VMEM((rows, 4, depth), jnp.float32),
            pltpu.VMEM((rows, 4, depth), jnp.float32),
            pltpu.VMEM((4, cols, depth), jnp.float32),
            pltpu.VMEM((rows, 8, depth), jnp.float32),
            pltpu.SemaphoreType.DMA((rows // tb, 4)),
            pltpu.SemaphoreType.DMA((4,)),
            pltpu.SemaphoreType.DMA((4,)),
        ]
        params = pltpu.CompilerParams(
            collective_id=collective_id, has_side_effects=True, vmem_limit_bytes=60 * 1024 * 1024
        )
    elif nf_ex:
        ex_shapes, ex_scratch = exchange_io(nf_ex, rows, cols, depth)
        k = len(outs)
        names = names[: len(names) - len(scratch)]
        names += [S.ex_b + m for m in range(4 * nf_ex)]
        names += [S.pad, S.fold][: len(scratch)]
        names += [S.ex_zx, S.ex_zy, S.ex_ss, S.ex_rs, S.ex_zs]
        out_shape += ex_shapes
        out_specs += [any_spec] * len(ex_shapes)
        scratch += ex_scratch
        params = pltpu.CompilerParams(
            collective_id=collective_id, has_side_effects=True, vmem_limit_bytes=60 * 1024 * 1024
        )
    else:
        params = pltpu.CompilerParams(vmem_limit_bytes=60 * 1024 * 1024)
    n_big = sum(1 for sp in in_specs if sp is block) + 1 + sum(1 for sp in out_specs if sp is block)
    cost = pl.CostEstimate(
        flops=60 * rows * cols * depth,
        transcendentals=0,
        bytes_accessed=4 * rows * cols * depth * n_big,
    )
    result = pl.pallas_call(
        functools.partial(step_kernel, kind, tuple(names), nf_ex),
        grid=grid,
        in_specs=in_specs,
        out_specs=out_specs,
        out_shape=out_shape,
        scratch_shapes=scratch,
        compiler_params=params,
        cost_estimate=cost,
        name=f"leap_{kind}",
    )(*args)
    if kind == "wave2":
        return result[: len(outs)], result[len(outs) :]
    if nf_ex:
        own = result[: len(outs)]
        ex = result[len(outs) :]
        return own, [ex[4 * j : 4 * j + 4] for j in range(nf_ex)]
    return result


def on_device(
    velocity,
    momentum,
    mass_diag,
    u_prev,
    u_cur,
    adj_next,
    adj_cur,
    observed,
    rec_depth,
    src_cell,
    wavelet,
):
    oldest = u_prev[0]
    present = u_cur[0]
    adj_later = adj_next[0]
    adj_now = adj_cur[0]
    rec = rec_depth[0][:, :, None]
    cell = src_cell[0]
    src = src_cell[0]
    amp = wavelet[0]

    (wave_h, adj_h), full_velocity = exchange([present, adj_now], 1, velocity)
    advanced, dw1, pick_adv = leap(
        "wave1", present, *wave_h, oldest, full_velocity, {S.rec: rec, S.src: src, S.amp: amp}
    )
    (adj_bulk,), (adv_h,) = leap(
        "adjbulk", adj_now, *adj_h, adj_later, full_velocity, {}, exchanged=[advanced], collective_id=2
    )
    (dw2, pick_far, adj_two, part), adj_two_h = leap(
        "wave2",
        advanced,
        *adv_h,
        present,
        full_velocity,
        {S.rec: rec, S.src: src, S.amp: amp, S.a2raw: adj_bulk, S.obs: observed[0, 1][:, :, None]},
        collective_id=3,
    )
    (summed,) = leap(
        "adj2",
        adj_two,
        *adj_two_h,
        adj_now,
        full_velocity,
        {
            S.rec: rec,
            S.pick: pick_adv,
            S.obs: observed[0, 0][:, :, None],
            S.dw: dw1,
            S.part: part,
        },
        collective_id=0,
    )
    gradient = 2.0 / velocity * summed
    p_half = momentum - 0.5 * leap_step * gradient
    v_new = velocity + leap_step * p_half / mass_diag
    return (v_new, p_half)


def solution(mesh):
    return jax.shard_map(
        on_device,
        mesh=mesh,
        in_specs=(
            P(("row", "shot"), "col", None),
            P(("row", "shot"), "col", None),
            P(("row", "shot"), "col", None),
            P("shot", "row", "col", None),
            P("shot", "row", "col", None),
            P("shot", "row", "col", None),
            P("shot", "row", "col", None),
            P("shot", None, "row", "col"),
            P("shot", "row", "col"),
            P("shot", None),
            P("shot", None),
        ),
        out_specs=(P(("row", "shot"), "col", None), P(("row", "shot"), "col", None)),
        check_vma=False,
    )
```

```python
import functools

import jax
import jax.numpy as jnp
from jax import lax
from jax.experimental import pallas as pl
from jax.experimental.pallas import tpu as pltpu
from jax.sharding import PartitionSpec as P

STENCIL = (-205.0 / 72.0, 8.0 / 5.0, -1.0 / 5.0, 8.0 / 315.0, -1.0 / 560.0)
squared_courant = 0.012
leap_step = 0.2

class S:
    a2raw = 0
    amp = 1
    dw = 2
    ex_rs = 3
    ex_ss = 4
    ex_zs = 5
    ex_zx = 6
    ex_zy = 7
    f = 8
    fhi = 9
    flo = 10
    fold = 11
    h_rs = 12
    h_ss = 13
    h_zs = 14
    h_zx = 15
    h_zy = 16
    mass = 17
    mis = 18
    mom = 19
    o_a2 = 20
    o_dw = 21
    o_f = 22
    o_p = 23
    o_part = 24
    o_pick = 25
    o_v = 26
    obs = 27
    pad = 28
    part = 29
    prev = 30
    rec = 31
    rs_own = 32
    rs_rs = 33
    rs_ss = 34
    slot_in = 35
    slot_out = 36
    src = 37
    stg_xhi = 38
    stg_xlo = 39
    stg_yhi = 40
    stg_ylo = 41
    vel = 42
    vslab = 43
    xhi = 44
    xlo = 45
    yhi = 46
    ylo = 47
    rl_top = 90
    rl_bot = 91
    rl_rs = 92
    ex_f = 100
    ex_b = 110
    h_b = 130
    pick = 140


ROWS_PER_STEP = 8
Y_CHUNK = 16


class Exchange:

    def __init__(self, fields, bufs, zero_x, zero_y, send_sem, recv_sem, zero_sem):
        self.fields, self.bufs = fields, bufs
        self.zero_x, self.zero_y = zero_x, zero_y
        self.send_sem, self.recv_sem, self.zero_sem = send_sem, recv_sem, zero_sem
        row, nrow = lax.axis_index("row"), lax.axis_size("row")
        col, ncol = lax.axis_index("col"), lax.axis_size("col")
        self.row, self.nrow, self.col, self.ncol = row, nrow, col, ncol
        self.has = (row < nrow - 1, row > 0, col < ncol - 1, col > 0)
        self.peer = ({"row": row + 1}, {"row": row - 1}, {"col": col + 1}, {"col": col - 1})
        self.filler = (1, 0, 3, 2)

    def source(self, f, d):
        rows, cols, _ = f.shape
        if d == 0:
            return f.at[pl.ds(rows - 4, 4)]
        if d == 1:
            return f.at[pl.ds(0, 4)]
        if d == 2:
            return f.at[:, pl.ds(cols - 4, 4)]
        return f.at[:, pl.ds(0, 4)]

    def target(self, j, b):
        if b == 2:
            return self.bufs[4 * j + b].at[:, pl.ds(4, 4)]
        if b == 3:
            return self.bufs[4 * j + b].at[:, pl.ds(0, 4)]
        return self.bufs[4 * j + b]

    def remote(self, j, d):
        return pltpu.make_async_remote_copy(
            src_ref=self.source(self.fields[j], d),
            dst_ref=self.target(j, d),
            send_sem=self.send_sem.at[j, d],
            recv_sem=self.recv_sem.at[j, d],
            device_id=self.peer[d],
            device_id_type=pl.DeviceIdType.MESH,
        )

    def start(self, extra=0):
        has, row, nrow, col, ncol = self.has, self.row, self.nrow, self.col, self.ncol
        barrier = pltpu.get_barrier_semaphore()
        for d in range(4):
            @pl.when(has[d])
            def _():
                pl.semaphore_signal(barrier, inc=1, device_id=self.peer[d], device_id_type=pl.DeviceIdType.MESH)

        count = (1 - row // (nrow - 1)) + (row + nrow - 1) // nrow + (1 - col // (ncol - 1)) + (col + ncol - 1) // ncol
        pl.semaphore_wait(barrier, count + extra)

        for j in range(len(self.fields)):
            for d in range(4):
                @pl.when(has[d])
                def _():
                    self.remote(j, d).start()

        @pl.when(jnp.logical_not(has[0] & has[1]))
        def _():
            self.zero_x[...] = jnp.zeros_like(self.zero_x)

        @pl.when(jnp.logical_not(has[2] & has[3]))
        def _():
            self.zero_y[...] = jnp.zeros_like(self.zero_y)

        for j in range(len(self.fields)):
            for b in range(4):
                @pl.when(jnp.logical_not(has[self.filler[b]]))
                def _():
                    zero = self.zero_x if b < 2 else self.zero_y
                    copy = pltpu.make_async_copy(zero, self.bufs[4 * j + b], self.zero_sem.at[j, b])
                    copy.start()
                    copy.wait()

    def finish(self):
        has = self.has
        for j in range(len(self.fields)):
            for d in range(4):
                @pl.when(has[d])
                def _():
                    self.remote(j, d).wait_send()
            for b in range(4):
                @pl.when(has[self.filler[b]])
                def _():
                    self.remote(j, b).wait_recv()


def exchange_io(nf, rows, cols, depth):
    shapes = []
    for _ in range(nf):
        shapes += [
            jax.ShapeDtypeStruct((4, cols, depth), jnp.float32),
            jax.ShapeDtypeStruct((4, cols, depth), jnp.float32),
            jax.ShapeDtypeStruct((rows, 8, depth), jnp.float32),
            jax.ShapeDtypeStruct((rows, 8, depth), jnp.float32),
        ]
    scratch = [
        pltpu.VMEM((4, cols, depth), jnp.float32),
        pltpu.VMEM((rows, 8, depth), jnp.float32),
        pltpu.SemaphoreType.DMA((nf, 4)),
        pltpu.SemaphoreType.DMA((nf, 4)),
        pltpu.SemaphoreType.DMA((nf, 4)),
    ]
    return shapes, scratch


def exchange_kernel(nf, gather, *refs):
    if not gather:
        ex = Exchange(refs[:nf], refs[nf : 5 * nf], *refs[5 * nf :])
        ex.start()
        ex.finish()
        return
    vel = refs[nf]
    bufs = refs[nf + 1 : 5 * nf + 1]
    full = refs[5 * nf + 1]
    ag_ss, ag_rs, ag_own = refs[-3:]
    ex = Exchange(refs[:nf], bufs, *refs[5 * nf + 2 : -3])
    me, n = lax.axis_index("shot"), lax.axis_size("shot")
    rows = vel.shape[0]
    barrier = pltpu.get_barrier_semaphore()
    for d in range(1, n):
        pl.semaphore_signal(barrier, inc=1, device_id={"shot": lax.rem(me + d, n)}, device_id_type=pl.DeviceIdType.MESH)

    def send(d):
        peer = lax.rem(me + d, n)
        return pltpu.make_async_remote_copy(
            src_ref=vel,
            dst_ref=full.at[pl.ds(pl.multiple_of(me * rows, rows), rows)],
            send_sem=ag_ss.at[d],
            recv_sem=ag_rs.at[me],
            device_id={"shot": peer},
            device_id_type=pl.DeviceIdType.MESH,
        )

    ex.start(extra=n - 1)
    for d in range(1, n):
        send(d).start()
    own = pltpu.make_async_copy(vel, full.at[pl.ds(pl.multiple_of(me * rows, rows), rows)], ag_own)
    own.start()
    ex.finish()
    for d in range(1, n):
        send(d).wait_send()
    own.wait()
    for d in range(1, n):
        src = lax.rem(me + d, n)
        pltpu.make_async_remote_copy(
            src_ref=vel,
            dst_ref=full.at[pl.ds(pl.multiple_of(src * rows, rows), rows)],
            send_sem=ag_ss.at[d],
            recv_sem=ag_rs.at[src],
            device_id={"shot": src},
            device_id_type=pl.DeviceIdType.MESH,
        ).wait_recv()


def exchange(fields, collective_id, velocity=None):
    nf = len(fields)
    rows, cols, depth = fields[0].shape
    any_spec = pl.BlockSpec(memory_space=pl.ANY)
    shapes, scratch = exchange_io(nf, rows, cols, depth)
    args = list(fields)
    gather = velocity is not None
    if gather:
        n = lax.axis_size("shot")
        args.append(velocity)
        shapes = shapes + [jax.ShapeDtypeStruct((n * velocity.shape[0],) + velocity.shape[1:], jnp.float32)]
        scratch = scratch + [pltpu.SemaphoreType.DMA((n,)), pltpu.SemaphoreType.DMA((n,)), pltpu.SemaphoreType.DMA(())]
    outs = pl.pallas_call(
        functools.partial(exchange_kernel, nf, gather),
        in_specs=[any_spec] * len(args),
        out_specs=[any_spec] * len(shapes),
        out_shape=shapes,
        scratch_shapes=scratch,
        compiler_params=pltpu.CompilerParams(collective_id=collective_id, has_side_effects=True),
        name=f"halo_exchange_{collective_id}",
    )(*args)
    halos = [outs[4 * j : 4 * j + 4] for j in range(nf)]
    if gather:
        return halos, outs[-1]
    return halos


class HaloSender:

    def __init__(self, ref, nblk, tb):
        self.ref, self.nblk, self.tb = ref, nblk, tb
        row, nrow = lax.axis_index("row"), lax.axis_size("row")
        col, ncol = lax.axis_index("col"), lax.axis_size("col")
        self.row, self.nrow, self.col, self.ncol = row, nrow, col, ncol
        self.has = (row < nrow - 1, row > 0, col < ncol - 1, col > 0)
        self.peer = ({"row": row + 1}, {"row": row - 1}, {"col": col + 1}, {"col": col - 1})
        self.filler = (1, 0, 3, 2)
        self.bufs = [ref[S.h_b + b] for b in range(4)]

    def copy(self, d, blk):
        ref, tb = self.ref, self.tb
        rows_here = pl.ds(pl.multiple_of(blk * tb, tb), tb)
        if d == 0:
            src, dst, sem = ref[S.stg_xlo], self.bufs[0], ref[S.h_ss].at[0, 0]
        elif d == 1:
            src, dst, sem = ref[S.stg_xhi], self.bufs[1], ref[S.h_ss].at[0, 1]
        elif d == 2:
            src, dst = ref[S.stg_ylo].at[rows_here], self.bufs[2].at[rows_here, pl.ds(4, 4)]
            sem = ref[S.h_ss].at[blk, 2]
        else:
            src, dst = ref[S.stg_yhi].at[rows_here], self.bufs[3].at[rows_here, pl.ds(0, 4)]
            sem = ref[S.h_ss].at[blk, 3]
        return pltpu.make_async_remote_copy(
            src_ref=src,
            dst_ref=dst,
            send_sem=sem,
            recv_sem=ref[S.h_rs].at[d],
            device_id=self.peer[d],
            device_id_type=pl.DeviceIdType.MESH,
        )

    def whole(self, b):
        ref = self.ref
        src = {0: ref[S.stg_xlo], 1: ref[S.stg_xhi], 2: ref[S.stg_ylo], 3: ref[S.stg_yhi]}[b]
        dst = {0: self.bufs[0], 1: self.bufs[1], 2: self.bufs[2].at[:, pl.ds(4, 4)], 3: self.bufs[3].at[:, pl.ds(0, 4)]}[b]
        return pltpu.make_async_remote_copy(
            src_ref=src,
            dst_ref=dst,
            send_sem=ref[S.h_ss].at[0, b],
            recv_sem=ref[S.h_rs].at[b],
            device_id=self.peer[b],
            device_id_type=pl.DeviceIdType.MESH,
        )

    def begin(self):
        ref, has, row, nrow, col, ncol = self.ref, self.has, self.row, self.nrow, self.col, self.ncol
        barrier = pltpu.get_barrier_semaphore()
        for d in range(4):
            @pl.when(has[d])
            def _():
                pl.semaphore_signal(barrier, inc=1, device_id=self.peer[d], device_id_type=pl.DeviceIdType.MESH)

        count = (1 - row // (nrow - 1)) + (row + nrow - 1) // nrow + (1 - col // (ncol - 1)) + (col + ncol - 1) // ncol
        pl.semaphore_wait(barrier, count)

        @pl.when(jnp.logical_not(has[0] & has[1]))
        def _():
            ref[S.h_zx][...] = jnp.zeros_like(ref[S.h_zx])

        @pl.when(jnp.logical_not(has[2] & has[3]))
        def _():
            ref[S.h_zy][...] = jnp.zeros_like(ref[S.h_zy])

        for b in range(4):
            @pl.when(jnp.logical_not(has[self.filler[b]]))
            def _():
                zero = ref[S.h_zx] if b < 2 else ref[S.h_zy]
                copy = pltpu.make_async_copy(zero, self.bufs[b], ref[S.h_zs].at[b])
                copy.start()
                copy.wait()

    def send_block(self, blk):
        ref, has, tb = self.ref, self.has, self.tb

        @pl.when(blk == 0)
        def _():
            ref[S.stg_xhi][...] = ref[S.o_a2][0:4]

        @pl.when(blk == self.nblk - 1)
        def _():
            ref[S.stg_xlo][...] = ref[S.o_a2][tb - 4 : tb]

        for d in (2, 3):
            @pl.when(has[d])
            def _():
                self.copy(d, blk).start()

        @pl.when(has[1] & (blk == 0))
        def _():
            self.copy(1, blk).start()

        @pl.when(has[0] & (blk == self.nblk - 1))
        def _():
            self.copy(0, blk).start()

    def finish(self):
        has = self.has
        for blk in range(self.nblk):
            for d in (2, 3):
                @pl.when(has[d])
                def _():
                    self.copy(d, blk).wait_send()

        @pl.when(has[1])
        def _():
            self.copy(1, 0).wait_send()

        @pl.when(has[0])
        def _():
            self.copy(0, self.nblk - 1).wait_send()

        for b in range(4):
            @pl.when(has[self.filler[b]])
            def _():
                self.whole(b).wait_recv()


class ReduceScatter:

    def __init__(self, ref, me, n):
        self.ref, self.me, self.n = ref, me, n
        self.up, self.down, self.far = lax.rem(me + 1, n), lax.rem(me + n - 1, n), lax.rem(me + 2, n)
        half = ref[S.slot_out].shape[1] // 2
        self.top, self.bot = pl.ds(0, half), pl.ds(half, half)

    def remote(self, src, dst, k, recv_sem, peer):
        return pltpu.make_async_remote_copy(
            src_ref=src,
            dst_ref=dst,
            send_sem=self.ref[S.rs_ss].at[k],
            recv_sem=recv_sem,
            device_id={"shot": peer},
            device_id_type=pl.DeviceIdType.MESH,
        )

    def direct(self, blk, k, peer):
        ref = self.ref
        return self.remote(ref[S.slot_out].at[blk], ref[S.slot_in].at[self.me], k, ref[S.rs_rs].at[self.me], peer)

    def relay_top(self):
        ref = self.ref
        src = ref[S.slot_out].at[self.far, self.top]
        return self.remote(src, ref[S.rl_top], 2, ref[S.rl_rs].at[0], self.up)

    def relay_bot(self):
        ref = self.ref
        src = ref[S.slot_out].at[self.far, self.bot]
        return self.remote(src, ref[S.rl_bot], 3, ref[S.rl_rs].at[1], self.down)

    def fwd_top(self):
        ref = self.ref
        dst = ref[S.slot_in].at[self.down, self.top]
        return self.remote(ref[S.rl_top], dst, 4, ref[S.rl_rs].at[2], self.up)

    def fwd_bot(self):
        ref = self.ref
        dst = ref[S.slot_in].at[self.up, self.bot]
        return self.remote(ref[S.rl_bot], dst, 5, ref[S.rl_rs].at[3], self.down)

    def begin(self):
        barrier = pltpu.get_barrier_semaphore()
        for peer in (self.up, self.down):
            pl.semaphore_signal(barrier, inc=1, device_id={"shot": peer}, device_id_type=pl.DeviceIdType.MESH)
        pl.semaphore_wait(barrier, 2)

    def at_step(self, step):
        @pl.when(step == 1)
        def _():
            self.direct(self.up, 0, self.up).start()

        @pl.when(step == 2)
        def _():
            self.relay_top().start()
            self.relay_bot().start()

        @pl.when(step == 3)
        def _():
            self.direct(self.down, 1, self.down).start()
            self.relay_top().wait_recv()
            self.relay_bot().wait_recv()
            self.fwd_top().start()
            self.fwd_bot().start()

    def finish(self):
        ref, me, n = self.ref, self.me, self.n
        own = pltpu.make_async_copy(ref[S.slot_out].at[me], ref[S.slot_in].at[me], ref[S.rs_own])
        own.start()
        self.direct(self.up, 0, self.up).wait_send()
        self.direct(self.down, 1, self.down).wait_send()
        self.relay_top().wait_send()
        self.relay_bot().wait_send()
        self.fwd_top().wait_send()
        self.fwd_bot().wait_send()
        own.wait()
        for src in (self.down, self.up):
            self.remote(ref[S.slot_out].at[src], ref[S.slot_in].at[src], 0, ref[S.rs_rs].at[src], src).wait_recv()
        far_in = ref[S.slot_in].at[self.far, self.top]
        self.remote(ref[S.rl_top], far_in, 4, ref[S.rl_rs].at[2], self.down).wait_recv()
        far_in = ref[S.slot_in].at[self.far, self.bot]
        self.remote(ref[S.rl_bot], far_in, 5, ref[S.rl_rs].at[3], self.up).wait_recv()

        slot_in = ref[S.slot_in]

        def row(r, carry):
            summed = slot_in[0, r]
            for s_ in range(1, n):
                summed = summed + slot_in[s_, r]
            ref[S.o_v][r] = summed
            return carry

        lax.fori_loop(0, slot_in.shape[1], row, 0)


def step_kernel(kind, names, nf_ex, *refs):
    ref = dict(zip(names, refs))
    if nf_ex:
        ex = Exchange(
            [ref[S.ex_f + j] for j in range(nf_ex)],
            [ref[S.ex_b + k] for k in range(4 * nf_ex)],
            *[ref[k] for k in (S.ex_zx, S.ex_zy, S.ex_ss, S.ex_rs, S.ex_zs)],
        )
    f_ref, pad = ref[S.f], ref[S.pad]
    tb, cols, depth = f_ref.shape
    n = pl.num_programs(0)
    step = pl.program_id(0)
    if kind == "adj2":
        me = lax.axis_index("shot")
        i = lax.rem(me + 1 + step, n)
        rs = ReduceScatter(ref, me, n)

        @pl.when(step == 0)
        def _():
            rs.begin()

        rs.at_step(step)
    elif kind == "wave2":
        i = lax.rem(step + n - 1, n)
    else:
        i = step

    if nf_ex:
        @pl.when(i == 0)
        def _():
            ex.start()

    lo = jnp.where(i == 0, ref[S.xlo][...], ref[S.flo][...])
    hi = jnp.where(i == n - 1, ref[S.xhi][...], ref[S.fhi][...])
    pad[0:4, 8 : 8 + cols, :] = lo
    pad[4 : 4 + tb, 8 : 8 + cols, :] = f_ref[...]
    pad[4 + tb : 8 + tb, 8 : 8 + cols, :] = hi
    pad[4 : 4 + tb, 0:8, :] = ref[S.ylo][...]
    pad[4 : 4 + tb, 8 + cols : 16 + cols, :] = ref[S.yhi][...]

    z_index = lax.broadcasted_iota(jnp.int32, (Y_CHUNK, depth), 1)
    y_index = lax.broadcasted_iota(jnp.int32, (Y_CHUNK, depth), 0)
    wave = kind in ("wave1", "wave2")
    if wave:
        src_ref = ref[S.src]
        src_x = src_ref[0] - lax.axis_index("row") * (tb * n) - i * tb
        src_y = src_ref[1] - lax.axis_index("col") * cols
        src_z = src_ref[2]
        amp = ref[S.amp][0 if kind == "wave1" else 1]

    def row(r, carry):
        for y0 in range(0, cols, Y_CHUNK):
            ys = pl.ds(y0, Y_CHUNK)
            pys = pl.ds(8 + y0, Y_CHUNK)
            c = pad[4 + r, pys, :]
            result = (3.0 * STENCIL[0]) * c
            for k in range(1, 5):
                along = pad[4 + r + k, pys, :] + pad[4 + r - k, pys, :]
                along = along + (
                    pad[4 + r, pl.ds(8 + y0 + k, Y_CHUNK), :]
                    + pad[4 + r, pl.ds(8 + y0 - k, Y_CHUNK), :]
                )
                zp = jnp.where(z_index < depth - k, pltpu.roll(c, depth - k, 1), 0.0)
                zm = jnp.where(z_index >= k, pltpu.roll(c, k, 1), 0.0)
                along = along + (zp + zm)
                result = result + STENCIL[k] * along
            v = ref[S.vel][r, ys, :]
            stiff = squared_courant * v * v
            prev = ref[S.prev][r, ys, :]
            out = 2.0 * c - prev + stiff * result
            if wave:
                at_rec = z_index == ref[S.rec][r, ys, :]
                hit = (r == src_x) & (y_index + y0 == src_y) & (z_index == src_z)
                out = out + jnp.where(hit, amp, 0.0)
                sel = jnp.where(at_rec, out, 0.0)
                folded = sel[:, 0:128]
                for t in range(128, depth, 128):
                    folded = folded + sel[:, t : t + 128]
                ref[S.fold][pl.ds(pl.multiple_of(r * cols + y0, Y_CHUNK), Y_CHUNK), :] = folded
                ref[S.o_dw][r, ys, :] = (out - 2.0 * c) + prev
                if kind == "wave1":
                    ref[S.o_f][r, ys, :] = out
            elif kind == "adjbulk":
                ref[S.o_f][r, ys, :] = out
            else:
                at_rec = z_index == ref[S.rec][r, ys, :]
                misfit = ref[S.pick][r, ys, :] - ref[S.obs][r, ys, :]
                out = out + jnp.where(at_rec, misfit, 0.0)
                ref[S.slot_out][i, r, ys, :] = ref[S.part][r, ys, :] + out * ref[S.dw][r, ys, :]
        return carry

    lax.fori_loop(0, tb, row, 0)
    if wave:
        ref[S.o_pick][...] = jnp.sum(ref[S.fold][...], axis=1, keepdims=True).reshape(ref[S.o_pick].shape)
    if kind == "wave2":
        sender = HaloSender(ref, n, tb)

        @pl.when(step == 0)
        def _():
            sender.begin()

        def inject(r, carry):
            for y0 in range(0, cols, Y_CHUNK):
                ys = pl.ds(y0, Y_CHUNK)
                at_rec = z_index == ref[S.rec][r, ys, :]
                misfit = ref[S.o_pick][r, ys, :] - ref[S.obs][r, ys, :]
                a2 = ref[S.a2raw][r, ys, :] + jnp.where(at_rec, misfit, 0.0)
                ref[S.o_a2][r, ys, :] = a2
                ref[S.o_part][r, ys, :] = a2 * ref[S.o_dw][r, ys, :]
                if y0 == 0:
                    ref[S.stg_yhi][i * tb + r] = a2[0:4]
                if y0 == cols - Y_CHUNK:
                    ref[S.stg_ylo][i * tb + r] = a2[Y_CHUNK - 4 : Y_CHUNK]
            return carry

        lax.fori_loop(0, tb, inject, 0)
        sender.send_block(i)

        @pl.when(step == n - 1)
        def _():
            sender.finish()

    if nf_ex:
        @pl.when(i == n - 1)
        def _():
            ex.finish()
    if kind == "adj2":
        @pl.when(step == n - 1)
        def _():
            rs.finish()


def leap(kind, f, xlo, xhi, ylo, yhi, prev, vel, extra, exchanged=(), collective_id=None):
    rows, cols, depth = f.shape
    tb = ROWS_PER_STEP
    nblk = rows // tb
    grid = (nblk,)
    nq = rows // 4
    if kind == "adj2":
        def at(fn):
            return lambda i: fn(lax.rem(lax.axis_index("shot") + 1 + i, nblk))

        fixed = at
    elif kind == "wave2":
        def at(fn):
            return lambda i: fn(lax.rem(i + nblk - 1, nblk))

        def fixed(fn):
            return fn
    else:
        def at(fn):
            return fn

        fixed = at
    block = pl.BlockSpec((tb, cols, depth), at(lambda i: (i, 0, 0)))
    lo_spec = pl.BlockSpec((4, cols, depth), at(lambda i: (jnp.maximum(2 * i - 1, 0), 0, 0)))
    hi_spec = pl.BlockSpec((4, cols, depth), at(lambda i: (jnp.minimum(2 * i + 2, nq - 1), 0, 0)))
    whole4 = pl.BlockSpec((4, cols, depth), fixed(lambda i: (0, 0, 0)))
    yspec = pl.BlockSpec((tb, 8, depth), at(lambda i: (i, 0, 0)))
    col1 = pl.BlockSpec((tb, cols, 1), at(lambda i: (i, 0, 0)))
    slab = pl.BlockSpec((tb, cols, depth), fixed(lambda i: (0, 0, 0)))
    smem = pl.BlockSpec(memory_space=pltpu.SMEM)
    any_spec = pl.BlockSpec(memory_space=pl.ANY)
    field = jax.ShapeDtypeStruct((rows, cols, depth), jnp.float32)
    picked = jax.ShapeDtypeStruct((rows, cols, 1), jnp.float32)
    spec_of = {S.src: smem, S.amp: smem, S.rec: col1, S.mis: col1, S.obs: col1, S.pick: col1, S.vslab: slab, S.mom: slab, S.mass: slab}

    names = [S.f, S.flo, S.fhi, S.xlo, S.xhi, S.ylo, S.yhi, S.prev, S.vel]
    in_specs = [block, lo_spec, hi_spec, whole4, whole4, yspec, yspec, block, block]
    args = [f, f, f, xlo, xhi, ylo, yhi, prev, vel]
    for key, value in extra.items():
        names.append(key)
        in_specs.append(spec_of.get(key, block))
        args.append(value)
    nf_ex = len(exchanged)
    for j, g in enumerate(exchanged):
        names.append(S.ex_f + j)
        in_specs.append(any_spec)
        args.append(g)

    outs = {
        "wave1": [(S.o_f, field, block), (S.o_dw, field, block), (S.o_pick, picked, col1)],
        "wave2": [(S.o_dw, field, block), (S.o_pick, picked, col1), (S.o_a2, field, block), (S.o_part, field, block)],
        "adjbulk": [(S.o_f, field, block)],
        "adj2": [(S.o_v, jax.ShapeDtypeStruct((tb, cols, depth), jnp.float32), slab)],
    }[kind]
    names += [o[0] for o in outs]
    out_shape = [o[1] for o in outs]
    out_specs = [o[2] for o in outs]
    scratch = [pltpu.VMEM((tb + 8, cols + 16, depth), jnp.float32)]
    names.append(S.pad)
    if kind in ("wave1", "wave2"):
        scratch.append(pltpu.VMEM((tb * cols, 128), jnp.float32))
        names.append(S.fold)
    if kind == "adj2":
        names += [S.slot_out, S.slot_in, S.rs_ss, S.rs_rs, S.rs_own, S.rl_top, S.rl_bot, S.rl_rs]
        scratch += [
            pltpu.VMEM((nblk, tb, cols, depth), jnp.float32),
            pltpu.VMEM((nblk, tb, cols, depth), jnp.float32),
            pltpu.SemaphoreType.DMA((6,)),
            pltpu.SemaphoreType.DMA((nblk,)),
            pltpu.SemaphoreType.DMA(()),
            pltpu.VMEM((tb // 2, cols, depth), jnp.float32),
            pltpu.VMEM((tb // 2, cols, depth), jnp.float32),
            pltpu.SemaphoreType.DMA((4,)),
        ]
        params = pltpu.CompilerParams(
            collective_id=collective_id, has_side_effects=True, vmem_limit_bytes=60 * 1024 * 1024
        )
    elif kind == "wave2":
        h_shapes, _ = exchange_io(1, rows, cols, depth)
        names = names[: len(names) - len(scratch)]
        names += [S.h_b + m for m in range(4)]
        names += [S.pad, S.fold]
        names += [S.stg_xlo, S.stg_xhi, S.stg_ylo, S.stg_yhi, S.h_zx, S.h_zy, S.h_ss, S.h_rs, S.h_zs]
        out_shape += h_shapes
        out_specs += [any_spec] * 4
        scratch += [
            pltpu.VMEM((4, cols, depth), jnp.float32),
            pltpu.VMEM((4, cols, depth), jnp.float32),
            pltpu.VMEM((rows, 4, depth), jnp.float32),
            pltpu.VMEM((rows, 4, depth), jnp.float32),
            pltpu.VMEM((4, cols, depth), jnp.float32),
            pltpu.VMEM((rows, 8, depth), jnp.float32),
            pltpu.SemaphoreType.DMA((rows // tb, 4)),
            pltpu.SemaphoreType.DMA((4,)),
            pltpu.SemaphoreType.DMA((4,)),
        ]
        params = pltpu.CompilerParams(
            collective_id=collective_id, has_side_effects=True, vmem_limit_bytes=60 * 1024 * 1024
        )
    elif nf_ex:
        ex_shapes, ex_scratch = exchange_io(nf_ex, rows, cols, depth)
        k = len(outs)
        names = names[: len(names) - len(scratch)]
        names += [S.ex_b + m for m in range(4 * nf_ex)]
        names += [S.pad, S.fold][: len(scratch)]
        names += [S.ex_zx, S.ex_zy, S.ex_ss, S.ex_rs, S.ex_zs]
        out_shape += ex_shapes
        out_specs += [any_spec] * len(ex_shapes)
        scratch += ex_scratch
        params = pltpu.CompilerParams(
            collective_id=collective_id, has_side_effects=True, vmem_limit_bytes=60 * 1024 * 1024
        )
    else:
        params = pltpu.CompilerParams(vmem_limit_bytes=60 * 1024 * 1024)
    n_big = sum(1 for sp in in_specs if sp is block) + 1 + sum(1 for sp in out_specs if sp is block)
    cost = pl.CostEstimate(
        flops=60 * rows * cols * depth,
        transcendentals=0,
        bytes_accessed=4 * rows * cols * depth * n_big,
    )
    result = pl.pallas_call(
        functools.partial(step_kernel, kind, tuple(names), nf_ex),
        grid=grid,
        in_specs=in_specs,
        out_specs=out_specs,
        out_shape=out_shape,
        scratch_shapes=scratch,
        compiler_params=params,
        cost_estimate=cost,
        name=f"leap_{kind}",
    )(*args)
    if kind == "wave2":
        return result[: len(outs)], result[len(outs) :]
    if nf_ex:
        own = result[: len(outs)]
        ex = result[len(outs) :]
        return own, [ex[4 * j : 4 * j + 4] for j in range(nf_ex)]
    return result


def on_device(
    velocity,
    momentum,
    mass_diag,
    u_prev,
    u_cur,
    adj_next,
    adj_cur,
    observed,
    rec_depth,
    src_cell,
    wavelet,
):
    oldest = u_prev[0]
    present = u_cur[0]
    adj_later = adj_next[0]
    adj_now = adj_cur[0]
    rec = rec_depth[0][:, :, None]
    cell = src_cell[0]
    src = src_cell[0]
    amp = wavelet[0]

    (wave_h, adj_h), full_velocity = exchange([present, adj_now], 1, velocity)
    advanced, dw1, pick_adv = leap(
        "wave1", present, *wave_h, oldest, full_velocity, {S.rec: rec, S.src: src, S.amp: amp}
    )
    (adj_bulk,), (adv_h,) = leap(
        "adjbulk", adj_now, *adj_h, adj_later, full_velocity, {}, exchanged=[advanced], collective_id=2
    )
    (dw2, pick_far, adj_two, part), adj_two_h = leap(
        "wave2",
        advanced,
        *adv_h,
        present,
        full_velocity,
        {S.rec: rec, S.src: src, S.amp: amp, S.a2raw: adj_bulk, S.obs: observed[0, 1][:, :, None]},
        collective_id=3,
    )
    (summed,) = leap(
        "adj2",
        adj_two,
        *adj_two_h,
        adj_now,
        full_velocity,
        {
            S.rec: rec,
            S.pick: pick_adv,
            S.obs: observed[0, 0][:, :, None],
            S.dw: dw1,
            S.part: part,
        },
        collective_id=0,
    )
    gradient = 2.0 / velocity * summed
    p_half = momentum - 0.5 * leap_step * gradient
    v_new = velocity + leap_step * p_half / mass_diag
    return (v_new, p_half)


def solution(mesh):
    return jax.shard_map(
        on_device,
        mesh=mesh,
        in_specs=(
            P(("row", "shot"), "col", None),
            P(("row", "shot"), "col", None),
            P(("row", "shot"), "col", None),
            P("shot", "row", "col", None),
            P("shot", "row", "col", None),
            P("shot", "row", "col", None),
            P("shot", "row", "col", None),
            P("shot", None, "row", "col"),
            P("shot", "row", "col"),
            P("shot", None),
            P("shot", None),
        ),
        out_specs=(P(("row", "shot"), "col", None), P(("row", "shot"), "col", None)),
        check_vma=False,
    )
```

```python
import functools

import jax
import jax.numpy as jnp
from jax import lax
from jax.experimental import pallas as pl
from jax.experimental.pallas import tpu as pltpu
from jax.sharding import PartitionSpec as P

STENCIL = (-205.0 / 72.0, 8.0 / 5.0, -1.0 / 5.0, 8.0 / 315.0, -1.0 / 560.0)
squared_courant = 0.012
leap_step = 0.2

class S:
    a2raw = 0
    amp = 1
    dw = 2
    ex_rs = 3
    ex_ss = 4
    ex_zs = 5
    ex_zx = 6
    ex_zy = 7
    f = 8
    fhi = 9
    flo = 10
    fold = 11
    h_rs = 12
    h_ss = 13
    h_zs = 14
    h_zx = 15
    h_zy = 16
    mass = 17
    mis = 18
    mom = 19
    o_a2 = 20
    o_dw = 21
    o_f = 22
    o_p = 23
    o_part = 24
    o_pick = 25
    o_v = 26
    obs = 27
    pad = 28
    part = 29
    prev = 30
    rec = 31
    rs_own = 32
    rs_rs = 33
    rs_ss = 34
    slot_in = 35
    slot_out = 36
    src = 37
    stg_xhi = 38
    stg_xlo = 39
    stg_yhi = 40
    stg_ylo = 41
    vel = 42
    vslab = 43
    xhi = 44
    xlo = 45
    yhi = 46
    ylo = 47
    rl_top = 90
    rl_bot = 91
    rl_rs = 92
    ex_f = 100
    ex_b = 110
    h_b = 130
    pick = 140


ROWS_PER_STEP = 8
Y_CHUNK = 8


class Exchange:

    def __init__(self, fields, bufs, zero_x, zero_y, send_sem, recv_sem, zero_sem):
        self.fields, self.bufs = fields, bufs
        self.zero_x, self.zero_y = zero_x, zero_y
        self.send_sem, self.recv_sem, self.zero_sem = send_sem, recv_sem, zero_sem
        row, nrow = lax.axis_index("row"), lax.axis_size("row")
        col, ncol = lax.axis_index("col"), lax.axis_size("col")
        self.row, self.nrow, self.col, self.ncol = row, nrow, col, ncol
        self.has = (row < nrow - 1, row > 0, col < ncol - 1, col > 0)
        self.peer = ({"row": row + 1}, {"row": row - 1}, {"col": col + 1}, {"col": col - 1})
        self.filler = (1, 0, 3, 2)

    def source(self, f, d):
        rows, cols, _ = f.shape
        if d == 0:
            return f.at[pl.ds(rows - 4, 4)]
        if d == 1:
            return f.at[pl.ds(0, 4)]
        if d == 2:
            return f.at[:, pl.ds(cols - 4, 4)]
        return f.at[:, pl.ds(0, 4)]

    def target(self, j, b):
        if b == 2:
            return self.bufs[4 * j + b].at[:, pl.ds(4, 4)]
        if b == 3:
            return self.bufs[4 * j + b].at[:, pl.ds(0, 4)]
        return self.bufs[4 * j + b]

    def remote(self, j, d):
        return pltpu.make_async_remote_copy(
            src_ref=self.source(self.fields[j], d),
            dst_ref=self.target(j, d),
            send_sem=self.send_sem.at[j, d],
            recv_sem=self.recv_sem.at[j, d],
            device_id=self.peer[d],
            device_id_type=pl.DeviceIdType.MESH,
        )

    def start(self, extra=0, first=None):
        has, row, nrow, col, ncol = self.has, self.row, self.nrow, self.col, self.ncol
        barrier = pltpu.get_barrier_semaphore()
        for d in range(4):
            @pl.when(has[d])
            def _():
                pl.semaphore_signal(barrier, inc=1, device_id=self.peer[d], device_id_type=pl.DeviceIdType.MESH)

        count = (1 - row // (nrow - 1)) + (row + nrow - 1) // nrow + (1 - col // (ncol - 1)) + (col + ncol - 1) // ncol
        pl.semaphore_wait(barrier, count + extra)
        if first is not None:
            first()

        for j in range(len(self.fields)):
            for d in range(4):
                @pl.when(has[d])
                def _():
                    self.remote(j, d).start()

        @pl.when(jnp.logical_not(has[0] & has[1]))
        def _():
            self.zero_x[...] = jnp.zeros_like(self.zero_x)

        @pl.when(jnp.logical_not(has[2] & has[3]))
        def _():
            self.zero_y[...] = jnp.zeros_like(self.zero_y)

        for j in range(len(self.fields)):
            for b in range(4):
                @pl.when(jnp.logical_not(has[self.filler[b]]))
                def _():
                    zero = self.zero_x if b < 2 else self.zero_y
                    copy = pltpu.make_async_copy(zero, self.bufs[4 * j + b], self.zero_sem.at[j, b])
                    copy.start()
                    copy.wait()

    def finish(self):
        has = self.has
        for j in range(len(self.fields)):
            for d in range(4):
                @pl.when(has[d])
                def _():
                    self.remote(j, d).wait_send()
            for b in range(4):
                @pl.when(has[self.filler[b]])
                def _():
                    self.remote(j, b).wait_recv()


def exchange_io(nf, rows, cols, depth):
    shapes = []
    for _ in range(nf):
        shapes += [
            jax.ShapeDtypeStruct((4, cols, depth), jnp.float32),
            jax.ShapeDtypeStruct((4, cols, depth), jnp.float32),
            jax.ShapeDtypeStruct((rows, 8, depth), jnp.float32),
            jax.ShapeDtypeStruct((rows, 8, depth), jnp.float32),
        ]
    scratch = [
        pltpu.VMEM((4, cols, depth), jnp.float32),
        pltpu.VMEM((rows, 8, depth), jnp.float32),
        pltpu.SemaphoreType.DMA((nf, 4)),
        pltpu.SemaphoreType.DMA((nf, 4)),
        pltpu.SemaphoreType.DMA((nf, 4)),
    ]
    return shapes, scratch


def exchange_kernel(nf, gather, *refs):
    if not gather:
        ex = Exchange(refs[:nf], refs[nf : 5 * nf], *refs[5 * nf :])
        ex.start()
        ex.finish()
        return
    vel = refs[nf]
    bufs = refs[nf + 1 : 5 * nf + 1]
    full = refs[5 * nf + 1]
    ag_ss, ag_rs, ag_own = refs[-3:]
    ex = Exchange(refs[:nf], bufs, *refs[5 * nf + 2 : -3])
    me, n = lax.axis_index("shot"), lax.axis_size("shot")
    rows = vel.shape[0]
    barrier = pltpu.get_barrier_semaphore()
    for d in range(1, n):
        pl.semaphore_signal(barrier, inc=1, device_id={"shot": lax.rem(me + d, n)}, device_id_type=pl.DeviceIdType.MESH)

    def send(d):
        peer = lax.rem(me + d, n)
        return pltpu.make_async_remote_copy(
            src_ref=vel,
            dst_ref=full.at[pl.ds(pl.multiple_of(me * rows, rows), rows)],
            send_sem=ag_ss.at[d],
            recv_sem=ag_rs.at[me],
            device_id={"shot": peer},
            device_id_type=pl.DeviceIdType.MESH,
        )

    def gather_first():
        for d in range(1, n):
            send(d).start()

    ex.start(extra=n - 1, first=gather_first)
    own = pltpu.make_async_copy(vel, full.at[pl.ds(pl.multiple_of(me * rows, rows), rows)], ag_own)
    own.start()
    ex.finish()
    for d in range(1, n):
        send(d).wait_send()
    own.wait()
    for d in range(1, n):
        src = lax.rem(me + d, n)
        pltpu.make_async_remote_copy(
            src_ref=vel,
            dst_ref=full.at[pl.ds(pl.multiple_of(src * rows, rows), rows)],
            send_sem=ag_ss.at[d],
            recv_sem=ag_rs.at[src],
            device_id={"shot": src},
            device_id_type=pl.DeviceIdType.MESH,
        ).wait_recv()


def exchange(fields, collective_id, velocity=None):
    nf = len(fields)
    rows, cols, depth = fields[0].shape
    any_spec = pl.BlockSpec(memory_space=pl.ANY)
    shapes, scratch = exchange_io(nf, rows, cols, depth)
    args = list(fields)
    gather = velocity is not None
    if gather:
        n = lax.axis_size("shot")
        args.append(velocity)
        shapes = shapes + [jax.ShapeDtypeStruct((n * velocity.shape[0],) + velocity.shape[1:], jnp.float32)]
        scratch = scratch + [pltpu.SemaphoreType.DMA((n,)), pltpu.SemaphoreType.DMA((n,)), pltpu.SemaphoreType.DMA(())]
    outs = pl.pallas_call(
        functools.partial(exchange_kernel, nf, gather),
        in_specs=[any_spec] * len(args),
        out_specs=[any_spec] * len(shapes),
        out_shape=shapes,
        scratch_shapes=scratch,
        compiler_params=pltpu.CompilerParams(collective_id=collective_id, has_side_effects=True),
        name=f"halo_exchange_{collective_id}",
    )(*args)
    halos = [outs[4 * j : 4 * j + 4] for j in range(nf)]
    if gather:
        return halos, outs[-1]
    return halos


class HaloSender:

    def __init__(self, ref, nblk, tb):
        self.ref, self.nblk, self.tb = ref, nblk, tb
        row, nrow = lax.axis_index("row"), lax.axis_size("row")
        col, ncol = lax.axis_index("col"), lax.axis_size("col")
        self.row, self.nrow, self.col, self.ncol = row, nrow, col, ncol
        self.has = (row < nrow - 1, row > 0, col < ncol - 1, col > 0)
        self.peer = ({"row": row + 1}, {"row": row - 1}, {"col": col + 1}, {"col": col - 1})
        self.filler = (1, 0, 3, 2)
        self.bufs = [ref[S.h_b + b] for b in range(4)]

    def copy(self, d, blk):
        ref, tb = self.ref, self.tb
        rows_here = pl.ds(pl.multiple_of(blk * tb, tb), tb)
        if d == 0:
            src, dst, sem = ref[S.stg_xlo], self.bufs[0], ref[S.h_ss].at[0, 0]
        elif d == 1:
            src, dst, sem = ref[S.stg_xhi], self.bufs[1], ref[S.h_ss].at[0, 1]
        elif d == 2:
            src, dst = ref[S.stg_ylo].at[rows_here], self.bufs[2].at[rows_here, pl.ds(4, 4)]
            sem = ref[S.h_ss].at[blk, 2]
        else:
            src, dst = ref[S.stg_yhi].at[rows_here], self.bufs[3].at[rows_here, pl.ds(0, 4)]
            sem = ref[S.h_ss].at[blk, 3]
        return pltpu.make_async_remote_copy(
            src_ref=src,
            dst_ref=dst,
            send_sem=sem,
            recv_sem=ref[S.h_rs].at[d],
            device_id=self.peer[d],
            device_id_type=pl.DeviceIdType.MESH,
        )

    def whole(self, b):
        ref = self.ref
        src = {0: ref[S.stg_xlo], 1: ref[S.stg_xhi], 2: ref[S.stg_ylo], 3: ref[S.stg_yhi]}[b]
        dst = {0: self.bufs[0], 1: self.bufs[1], 2: self.bufs[2].at[:, pl.ds(4, 4)], 3: self.bufs[3].at[:, pl.ds(0, 4)]}[b]
        return pltpu.make_async_remote_copy(
            src_ref=src,
            dst_ref=dst,
            send_sem=ref[S.h_ss].at[0, b],
            recv_sem=ref[S.h_rs].at[b],
            device_id=self.peer[b],
            device_id_type=pl.DeviceIdType.MESH,
        )

    def begin(self):
        ref, has, row, nrow, col, ncol = self.ref, self.has, self.row, self.nrow, self.col, self.ncol
        barrier = pltpu.get_barrier_semaphore()
        for d in range(4):
            @pl.when(has[d])
            def _():
                pl.semaphore_signal(barrier, inc=1, device_id=self.peer[d], device_id_type=pl.DeviceIdType.MESH)

        count = (1 - row // (nrow - 1)) + (row + nrow - 1) // nrow + (1 - col // (ncol - 1)) + (col + ncol - 1) // ncol
        pl.semaphore_wait(barrier, count)

        @pl.when(jnp.logical_not(has[0] & has[1]))
        def _():
            ref[S.h_zx][...] = jnp.zeros_like(ref[S.h_zx])

        @pl.when(jnp.logical_not(has[2] & has[3]))
        def _():
            ref[S.h_zy][...] = jnp.zeros_like(ref[S.h_zy])

        for b in range(4):
            @pl.when(jnp.logical_not(has[self.filler[b]]))
            def _():
                zero = ref[S.h_zx] if b < 2 else ref[S.h_zy]
                copy = pltpu.make_async_copy(zero, self.bufs[b], ref[S.h_zs].at[b])
                copy.start()
                copy.wait()

    def send_block(self, blk):
        ref, has, tb = self.ref, self.has, self.tb

        @pl.when(blk == 0)
        def _():
            ref[S.stg_xhi][...] = ref[S.o_a2][0:4]

        @pl.when(blk == self.nblk - 1)
        def _():
            ref[S.stg_xlo][...] = ref[S.o_a2][tb - 4 : tb]

        for d in (2, 3):
            @pl.when(has[d])
            def _():
                self.copy(d, blk).start()

        @pl.when(has[1] & (blk == 0))
        def _():
            self.copy(1, blk).start()

        @pl.when(has[0] & (blk == self.nblk - 1))
        def _():
            self.copy(0, blk).start()

    def finish(self):
        has = self.has
        for blk in range(self.nblk):
            for d in (2, 3):
                @pl.when(has[d])
                def _():
                    self.copy(d, blk).wait_send()

        @pl.when(has[1])
        def _():
            self.copy(1, 0).wait_send()

        @pl.when(has[0])
        def _():
            self.copy(0, self.nblk - 1).wait_send()

        for b in range(4):
            @pl.when(has[self.filler[b]])
            def _():
                self.whole(b).wait_recv()


class ReduceScatter:

    def __init__(self, ref, me, n):
        self.ref, self.me, self.n = ref, me, n
        self.up, self.down, self.far = lax.rem(me + 1, n), lax.rem(me + n - 1, n), lax.rem(me + 2, n)
        half = ref[S.slot_out].shape[1] // 2
        self.top, self.bot = pl.ds(0, half), pl.ds(half, half)

    def remote(self, src, dst, k, recv_sem, peer):
        return pltpu.make_async_remote_copy(
            src_ref=src,
            dst_ref=dst,
            send_sem=self.ref[S.rs_ss].at[k],
            recv_sem=recv_sem,
            device_id={"shot": peer},
            device_id_type=pl.DeviceIdType.MESH,
        )

    def direct(self, blk, k, peer):
        ref = self.ref
        return self.remote(ref[S.slot_out].at[blk], ref[S.slot_in].at[self.me], k, ref[S.rs_rs].at[self.me], peer)

    def relay_top(self):
        ref = self.ref
        src = ref[S.slot_out].at[self.far, self.top]
        return self.remote(src, ref[S.rl_top], 2, ref[S.rl_rs].at[0], self.up)

    def relay_bot(self):
        ref = self.ref
        src = ref[S.slot_out].at[self.far, self.bot]
        return self.remote(src, ref[S.rl_bot], 3, ref[S.rl_rs].at[1], self.down)

    def fwd_top(self):
        ref = self.ref
        dst = ref[S.slot_in].at[self.down, self.top]
        return self.remote(ref[S.rl_top], dst, 4, ref[S.rl_rs].at[2], self.up)

    def fwd_bot(self):
        ref = self.ref
        dst = ref[S.slot_in].at[self.up, self.bot]
        return self.remote(ref[S.rl_bot], dst, 5, ref[S.rl_rs].at[3], self.down)

    def begin(self):
        barrier = pltpu.get_barrier_semaphore()
        for peer in (self.up, self.down):
            pl.semaphore_signal(barrier, inc=1, device_id={"shot": peer}, device_id_type=pl.DeviceIdType.MESH)
        pl.semaphore_wait(barrier, 2)

    def at_step(self, step):
        @pl.when(step == 1)
        def _():
            self.direct(self.up, 0, self.up).start()

        @pl.when(step == 2)
        def _():
            self.relay_top().start()
            self.relay_bot().start()

        @pl.when(step == 3)
        def _():
            self.direct(self.down, 1, self.down).start()
            self.relay_top().wait_recv()
            self.relay_bot().wait_recv()
            self.fwd_top().start()
            self.fwd_bot().start()

    def finish(self):
        ref, me, n = self.ref, self.me, self.n
        own = pltpu.make_async_copy(ref[S.slot_out].at[me], ref[S.slot_in].at[me], ref[S.rs_own])
        own.start()
        self.direct(self.up, 0, self.up).wait_send()
        self.direct(self.down, 1, self.down).wait_send()
        self.relay_top().wait_send()
        self.relay_bot().wait_send()
        self.fwd_top().wait_send()
        self.fwd_bot().wait_send()
        own.wait()
        for src in (self.down, self.up):
            self.remote(ref[S.slot_out].at[src], ref[S.slot_in].at[src], 0, ref[S.rs_rs].at[src], src).wait_recv()
        far_in = ref[S.slot_in].at[self.far, self.top]
        self.remote(ref[S.rl_top], far_in, 4, ref[S.rl_rs].at[2], self.down).wait_recv()
        far_in = ref[S.slot_in].at[self.far, self.bot]
        self.remote(ref[S.rl_bot], far_in, 5, ref[S.rl_rs].at[3], self.up).wait_recv()

        slot_in = ref[S.slot_in]

        def row(r, carry):
            summed = slot_in[0, r]
            for s_ in range(1, n):
                summed = summed + slot_in[s_, r]
            ref[S.o_v][r] = summed
            return carry

        lax.fori_loop(0, slot_in.shape[1], row, 0)


def step_kernel(kind, names, nf_ex, *refs):
    ref = dict(zip(names, refs))
    if nf_ex:
        ex = Exchange(
            [ref[S.ex_f + j] for j in range(nf_ex)],
            [ref[S.ex_b + k] for k in range(4 * nf_ex)],
            *[ref[k] for k in (S.ex_zx, S.ex_zy, S.ex_ss, S.ex_rs, S.ex_zs)],
        )
    f_ref, pad = ref[S.f], ref[S.pad]
    tb, cols, depth = f_ref.shape
    n = pl.num_programs(0)
    step = pl.program_id(0)
    if kind == "adj2":
        me = lax.axis_index("shot")
        i = lax.rem(me + 1 + step, n)
        rs = ReduceScatter(ref, me, n)

        @pl.when(step == 0)
        def _():
            rs.begin()

        rs.at_step(step)
    elif kind == "wave2":
        i = lax.rem(step + n - 1, n)
    else:
        i = step

    if nf_ex:
        @pl.when(i == 0)
        def _():
            ex.start()

    lo = jnp.where(i == 0, ref[S.xlo][...], ref[S.flo][...])
    hi = jnp.where(i == n - 1, ref[S.xhi][...], ref[S.fhi][...])
    pad[0:4, 8 : 8 + cols, :] = lo
    pad[4 : 4 + tb, 8 : 8 + cols, :] = f_ref[...]
    pad[4 + tb : 8 + tb, 8 : 8 + cols, :] = hi
    pad[4 : 4 + tb, 0:8, :] = ref[S.ylo][...]
    pad[4 : 4 + tb, 8 + cols : 16 + cols, :] = ref[S.yhi][...]

    z_index = lax.broadcasted_iota(jnp.int32, (Y_CHUNK, depth), 1)
    y_index = lax.broadcasted_iota(jnp.int32, (Y_CHUNK, depth), 0)
    wave = kind in ("wave1", "wave2")
    if wave:
        src_ref = ref[S.src]
        src_x = src_ref[0] - lax.axis_index("row") * (tb * n) - i * tb
        src_y = src_ref[1] - lax.axis_index("col") * cols
        src_z = src_ref[2]
        amp = ref[S.amp][0 if kind == "wave1" else 1]

    def row(r, carry):
        for y0 in range(0, cols, Y_CHUNK):
            ys = pl.ds(y0, Y_CHUNK)
            pys = pl.ds(8 + y0, Y_CHUNK)
            c = pad[4 + r, pys, :]
            result = (3.0 * STENCIL[0]) * c
            for k in range(1, 5):
                along = pad[4 + r + k, pys, :] + pad[4 + r - k, pys, :]
                along = along + (
                    pad[4 + r, pl.ds(8 + y0 + k, Y_CHUNK), :]
                    + pad[4 + r, pl.ds(8 + y0 - k, Y_CHUNK), :]
                )
                zp = jnp.where(z_index < depth - k, pltpu.roll(c, depth - k, 1), 0.0)
                zm = jnp.where(z_index >= k, pltpu.roll(c, k, 1), 0.0)
                along = along + (zp + zm)
                result = result + STENCIL[k] * along
            v = ref[S.vel][r, ys, :]
            stiff = squared_courant * v * v
            prev = ref[S.prev][r, ys, :]
            out = 2.0 * c - prev + stiff * result
            if wave:
                at_rec = z_index == ref[S.rec][r, ys, :]
                hit = (r == src_x) & (y_index + y0 == src_y) & (z_index == src_z)
                out = out + jnp.where(hit, amp, 0.0)
                sel = jnp.where(at_rec, out, 0.0)
                folded = sel[:, 0:128]
                for t in range(128, depth, 128):
                    folded = folded + sel[:, t : t + 128]
                ref[S.fold][pl.ds(pl.multiple_of(r * cols + y0, Y_CHUNK), Y_CHUNK), :] = folded
                ref[S.o_dw][r, ys, :] = (out - 2.0 * c) + prev
                if kind == "wave1":
                    ref[S.o_f][r, ys, :] = out
            elif kind == "adjbulk":
                ref[S.o_f][r, ys, :] = out
            else:
                at_rec = z_index == ref[S.rec][r, ys, :]
                misfit = ref[S.pick][r, ys, :] - ref[S.obs][r, ys, :]
                out = out + jnp.where(at_rec, misfit, 0.0)
                ref[S.slot_out][i, r, ys, :] = ref[S.part][r, ys, :] + out * ref[S.dw][r, ys, :]
        return carry

    lax.fori_loop(0, tb, row, 0)
    if wave:
        ref[S.o_pick][...] = jnp.sum(ref[S.fold][...], axis=1, keepdims=True).reshape(ref[S.o_pick].shape)
    if kind == "wave2":
        sender = HaloSender(ref, n, tb)

        @pl.when(step == 0)
        def _():
            sender.begin()

        def inject(r, carry):
            for y0 in range(0, cols, Y_CHUNK):
                ys = pl.ds(y0, Y_CHUNK)
                at_rec = z_index == ref[S.rec][r, ys, :]
                misfit = ref[S.o_pick][r, ys, :] - ref[S.obs][r, ys, :]
                a2 = ref[S.a2raw][r, ys, :] + jnp.where(at_rec, misfit, 0.0)
                ref[S.o_a2][r, ys, :] = a2
                ref[S.o_part][r, ys, :] = a2 * ref[S.o_dw][r, ys, :]
                if y0 == 0:
                    ref[S.stg_yhi][i * tb + r] = a2[0:4]
                if y0 == cols - Y_CHUNK:
                    ref[S.stg_ylo][i * tb + r] = a2[Y_CHUNK - 4 : Y_CHUNK]
            return carry

        lax.fori_loop(0, tb, inject, 0)
        sender.send_block(i)

        @pl.when(step == n - 1)
        def _():
            sender.finish()

    if nf_ex:
        @pl.when(i == n - 1)
        def _():
            ex.finish()
    if kind == "adj2":
        @pl.when(step == n - 1)
        def _():
            rs.finish()


def leap(kind, f, xlo, xhi, ylo, yhi, prev, vel, extra, exchanged=(), collective_id=None):
    rows, cols, depth = f.shape
    tb = ROWS_PER_STEP
    nblk = rows // tb
    grid = (nblk,)
    nq = rows // 4
    if kind == "adj2":
        def at(fn):
            return lambda i: fn(lax.rem(lax.axis_index("shot") + 1 + i, nblk))

        fixed = at
    elif kind == "wave2":
        def at(fn):
            return lambda i: fn(lax.rem(i + nblk - 1, nblk))

        def fixed(fn):
            return fn
    else:
        def at(fn):
            return fn

        fixed = at
    block = pl.BlockSpec((tb, cols, depth), at(lambda i: (i, 0, 0)))
    lo_spec = pl.BlockSpec((4, cols, depth), at(lambda i: (jnp.maximum(2 * i - 1, 0), 0, 0)))
    hi_spec = pl.BlockSpec((4, cols, depth), at(lambda i: (jnp.minimum(2 * i + 2, nq - 1), 0, 0)))
    whole4 = pl.BlockSpec((4, cols, depth), fixed(lambda i: (0, 0, 0)))
    yspec = pl.BlockSpec((tb, 8, depth), at(lambda i: (i, 0, 0)))
    col1 = pl.BlockSpec((tb, cols, 1), at(lambda i: (i, 0, 0)))
    slab = pl.BlockSpec((tb, cols, depth), fixed(lambda i: (0, 0, 0)))
    smem = pl.BlockSpec(memory_space=pltpu.SMEM)
    any_spec = pl.BlockSpec(memory_space=pl.ANY)
    field = jax.ShapeDtypeStruct((rows, cols, depth), jnp.float32)
    picked = jax.ShapeDtypeStruct((rows, cols, 1), jnp.float32)
    spec_of = {S.src: smem, S.amp: smem, S.rec: col1, S.mis: col1, S.obs: col1, S.pick: col1, S.vslab: slab, S.mom: slab, S.mass: slab}

    names = [S.f, S.flo, S.fhi, S.xlo, S.xhi, S.ylo, S.yhi, S.prev, S.vel]
    in_specs = [block, lo_spec, hi_spec, whole4, whole4, yspec, yspec, block, block]
    args = [f, f, f, xlo, xhi, ylo, yhi, prev, vel]
    for key, value in extra.items():
        names.append(key)
        in_specs.append(spec_of.get(key, block))
        args.append(value)
    nf_ex = len(exchanged)
    for j, g in enumerate(exchanged):
        names.append(S.ex_f + j)
        in_specs.append(any_spec)
        args.append(g)

    outs = {
        "wave1": [(S.o_f, field, block), (S.o_dw, field, block), (S.o_pick, picked, col1)],
        "wave2": [(S.o_dw, field, block), (S.o_pick, picked, col1), (S.o_a2, field, block), (S.o_part, field, block)],
        "adjbulk": [(S.o_f, field, block)],
        "adj2": [(S.o_v, jax.ShapeDtypeStruct((tb, cols, depth), jnp.float32), slab)],
    }[kind]
    names += [o[0] for o in outs]
    out_shape = [o[1] for o in outs]
    out_specs = [o[2] for o in outs]
    scratch = [pltpu.VMEM((tb + 8, cols + 16, depth), jnp.float32)]
    names.append(S.pad)
    if kind in ("wave1", "wave2"):
        scratch.append(pltpu.VMEM((tb * cols, 128), jnp.float32))
        names.append(S.fold)
    if kind == "adj2":
        names += [S.slot_out, S.slot_in, S.rs_ss, S.rs_rs, S.rs_own, S.rl_top, S.rl_bot, S.rl_rs]
        scratch += [
            pltpu.VMEM((nblk, tb, cols, depth), jnp.float32),
            pltpu.VMEM((nblk, tb, cols, depth), jnp.float32),
            pltpu.SemaphoreType.DMA((6,)),
            pltpu.SemaphoreType.DMA((nblk,)),
            pltpu.SemaphoreType.DMA(()),
            pltpu.VMEM((tb // 2, cols, depth), jnp.float32),
            pltpu.VMEM((tb // 2, cols, depth), jnp.float32),
            pltpu.SemaphoreType.DMA((4,)),
        ]
        params = pltpu.CompilerParams(
            collective_id=collective_id, has_side_effects=True, vmem_limit_bytes=60 * 1024 * 1024
        )
    elif kind == "wave2":
        h_shapes, _ = exchange_io(1, rows, cols, depth)
        names = names[: len(names) - len(scratch)]
        names += [S.h_b + m for m in range(4)]
        names += [S.pad, S.fold]
        names += [S.stg_xlo, S.stg_xhi, S.stg_ylo, S.stg_yhi, S.h_zx, S.h_zy, S.h_ss, S.h_rs, S.h_zs]
        out_shape += h_shapes
        out_specs += [any_spec] * 4
        scratch += [
            pltpu.VMEM((4, cols, depth), jnp.float32),
            pltpu.VMEM((4, cols, depth), jnp.float32),
            pltpu.VMEM((rows, 4, depth), jnp.float32),
            pltpu.VMEM((rows, 4, depth), jnp.float32),
            pltpu.VMEM((4, cols, depth), jnp.float32),
            pltpu.VMEM((rows, 8, depth), jnp.float32),
            pltpu.SemaphoreType.DMA((rows // tb, 4)),
            pltpu.SemaphoreType.DMA((4,)),
            pltpu.SemaphoreType.DMA((4,)),
        ]
        params = pltpu.CompilerParams(
            collective_id=collective_id, has_side_effects=True, vmem_limit_bytes=60 * 1024 * 1024
        )
    elif nf_ex:
        ex_shapes, ex_scratch = exchange_io(nf_ex, rows, cols, depth)
        k = len(outs)
        names = names[: len(names) - len(scratch)]
        names += [S.ex_b + m for m in range(4 * nf_ex)]
        names += [S.pad, S.fold][: len(scratch)]
        names += [S.ex_zx, S.ex_zy, S.ex_ss, S.ex_rs, S.ex_zs]
        out_shape += ex_shapes
        out_specs += [any_spec] * len(ex_shapes)
        scratch += ex_scratch
        params = pltpu.CompilerParams(
            collective_id=collective_id, has_side_effects=True, vmem_limit_bytes=60 * 1024 * 1024
        )
    else:
        params = pltpu.CompilerParams(vmem_limit_bytes=60 * 1024 * 1024)
    n_big = sum(1 for sp in in_specs if sp is block) + 1 + sum(1 for sp in out_specs if sp is block)
    cost = pl.CostEstimate(
        flops=60 * rows * cols * depth,
        transcendentals=0,
        bytes_accessed=4 * rows * cols * depth * n_big,
    )
    result = pl.pallas_call(
        functools.partial(step_kernel, kind, tuple(names), nf_ex),
        grid=grid,
        in_specs=in_specs,
        out_specs=out_specs,
        out_shape=out_shape,
        scratch_shapes=scratch,
        compiler_params=params,
        cost_estimate=cost,
        name=f"leap_{kind}",
    )(*args)
    if kind == "wave2":
        return result[: len(outs)], result[len(outs) :]
    if nf_ex:
        own = result[: len(outs)]
        ex = result[len(outs) :]
        return own, [ex[4 * j : 4 * j + 4] for j in range(nf_ex)]
    return result


def on_device(
    velocity,
    momentum,
    mass_diag,
    u_prev,
    u_cur,
    adj_next,
    adj_cur,
    observed,
    rec_depth,
    src_cell,
    wavelet,
):
    oldest = u_prev[0]
    present = u_cur[0]
    adj_later = adj_next[0]
    adj_now = adj_cur[0]
    rec = rec_depth[0][:, :, None]
    cell = src_cell[0]
    src = src_cell[0]
    amp = wavelet[0]

    (wave_h, adj_h), full_velocity = exchange([present, adj_now], 1, velocity)
    advanced, dw1, pick_adv = leap(
        "wave1", present, *wave_h, oldest, full_velocity, {S.rec: rec, S.src: src, S.amp: amp}
    )
    (adj_bulk,), (adv_h,) = leap(
        "adjbulk", adj_now, *adj_h, adj_later, full_velocity, {}, exchanged=[advanced], collective_id=2
    )
    (dw2, pick_far, adj_two, part), adj_two_h = leap(
        "wave2",
        advanced,
        *adv_h,
        present,
        full_velocity,
        {S.rec: rec, S.src: src, S.amp: amp, S.a2raw: adj_bulk, S.obs: observed[0, 1][:, :, None]},
        collective_id=3,
    )
    (summed,) = leap(
        "adj2",
        adj_two,
        *adj_two_h,
        adj_now,
        full_velocity,
        {
            S.rec: rec,
            S.pick: pick_adv,
            S.obs: observed[0, 0][:, :, None],
            S.dw: dw1,
            S.part: part,
        },
        collective_id=0,
    )
    gradient = 2.0 / velocity * summed
    p_half = momentum - 0.5 * leap_step * gradient
    v_new = velocity + leap_step * p_half / mass_diag
    return (v_new, p_half)


def solution(mesh):
    return jax.shard_map(
        on_device,
        mesh=mesh,
        in_specs=(
            P(("row", "shot"), "col", None),
            P(("row", "shot"), "col", None),
            P(("row", "shot"), "col", None),
            P("shot", "row", "col", None),
            P("shot", "row", "col", None),
            P("shot", "row", "col", None),
            P("shot", "row", "col", None),
            P("shot", None, "row", "col"),
            P("shot", "row", "col"),
            P("shot", None),
            P("shot", None),
        ),
        out_specs=(P(("row", "shot"), "col", None), P(("row", "shot"), "col", None)),
        check_vma=False,
    )
```
